32 devices in a mesh: dp: 4 (over x, core), expert: 2 (over y), tensor: 4 (over z).
Axes of the slice: x: 2, y: 2, z: 4, core: 2. Of those that a mesh axis runs over, the one named last changes fastest.
Arguments:
- tokens: bfloat16 [8, 256, 2048], P(('dp', 'expert')), may hold values from -6 to 6
- cotangent: bfloat16 [8, 256, 2048], P(('dp', 'expert')), may hold values from -6 to 6
- head_counts: int32 [8], P(('dp', 'expert')), may hold values from 4 to 16, as said below
- positions: int32 [8, 256], P(('dp', 'expert')), may hold values from 0 to 255, as said below
- buckets: int32 [8, 256], P(('dp', 'expert')), may hold values from 0 to 3, as said below
- in_master: float32 [3, 2048, 2048], P(None, ('dp', 'expert'), 'tensor'), may hold values from -0.13258252 to 0.13258252
- out_master: float32 [2048, 2048], P('tensor', ('dp', 'expert')), may hold values from -1.5 to 1.5
- up_master: float32 [4, 2048, 2048], P(None, ('dp', 'expert'), 'tensor'), may hold values from -0.13258252 to 0.13258252
- down_master: float32 [4, 2048, 2048], P(None, 'tensor', ('dp', 'expert')), may hold values from -0.06629126 to 0.06629126
- norm_master: float32 [4, 2048], P(None, ('dp', 'expert')), may hold values from -0.6 to 2.4
- in_first: float32 [3, 2048, 2048], P(None, ('dp', 'expert'), 'tensor'), may hold values from -32 to 32
- out_first: float32 [2048, 2048], P('tensor', ('dp', 'expert')), may hold values from -6 to 6
- up_first: float32 [4, 2048, 2048], P(None, ('dp', 'expert'), 'tensor'), may hold values from -16 to 16
- down_first: float32 [4, 2048, 2048], P(None, 'tensor', ('dp', 'expert')), may hold values from -28 to 28
- norm_first: float32 [4, 2048], P(None, ('dp', 'expert')), may hold values from -32 to 32
- in_second: float32 [3, 2048, 2048], P(None, ('dp', 'expert'), 'tensor'), may hold values from 1.024 to 16.384
- out_second: float32 [2048, 2048], P('tensor', ('dp', 'expert')), may hold values from 0.0065536 to 0.1048576
- up_second: float32 [4, 2048, 2048], P(None, ('dp', 'expert'), 'tensor'), may hold values from 0.3072 to 4.9152
- down_second: float32 [4, 2048, 2048], P(None, 'tensor', ('dp', 'expert')), may hold values from 0.9216 to 14.7456
- norm_second: float32 [4, 2048], P(None, ('dp', 'expert')), may hold values from 1.024 to 16.384
Outputs:
- output: float32 [8, 256, 2048], P(('dp', 'expert'))
- input_grad: float32 [8, 256, 2048], P(('dp', 'expert'))
- bucket_share: float32 [4], replicated
- lamb_norms: float32 [2, 8], replicated
- in_weight: float32 [3, 2048, 2048], P(None, ('dp', 'expert'), 'tensor')
- out_weight: float32 [2048, 2048], P('tensor', ('dp', 'expert'))
- up_weight: float32 [4, 2048, 2048], P(None, ('dp', 'expert'), 'tensor')
- down_weight: float32 [4, 2048, 2048], P(None, 'tensor', ('dp', 'expert'))
- norm_weight: float32 [4, 2048], P(None, ('dp', 'expert'))
- in_moment: float32 [3, 2048, 2048], P(None, ('dp', 'expert'), 'tensor')
- out_moment: float32 [2048, 2048], P('tensor', ('dp', 'expert'))
- up_moment: float32 [4, 2048, 2048], P(None, ('dp', 'expert'), 'tensor')
- down_moment: float32 [4, 2048, 2048], P(None, 'tensor', ('dp', 'expert'))
- norm_moment: float32 [4, 2048], P(None, ('dp', 'expert'))
- in_square: float32 [3, 2048, 2048], P(None, ('dp', 'expert'), 'tensor')
- out_square: float32 [2048, 2048], P('tensor', ('dp', 'expert'))
- up_square: float32 [4, 2048, 2048], P(None, ('dp', 'expert'), 'tensor')
- down_square: float32 [4, 2048, 2048], P(None, 'tensor', ('dp', 'expert'))
- norm_square: float32 [4, 2048], P(None, ('dp', 'expert'))
The draws below stay inside these ranges and needn't reach their ends.
Inputs may be any that keep to these rules, and one draw needn't show every extreme that they name: `head_counts`: each is a whole multiple of a quarter of 16. Within each sequence positions count up by one from 0 and restart at 0 at a document's first token; each sequence's first token has position 0. `buckets`: in each sequence no bucket id is carried by more than 80 tokens; one bucket id, the same for all sequences, is carried by exactly 80 tokens of every sequence.
All inputs are finite; a program needn't handle non-finite values.
Results may differ from the reference program's by a relative error of at most 0.014.
The reference program's roundings to bfloat16 on the way count: a program that leaves them out, or rounds other values in their place, can miss the bound.
Values may be sent and summed in bfloat16 or wider, within the bound.
A program may use at most 448 MiB of HBM per device.

```python
import math
import jax
import jax.numpy as jnp
from jax import lax

D = 2048
HEADS = 16
HEAD_DIM = 128
FF = 8192
QUARTER = 2048
BUCKETS = 4
LEN = 256
MOST = 80
SEQS = 8
TOKENS = 2048
STEP = 10


def ramped(key, shape, ramp_axis, fan_in):
    base_draw = jnp.clip(jax.random.normal(key, shape, jnp.float32), -4.0, 4.0)
    ramp_count = shape[ramp_axis]
    ramp_row = 0.5 + jnp.arange(ramp_count, dtype=jnp.float32) / ramp_count
    view_shape = tuple((ramp_count if axis_pos == ramp_axis else 1 for axis_pos in range(len(shape))))
    return base_draw * ramp_row.reshape(view_shape) * fan_in ** (-0.5)


def draw_in_master(key, part):
    return ramped(key, (3, D, D), 1, D)


def draw_out_master(key, part):
    return ramped(key, (D, D), 1, 16)


def draw_up_master(key, part):
    return ramped(key, (BUCKETS, D, QUARTER), 1, D)


def draw_down_master(key, part):
    return ramped(key, (BUCKETS, QUARTER, D), 2, FF)


def draw_norm_master(key, part):
    gain_key, shift_key = jax.random.split(key)
    fraction = jnp.arange(D, dtype=jnp.float32) / D
    gain_noise = jnp.clip(jax.random.normal(gain_key, (2, D), jnp.float32), -3.0, 3.0)
    shift_noise = jnp.clip(jax.random.normal(shift_key, (2, D), jnp.float32), -3.0, 3.0)
    gain_rows = (0.6 + 1.2 * fraction)[None, :] * (1.0 + 0.1 * gain_noise)
    shift_rows = 0.2 * shift_noise
    return jnp.stack([gain_rows[0], shift_rows[0], gain_rows[1], shift_rows[1]])


def draw_head_counts(key, part):
    quarter_heads = HEADS // 4
    counts_drawn = quarter_heads * jax.random.randint(key, (SEQS,), 1, 5)
    counts_drawn = counts_drawn.at[0].set(HEADS).at[SEQS - 1].set(quarter_heads)
    return counts_drawn.astype(jnp.int32)


def draw_positions(key, part):
    key_index = jnp.arange(LEN, dtype=jnp.int32)
    marks = jax.random.randint(key, (SEQS, LEN), 0, LEN) < 4
    starts_doc = marks | (key_index == 0)[None, :]
    starts_doc = starts_doc.at[0].set(key_index == 0)
    last_start = lax.cummax(jnp.where(starts_doc, key_index[None, :], 0), axis=1)
    return (key_index[None, :] - last_start).astype(jnp.int32)


def draw_buckets(key, part):
    perm_key, count_key, shuffle_key = jax.random.split(key, 3)
    first_key, second_key = jax.random.split(count_key)
    bucket_order = jax.random.permutation(perm_key, 4).astype(jnp.int32)
    rest_rows = LEN - MOST
    first_count = jax.random.randint(first_key, (SEQS,), max(0, rest_rows - 2 * MOST), min(MOST, rest_rows) + 1)
    remain_rows = rest_rows - first_count
    second_count = jax.random.randint(second_key, (SEQS,), jnp.maximum(0, remain_rows - MOST), jnp.minimum(MOST, remain_rows) + 1)
    key_index = jnp.arange(LEN, dtype=jnp.int32)[None, :]
    labels = (key_index >= MOST).astype(jnp.int32) + (key_index >= MOST + first_count[:, None]).astype(jnp.int32) + (key_index >= MOST + first_count[:, None] + second_count[:, None]).astype(jnp.int32)
    seq_keys = jax.random.split(shuffle_key, SEQS)

    def shuffle_row(key_one, label_row):
        return label_row[jax.random.permutation(key_one, LEN)]
    mixed_labels = jax.vmap(shuffle_row)(seq_keys, labels)
    return bucket_order[mixed_labels].astype(jnp.int32)


def level_of(own_key, shape, shards, least, largest):
    level = 1.0
    for position, parts in shards:
        heights = jax.random.uniform(jax.random.fold_in(jax.random.fold_in(own_key, 6), position), (parts,), jnp.float32, least / len(shards), largest / len(shards))
        level = level * jnp.repeat(jnp.exp(heights), shape[position] // parts).reshape((-1,) + (1,) * (len(shape) - 1 - position))
    return level


def centred(own_key, shape, width, reach, cuts=(), kind=jnp.bfloat16):
    array = jax.random.normal(own_key, shape, jnp.float32) * width
    if len(cuts) > 0:
        array = level_of(own_key, shape, cuts, -0.22, 0.18) * array
    return jnp.clip(array, min=-reach, max=reach).astype(kind)


def setup_inputs(seed: int = 0) -> dict:
    key_of = jax.random.split(jax.random.key(seed), 21)
    return {
        "tokens": centred(key_of[0], (SEQS, LEN, D), 1.0, 6.0, ((0, 8),)),
        "cotangent": centred(key_of[1], (SEQS, LEN, D), 1.0, 6.0, ((0, 8),)),
        "head_counts": draw_head_counts(jax.random.fold_in(key_of[20], 71), 0),
        "positions": draw_positions(jax.random.fold_in(key_of[20], 71), 0),
        "buckets": draw_buckets(jax.random.fold_in(key_of[20], 71), 0),
        "in_master": draw_in_master(jax.random.fold_in(key_of[20], 71), 0),
        "out_master": draw_out_master(jax.random.fold_in(key_of[20], 71), 0),
        "up_master": draw_up_master(jax.random.fold_in(key_of[20], 71), 0),
        "down_master": draw_down_master(jax.random.fold_in(key_of[20], 71), 0),
        "norm_master": draw_norm_master(jax.random.fold_in(key_of[20], 71), 0),
        "in_first": centred(key_of[10], (3, D, D), (0.11 * TOKENS ** 0.5), 32.0, ((1, 8), (2, 4)), jnp.float32),
        "out_first": centred(key_of[11], (D, D), (0.009 * TOKENS ** 0.5), 6.0, ((0, 4), (1, 8)), jnp.float32),
        "up_first": centred(key_of[12], (BUCKETS, D, QUARTER), (0.06 * TOKENS ** 0.5), 16.0, ((1, 8), (2, 4)), jnp.float32),
        "down_first": centred(key_of[13], (BUCKETS, QUARTER, D), (0.1 * TOKENS ** 0.5), 28.0, ((1, 4), (2, 8)), jnp.float32),
        "norm_first": centred(key_of[14], (4, D), (0.11 * TOKENS ** 0.5), 32.0, ((1, 8),), jnp.float32),
        "in_second": jnp.clip(jnp.exp(math.log(16.384) - 2.7725887 * jax.random.uniform(key_of[15], (3, D, D), jnp.float32) ** level_of(key_of[15], (3, D, D), ((1, 8), (2, 4)), -0.2, 0.2)), 1.024, 16.384),
        "out_second": jnp.clip(jnp.exp(math.log(0.1048576) - 2.7725887 * jax.random.uniform(key_of[16], (D, D), jnp.float32) ** level_of(key_of[16], (D, D), ((0, 4), (1, 8)), -0.2, 0.2)), 0.0065536, 0.1048576),
        "up_second": jnp.clip(jnp.exp(math.log(4.9152) - 2.7725887 * jax.random.uniform(key_of[17], (BUCKETS, D, QUARTER), jnp.float32) ** level_of(key_of[17], (BUCKETS, D, QUARTER), ((1, 8), (2, 4)), -0.2, 0.2)), 0.3072, 4.9152),
        "down_second": jnp.clip(jnp.exp(math.log(14.7456) - 2.7725887 * jax.random.uniform(key_of[18], (BUCKETS, QUARTER, D), jnp.float32) ** level_of(key_of[18], (BUCKETS, QUARTER, D), ((1, 4), (2, 8)), -0.2, 0.2)), 0.9216, 14.7456),
        "norm_second": jnp.clip(jnp.exp(math.log(16.384) - 2.7725887 * jax.random.uniform(key_of[19], (4, D), jnp.float32) ** level_of(key_of[19], (4, D), ((1, 8),), -0.2, 0.2)), 1.024, 16.384),
    }


@jax.custom_vjp
def low(v):
    return lax.optimization_barrier(v.astype(jnp.bfloat16)).astype(jnp.float32)

@jax.custom_vjp
def low_back(v):
    return v

def low_keep(v):
    return (low(v), None)

def low_pass(kept, grad):
    return (grad,)

def back_keep(v):
    return (v, None)

def back_low(kept, grad):
    return (low(grad),)
low.defvjp(low_keep, low_pass)
low_back.defvjp(back_keep, back_low)
HIGHEST = lax.Precision.HIGHEST
NORM_EPS = 1e-05
BETA_FIRST = 0.9
BETA_SECOND = 0.999
ADAM_EPS = 1e-06
WEIGHT_DECAY = 0.01
LEARN_RATE = 0.25
MASKED = -1e+30
ROPE_BASE = 10000.0

def layer_norm(values, gain_row, shift_row):
    center = values - lax.optimization_barrier(jnp.mean(values, -1, keepdims=True))
    variance = lax.optimization_barrier(jnp.mean(center * center, -1, keepdims=True))
    return center * lax.rsqrt(variance + NORM_EPS) * gain_row + shift_row

def rope_angles(position_row):
    freq_index = jnp.arange(HEAD_DIM // 2, dtype=jnp.float32)
    inverse = jnp.exp(freq_index * (-2.0 * jnp.log(ROPE_BASE) / HEAD_DIM))
    return position_row.astype(jnp.float32)[:, None] * inverse[None, :]

def rotary(values, angles):
    half_dim = values.shape[-1] // 2
    cosine = jnp.cos(angles)[:, None, :]
    sine_part = jnp.sin(angles)[:, None, :]
    first_half = values[..., :half_dim]
    second_half = values[..., half_dim:]
    return jnp.concatenate([first_half * cosine - second_half * sine_part, second_half * cosine + first_half * sine_part], -1)

def forward_sequence(params, tokens_seq, head_total, position_row, bucket_row):
    in_master, out_master, up_master, down_master, norm_master = params
    in_work = low(in_master)
    out_work = low(out_master)
    up_work = low(up_master)
    down_work = low(down_master)
    norm_work = low(norm_master)
    first_norm = low(layer_norm(tokens_seq, norm_work[0], norm_work[1]))
    projected = low_back(jnp.einsum('td,jde->jte', first_norm, in_work, precision=HIGHEST))
    projected = projected.reshape(3, LEN, HEADS, HEAD_DIM)
    angles = rope_angles(position_row)
    queries = low(rotary(projected[0], angles) * HEAD_DIM ** (-0.5))
    key_rows = low(rotary(projected[1], angles))
    value_rows = low(projected[2])
    block_rows = min(512, LEN)
    key_index = jnp.arange(LEN, dtype=jnp.int32)

    def one_block(block_start):
        query_block = lax.dynamic_slice_in_dim(queries, block_start, block_rows, 0)
        query_index = block_start + jnp.arange(block_rows, dtype=jnp.int32)
        doc_offset = lax.dynamic_slice_in_dim(position_row, block_start, block_rows, 0)
        allowed = (key_index[None, :] <= query_index[:, None]) & (key_index[None, :] >= (query_index - doc_offset)[:, None])
        scores = low_back(jnp.einsum('qhd,khd->hqk', query_block, key_rows, precision=HIGHEST))
        scores = jnp.where(allowed[None], scores, MASKED)
        attn_weights = jax.nn.softmax(scores, axis=-1)
        return jnp.einsum('hqk,khd->qhd', low(attn_weights), value_rows, precision=HIGHEST)
    starts = jnp.arange(LEN // block_rows, dtype=jnp.int32) * block_rows
    attended = lax.map(jax.checkpoint(one_block), starts).reshape(LEN, HEADS, HEAD_DIM)
    active = (jnp.arange(HEADS, dtype=jnp.int32) < head_total).astype(jnp.float32)
    attended = low(low_back(attended * active[None, :, None])).reshape(LEN, HEADS * HEAD_DIM)
    branch = low_back(jnp.dot(attended, out_work, precision=HIGHEST))
    middle = tokens_seq + branch
    second_norm = low(low_back(layer_norm(middle, norm_work[2], norm_work[3])))
    mixed_sum = jnp.zeros_like(middle)
    for quarter in range(4):
        live = (bucket_row >= quarter)[:, None]
        hidden = low_back(jnp.where(live, jnp.dot(second_norm, up_work[quarter], precision=HIGHEST), 0.0))
        squared = low(jnp.square(jnp.maximum(hidden, 0.0)))
        mixed_sum = mixed_sum + jnp.dot(squared, down_work[quarter], precision=HIGHEST)
    return middle + low(low_back(mixed_sum))

def adam_terms(weight, gradient, first_old, second_old):
    first_new = BETA_FIRST * first_old + (1.0 - BETA_FIRST) * gradient
    second_new = BETA_SECOND * second_old + (1.0 - BETA_SECOND) * gradient * gradient
    update = first_new / (1.0 - BETA_FIRST ** STEP) / (jnp.sqrt(second_new / (1.0 - BETA_SECOND ** STEP)) + ADAM_EPS) + WEIGHT_DECAY * weight
    return (update, first_new, second_new)

def reference(tokens, cotangent, head_counts, positions, buckets, in_master, out_master, up_master, down_master, norm_master, in_first, out_first, up_first, down_first, norm_first, in_second, out_second, up_second, down_second, norm_second):
    params = (in_master, out_master, up_master, down_master, norm_master)

    def per_sequence(carried, inputs):
        tokens_seq, cot_seq, head_total, position_row, bucket_row = inputs

        def forward(weights, tokens_in):
            return forward_sequence(weights, tokens_in, head_total, position_row, bucket_row)
        result, pullback = jax.vjp(forward, params, tokens_seq.astype(jnp.float32))
        grad_params, grad_tokens = pullback(cot_seq.astype(jnp.float32))
        carried = jax.tree.map(jnp.add, carried, grad_params)
        return (carried, (result, grad_tokens))
    zero_grads = jax.tree.map(jnp.zeros_like, params)
    grad_sums, (outputs, input_grad) = lax.scan(per_sequence, zero_grads, (tokens, cotangent, head_counts, positions, buckets))
    onehot = (buckets[..., None] == jnp.arange(BUCKETS, dtype=jnp.int32)).astype(jnp.float32)
    bucket_share = lax.optimization_barrier(jnp.sum(onehot, (0, 1))) / (SEQS * LEN)
    firsts = (in_first, out_first, up_first, down_first, norm_first)
    seconds = (in_second, out_second, up_second, down_second, norm_second)
    adam_out = [adam_terms(params[member], grad_sums[member], firsts[member], seconds[member]) for member in range(5)]
    weight_norms = jnp.concatenate([jnp.stack([jnp.sqrt(jnp.sum(params[member] * params[member])) for member in range(4)]), jnp.sqrt(lax.optimization_barrier(jnp.sum(norm_master * norm_master, 1)))])
    update_norms = jnp.concatenate([jnp.stack([jnp.sqrt(jnp.sum(adam_out[member][0] * adam_out[member][0])) for member in range(4)]), jnp.sqrt(lax.optimization_barrier(jnp.sum(adam_out[4][0] * adam_out[4][0], 1)))])
    ratios = weight_norms / update_norms
    new_weights = [params[member] - LEARN_RATE * ratios[member] * adam_out[member][0] for member in range(4)]
    norm_new = norm_master - LEARN_RATE * ratios[4:, None] * adam_out[4][0]
    lamb_norms = jnp.stack([weight_norms, update_norms])
    return (outputs, input_grad, bucket_share, lamb_norms, new_weights[0], new_weights[1], new_weights[2], new_weights[3], norm_new, adam_out[0][1], adam_out[1][1], adam_out[2][1], adam_out[3][1], adam_out[4][1], adam_out[0][2], adam_out[1][2], adam_out[2][2], adam_out[3][2], adam_out[4][2])
```

```python
import jax
import jax.numpy as jnp
from jax import lax
from jax.experimental import pallas as pl
from jax.experimental.pallas import tpu as pltpu
from jax.sharding import PartitionSpec as P

HEAD_DIM = 128
STEP = 10


NORM_EPS = 1e-05
BETA_FIRST = 0.9
BETA_SECOND = 0.999
ADAM_EPS = 1e-06
WEIGHT_DECAY = 0.01
LEARN_RATE = 0.25
MASKED = -1e30
ROPE_BASE = 10000.0


def layer_norm(values, gain_row, shift_row):
    center = values - jnp.mean(values, -1, keepdims=True)
    variance = jnp.mean(center * center, -1, keepdims=True)
    inv_std = lax.rsqrt(variance + NORM_EPS)
    normed = center * inv_std
    return (normed * gain_row + shift_row, normed, inv_std)


def norm_back_rows(grad_out, normed, inv_std, gain_row):
    scaled = grad_out * gain_row
    inner_part = (
        scaled
        - jnp.mean(scaled, -1, keepdims=True)
        - normed * jnp.mean(scaled * normed, -1, keepdims=True)
    )
    return (inner_part * inv_std, jnp.sum(grad_out * normed, 0), jnp.sum(grad_out, 0))


def rope_angles(position_row):
    freq_index = jnp.arange(HEAD_DIM // 2, dtype=jnp.float32)
    inverse = jnp.exp(freq_index * (-2.0 * jnp.log(ROPE_BASE) / HEAD_DIM))
    return position_row.astype(jnp.float32)[:, None] * inverse[None, :]


def rotary(values, angles, sign_value):
    half_dim = values.shape[-1] // 2
    cosine = jnp.cos(angles)[:, None, :]
    sine_part = sign_value * jnp.sin(angles)[:, None, :]
    first_half = values[..., :half_dim]
    second_half = values[..., half_dim:]
    return jnp.concatenate(
        [
            first_half * cosine - second_half * sine_part,
            second_half * cosine + first_half * sine_part,
        ],
        -1,
    )


def block_mask(key_index, position_row, block_start, block_rows):
    query_index = block_start + jnp.arange(block_rows, dtype=jnp.int32)
    return (key_index[None, :] <= query_index[:, None]) & (
        key_index[None, :] >= (query_index - position_row)[:, None]
    )


def attend_forward(queries, key_rows, value_rows, position_row, block_rows):
    length = queries.shape[0]
    key_index = jnp.arange(length, dtype=jnp.int32)

    def one_block(block_start):
        allowed = block_mask(key_index, position_row, block_start, block_rows)
        scores = jnp.einsum("qhd,khd->hqk", queries, key_rows, preferred_element_type=jnp.float32)
        scores = jnp.where(allowed[None], scores, MASKED)
        row_peak = jnp.max(scores, -1, keepdims=True)
        exp_scores = jnp.exp(scores - row_peak)
        row_total = jnp.sum(exp_scores, -1, keepdims=True)
        attn_weights = (exp_scores / row_total).astype(jnp.bfloat16)
        block_out = jnp.einsum(
            "hqk,khd->qhd", attn_weights, value_rows, preferred_element_type=jnp.float32
        )
        return (block_out, row_peak[..., 0] + jnp.log(row_total[..., 0]))

    starts = jnp.arange(length // block_rows, dtype=jnp.int32) * block_rows
    block_outs, log_totals = lax.map(one_block, starts)
    return (block_outs.reshape(queries.shape), log_totals, starts)


def attend_backward(
    queries, key_rows, value_rows, position_row, grad_heads, log_totals, starts, block_rows
):
    length = queries.shape[0]
    key_index = jnp.arange(length, dtype=jnp.int32)

    def one_block(carried, inputs):
        block_start, block_log = inputs
        allowed = block_mask(key_index, position_row, block_start, block_rows)
        scores = jnp.einsum("qhd,khd->hqk", queries, key_rows, preferred_element_type=jnp.float32)
        scores = jnp.where(allowed[None], scores, MASKED)
        attn_probs = jnp.exp(scores - block_log[..., None])
        grad_probs = jnp.einsum(
            "qhd,khd->hqk", grad_heads, value_rows, preferred_element_type=jnp.float32
        )
        row_inner = jnp.sum(attn_probs * grad_probs, -1, keepdims=True)
        grad_scores = (attn_probs * (grad_probs - row_inner)).astype(jnp.bfloat16)
        grad_query = jnp.einsum(
            "hqk,khd->qhd", grad_scores, key_rows, preferred_element_type=jnp.float32
        )
        grad_keys = carried[0] + jnp.einsum(
            "hqk,qhd->khd", grad_scores, queries, preferred_element_type=jnp.float32
        )
        grad_values = carried[1] + jnp.einsum(
            "hqk,qhd->khd",
            attn_probs.astype(jnp.bfloat16),
            grad_heads,
            preferred_element_type=jnp.float32,
        )
        return ((grad_keys, grad_values), grad_query)

    start_state = (jnp.zeros(key_rows.shape, jnp.float32), jnp.zeros(value_rows.shape, jnp.float32))
    (grad_keys, grad_values), grad_query = lax.scan(one_block, start_state, (starts, log_totals))
    return (grad_query.reshape(queries.shape), grad_keys, grad_values)


def gather_rows(values, source_rows):
    padded = jnp.concatenate([values, jnp.zeros((1, values.shape[1]), values.dtype)], 0)
    return padded[source_rows]


def ffn_forward(rows_in, bucket, up_work, down_work):
    row_count = rows_in.shape[0]
    mixed_sum = jnp.zeros((row_count, down_work.shape[2]), jnp.float32)
    hiddens = []
    for quarter in range(4):

        def live_part():
            hidden = jnp.dot(rows_in, up_work[quarter], preferred_element_type=jnp.float32)
            squared = jnp.square(jnp.maximum(hidden, 0.0)).astype(jnp.bfloat16)
            return (
                hidden,
                jnp.dot(squared, down_work[quarter], preferred_element_type=jnp.float32),
            )

        def dead_part():
            return (
                jnp.zeros((row_count, up_work.shape[2]), jnp.float32),
                jnp.zeros_like(mixed_sum),
            )

        hidden, contribution = lax.cond(bucket >= quarter, live_part, dead_part)
        hiddens.append(hidden)
        mixed_sum = mixed_sum + contribution
    return (mixed_sum, hiddens)


def ffn_backward(rows_in, grads_in, bucket, hiddens, up_work, down_work):
    grad_rows = jnp.zeros((rows_in.shape[0], up_work.shape[1]), jnp.float32)
    grad_up = []
    grad_down = []
    for quarter in range(4):
        hidden = hiddens[quarter]

        def live_part():
            rectified = jnp.maximum(hidden, 0.0)
            squared = jnp.square(rectified).astype(jnp.bfloat16)
            grad_square = jnp.einsum(
                "rd,ud->ru", grads_in, down_work[quarter], preferred_element_type=jnp.float32
            )
            grad_hidden = (grad_square * 2.0 * rectified).astype(jnp.bfloat16)
            return (
                jnp.einsum("rd,ru->du", rows_in, grad_hidden, preferred_element_type=jnp.float32),
                jnp.einsum("ru,rd->ud", squared, grads_in, preferred_element_type=jnp.float32),
                jnp.einsum(
                    "ru,du->rd", grad_hidden, up_work[quarter], preferred_element_type=jnp.float32
                ),
            )

        def dead_part():
            return (
                jnp.zeros(up_work.shape[1:], jnp.float32),
                jnp.zeros(down_work.shape[1:], jnp.float32),
                jnp.zeros_like(grad_rows),
            )

        part_up, part_down, part_rows = lax.cond(bucket >= quarter, live_part, dead_part)
        grad_up.append(part_up)
        grad_down.append(part_down)
        grad_rows = grad_rows + part_rows
    return (grad_rows, jnp.stack(grad_up), jnp.stack(grad_down))


def ffn_total(partial_value):
    return lax.psum(partial_value, "tensor")


def ffn_grad_total(partial_value):
    return lax.psum(partial_value, "tensor")


def adam_terms(weight, gradient, first_old, second_old):
    first_new = BETA_FIRST * first_old + (1.0 - BETA_FIRST) * gradient
    second_new = BETA_SECOND * second_old + (1.0 - BETA_SECOND) * gradient * gradient
    update = (
        first_new
        / (1.0 - BETA_FIRST**STEP)
        / (jnp.sqrt(second_new / (1.0 - BETA_SECOND**STEP)) + ADAM_EPS)
        + WEIGHT_DECAY * weight
    )
    return (update, first_new, second_new)


def finish(output, input_grad, bucket_share, masters, firsts, seconds, grad_shards, tensor_count):
    norm_master = masters[4]
    adam_out = [
        adam_terms(masters[member], grad_shards[member], firsts[member], seconds[member])
        for member in range(5)
    ]
    weight_sq = jnp.concatenate(
        [
            jnp.stack([jnp.sum(masters[member] * masters[member]) for member in range(4)]),
            jnp.sum(norm_master * norm_master, 1) / tensor_count,
        ]
    )
    update_sq = jnp.concatenate(
        [
            jnp.stack([jnp.sum(adam_out[member][0] * adam_out[member][0]) for member in range(4)]),
            jnp.sum(adam_out[4][0] * adam_out[4][0], 1) / tensor_count,
        ]
    )
    weight_tot, update_tot = lax.psum((weight_sq, update_sq), ("dp", "expert", "tensor"))
    weight_norms = jnp.sqrt(weight_tot)
    update_norms = jnp.sqrt(update_tot)
    ratios = weight_norms / update_norms
    new_weights = [
        masters[member] - LEARN_RATE * ratios[member] * adam_out[member][0] for member in range(4)
    ]
    norm_new = norm_master - LEARN_RATE * ratios[4:, None] * adam_out[4][0]
    lamb_norms = jnp.stack([weight_norms, update_norms])
    return (
        output[None],
        input_grad[None],
        bucket_share,
        lamb_norms,
        new_weights[0],
        new_weights[1],
        new_weights[2],
        new_weights[3],
        norm_new,
        adam_out[0][1],
        adam_out[1][1],
        adam_out[2][1],
        adam_out[3][1],
        adam_out[4][1],
        adam_out[0][2],
        adam_out[1][2],
        adam_out[2][2],
        adam_out[3][2],
        adam_out[4][2],
    )


def body(
    tokens,
    cotangent,
    head_counts,
    positions,
    buckets,
    in_master,
    out_master,
    up_master,
    down_master,
    norm_master,
    in_first,
    out_first,
    up_first,
    down_first,
    norm_first,
    in_second,
    out_second,
    up_second,
    down_second,
    norm_second,
):
    in_work, out_work, up_work, down_work, norm_work = (
        lax.all_gather(in_master.astype(jnp.bfloat16), ("dp", "expert"), axis=1, tiled=True),
        lax.all_gather(out_master.astype(jnp.bfloat16), ("dp", "expert"), axis=1, tiled=True),
        lax.all_gather(up_master.astype(jnp.bfloat16), ("dp", "expert"), axis=1, tiled=True),
        lax.all_gather(down_master.astype(jnp.bfloat16), ("dp", "expert"), axis=2, tiled=True),
        lax.all_gather(norm_master.astype(jnp.bfloat16), ("dp", "expert"), axis=1, tiled=True),
    )
    length = tokens.shape[1]
    model_width = tokens.shape[2]
    heads_here = in_work.shape[2] // HEAD_DIM
    block_rows = min(512, length)
    head_scale = HEAD_DIM ** (-0.5)
    groups_data = lax.axis_size("dp") * lax.axis_size("expert")
    tensor_count = lax.axis_size("tensor")
    experts = lax.axis_size("expert")
    norm_gains = norm_work.astype(jnp.float32)
    inputs = tokens[0].astype(jnp.float32)
    first_norm, first_hat, first_inv = layer_norm(inputs, norm_gains[0], norm_gains[1])
    first_in = first_norm.astype(jnp.bfloat16)
    projected = jnp.einsum("td,jde->jte", first_in, in_work, preferred_element_type=jnp.float32)
    projected = projected.reshape(3, length, heads_here, HEAD_DIM)
    angles = rope_angles(positions[0])
    queries = (rotary(projected[0], angles, 1.0) * head_scale).astype(jnp.bfloat16)
    key_rows = rotary(projected[1], angles, 1.0).astype(jnp.bfloat16)
    value_rows = projected[2].astype(jnp.bfloat16)
    head_ids = lax.axis_index("tensor") * heads_here + jnp.arange(heads_here, dtype=jnp.int32)
    active = (head_ids < head_counts[0]).astype(jnp.float32)
    head_outs, log_totals, starts = attend_forward(
        queries, key_rows, value_rows, positions[0], block_rows
    )
    attended = (
        (head_outs * active[None, :, None])
        .astype(jnp.bfloat16)
        .reshape(length, heads_here * HEAD_DIM)
    )
    attn_part = jnp.dot(attended, out_work, preferred_element_type=jnp.float32)
    middle = inputs + lax.psum(attn_part, "tensor")
    second_norm, second_hat, second_inv = layer_norm(middle, norm_gains[2], norm_gains[3])
    second_in = second_norm.astype(jnp.bfloat16)
    bucket_ids = buckets[0]
    onehot = (bucket_ids[:, None] == jnp.arange(4, dtype=jnp.int32)[None, :]).astype(jnp.int32)
    bucket_rank = jnp.sum((jnp.cumsum(onehot, 0) - onehot) * onehot, 1)
    local_counts = jnp.sum(onehot, 0).astype(jnp.float32)
    bucket_share = lax.psum(local_counts, ("dp", "expert")) / (length * groups_data)
    most_rows = 5 * length // 16
    owner_group = max(experts // 4, 1)
    per_owner = max(4 // experts, 1)
    slot_rows = (most_rows + owner_group - 1) // owner_group
    capacity = per_owner * slot_rows
    slot_of = (
        (bucket_ids // per_owner * owner_group + bucket_rank % owner_group) * capacity
        + bucket_ids % per_owner * slot_rows
        + bucket_rank // owner_group
    )
    slot_total = experts * capacity
    source_rows = (
        jnp.full((slot_total,), length, jnp.int32)
        .at[slot_of]
        .set(jnp.arange(length, dtype=jnp.int32))
    )
    outgoing = gather_rows(second_in, source_rows).reshape(experts, capacity, model_width)
    incoming = lax.all_to_all(outgoing, "expert", split_axis=0, concat_axis=0, tiled=True).reshape(
        experts, per_owner, slot_rows, model_width
    )
    owner_index = lax.axis_index("expert")
    owned_ids = [owner_index // owner_group * per_owner + member for member in range(per_owner)]
    ffn_inputs = [
        incoming[:, member].reshape(experts * slot_rows, model_width) for member in range(per_owner)
    ]
    results = [
        ffn_forward(ffn_inputs[member], owned_ids[member], up_work, down_work)
        for member in range(per_owner)
    ]
    partial_value = jnp.stack(
        [
            results[member][0].reshape(experts, slot_rows, model_width)
            for member in range(per_owner)
        ],
        1,
    )
    summed = ffn_total(partial_value.reshape(experts, capacity, model_width)).astype(jnp.bfloat16)
    returned = lax.all_to_all(summed, "expert", split_axis=0, concat_axis=0, tiled=True)
    branch_out = returned.reshape(slot_total, model_width)[slot_of]
    output = middle + branch_out.astype(jnp.float32)
    grad_branch = cotangent[0]
    outgoing_grad = gather_rows(grad_branch, source_rows).reshape(experts, capacity, model_width)
    incoming_grad = lax.all_to_all(
        outgoing_grad, "expert", split_axis=0, concat_axis=0, tiled=True
    ).reshape(experts, per_owner, slot_rows, model_width)
    ffn_grads = [
        incoming_grad[:, member].reshape(experts * slot_rows, model_width)
        for member in range(per_owner)
    ]
    back_parts = [
        ffn_backward(
            ffn_inputs[member],
            ffn_grads[member],
            owned_ids[member],
            results[member][1],
            up_work,
            down_work,
        )
        for member in range(len(owned_ids))
    ]
    grad_up = back_parts[0][1]
    grad_down = back_parts[0][2]
    for member in range(1, len(owned_ids)):
        grad_up = grad_up + back_parts[member][1]
        grad_down = grad_down + back_parts[member][2]
    rows_back = jnp.stack(
        [
            back_parts[member][0].reshape(experts, slot_rows, model_width)
            for member in range(per_owner)
        ],
        1,
    )
    summed_back = ffn_grad_total(rows_back.reshape(experts, capacity, model_width)).astype(
        jnp.bfloat16
    )
    returned_back = lax.all_to_all(summed_back, "expert", split_axis=0, concat_axis=0, tiled=True)
    grad_second = returned_back.reshape(slot_total, model_width)[slot_of].astype(jnp.float32)
    grad_mid_norm, gain_second, shift_second = norm_back_rows(
        grad_second, second_hat, second_inv, norm_gains[2]
    )
    grad_middle = grad_branch.astype(jnp.float32) + grad_mid_norm
    grad_attn = grad_middle.astype(jnp.bfloat16)
    grad_attended = jnp.einsum("td,ed->te", grad_attn, out_work, preferred_element_type=jnp.float32)
    grad_out_w = jnp.einsum("te,td->ed", attended, grad_attn, preferred_element_type=jnp.float32)
    grad_heads = (
        grad_attended.astype(jnp.bfloat16).reshape(length, heads_here, HEAD_DIM)
        * active.astype(jnp.bfloat16)[None, :, None]
    )
    grad_query, grad_keys, grad_values = attend_backward(
        queries, key_rows, value_rows, positions[0], grad_heads, log_totals, starts, block_rows
    )
    grad_projected = jnp.stack(
        [
            rotary(grad_query * head_scale, angles, -1.0),
            rotary(grad_keys, angles, -1.0),
            grad_values,
        ]
    )
    grad_projected = grad_projected.reshape(3, length, heads_here * HEAD_DIM).astype(jnp.bfloat16)
    grad_in_w = jnp.einsum(
        "td,jte->jde", first_in, grad_projected, preferred_element_type=jnp.float32
    )
    grad_first_part = jnp.einsum(
        "jte,jde->td", grad_projected, in_work, preferred_element_type=jnp.float32
    )
    grad_first = lax.psum(grad_first_part, "tensor")
    grad_input_norm, gain_first, shift_first = norm_back_rows(
        grad_first, first_hat, first_inv, norm_gains[0]
    )
    input_grad = grad_middle + grad_input_norm
    grad_norm = jnp.stack([gain_first, shift_first, gain_second, shift_second])
    in_sum, out_sum, up_sum, down_sum, norm_sum = (
        lax.psum_scatter(grad_in_w, ("dp", "expert"), scatter_dimension=1, tiled=True),
        lax.psum_scatter(grad_out_w, ("dp", "expert"), scatter_dimension=1, tiled=True),
        lax.psum_scatter(grad_up, ("dp", "expert"), scatter_dimension=1, tiled=True),
        lax.psum_scatter(grad_down, ("dp", "expert"), scatter_dimension=2, tiled=True),
        lax.psum_scatter(grad_norm, ("dp", "expert"), scatter_dimension=1, tiled=True),
    )
    masters = (in_master, out_master, up_master, down_master, norm_master)
    firsts = (in_first, out_first, up_first, down_first, norm_first)
    seconds = (in_second, out_second, up_second, down_second, norm_second)
    grad_shards = (in_sum, out_sum, up_sum, down_sum, norm_sum)
    return finish(output, input_grad, bucket_share, masters, firsts, seconds, grad_shards, tensor_count)


MESH = pl.DeviceIdType.MESH
ANY = pl.BlockSpec(memory_space=pl.ANY)
VM = pl.BlockSpec(memory_space=pltpu.VMEM)
F32 = jnp.float32
BF16 = jnp.bfloat16
SUM_ONE = BF16
SUM_TWO = BF16
SUM_FFN = BF16
SUM_THREE = BF16
CHUNK = 256
HALF = 128
ROWS = 64


class Here:
    def __init__(self):
        d = lax.axis_index("dp")
        self.x, self.c = d // 2, lax.rem(d, 2)
        self.y = lax.axis_index("expert")
        self.z = lax.axis_index("tensor")

    def plane(self, dx, dc, dy):
        x = 1 - self.x if dx else self.x
        c = 1 - self.c if dc else self.c
        y = 1 - self.y if dy else self.y
        return (x * 2 + c, y, self.z)

    def chunk(self, dx, dc, dy):
        x = 1 - self.x if dx else self.x
        c = 1 - self.c if dc else self.c
        y = 1 - self.y if dy else self.y
        return (x * 2 + c) * 2 + y

    def chunk_of(self, dx, dy, core):
        x = 1 - self.x if dx else self.x
        y = 1 - self.y if dy else self.y
        return (x * 2 + core) * 2 + y

    def along(self, step):
        return (self.x * 2 + self.c, self.y, lax.rem(self.z + step, 4))

    def behind(self, step):
        return lax.rem(self.z + 4 - step, 4)


PARTNER = (0, 1, 0)
PLANE = [(a, b, g) for a in (0, 1) for b in (0, 1) for g in (0, 1) if a + b + g > 0]
SIDES = [(1, 0, 0), (1, 1, 0), (0, 0, 1), (0, 1, 1)]


def greet(here, plane_peers, tensor_peers):
    barrier = pltpu.get_barrier_semaphore()
    for peer in plane_peers:
        pl.semaphore_signal(barrier, inc=1, device_id=here.plane(*peer), device_id_type=MESH)
    for step in tensor_peers:
        pl.semaphore_signal(barrier, inc=1, device_id=here.along(step), device_id_type=MESH)
    pl.semaphore_wait(barrier, len(plane_peers) + len(tensor_peers))


def push(src, dst, send, recv, device):
    copy = pltpu.make_async_remote_copy(
        src_ref=src, dst_ref=dst, send_sem=send, recv_sem=recv, device_id=device, device_id_type=MESH
    )
    copy.start()
    return copy


def block(index, size):
    return pl.ds(pl.multiple_of(index * size, size), size)


def rows_chunk(ref, k):
    return ref.at[:, block(k, CHUNK), :]


def rows_part(ref, k, part):
    return ref.at[:, pl.ds(pl.multiple_of(k * CHUNK + part * HALF, HALF), HALF), :]


def cols_chunk(ref, k):
    return ref.at[:, :, block(k, CHUNK)]


def cols_part(ref, k, part):
    return ref.at[:, part * HALF : part * HALF + HALF, block(k, CHUNK)]


class Gather:
    def __init__(self, here, by_rows, shard, whole, first, relay, local):
        self.here, self.by_rows, self.shard, self.whole = here, by_rows, shard, whole
        self.first, self.relay, self.local = first, relay, local
        self.copies = []

    def half(self, core):
        if self.by_rows:
            return self.shard.at[:, :, block(core, CHUNK)]
        return self.shard.at[:, block(core, CHUNK), :]

    def chunk(self, k):
        return rows_chunk(self.whole, k) if self.by_rows else cols_chunk(self.whole, k)

    def part(self, k, part):
        return rows_part(self.whole, k, part) if self.by_rows else cols_part(self.whole, k, part)

    def start(self):
        here = self.here
        mine = self.chunk(here.chunk(0, 0, 0))
        for index, side in enumerate(SIDES + [PARTNER]):
            core = 1 - here.c if side[1] else here.c
            self.copies.append(
                push(
                    self.half(core),
                    mine,
                    self.first.at[0, index],
                    self.first.at[1, index],
                    here.plane(*side),
                )
            )
        self.own = pltpu.make_async_copy(self.half(here.c), mine, self.local)
        self.own.start()

    def forward(self):
        here = self.here
        self.onward = []
        for index in range(4):
            side = SIDES[index]
            self.copies[index].wait_recv()
            part = 0 if side[0] else 1
            where = self.part(here.chunk(*side), part)
            target = (0, 0, 1) if side[0] else (1, 0, 0)
            self.onward.append(
                push(
                    where,
                    where,
                    self.relay.at[0, index],
                    self.relay.at[1, index],
                    here.plane(*target),
                )
            )

    def finish(self):
        for index in range(4):
            self.copies[index].wait_send()
        self.copies[4].wait()
        self.own.wait()
        for copy in self.onward:
            copy.wait()


def gather_sems():
    return [
        pltpu.SemaphoreType.DMA((2, 5)),
        pltpu.SemaphoreType.DMA((2, 4)),
        pltpu.SemaphoreType.DMA,
    ]


class Scatter:
    def __init__(self, here, by_rows, grad, total, bufs):
        self.here, self.by_rows, self.grad, self.total = here, by_rows, grad, total
        (self.own, self.got, self.got_two, self.final) = bufs[:4]
        (self.load_sem, self.one_sem, self.two_sem, self.last_sem, self.local) = bufs[4:]

    def part(self, k, part):
        return rows_part(self.grad, k, part) if self.by_rows else cols_part(self.grad, k, part)

    def start(self):
        here = self.here
        self.first = []
        for side in (0, 1):
            near, far = ((1, 0), (1, 1)) if side == 0 else ((0, 1), (1, 1))
            target = here.plane(1, 0, 0) if side == 0 else here.plane(0, 0, 1)
            for slot in range(4):
                chip = far if slot >= 2 else near
                src = self.part(here.chunk_of(chip[0], chip[1], slot % 2), side)
                index = side * 4 + slot
                self.first.append(
                    push(
                        src,
                        self.got.at[index],
                        self.one_sem.at[0, index],
                        self.one_sem.at[1, index],
                        target,
                    )
                )
        self.loads = []
        for side in (0, 1):
            for slot in range(4):
                chip = (0, 0) if slot < 2 else ((0, 1) if side == 0 else (1, 0))
                src = self.part(here.chunk_of(chip[0], chip[1], slot % 2), side)
                index = side * 4 + slot
                copy = pltpu.make_async_copy(src, self.own.at[index], self.load_sem.at[index])
                copy.start()
                self.loads.append(copy)

    def middle(self):
        here = self.here
        self.second = []
        for side in (0, 1):
            target = here.plane(0, 0, 1) if side == 0 else here.plane(1, 0, 0)
            for slot in (2, 3):
                index = side * 4 + slot
                self.loads[index].wait()
                self.first[index].wait_recv()
                self.own[index] = (
                    self.own[index].astype(F32) + self.got[index].astype(F32)
                ).astype(BF16)
                two = side * 2 + slot - 2
                self.second.append(
                    push(
                        self.own.at[index],
                        self.got_two.at[two],
                        self.two_sem.at[0, two],
                        self.two_sem.at[1, two],
                        target,
                    )
                )

    def last(self):
        here = self.here
        for side in (0, 1):
            for slot in (0, 1):
                index = side * 4 + slot
                two = side * 2 + slot
                self.loads[index].wait()
                self.first[index].wait_recv()
                self.second[two].wait_recv()
                self.final[slot, :, side * HALF : side * HALF + HALF, :] = (
                    self.own[index].astype(F32) + self.got[index].astype(F32)
                ) + self.got_two[two].astype(F32)
        if self.by_rows:
            where = self.total.at[:, :, block(here.c, CHUNK)]
        else:
            where = self.total.at[:, block(here.c, CHUNK), :]
        self.keep = pltpu.make_async_copy(self.final.at[here.c], where, self.local)
        self.keep.start()
        self.give = push(
            self.final.at[1 - here.c],
            where,
            self.last_sem.at[0],
            self.last_sem.at[1],
            here.plane(*PARTNER),
        )

    def finish(self):
        for copy in self.first:
            copy.wait_send()
        for copy in self.second:
            copy.wait_send()
        self.keep.wait()
        self.give.wait()


def scatter_scratch(width):
    return [
        pltpu.VMEM((8, width, HALF, CHUNK), BF16),
        pltpu.VMEM((8, width, HALF, CHUNK), BF16),
        pltpu.VMEM((4, width, HALF, CHUNK), BF16),
        pltpu.VMEM((2, width, CHUNK, CHUNK), F32),
        pltpu.SemaphoreType.DMA((8,)),
        pltpu.SemaphoreType.DMA((2, 8)),
        pltpu.SemaphoreType.DMA((2, 4)),
        pltpu.SemaphoreType.DMA((2,)),
        pltpu.SemaphoreType.DMA,
    ]


SCATTER = 9


class TensorSum:
    def __init__(self, here, part, bufs):
        self.here, self.part = here, part
        self.pair, self.out, self.inn, self.pair_sem, self.sem = bufs

    def start(self):
        here = self.here
        self.swap = push(
            self.part.at[1 - here.c],
            self.pair,
            self.pair_sem.at[0],
            self.pair_sem.at[1],
            here.plane(*PARTNER),
        )

    def spread(self):
        here = self.here
        self.swap.wait_recv()
        self.sent = []
        for step in (2, 1, 3):
            rows = block(lax.rem(here.z + step, 4), ROWS)
            self.out[step - 1] = (
                self.part[here.c, rows, :].astype(F32) + self.pair[rows, :].astype(F32)
            ).astype(self.out.dtype)
            self.sent.append(
                push(
                    self.out.at[step - 1],
                    self.inn.at[step - 1],
                    self.sem.at[0, step - 1],
                    self.sem.at[1, step - 1],
                    here.along(step),
                )
            )

    def result(self):
        here = self.here
        rows = block(here.z, ROWS)
        total = self.part[here.c, rows, :].astype(F32) + self.pair[rows, :].astype(F32)
        for copy in self.sent:
            copy.wait_recv()
        for step in (1, 2, 3):
            total = total + self.inn[step - 1].astype(F32)
        return total

    def finish(self):
        self.swap.wait_send()
        for copy in self.sent:
            copy.wait_send()


def sum_scratch(length, width, kind):
    return [
        pltpu.VMEM((length, width), kind),
        pltpu.VMEM((3, ROWS, width), kind),
        pltpu.VMEM((3, ROWS, width), kind),
        pltpu.SemaphoreType.DMA((2,)),
        pltpu.SemaphoreType.DMA((2, 3)),
    ]


class TensorGather:
    def __init__(self, here, mine, whole, sem, pair_sem, local):
        self.here, self.mine, self.whole = here, mine, whole
        self.sem, self.pair_sem, self.local = sem, pair_sem, local

    def start(self):
        here = self.here
        place = self.whole.at[here.c, block(here.z, ROWS), :]
        self.sent = []
        for step in (2, 1, 3):
            self.sent.append(
                push(
                    self.mine,
                    place,
                    self.sem.at[0, step - 1],
                    self.sem.at[1, step - 1],
                    here.along(step),
                )
            )
        self.shared = [
            push(
                self.mine,
                place,
                self.pair_sem.at[0, 0],
                self.pair_sem.at[1, 0],
                here.plane(*PARTNER),
            )
        ]
        self.own = pltpu.make_async_copy(self.mine, place, self.local)
        self.own.start()

    def forward(self):
        here = self.here
        for index, step in enumerate((2, 1, 3)):
            self.sent[index].wait_recv()
            place = self.whole.at[here.c, block(here.behind(step), ROWS), :]
            self.shared.append(
                push(
                    place,
                    place,
                    self.pair_sem.at[0, step],
                    self.pair_sem.at[1, step],
                    here.plane(*PARTNER),
                )
            )

    def finish(self):
        for copy in self.sent:
            copy.wait_send()
        for copy in self.shared:
            copy.wait()
        self.own.wait()


def normed(values):
    center = values - jnp.mean(values, -1, keepdims=True)
    variance = jnp.mean(center * center, -1, keepdims=True)
    inv_std = lax.rsqrt(variance + NORM_EPS)
    return (center * inv_std, inv_std)


def norm_row(packs, row):
    return jnp.concatenate([packs[k, row : row + 1, :] for k in range(8)], 1)


def params(ident, limit=60):
    return pltpu.CompilerParams(
        collective_id=ident, has_side_effects=True, vmem_limit_bytes=limit << 20
    )


def first_kernel(
    tok, cot, table, pack, wq, wo,
    n1, both_cot, tables, packs, wq_all, wo_all,
    n1_own, small, pair, local, q0, q1, q2, o0, o1, o2,
):
    here = Here()
    greet(here, PLANE, ())
    me = here.chunk(0, 0, 0)
    packed = []
    for index, peer in enumerate(PLANE):
        packed.append(
            push(pack, packs.at[me], small.at[0, index], small.at[1, index], here.plane(*peer))
        )
    packs[pl.ds(me, 1)] = pack[...][None]
    gather_q = Gather(here, True, wq, wq_all, q0, q1, q2)
    gather_o = Gather(here, False, wo, wo_all, o0, o1, o2)
    gather_q.start()
    gather_o.start()
    partner = here.plane(*PARTNER)
    shared = [
        push(table, tables.at[here.c], pair.at[0, 0], pair.at[1, 0], partner),
        push(cot, both_cot.at[here.c], pair.at[0, 1], pair.at[1, 1], partner),
    ]
    kept = [
        pltpu.make_async_copy(table, tables.at[here.c], local.at[0]),
        pltpu.make_async_copy(cot, both_cot.at[here.c], local.at[1]),
    ]
    for copy in kept:
        copy.start()
    for copy in packed:
        copy.wait()
    gain, shift = norm_row(packs, 0), norm_row(packs, 1)

    def rows_step(i, carry):
        rows = block(i, 32)
        hat, _ = normed(tok[rows, :].astype(F32))
        n1_own[rows, :] = (hat * gain + shift).astype(BF16)
        return carry

    lax.fori_loop(0, tok.shape[0] // 32, rows_step, 0)
    shared.append(push(n1_own, n1.at[here.c], pair.at[0, 2], pair.at[1, 2], partner))
    kept.append(pltpu.make_async_copy(n1_own, n1.at[here.c], local.at[2]))
    kept[2].start()
    gather_q.forward()
    gather_o.forward()
    gather_q.finish()
    gather_o.finish()
    for copy in kept:
        copy.wait()
    for copy in shared:
        copy.wait()


def first_call(tok, cot, table, pack, wq, wo):
    length, width = tok.shape
    return pl.pallas_call(
        first_kernel,
        out_shape=(
            jax.ShapeDtypeStruct((2, length, width), BF16),
            jax.ShapeDtypeStruct((2, length, width), BF16),
            jax.ShapeDtypeStruct((2,) + table.shape, F32),
            jax.ShapeDtypeStruct((8,) + pack.shape, F32),
            jax.ShapeDtypeStruct((wq.shape[0], width, CHUNK), BF16),
            jax.ShapeDtypeStruct((1, CHUNK, width), BF16),
        ),
        in_specs=[VM, ANY, ANY, VM, ANY, ANY],
        out_specs=(ANY, ANY, ANY, VM, ANY, ANY),
        scratch_shapes=[
            pltpu.VMEM((length, width), BF16),
            pltpu.SemaphoreType.DMA((2, 7)),
            pltpu.SemaphoreType.DMA((2, 3)),
            pltpu.SemaphoreType.DMA((3,)),
        ]
        + gather_sems()
        + gather_sems(),
        compiler_params=params(1),
        name="gather_attention",
    )(tok, cot, table, pack, wq, wo)


def second_kernel(
    part, tok, packs, wu, wd,
    n2, mid, wu_all, wd_all,
    n2_own, s0, s1, s2, s3, s4, tg, tgp, tgl, u0, u1, u2, d0, d1, d2,
):
    here = Here()
    greet(here, SIDES + [PARTNER], (1, 2, 3))
    total = TensorSum(here, part, (s0, s1, s2, s3, s4))
    total.start()
    gather_u = Gather(here, True, wu, wu_all, u0, u1, u2)
    gather_d = Gather(here, False, wd, wd_all, d0, d1, d2)
    gather_u.start()
    gather_d.start()
    total.spread()
    middle = tok[...].astype(F32) + total.result()
    mid[...] = middle
    hat, _ = normed(middle)
    n2_own[...] = (hat * norm_row(packs, 2) + norm_row(packs, 3)).astype(BF16)
    gather = TensorGather(here, n2_own, n2, tg, tgp, tgl)
    gather.start()
    gather.forward()
    gather_u.forward()
    gather_d.forward()
    total.finish()
    gather.finish()
    gather_u.finish()
    gather_d.finish()


def tensor_gather_sems():
    return [
        pltpu.SemaphoreType.DMA((2, 3)),
        pltpu.SemaphoreType.DMA((2, 4)),
        pltpu.SemaphoreType.DMA,
    ]


def second_call(part, tok, packs, wu, wd):
    _, length, width = part.shape
    return pl.pallas_call(
        second_kernel,
        out_shape=(
            jax.ShapeDtypeStruct((2, length, width), BF16),
            jax.ShapeDtypeStruct((ROWS, width), F32),
            jax.ShapeDtypeStruct((wu.shape[0], width, CHUNK), BF16),
            jax.ShapeDtypeStruct((wd.shape[0], CHUNK, width), BF16),
        ),
        in_specs=[VM, VM, VM, ANY, ANY],
        out_specs=(ANY, VM, ANY, ANY),
        scratch_shapes=[pltpu.VMEM((ROWS, width), BF16)]
        + sum_scratch(length, width, part.dtype)
        + tensor_gather_sems()
        + gather_sems()
        + gather_sems(),
        compiler_params=params(2),
        name="gather_ffn",
    )(part, tok, packs, wu, wd)


def norm_back(grad_out, hat, inv_std, gain):
    scaled = grad_out * gain
    inner = (
        scaled
        - jnp.mean(scaled, -1, keepdims=True)
        - hat * jnp.mean(scaled * hat, -1, keepdims=True)
    )
    return (
        inner * inv_std,
        jnp.sum(grad_out * hat, 0, keepdims=True),
        jnp.sum(grad_out, 0, keepdims=True),
    )


def third_kernel(
    dn2, ffn, mid, cot, packs, gu, gd,
    gm, dmid, out_own, sums, up_sum, down_sum,
    gm_own, *rest,
):
    here = Here()
    greet(here, [(1, 0, 0), (0, 0, 1), PARTNER], (1, 2, 3))
    back = TensorSum(here, dn2, rest[0:5])
    branch = TensorSum(here, ffn, rest[5:10])
    scatter_u = Scatter(here, True, gu, up_sum, rest[13 : 13 + SCATTER])
    scatter_d = Scatter(here, False, gd, down_sum, rest[13 + SCATTER : 13 + 2 * SCATTER])
    back.start()
    branch.start()
    scatter_u.start()
    scatter_d.start()
    back.spread()
    branch.spread()
    grad_n2 = back.result().astype(BF16).astype(F32)
    middle = mid[...]
    hat, inv_std = normed(middle)
    grad_mid, gain_sum, shift_sum = norm_back(grad_n2, hat, inv_std, norm_row(packs, 2))
    grad_mid = cot[...].astype(F32) + grad_mid
    dmid[...] = grad_mid
    gm_own[...] = grad_mid.astype(BF16)
    gather = TensorGather(here, gm_own, gm, *rest[10:13])
    gather.start()
    sums[0:1, :] = gain_sum
    sums[1:2, :] = shift_sum
    scatter_u.middle()
    scatter_d.middle()
    out_own[...] = (mid[...] + branch.result().astype(BF16).astype(F32)).astype(BF16)
    gather.forward()
    scatter_u.last()
    scatter_d.last()
    back.finish()
    branch.finish()
    gather.finish()
    scatter_u.finish()
    scatter_d.finish()


def third_call(dn2, ffn, mid, cot, packs, gu, gd):
    _, length, width = dn2.shape
    return pl.pallas_call(
        third_kernel,
        out_shape=(
            jax.ShapeDtypeStruct((2, length, width), BF16),
            jax.ShapeDtypeStruct((ROWS, width), F32),
            jax.ShapeDtypeStruct((ROWS, width), BF16),
            jax.ShapeDtypeStruct((2, width), F32),
            jax.ShapeDtypeStruct((gu.shape[0], CHUNK, 2 * CHUNK), F32),
            jax.ShapeDtypeStruct((gd.shape[0], 2 * CHUNK, CHUNK), F32),
        ),
        in_specs=[VM, VM, VM, VM, VM, ANY, ANY],
        out_specs=(ANY, VM, VM, VM, ANY, ANY),
        scratch_shapes=[pltpu.VMEM((ROWS, width), BF16)]
        + sum_scratch(length, width, dn2.dtype)
        + sum_scratch(length, width, ffn.dtype)
        + tensor_gather_sems()
        + scatter_scratch(gu.shape[0])
        + scatter_scratch(gd.shape[0]),
        compiler_params=params(3),
        name="scatter_ffn",
    )(dn2, ffn, mid, cot, packs, gu, gd)


def fourth_kernel(
    dn1, tok, dmid, out_own, sums, packs, gq, go,
    output, igrad, norm_total, q_sum, o_sum,
    ig_own, out_all, ig_all, slices, heard, plane_sum, heard_z, og, ig, ns, nz, *rest,
):
    here = Here()
    greet(here, PLANE, (1, 2, 3))
    back = TensorSum(here, dn1, rest[0:5])
    scatter_q = Scatter(here, True, gq, q_sum, rest[5 : 5 + SCATTER])
    scatter_o = Scatter(here, False, go, o_sum, rest[5 + SCATTER : 5 + 2 * SCATTER])
    back.start()
    scatter_q.start()
    scatter_o.start()
    back.spread()
    copies = []

    def spread_rows(mine, whole, sem):
        made = []
        for step in (2, 1, 3):
            made.append(
                push(
                    mine,
                    whole.at[block(here.z, ROWS), :],
                    sem.at[0, step - 1],
                    sem.at[1, step - 1],
                    here.along(step),
                )
            )
        return made

    copies += spread_rows(out_own, out_all, og)
    grad_n1 = back.result()
    hat, inv_std = normed(tok[...].astype(F32))
    grad_in, gain_sum, shift_sum = norm_back(grad_n1, hat, inv_std, norm_row(packs, 0))
    ig_own[...] = (dmid[...] + grad_in).astype(BF16)
    copies += spread_rows(ig_own, ig_all, ig)
    for k in range(8):
        cols = slice(k * CHUNK, (k + 1) * CHUNK)
        slices[k, 0:1, :] = gain_sum[:, cols]
        slices[k, 1:2, :] = shift_sum[:, cols]
        slices[k, 2:4, :] = sums[:, cols]
        slices[k, 4:8, :] = jnp.zeros((4, CHUNK), F32)
    norm_copies = []
    for index, peer in enumerate(PLANE):
        norm_copies.append(
            push(
                slices.at[here.chunk(*peer)],
                heard.at[index],
                ns.at[0, index],
                ns.at[1, index],
                here.plane(*peer),
            )
        )
    scatter_q.middle()
    scatter_o.middle()
    mine = slices[here.chunk(0, 0, 0)]
    for index in range(7):
        norm_copies[index].wait()
        mine = mine + heard[index]
    plane_sum[...] = mine
    z_copies = []
    for step in (1, 2, 3):
        z_copies.append(
            push(
                plane_sum,
                heard_z.at[here.z],
                nz.at[0, step - 1],
                nz.at[1, step - 1],
                here.along(step),
            )
        )
    heard_z[pl.ds(here.z, 1)] = mine[None]
    scatter_q.last()
    scatter_o.last()
    for copy in z_copies:
        copy.wait()
    norm_total[...] = ((heard_z[0] + heard_z[1]) + heard_z[2]) + heard_z[3]
    for copy in copies:
        copy.wait()
    out_all[block(here.z, ROWS), :] = out_own[...]
    ig_all[block(here.z, ROWS), :] = ig_own[...]
    output[...] = out_all[...].astype(F32)
    igrad[...] = ig_all[...].astype(F32)
    back.finish()
    scatter_q.finish()
    scatter_o.finish()


def fourth_call(dn1, tok, dmid, out_own, sums, packs, gq, go):
    _, length, width = dn1.shape
    return pl.pallas_call(
        fourth_kernel,
        out_shape=(
            jax.ShapeDtypeStruct((length, width), F32),
            jax.ShapeDtypeStruct((length, width), F32),
            jax.ShapeDtypeStruct((8, CHUNK), F32),
            jax.ShapeDtypeStruct((gq.shape[0], CHUNK, 2 * CHUNK), F32),
            jax.ShapeDtypeStruct((1, 2 * CHUNK, CHUNK), F32),
        ),
        in_specs=[VM] * 6 + [ANY, ANY],
        out_specs=(VM, VM, VM, ANY, ANY),
        scratch_shapes=[
            pltpu.VMEM((ROWS, width), BF16),
            pltpu.VMEM((length, width), BF16),
            pltpu.VMEM((length, width), BF16),
            pltpu.VMEM((8, 8, CHUNK), F32),
            pltpu.VMEM((7, 8, CHUNK), F32),
            pltpu.VMEM((8, CHUNK), F32),
            pltpu.VMEM((4, 8, CHUNK), F32),
            pltpu.SemaphoreType.DMA((2, 3)),
            pltpu.SemaphoreType.DMA((2, 3)),
            pltpu.SemaphoreType.DMA((2, 7)),
            pltpu.SemaphoreType.DMA((2, 3)),
        ]
        + sum_scratch(length, width, dn1.dtype)
        + scatter_scratch(gq.shape[0])
        + scatter_scratch(1),
        compiler_params=params(4),
        name="scatter_attention",
    )(dn1, tok, dmid, out_own, sums, packs, gq, go)


def turn(values, cosine, sine):
    return values * cosine + pltpu.roll(values, HEAD_DIM // 2, 1) * sine


def dot(left, right, dims=((1,), (0,))):
    return lax.dot_general(left, right, (dims, ((), ())), preferred_element_type=F32)


def attention_weights(queries, key_rows, lowest):
    scores = dot(queries, key_rows, ((1,), (1,)))
    row = lax.broadcasted_iota(jnp.int32, scores.shape, 0)
    col = lax.broadcasted_iota(jnp.int32, scores.shape, 1)
    allowed = (col <= row) & (col.astype(F32) >= lowest)
    scores = jnp.where(allowed, scores, MASKED)
    exp_scores = jnp.exp(scores - jnp.max(scores, -1, keepdims=True))
    return exp_scores / jnp.sum(exp_scores, -1, keepdims=True)


def attend_kernel(head0, n1, wq, wo, tables, q_out, k_out, v_out, a_out, part):
    length = tables.shape[2]
    rows_in = n1[...]
    projected = [dot(rows_in, wq[j]) for j in range(3)]
    for s in range(2):
        rows = slice(s * length, (s + 1) * length)
        cosine, sine = tables[s, 0], tables[s, 1]
        lowest = tables[s, 2, :, 0:1]
        for h in range(2):
            cols = slice(h * HEAD_DIM, (h + 1) * HEAD_DIM)
            queries = (turn(projected[0][rows, cols], cosine, sine) * HEAD_DIM ** (-0.5)).astype(BF16)
            key_rows = turn(projected[1][rows, cols], cosine, sine).astype(BF16)
            value_rows = projected[2][rows, cols].astype(BF16)
            weights = attention_weights(queries, key_rows, lowest).astype(BF16)
            heads = dot(weights, value_rows)
            active = tables[s, 4] > (head0[0] + h).astype(F32)
            q_out[rows, cols] = queries
            k_out[rows, cols] = key_rows
            v_out[rows, cols] = value_rows
            a_out[rows, cols] = jnp.where(active, heads, 0.0).astype(BF16)
    for s in range(2):
        rows = slice(s * length, (s + 1) * length)
        part[s] = dot(a_out[rows, :], wo[0]).astype(part.dtype)


SM = pl.BlockSpec(memory_space=pltpu.SMEM)


def local_params():
    return pltpu.CompilerParams(vmem_limit_bytes=60 << 20)


def attend_call(head0, n1, wq, wo, tables):
    _, length, width = n1.shape
    thin = jax.ShapeDtypeStruct((2 * length, CHUNK), BF16)
    return pl.pallas_call(
        attend_kernel,
        out_shape=(thin, thin, thin, thin, jax.ShapeDtypeStruct((2, length, width), SUM_ONE)),
        in_specs=[SM, VM, VM, VM, VM],
        out_specs=(VM,) * 5,
        compiler_params=local_params(),
        name="attend",
    )(head0, n1.reshape(2 * length, width), wq, wo, tables)


def ffn_kernel(n2, cot, bucket, wu, wd, dn2, ffn, gu, gd, back_sum, ffn_sum):
    quarter = pl.program_id(0)

    @pl.when(quarter == 0)
    def _():
        back_sum[...] = jnp.zeros_like(back_sum)
        ffn_sum[...] = jnp.zeros_like(ffn_sum)

    rows_in = n2[...]
    grads_in = cot[...]
    hidden = dot(rows_in, wu[0])
    live = bucket[:, 0:1] >= quarter.astype(F32)
    rectified = jnp.maximum(jnp.where(live, hidden, 0.0), 0.0)
    squared = (rectified * rectified).astype(BF16)
    grad_square = dot(grads_in, wd[0], ((1,), (1,)))
    grad_hidden = (grad_square * 2.0 * rectified).astype(BF16)
    ffn_sum[...] += dot(squared, wd[0])
    back_sum[...] += dot(grad_hidden, wu[0], ((1,), (1,)))
    gu[0] = dot(rows_in, grad_hidden, ((0,), (0,))).astype(BF16)
    gd[0] = dot(squared, grads_in, ((0,), (0,))).astype(BF16)

    @pl.when(quarter == 3)
    def _():
        dn2[...] = back_sum[...].astype(dn2.dtype)
        ffn[...] = ffn_sum[...].astype(ffn.dtype)


def ffn_call(n2, cot, bucket, wu, wd):
    _, length, width = n2.shape
    total = 2 * length
    whole = lambda shape: pl.BlockSpec(shape, lambda r: (0,) * len(shape))
    per = lambda shape: pl.BlockSpec((1,) + shape, lambda r: (r, 0, 0))
    dn2, ffn, gu, gd = pl.pallas_call(
        ffn_kernel,
        grid=(4,),
        out_shape=(
            jax.ShapeDtypeStruct((total, width), SUM_TWO),
            jax.ShapeDtypeStruct((total, width), SUM_FFN),
            jax.ShapeDtypeStruct((4, width, CHUNK), BF16),
            jax.ShapeDtypeStruct((4, CHUNK, width), BF16),
        ),
        in_specs=[
            whole((total, width)),
            whole((total, width)),
            whole((total, HALF)),
            per((width, CHUNK)),
            per((CHUNK, width)),
        ],
        out_specs=(
            whole((total, width)),
            whole((total, width)),
            per((width, CHUNK)),
            per((CHUNK, width)),
        ),
        scratch_shapes=[pltpu.VMEM((total, width), F32), pltpu.VMEM((total, width), F32)],
        compiler_params=local_params(),
        name="ffn",
    )(n2.reshape(total, width), cot.reshape(total, width), bucket, wu, wd)
    return dn2.reshape(2, length, width), ffn.reshape(2, length, width), gu, gd


def attend_back_kernel(
    head0, gm, n1, a_rows, q_rows, k_rows, v_rows, wq, wo, tables,
    dn1, gq, go, dp,
):
    length = tables.shape[2]
    grads = gm[...]
    go[0] = dot(a_rows[...], grads, ((0,), (0,))).astype(BF16)
    grad_att = dot(grads, wo[0], ((1,), (1,))).astype(BF16)
    for s in range(2):
        rows = slice(s * length, (s + 1) * length)
        cosine, sine = tables[s, 0], tables[s, 1]
        lowest = tables[s, 2, :, 0:1]
        for h in range(2):
            cols = slice(h * HEAD_DIM, (h + 1) * HEAD_DIM)
            active = tables[s, 4] > (head0[0] + h).astype(F32)
            grad_heads = jnp.where(active, grad_att[rows, cols].astype(F32), 0.0).astype(BF16)
            queries, key_rows, value_rows = q_rows[rows, cols], k_rows[rows, cols], v_rows[rows, cols]
            weights = attention_weights(queries, key_rows, lowest)
            grad_weights = dot(grad_heads, value_rows, ((1,), (1,)))
            inner = jnp.sum(weights * grad_weights, -1, keepdims=True)
            grad_scores = (weights * (grad_weights - inner)).astype(BF16)
            grad_query = dot(grad_scores, key_rows) * HEAD_DIM ** (-0.5)
            grad_keys = dot(grad_scores, queries, ((0,), (0,)))
            grad_values = dot(weights.astype(BF16), grad_heads, ((0,), (0,)))
            dp[0, rows, cols] = turn(grad_query, cosine, -sine).astype(BF16)
            dp[1, rows, cols] = turn(grad_keys, cosine, -sine).astype(BF16)
            dp[2, rows, cols] = grad_values.astype(BF16)
    for s in range(2):
        rows = slice(s * length, (s + 1) * length)
        total = dot(dp[0, rows, :], wq[0], ((1,), (1,)))
        total = total + dot(dp[1, rows, :], wq[1], ((1,), (1,)))
        total = total + dot(dp[2, rows, :], wq[2], ((1,), (1,)))
        dn1[s] = total.astype(dn1.dtype)
    rows_in = n1[...]
    for j in range(3):
        gq[j] = dot(rows_in, dp[j], ((0,), (0,))).astype(BF16)


def attend_back_call(head0, gm, n1, a_rows, q_rows, k_rows, v_rows, wq, wo, tables):
    _, length, width = n1.shape
    return pl.pallas_call(
        attend_back_kernel,
        out_shape=(
            jax.ShapeDtypeStruct((2, length, width), SUM_THREE),
            jax.ShapeDtypeStruct((3, width, CHUNK), BF16),
            jax.ShapeDtypeStruct((1, CHUNK, width), BF16),
        ),
        in_specs=[SM] + [VM] * 9,
        out_specs=(VM,) * 3,
        scratch_shapes=[pltpu.VMEM((3, 2 * length, CHUNK), BF16)],
        compiler_params=local_params(),
        name="attend_back",
    )(
        head0, gm.reshape(2 * length, width), n1.reshape(2 * length, width),
        a_rows, q_rows, k_rows, v_rows, wq, wo, tables,
    )


def make_table(positions, buckets, head_count):
    length = positions.shape[0]
    angles = rope_angles(positions)
    cosine, sine = jnp.cos(angles), jnp.sin(angles)
    lowest = (jnp.arange(length, dtype=jnp.int32) - positions).astype(F32)
    wide = lambda column: jnp.broadcast_to(column, (length, HALF))
    return jnp.stack(
        [
            jnp.concatenate([cosine, cosine], 1),
            jnp.concatenate([-sine, sine], 1),
            wide(lowest[:, None]),
            wide(buckets.astype(F32)[:, None]),
            wide(head_count.astype(F32)),
        ]
    )


def fast_body(
    tokens, cotangent, head_counts, positions, buckets,
    in_master, out_master, up_master, down_master, norm_master,
    in_first, out_first, up_first, down_first, norm_first,
    in_second, out_second, up_second, down_second, norm_second,
):
    length = tokens.shape[1]
    groups_data = lax.axis_size("dp") * lax.axis_size("expert")
    tensor_count = lax.axis_size("tensor")
    tok, cot = tokens[0], cotangent[0]
    table = make_table(positions[0], buckets[0], head_counts)
    onehot = (buckets[0][:, None] == jnp.arange(CHUNK, dtype=jnp.int32)[None, :]).astype(F32)
    pack = jnp.concatenate(
        [
            lax.reduce_precision(norm_master, 8, 7),
            jnp.sum(onehot, 0, keepdims=True),
            jnp.zeros((3, CHUNK), F32),
        ],
        0,
    )
    n1, both_cot, tables, packs, wq, wo = first_call(
        tok, cot, table, pack, in_master.astype(BF16), out_master.astype(BF16)[None]
    )
    bucket_share = jnp.sum(packs[:, 4, :4], 0) / (length * groups_data)
    heads_here = 2 * CHUNK // HEAD_DIM
    core = lax.rem(lax.axis_index("dp"), 2)
    head0 = (lax.axis_index("tensor") * heads_here + core * (heads_here // 2))[None].astype(jnp.int32)
    q_rows, k_rows, v_rows, a_rows, part = attend_call(head0, n1, wq, wo, tables)
    place = lax.axis_index("tensor") * ROWS
    tok_own = lax.dynamic_slice_in_dim(tok, place, ROWS, 0)
    cot_own = lax.dynamic_slice_in_dim(cot, place, ROWS, 0)
    n2, mid, wu, wd = second_call(
        part, tok_own, packs, up_master.astype(BF16), down_master.astype(BF16)
    )
    bucket = tables[:, 3].reshape(2 * length, HALF)
    dn2, ffn, gu, gd = ffn_call(n2, both_cot, bucket, wu, wd)
    gm, dmid, out_own, sums, up_sum, down_sum = third_call(dn2, ffn, mid, cot_own, packs, gu, gd)
    dn1, gq, go = attend_back_call(head0, gm, n1, a_rows, q_rows, k_rows, v_rows, wq, wo, tables)
    output, input_grad, norm_sum, in_sum, out_sum = fourth_call(
        dn1, tok_own, dmid, out_own, sums, packs, gq, go
    )
    masters = (in_master, out_master, up_master, down_master, norm_master)
    firsts = (in_first, out_first, up_first, down_first, norm_first)
    seconds = (in_second, out_second, up_second, down_second, norm_second)
    grad_shards = (in_sum, out_sum[0], up_sum, down_sum, norm_sum[:4])
    return finish(
        output, input_grad, bucket_share, masters, firsts, seconds, grad_shards, tensor_count
    )


def solution(mesh):
    placed = (
        P(("dp", "expert"), None, None),
        P(("dp", "expert"), None, None),
        P(("dp", "expert")),
        P(("dp", "expert"), None),
        P(("dp", "expert"), None),
        P(None, ("dp", "expert"), "tensor"),
        P("tensor", ("dp", "expert")),
        P(None, ("dp", "expert"), "tensor"),
        P(None, "tensor", ("dp", "expert")),
        P(None, ("dp", "expert")),
        P(None, ("dp", "expert"), "tensor"),
        P("tensor", ("dp", "expert")),
        P(None, ("dp", "expert"), "tensor"),
        P(None, "tensor", ("dp", "expert")),
        P(None, ("dp", "expert")),
        P(None, ("dp", "expert"), "tensor"),
        P("tensor", ("dp", "expert")),
        P(None, ("dp", "expert"), "tensor"),
        P(None, "tensor", ("dp", "expert")),
        P(None, ("dp", "expert")),
    )
    shape = dict(mesh.shape)
    fits = shape == {"dp": 4, "expert": 2, "tensor": 4}
    return jax.shard_map(
        fast_body if fits else body,
        mesh=mesh,
        in_specs=placed,
        out_specs=(
            P(("dp", "expert"), None, None),
            P(("dp", "expert"), None, None),
            P(),
            P(),
            P(None, ("dp", "expert"), "tensor"),
            P("tensor", ("dp", "expert")),
            P(None, ("dp", "expert"), "tensor"),
            P(None, "tensor", ("dp", "expert")),
            P(None, ("dp", "expert")),
            P(None, ("dp", "expert"), "tensor"),
            P("tensor", ("dp", "expert")),
            P(None, ("dp", "expert"), "tensor"),
            P(None, "tensor", ("dp", "expert")),
            P(None, ("dp", "expert")),
            P(None, ("dp", "expert"), "tensor"),
            P("tensor", ("dp", "expert")),
            P(None, ("dp", "expert"), "tensor"),
            P(None, "tensor", ("dp", "expert")),
            P(None, ("dp", "expert")),
        ),
        check_vma=False,
    )
```

```python
import math

import jax
import jax.numpy as jnp
from jax import lax
from jax.experimental import pallas as pl
from jax.experimental.pallas import tpu as pltpu
from jax.sharding import PartitionSpec as P

HEAD_DIM = 128
STEP = 10


NORM_EPS = 1e-05
BETA_FIRST = 0.9
BETA_SECOND = 0.999
ADAM_EPS = 1e-06
WEIGHT_DECAY = 0.01
LEARN_RATE = 0.25
MASKED = -1e30
ROPE_BASE = 10000.0


def layer_norm(values, gain_row, shift_row):
    center = values - jnp.mean(values, -1, keepdims=True)
    variance = jnp.mean(center * center, -1, keepdims=True)
    inv_std = lax.rsqrt(variance + NORM_EPS)
    normed = center * inv_std
    return (normed * gain_row + shift_row, normed, inv_std)


def norm_back_rows(grad_out, normed, inv_std, gain_row):
    scaled = grad_out * gain_row
    inner_part = (
        scaled
        - jnp.mean(scaled, -1, keepdims=True)
        - normed * jnp.mean(scaled * normed, -1, keepdims=True)
    )
    return (inner_part * inv_std, jnp.sum(grad_out * normed, 0), jnp.sum(grad_out, 0))


def rope_angles(position_row):
    freq_index = jnp.arange(HEAD_DIM // 2, dtype=jnp.float32)
    inverse = jnp.exp(freq_index * (-2.0 * jnp.log(ROPE_BASE) / HEAD_DIM))
    return position_row.astype(jnp.float32)[:, None] * inverse[None, :]


def rotary(values, angles, sign_value):
    half_dim = values.shape[-1] // 2
    cosine = jnp.cos(angles)[:, None, :]
    sine_part = sign_value * jnp.sin(angles)[:, None, :]
    first_half = values[..., :half_dim]
    second_half = values[..., half_dim:]
    return jnp.concatenate(
        [
            first_half * cosine - second_half * sine_part,
            second_half * cosine + first_half * sine_part,
        ],
        -1,
    )


def block_mask(key_index, position_row, block_start, block_rows):
    query_index = block_start + jnp.arange(block_rows, dtype=jnp.int32)
    return (key_index[None, :] <= query_index[:, None]) & (
        key_index[None, :] >= (query_index - position_row)[:, None]
    )


def attend_forward(queries, key_rows, value_rows, position_row, block_rows):
    length = queries.shape[0]
    key_index = jnp.arange(length, dtype=jnp.int32)

    def one_block(block_start):
        allowed = block_mask(key_index, position_row, block_start, block_rows)
        scores = jnp.einsum("qhd,khd->hqk", queries, key_rows, preferred_element_type=jnp.float32)
        scores = jnp.where(allowed[None], scores, MASKED)
        row_peak = jnp.max(scores, -1, keepdims=True)
        exp_scores = jnp.exp(scores - row_peak)
        row_total = jnp.sum(exp_scores, -1, keepdims=True)
        attn_weights = (exp_scores / row_total).astype(jnp.bfloat16)
        block_out = jnp.einsum(
            "hqk,khd->qhd", attn_weights, value_rows, preferred_element_type=jnp.float32
        )
        return (block_out, row_peak[..., 0] + jnp.log(row_total[..., 0]))

    starts = jnp.arange(length // block_rows, dtype=jnp.int32) * block_rows
    block_outs, log_totals = lax.map(one_block, starts)
    return (block_outs.reshape(queries.shape), log_totals, starts)


def attend_backward(
    queries, key_rows, value_rows, position_row, grad_heads, log_totals, starts, block_rows
):
    length = queries.shape[0]
    key_index = jnp.arange(length, dtype=jnp.int32)

    def one_block(carried, inputs):
        block_start, block_log = inputs
        allowed = block_mask(key_index, position_row, block_start, block_rows)
        scores = jnp.einsum("qhd,khd->hqk", queries, key_rows, preferred_element_type=jnp.float32)
        scores = jnp.where(allowed[None], scores, MASKED)
        attn_probs = jnp.exp(scores - block_log[..., None])
        grad_probs = jnp.einsum(
            "qhd,khd->hqk", grad_heads, value_rows, preferred_element_type=jnp.float32
        )
        row_inner = jnp.sum(attn_probs * grad_probs, -1, keepdims=True)
        grad_scores = (attn_probs * (grad_probs - row_inner)).astype(jnp.bfloat16)
        grad_query = jnp.einsum(
            "hqk,khd->qhd", grad_scores, key_rows, preferred_element_type=jnp.float32
        )
        grad_keys = carried[0] + jnp.einsum(
            "hqk,qhd->khd", grad_scores, queries, preferred_element_type=jnp.float32
        )
        grad_values = carried[1] + jnp.einsum(
            "hqk,qhd->khd",
            attn_probs.astype(jnp.bfloat16),
            grad_heads,
            preferred_element_type=jnp.float32,
        )
        return ((grad_keys, grad_values), grad_query)

    start_state = (jnp.zeros(key_rows.shape, jnp.float32), jnp.zeros(value_rows.shape, jnp.float32))
    (grad_keys, grad_values), grad_query = lax.scan(one_block, start_state, (starts, log_totals))
    return (grad_query.reshape(queries.shape), grad_keys, grad_values)


def gather_rows(values, source_rows):
    padded = jnp.concatenate([values, jnp.zeros((1, values.shape[1]), values.dtype)], 0)
    return padded[source_rows]


def ffn_forward(rows_in, bucket, up_work, down_work):
    row_count = rows_in.shape[0]
    mixed_sum = jnp.zeros((row_count, down_work.shape[2]), jnp.float32)
    hiddens = []
    for quarter in range(4):

        def live_part():
            hidden = jnp.dot(rows_in, up_work[quarter], preferred_element_type=jnp.float32)
            squared = jnp.square(jnp.maximum(hidden, 0.0)).astype(jnp.bfloat16)
            return (
                hidden,
                jnp.dot(squared, down_work[quarter], preferred_element_type=jnp.float32),
            )

        def dead_part():
            return (
                jnp.zeros((row_count, up_work.shape[2]), jnp.float32),
                jnp.zeros_like(mixed_sum),
            )

        hidden, contribution = lax.cond(bucket >= quarter, live_part, dead_part)
        hiddens.append(hidden)
        mixed_sum = mixed_sum + contribution
    return (mixed_sum, hiddens)


def ffn_backward(rows_in, grads_in, bucket, hiddens, up_work, down_work):
    grad_rows = jnp.zeros((rows_in.shape[0], up_work.shape[1]), jnp.float32)
    grad_up = []
    grad_down = []
    for quarter in range(4):
        hidden = hiddens[quarter]

        def live_part():
            rectified = jnp.maximum(hidden, 0.0)
            squared = jnp.square(rectified).astype(jnp.bfloat16)
            grad_square = jnp.einsum(
                "rd,ud->ru", grads_in, down_work[quarter], preferred_element_type=jnp.float32
            )
            grad_hidden = (grad_square * 2.0 * rectified).astype(jnp.bfloat16)
            return (
                jnp.einsum("rd,ru->du", rows_in, grad_hidden, preferred_element_type=jnp.float32),
                jnp.einsum("ru,rd->ud", squared, grads_in, preferred_element_type=jnp.float32),
                jnp.einsum(
                    "ru,du->rd", grad_hidden, up_work[quarter], preferred_element_type=jnp.float32
                ),
            )

        def dead_part():
            return (
                jnp.zeros(up_work.shape[1:], jnp.float32),
                jnp.zeros(down_work.shape[1:], jnp.float32),
                jnp.zeros_like(grad_rows),
            )

        part_up, part_down, part_rows = lax.cond(bucket >= quarter, live_part, dead_part)
        grad_up.append(part_up)
        grad_down.append(part_down)
        grad_rows = grad_rows + part_rows
    return (grad_rows, jnp.stack(grad_up), jnp.stack(grad_down))


def ffn_total(partial_value):
    return lax.psum(partial_value, "tensor")


def ffn_grad_total(partial_value):
    return lax.psum(partial_value, "tensor")


def adam_terms(weight, gradient, first_old, second_old):
    first_new = BETA_FIRST * first_old + (1.0 - BETA_FIRST) * gradient
    second_new = BETA_SECOND * second_old + (1.0 - BETA_SECOND) * gradient * gradient
    update = (
        first_new
        / (1.0 - BETA_FIRST**STEP)
        / (jnp.sqrt(second_new / (1.0 - BETA_SECOND**STEP)) + ADAM_EPS)
        + WEIGHT_DECAY * weight
    )
    return (update, first_new, second_new)


def finish(output, input_grad, bucket_share, masters, firsts, seconds, grad_shards, tensor_count):
    norm_master = masters[4]
    adam_out = [
        adam_terms(masters[member], grad_shards[member], firsts[member], seconds[member])
        for member in range(5)
    ]
    weight_sq = jnp.concatenate(
        [
            jnp.stack([jnp.sum(masters[member] * masters[member]) for member in range(4)]),
            jnp.sum(norm_master * norm_master, 1) / tensor_count,
        ]
    )
    update_sq = jnp.concatenate(
        [
            jnp.stack([jnp.sum(adam_out[member][0] * adam_out[member][0]) for member in range(4)]),
            jnp.sum(adam_out[4][0] * adam_out[4][0], 1) / tensor_count,
        ]
    )
    weight_tot, update_tot = lax.psum((weight_sq, update_sq), ("dp", "expert", "tensor"))
    weight_norms = jnp.sqrt(weight_tot)
    update_norms = jnp.sqrt(update_tot)
    ratios = weight_norms / update_norms
    new_weights = [
        masters[member] - LEARN_RATE * ratios[member] * adam_out[member][0] for member in range(4)
    ]
    norm_new = norm_master - LEARN_RATE * ratios[4:, None] * adam_out[4][0]
    lamb_norms = jnp.stack([weight_norms, update_norms])
    return (
        output[None],
        input_grad[None],
        bucket_share,
        lamb_norms,
        new_weights[0],
        new_weights[1],
        new_weights[2],
        new_weights[3],
        norm_new,
        adam_out[0][1],
        adam_out[1][1],
        adam_out[2][1],
        adam_out[3][1],
        adam_out[4][1],
        adam_out[0][2],
        adam_out[1][2],
        adam_out[2][2],
        adam_out[3][2],
        adam_out[4][2],
    )


def body(
    tokens,
    cotangent,
    head_counts,
    positions,
    buckets,
    in_master,
    out_master,
    up_master,
    down_master,
    norm_master,
    in_first,
    out_first,
    up_first,
    down_first,
    norm_first,
    in_second,
    out_second,
    up_second,
    down_second,
    norm_second,
):
    in_work, out_work, up_work, down_work, norm_work = (
        lax.all_gather(in_master.astype(jnp.bfloat16), ("dp", "expert"), axis=1, tiled=True),
        lax.all_gather(out_master.astype(jnp.bfloat16), ("dp", "expert"), axis=1, tiled=True),
        lax.all_gather(up_master.astype(jnp.bfloat16), ("dp", "expert"), axis=1, tiled=True),
        lax.all_gather(down_master.astype(jnp.bfloat16), ("dp", "expert"), axis=2, tiled=True),
        lax.all_gather(norm_master.astype(jnp.bfloat16), ("dp", "expert"), axis=1, tiled=True),
    )
    length = tokens.shape[1]
    model_width = tokens.shape[2]
    heads_here = in_work.shape[2] // HEAD_DIM
    block_rows = min(512, length)
    head_scale = HEAD_DIM ** (-0.5)
    groups_data = lax.axis_size("dp") * lax.axis_size("expert")
    tensor_count = lax.axis_size("tensor")
    experts = lax.axis_size("expert")
    norm_gains = norm_work.astype(jnp.float32)
    inputs = tokens[0].astype(jnp.float32)
    first_norm, first_hat, first_inv = layer_norm(inputs, norm_gains[0], norm_gains[1])
    first_in = first_norm.astype(jnp.bfloat16)
    projected = jnp.einsum("td,jde->jte", first_in, in_work, preferred_element_type=jnp.float32)
    projected = projected.reshape(3, length, heads_here, HEAD_DIM)
    angles = rope_angles(positions[0])
    queries = (rotary(projected[0], angles, 1.0) * head_scale).astype(jnp.bfloat16)
    key_rows = rotary(projected[1], angles, 1.0).astype(jnp.bfloat16)
    value_rows = projected[2].astype(jnp.bfloat16)
    head_ids = lax.axis_index("tensor") * heads_here + jnp.arange(heads_here, dtype=jnp.int32)
    active = (head_ids < head_counts[0]).astype(jnp.float32)
    head_outs, log_totals, starts = attend_forward(
        queries, key_rows, value_rows, positions[0], block_rows
    )
    attended = (
        (head_outs * active[None, :, None])
        .astype(jnp.bfloat16)
        .reshape(length, heads_here * HEAD_DIM)
    )
    attn_part = jnp.dot(attended, out_work, preferred_element_type=jnp.float32)
    middle = inputs + lax.psum(attn_part, "tensor")
    second_norm, second_hat, second_inv = layer_norm(middle, norm_gains[2], norm_gains[3])
    second_in = second_norm.astype(jnp.bfloat16)
    bucket_ids = buckets[0]
    onehot = (bucket_ids[:, None] == jnp.arange(4, dtype=jnp.int32)[None, :]).astype(jnp.int32)
    bucket_rank = jnp.sum((jnp.cumsum(onehot, 0) - onehot) * onehot, 1)
    local_counts = jnp.sum(onehot, 0).astype(jnp.float32)
    bucket_share = lax.psum(local_counts, ("dp", "expert")) / (length * groups_data)
    most_rows = 5 * length // 16
    owner_group = max(experts // 4, 1)
    per_owner = max(4 // experts, 1)
    slot_rows = (most_rows + owner_group - 1) // owner_group
    capacity = per_owner * slot_rows
    slot_of = (
        (bucket_ids // per_owner * owner_group + bucket_rank % owner_group) * capacity
        + bucket_ids % per_owner * slot_rows
        + bucket_rank // owner_group
    )
    slot_total = experts * capacity
    source_rows = (
        jnp.full((slot_total,), length, jnp.int32)
        .at[slot_of]
        .set(jnp.arange(length, dtype=jnp.int32))
    )
    outgoing = gather_rows(second_in, source_rows).reshape(experts, capacity, model_width)
    incoming = lax.all_to_all(outgoing, "expert", split_axis=0, concat_axis=0, tiled=True).reshape(
        experts, per_owner, slot_rows, model_width
    )
    owner_index = lax.axis_index("expert")
    owned_ids = [owner_index // owner_group * per_owner + member for member in range(per_owner)]
    ffn_inputs = [
        incoming[:, member].reshape(experts * slot_rows, model_width) for member in range(per_owner)
    ]
    results = [
        ffn_forward(ffn_inputs[member], owned_ids[member], up_work, down_work)
        for member in range(per_owner)
    ]
    partial_value = jnp.stack(
        [
            results[member][0].reshape(experts, slot_rows, model_width)
            for member in range(per_owner)
        ],
        1,
    )
    summed = ffn_total(partial_value.reshape(experts, capacity, model_width)).astype(jnp.bfloat16)
    returned = lax.all_to_all(summed, "expert", split_axis=0, concat_axis=0, tiled=True)
    branch_out = returned.reshape(slot_total, model_width)[slot_of]
    output = middle + branch_out.astype(jnp.float32)
    grad_branch = cotangent[0]
    outgoing_grad = gather_rows(grad_branch, source_rows).reshape(experts, capacity, model_width)
    incoming_grad = lax.all_to_all(
        outgoing_grad, "expert", split_axis=0, concat_axis=0, tiled=True
    ).reshape(experts, per_owner, slot_rows, model_width)
    ffn_grads = [
        incoming_grad[:, member].reshape(experts * slot_rows, model_width)
        for member in range(per_owner)
    ]
    back_parts = [
        ffn_backward(
            ffn_inputs[member],
            ffn_grads[member],
            owned_ids[member],
            results[member][1],
            up_work,
            down_work,
        )
        for member in range(len(owned_ids))
    ]
    grad_up = back_parts[0][1]
    grad_down = back_parts[0][2]
    for member in range(1, len(owned_ids)):
        grad_up = grad_up + back_parts[member][1]
        grad_down = grad_down + back_parts[member][2]
    rows_back = jnp.stack(
        [
            back_parts[member][0].reshape(experts, slot_rows, model_width)
            for member in range(per_owner)
        ],
        1,
    )
    summed_back = ffn_grad_total(rows_back.reshape(experts, capacity, model_width)).astype(
        jnp.bfloat16
    )
    returned_back = lax.all_to_all(summed_back, "expert", split_axis=0, concat_axis=0, tiled=True)
    grad_second = returned_back.reshape(slot_total, model_width)[slot_of].astype(jnp.float32)
    grad_mid_norm, gain_second, shift_second = norm_back_rows(
        grad_second, second_hat, second_inv, norm_gains[2]
    )
    grad_middle = grad_branch.astype(jnp.float32) + grad_mid_norm
    grad_attn = grad_middle.astype(jnp.bfloat16)
    grad_attended = jnp.einsum("td,ed->te", grad_attn, out_work, preferred_element_type=jnp.float32)
    grad_out_w = jnp.einsum("te,td->ed", attended, grad_attn, preferred_element_type=jnp.float32)
    grad_heads = (
        grad_attended.astype(jnp.bfloat16).reshape(length, heads_here, HEAD_DIM)
        * active.astype(jnp.bfloat16)[None, :, None]
    )
    grad_query, grad_keys, grad_values = attend_backward(
        queries, key_rows, value_rows, positions[0], grad_heads, log_totals, starts, block_rows
    )
    grad_projected = jnp.stack(
        [
            rotary(grad_query * head_scale, angles, -1.0),
            rotary(grad_keys, angles, -1.0),
            grad_values,
        ]
    )
    grad_projected = grad_projected.reshape(3, length, heads_here * HEAD_DIM).astype(jnp.bfloat16)
    grad_in_w = jnp.einsum(
        "td,jte->jde", first_in, grad_projected, preferred_element_type=jnp.float32
    )
    grad_first_part = jnp.einsum(
        "jte,jde->td", grad_projected, in_work, preferred_element_type=jnp.float32
    )
    grad_first = lax.psum(grad_first_part, "tensor")
    grad_input_norm, gain_first, shift_first = norm_back_rows(
        grad_first, first_hat, first_inv, norm_gains[0]
    )
    input_grad = grad_middle + grad_input_norm
    grad_norm = jnp.stack([gain_first, shift_first, gain_second, shift_second])
    in_sum, out_sum, up_sum, down_sum, norm_sum = (
        lax.psum_scatter(grad_in_w, ("dp", "expert"), scatter_dimension=1, tiled=True),
        lax.psum_scatter(grad_out_w, ("dp", "expert"), scatter_dimension=1, tiled=True),
        lax.psum_scatter(grad_up, ("dp", "expert"), scatter_dimension=1, tiled=True),
        lax.psum_scatter(grad_down, ("dp", "expert"), scatter_dimension=2, tiled=True),
        lax.psum_scatter(grad_norm, ("dp", "expert"), scatter_dimension=1, tiled=True),
    )
    masters = (in_master, out_master, up_master, down_master, norm_master)
    firsts = (in_first, out_first, up_first, down_first, norm_first)
    seconds = (in_second, out_second, up_second, down_second, norm_second)
    grad_shards = (in_sum, out_sum, up_sum, down_sum, norm_sum)
    return finish(output, input_grad, bucket_share, masters, firsts, seconds, grad_shards, tensor_count)


MESH = pl.DeviceIdType.MESH
ANY = pl.BlockSpec(memory_space=pl.ANY)
VM = pl.BlockSpec(memory_space=pltpu.VMEM)
SM = pl.BlockSpec(memory_space=pltpu.SMEM)
F32 = jnp.float32
BF16 = jnp.bfloat16
CHUNK = 256
HALF = 128
ROWS = 64


class Here:
    def __init__(self):
        d = lax.axis_index("dp")
        self.x, self.c = d // 2, lax.rem(d, 2)
        self.y = lax.axis_index("expert")
        self.z = lax.axis_index("tensor")

    def plane(self, dx, dc, dy):
        x = 1 - self.x if dx else self.x
        c = 1 - self.c if dc else self.c
        y = 1 - self.y if dy else self.y
        return (x * 2 + c, y, self.z)

    def chunk(self, dx, dc, dy):
        x = 1 - self.x if dx else self.x
        c = 1 - self.c if dc else self.c
        y = 1 - self.y if dy else self.y
        return (x * 2 + c) * 2 + y

    def chunk_of(self, dx, dy, core):
        x = 1 - self.x if dx else self.x
        y = 1 - self.y if dy else self.y
        return (x * 2 + core) * 2 + y

    def along(self, step):
        return (self.x * 2 + self.c, self.y, lax.rem(self.z + step, 4))

    def behind(self, step):
        return lax.rem(self.z + 4 - step, 4)


PARTNER = (0, 1, 0)
PLANE = [(a, b, g) for a in (0, 1) for b in (0, 1) for g in (0, 1) if a + b + g > 0]
SIDES = [(1, 0, 0), (1, 1, 0), (0, 0, 1), (0, 1, 1)]


def greet(here, plane_peers, tensor_peers):
    barrier = pltpu.get_barrier_semaphore()
    for peer in plane_peers:
        pl.semaphore_signal(barrier, inc=1, device_id=here.plane(*peer), device_id_type=MESH)
    for step in tensor_peers:
        pl.semaphore_signal(barrier, inc=1, device_id=here.along(step), device_id_type=MESH)
    pl.semaphore_wait(barrier, len(plane_peers) + len(tensor_peers))


def push(src, dst, send, recv, device):
    copy = pltpu.make_async_remote_copy(
        src_ref=src, dst_ref=dst, send_sem=send, recv_sem=recv, device_id=device, device_id_type=MESH
    )
    copy.start()
    return copy


def block(index, size):
    return pl.ds(pl.multiple_of(index * size, size), size)


def rows_chunk(ref, k):
    return ref.at[:, block(k, CHUNK), :]


def rows_part(ref, k, part):
    return ref.at[:, pl.ds(pl.multiple_of(k * CHUNK + part * HALF, HALF), HALF), :]


def cols_chunk(ref, k):
    return ref.at[:, :, block(k, CHUNK)]


def cols_part(ref, k, part):
    return ref.at[:, part * HALF : part * HALF + HALF, block(k, CHUNK)]


class Gather:
    def __init__(self, here, by_rows, shard, whole, first, relay, local):
        self.here, self.by_rows, self.shard, self.whole = here, by_rows, shard, whole
        self.first, self.relay, self.local = first, relay, local
        self.copies = []

    def half(self, core):
        if self.by_rows:
            return self.shard.at[:, :, block(core, CHUNK)]
        return self.shard.at[:, block(core, CHUNK), :]

    def chunk(self, k):
        return rows_chunk(self.whole, k) if self.by_rows else cols_chunk(self.whole, k)

    def part(self, k, part):
        return rows_part(self.whole, k, part) if self.by_rows else cols_part(self.whole, k, part)

    def start(self):
        here = self.here
        mine = self.chunk(here.chunk(0, 0, 0))
        for index, side in enumerate(SIDES + [PARTNER]):
            core = 1 - here.c if side[1] else here.c
            self.copies.append(
                push(
                    self.half(core),
                    mine,
                    self.first.at[0, index],
                    self.first.at[1, index],
                    here.plane(*side),
                )
            )
        self.own = pltpu.make_async_copy(self.half(here.c), mine, self.local)
        self.own.start()

    def forward(self):
        here = self.here
        self.onward = []
        for index in range(4):
            side = SIDES[index]
            self.copies[index].wait_recv()
            part = 0 if side[0] else 1
            where = self.part(here.chunk(*side), part)
            target = (0, 0, 1) if side[0] else (1, 0, 0)
            self.onward.append(
                push(
                    where,
                    where,
                    self.relay.at[0, index],
                    self.relay.at[1, index],
                    here.plane(*target),
                )
            )

    def finish(self):
        for index in range(4):
            self.copies[index].wait_send()
        self.copies[4].wait()
        self.own.wait()
        for copy in self.onward:
            copy.wait()


def gather_sems():
    return [
        pltpu.SemaphoreType.DMA((2, 5)),
        pltpu.SemaphoreType.DMA((2, 4)),
        pltpu.SemaphoreType.DMA,
    ]


class Scatter:
    def __init__(self, here, by_rows, grad, total, bufs):
        self.here, self.by_rows, self.grad, self.total = here, by_rows, grad, total
        (self.own, self.got, self.got_two, self.final) = bufs[:4]
        (self.load_sem, self.one_sem, self.two_sem, self.last_sem, self.local) = bufs[4:]

    def part(self, k, part):
        return rows_part(self.grad, k, part) if self.by_rows else cols_part(self.grad, k, part)

    def start(self):
        here = self.here
        self.first = []
        for side in (0, 1):
            near, far = ((1, 0), (1, 1)) if side == 0 else ((0, 1), (1, 1))
            target = here.plane(1, 0, 0) if side == 0 else here.plane(0, 0, 1)
            for slot in range(4):
                chip = far if slot >= 2 else near
                src = self.part(here.chunk_of(chip[0], chip[1], slot % 2), side)
                index = side * 4 + slot
                self.first.append(
                    push(
                        src,
                        self.got.at[index],
                        self.one_sem.at[0, index],
                        self.one_sem.at[1, index],
                        target,
                    )
                )
        self.loads = []
        for side in (0, 1):
            for slot in range(4):
                chip = (0, 0) if slot < 2 else ((0, 1) if side == 0 else (1, 0))
                src = self.part(here.chunk_of(chip[0], chip[1], slot % 2), side)
                index = side * 4 + slot
                copy = pltpu.make_async_copy(src, self.own.at[index], self.load_sem.at[index])
                copy.start()
                self.loads.append(copy)

    def middle(self):
        here = self.here
        self.second = []
        for side in (0, 1):
            target = here.plane(0, 0, 1) if side == 0 else here.plane(1, 0, 0)
            for slot in (2, 3):
                index = side * 4 + slot
                self.loads[index].wait()
                self.first[index].wait_recv()
                self.own[index] = (
                    self.own[index].astype(F32) + self.got[index].astype(F32)
                ).astype(BF16)
                two = side * 2 + slot - 2
                self.second.append(
                    push(
                        self.own.at[index],
                        self.got_two.at[two],
                        self.two_sem.at[0, two],
                        self.two_sem.at[1, two],
                        target,
                    )
                )

    def last(self):
        here = self.here
        for side in (0, 1):
            for slot in (0, 1):
                index = side * 4 + slot
                two = side * 2 + slot
                self.loads[index].wait()
                self.first[index].wait_recv()
                self.second[two].wait_recv()
                self.final[slot, :, side * HALF : side * HALF + HALF, :] = (
                    self.own[index].astype(F32) + self.got[index].astype(F32)
                ) + self.got_two[two].astype(F32)
        if self.by_rows:
            where = self.total.at[:, :, block(here.c, CHUNK)]
        else:
            where = self.total.at[:, block(here.c, CHUNK), :]
        self.keep = pltpu.make_async_copy(self.final.at[here.c], where, self.local)
        self.keep.start()
        self.give = push(
            self.final.at[1 - here.c],
            where,
            self.last_sem.at[0],
            self.last_sem.at[1],
            here.plane(*PARTNER),
        )

    def finish(self):
        for copy in self.first:
            copy.wait_send()
        for copy in self.second:
            copy.wait_send()
        self.keep.wait()
        self.give.wait()


def scatter_scratch(width):
    return [
        pltpu.VMEM((8, width, HALF, CHUNK), BF16),
        pltpu.VMEM((8, width, HALF, CHUNK), BF16),
        pltpu.VMEM((4, width, HALF, CHUNK), BF16),
        pltpu.VMEM((2, width, CHUNK, CHUNK), F32),
        pltpu.SemaphoreType.DMA((8,)),
        pltpu.SemaphoreType.DMA((2, 8)),
        pltpu.SemaphoreType.DMA((2, 4)),
        pltpu.SemaphoreType.DMA((2,)),
        pltpu.SemaphoreType.DMA,
    ]


SCATTER = 9


class TensorSum:
    def __init__(self, here, part, bufs):
        self.here, self.part = here, part
        self.pair, self.out, self.inn, self.pair_sem, self.sem = bufs

    def start(self):
        here = self.here
        self.swap = push(
            self.part.at[1 - here.c],
            self.pair,
            self.pair_sem.at[0],
            self.pair_sem.at[1],
            here.plane(*PARTNER),
        )

    def spread(self):
        here = self.here
        self.swap.wait_recv()
        self.sent = []
        for step in (2, 1, 3):
            rows = block(lax.rem(here.z + step, 4), ROWS)
            self.out[step - 1] = (
                self.part[here.c, rows, :].astype(F32) + self.pair[rows, :].astype(F32)
            ).astype(self.out.dtype)
            self.sent.append(
                push(
                    self.out.at[step - 1],
                    self.inn.at[step - 1],
                    self.sem.at[0, step - 1],
                    self.sem.at[1, step - 1],
                    here.along(step),
                )
            )

    def result(self):
        here = self.here
        rows = block(here.z, ROWS)
        total = self.part[here.c, rows, :].astype(F32) + self.pair[rows, :].astype(F32)
        for copy in self.sent:
            copy.wait_recv()
        for step in (1, 2, 3):
            total = total + self.inn[step - 1].astype(F32)
        return total

    def finish(self):
        self.swap.wait_send()
        for copy in self.sent:
            copy.wait_send()


def sum_scratch(length, width):
    return [
        pltpu.VMEM((length, width), BF16),
        pltpu.VMEM((3, ROWS, width), BF16),
        pltpu.VMEM((3, ROWS, width), BF16),
        pltpu.SemaphoreType.DMA((2,)),
        pltpu.SemaphoreType.DMA((2, 3)),
    ]


class TensorGather:
    def __init__(self, here, mine, whole, sem, pair_sem, local):
        self.here, self.mine, self.whole = here, mine, whole
        self.sem, self.pair_sem, self.local = sem, pair_sem, local

    def start(self):
        here = self.here
        place = self.whole.at[here.c, block(here.z, ROWS), :]
        self.sent = []
        for step in (2, 1, 3):
            self.sent.append(
                push(
                    self.mine,
                    place,
                    self.sem.at[0, step - 1],
                    self.sem.at[1, step - 1],
                    here.along(step),
                )
            )
        self.shared = [
            push(
                self.mine,
                place,
                self.pair_sem.at[0, 0],
                self.pair_sem.at[1, 0],
                here.plane(*PARTNER),
            )
        ]
        self.own = pltpu.make_async_copy(self.mine, place, self.local)
        self.own.start()

    def forward(self):
        here = self.here
        for index, step in enumerate((2, 1, 3)):
            self.sent[index].wait_recv()
            place = self.whole.at[here.c, block(here.behind(step), ROWS), :]
            self.shared.append(
                push(
                    place,
                    place,
                    self.pair_sem.at[0, step],
                    self.pair_sem.at[1, step],
                    here.plane(*PARTNER),
                )
            )

    def finish(self):
        for copy in self.sent:
            copy.wait_send()
        for copy in self.shared:
            copy.wait()
        self.own.wait()


def normed(values):
    center = values - jnp.mean(values, -1, keepdims=True)
    variance = jnp.mean(center * center, -1, keepdims=True)
    inv_std = lax.rsqrt(variance + NORM_EPS)
    return (center * inv_std, inv_std)


def norm_row(packs, row):
    return jnp.concatenate([packs[k, row : row + 1, :] for k in range(8)], 1)


def params(ident, limit=60):
    return pltpu.CompilerParams(
        collective_id=ident, has_side_effects=True, vmem_limit_bytes=limit << 20
    )


def cast_rows(raw, shard):
    count, rows, _ = raw.shape
    for j in range(count):

        def step(i, carry):
            at = pl.ds(pl.multiple_of(i * 32, 32), 32)
            shard[j, at, :] = raw[j, at, :].astype(BF16)
            return carry

        lax.fori_loop(0, rows // 32, step, 0)


def front_kernel(*refs):
    head_count, position, bucket, tok, cot, norm_master = refs[:6]
    masters = refs[6:10]
    n1, both_cot, tables, packs, n2, mid, q_out, k_out, v_out, a_out = refs[10:20]
    wholes = refs[20:24]
    raws, shards = refs[24:28], refs[28:32]
    raw_sem, n2_own, part, small, pair, local = refs[32:38]
    sums, tensor_sems, gather_refs = refs[38:43], refs[43:46], refs[46:58]
    here = Here()
    loads = []
    for i in range(4):
        loads.append(pltpu.make_async_copy(masters[i], raws[i], raw_sem.at[i]))
        loads[i].start()
    table = tables.at[here.c]
    fill_table(table, position[...], bucket[...], head_count[0])
    me = here.chunk(0, 0, 0)
    lane = lax.broadcasted_iota(jnp.int32, (1, CHUNK), 1)
    counts = jnp.zeros((1, CHUNK), F32)
    for c in range(4):
        count = jnp.sum((bucket[...] == c).astype(F32), 1, keepdims=True)
        counts = counts + jnp.where(lane == c, count, 0.0)
    packs[pl.ds(me, 1)] = jnp.concatenate(
        [norm_master[...].astype(BF16).astype(F32), counts, jnp.zeros((3, CHUNK), F32)], 0
    )[None]
    greet(here, PLANE, (1, 2, 3))
    gathers = [
        Gather(here, i in (0, 2), shards[i], wholes[i], *gather_refs[i * 3 : i * 3 + 3])
        for i in range(4)
    ]
    loads[0].wait()
    cast_rows(raws[0], shards[0])
    gathers[0].start()
    packed = []
    for index, peer in enumerate(PLANE):
        packed.append(
            push(
                packs.at[me], packs.at[me],
                small.at[0, index], small.at[1, index], here.plane(*peer),
            )
        )
    partner = here.plane(*PARTNER)
    shared = [
        push(table, table, pair.at[0, 0], pair.at[1, 0], partner),
        push(cot, both_cot.at[here.c], pair.at[0, 1], pair.at[1, 1], partner),
    ]
    keep = pltpu.make_async_copy(cot, both_cot.at[here.c], local)
    keep.start()
    for i in range(1, 4):
        loads[i].wait()
        cast_rows(raws[i], shards[i])
    for copy in packed:
        copy.wait()
    gain, shift = norm_row(packs, 0), norm_row(packs, 1)
    mine = n1.at[here.c]

    def rows_step(i, carry):
        rows = block(i, 32)
        hat, _ = normed(tok[rows, :].astype(F32))
        mine[rows, :] = (hat * gain + shift).astype(BF16)
        return carry

    lax.fori_loop(0, tok.shape[0] // 32, rows_step, 0)
    shared.append(push(mine, mine, pair.at[0, 2], pair.at[1, 2], partner))
    gathers[0].forward()
    gathers[1].start()
    gathers[0].finish()
    gathers[1].forward()
    gathers[2].start()
    gathers[3].start()
    shared[0].wait_recv()
    shared[2].wait_recv()
    head0 = here.z * 4 + here.c * 2
    attend_body(head0, n1, wholes[0], wholes[1], tables, q_out, k_out, v_out, a_out, part)
    gathers[1].finish()
    total = TensorSum(here, part, sums)
    attend_out(a_out, wholes[1], part, 1 - here.c)
    total.start()
    attend_out(a_out, wholes[1], part, here.c)
    total.spread()
    rows = block(here.z, ROWS)
    middle = tok[rows, :].astype(F32) + total.result()
    mid[...] = middle
    hat, _ = normed(middle)
    n2_own[...] = (hat * norm_row(packs, 2) + norm_row(packs, 3)).astype(BF16)
    gather = TensorGather(here, n2_own, n2, *tensor_sems)
    gather.start()
    gathers[2].forward()
    gathers[3].forward()
    gather.forward()
    total.finish()
    gather.finish()
    gathers[2].finish()
    gathers[3].finish()
    keep.wait()
    shared[0].wait_send()
    shared[1].wait()
    shared[2].wait_send()


def front_call(head_count, position, bucket, tok, cot, norm_master, masters):
    length, width = tok.shape
    both = jax.ShapeDtypeStruct((2, length, width), BF16)
    thin = jax.ShapeDtypeStruct((2 * length, CHUNK), BF16)
    wholes = [
        jax.ShapeDtypeStruct((3, width, CHUNK), BF16),
        jax.ShapeDtypeStruct((1, CHUNK, width), BF16),
        jax.ShapeDtypeStruct((4, width, CHUNK), BF16),
        jax.ShapeDtypeStruct((4, CHUNK, width), BF16),
    ]
    results = pl.pallas_call(
        front_kernel,
        out_shape=[
            both,
            both,
            jax.ShapeDtypeStruct((2, 5, length, HALF), F32),
            jax.ShapeDtypeStruct((8, 8, CHUNK), F32),
            both,
            jax.ShapeDtypeStruct((ROWS, width), F32),
            thin, thin, thin, thin,
        ]
        + wholes,
        in_specs=[SM, VM, VM, VM, VM, VM] + [ANY] * 4,
        out_specs=[VM, ANY, VM, VM, ANY, VM, VM, VM, VM, VM, VM, VM, ANY, ANY],
        scratch_shapes=[pltpu.VMEM(master.shape, F32) for master in masters]
        + [pltpu.VMEM(master.shape, BF16) for master in masters]
        + [
            pltpu.SemaphoreType.DMA((4,)),
            pltpu.VMEM((ROWS, width), BF16),
            pltpu.VMEM((2, length, width), BF16),
            pltpu.SemaphoreType.DMA((2, 7)),
            pltpu.SemaphoreType.DMA((2, 3)),
            pltpu.SemaphoreType.DMA,
        ]
        + sum_scratch(length, width)
        + tensor_gather_sems()
        + gather_sems() * 4,
        compiler_params=params(1),
        name="front",
    )(head_count, position, bucket, tok, cot, norm_master, *masters)
    return results[:10], results[10:]


def tensor_gather_sems():
    return [
        pltpu.SemaphoreType.DMA((2, 3)),
        pltpu.SemaphoreType.DMA((2, 4)),
        pltpu.SemaphoreType.DMA,
    ]


def norm_back(grad_out, hat, inv_std, gain):
    scaled = grad_out * gain
    inner = (
        scaled
        - jnp.mean(scaled, -1, keepdims=True)
        - hat * jnp.mean(scaled * hat, -1, keepdims=True)
    )
    return (
        inner * inv_std,
        jnp.sum(grad_out * hat, 0, keepdims=True),
        jnp.sum(grad_out, 0, keepdims=True),
    )


def third_kernel(
    dn2, ffn, mid, cot, packs, gu, gd,
    gm, dmid, out_own, sums, up_sum, down_sum,
    gm_own, *rest,
):
    here = Here()
    greet(here, [(1, 0, 0), (0, 0, 1), PARTNER], (1, 2, 3))
    back = TensorSum(here, dn2, rest[0:5])
    branch = TensorSum(here, ffn, rest[5:10])
    scatter_u = Scatter(here, True, gu, up_sum, rest[13 : 13 + SCATTER])
    scatter_d = Scatter(here, False, gd, down_sum, rest[13 + SCATTER : 13 + 2 * SCATTER])
    back.start()
    branch.start()
    scatter_u.start()
    scatter_d.start()
    back.spread()
    branch.spread()
    grad_n2 = back.result().astype(BF16).astype(F32)
    middle = mid[...]
    hat, inv_std = normed(middle)
    grad_mid, gain_sum, shift_sum = norm_back(grad_n2, hat, inv_std, norm_row(packs, 2))
    grad_mid = cot[...].astype(F32) + grad_mid
    dmid[...] = grad_mid
    gm_own[...] = grad_mid.astype(BF16)
    gather = TensorGather(here, gm_own, gm, *rest[10:13])
    gather.start()
    sums[0:1, :] = gain_sum
    sums[1:2, :] = shift_sum
    scatter_u.middle()
    scatter_d.middle()
    out_own[...] = (mid[...] + branch.result().astype(BF16).astype(F32)).astype(BF16)
    gather.forward()
    scatter_u.last()
    scatter_d.last()
    back.finish()
    branch.finish()
    gather.finish()
    scatter_u.finish()
    scatter_d.finish()


def third_call(dn2, ffn, mid, cot, packs, gu, gd):
    _, length, width = dn2.shape
    return pl.pallas_call(
        third_kernel,
        out_shape=(
            jax.ShapeDtypeStruct((2, length, width), BF16),
            jax.ShapeDtypeStruct((ROWS, width), F32),
            jax.ShapeDtypeStruct((ROWS, width), BF16),
            jax.ShapeDtypeStruct((2, width), F32),
            jax.ShapeDtypeStruct((gu.shape[0], CHUNK, 2 * CHUNK), F32),
            jax.ShapeDtypeStruct((gd.shape[0], 2 * CHUNK, CHUNK), F32),
        ),
        in_specs=[VM, VM, VM, VM, VM, ANY, ANY],
        out_specs=(ANY, VM, VM, VM, ANY, ANY),
        scratch_shapes=[pltpu.VMEM((ROWS, width), BF16)]
        + sum_scratch(length, width)
        + sum_scratch(length, width)
        + tensor_gather_sems()
        + scatter_scratch(gu.shape[0])
        + scatter_scratch(gd.shape[0]),
        compiler_params=params(3),
        name="scatter_ffn",
    )(dn2, ffn, mid, cot, packs, gu, gd)


def fourth_kernel(
    dn1, tok, dmid, sums, packs, gq, go,
    ig_own, norm_total, q_sum, o_sum,
    slices, heard, plane_sum, heard_z, ns, nz, *rest,
):
    here = Here()
    greet(here, PLANE, (1, 2, 3))
    back = TensorSum(here, dn1, rest[0:5])
    scatter_q = Scatter(here, True, gq, q_sum, rest[5 : 5 + SCATTER])
    scatter_o = Scatter(here, False, go, o_sum, rest[5 + SCATTER : 5 + 2 * SCATTER])
    back.start()
    scatter_q.start()
    scatter_o.start()
    back.spread()
    grad_n1 = back.result()
    hat, inv_std = normed(tok[...].astype(F32))
    grad_in, gain_sum, shift_sum = norm_back(grad_n1, hat, inv_std, norm_row(packs, 0))
    ig_own[...] = (dmid[...] + grad_in).astype(BF16)
    for k in range(8):
        cols = slice(k * CHUNK, (k + 1) * CHUNK)
        slices[k, 0:1, :] = gain_sum[:, cols]
        slices[k, 1:2, :] = shift_sum[:, cols]
        slices[k, 2:4, :] = sums[:, cols]
        slices[k, 4:8, :] = jnp.zeros((4, CHUNK), F32)
    norm_copies = []
    for index, peer in enumerate(PLANE):
        norm_copies.append(
            push(
                slices.at[here.chunk(*peer)],
                heard.at[index],
                ns.at[0, index],
                ns.at[1, index],
                here.plane(*peer),
            )
        )
    scatter_q.middle()
    scatter_o.middle()
    mine = slices[here.chunk(0, 0, 0)]
    for index in range(7):
        norm_copies[index].wait()
        mine = mine + heard[index]
    plane_sum[...] = mine
    z_copies = []
    for step in (1, 2, 3):
        z_copies.append(
            push(
                plane_sum,
                heard_z.at[here.z],
                nz.at[0, step - 1],
                nz.at[1, step - 1],
                here.along(step),
            )
        )
    heard_z[pl.ds(here.z, 1)] = mine[None]
    scatter_q.last()
    scatter_o.last()
    for copy in z_copies:
        copy.wait()
    norm_total[...] = ((heard_z[0] + heard_z[1]) + heard_z[2]) + heard_z[3]
    back.finish()
    scatter_q.finish()
    scatter_o.finish()


def fourth_call(dn1, tok, dmid, sums, packs, gq, go):
    _, length, width = dn1.shape
    return pl.pallas_call(
        fourth_kernel,
        out_shape=(
            jax.ShapeDtypeStruct((ROWS, width), BF16),
            jax.ShapeDtypeStruct((8, CHUNK), F32),
            jax.ShapeDtypeStruct((gq.shape[0], CHUNK, 2 * CHUNK), F32),
            jax.ShapeDtypeStruct((1, 2 * CHUNK, CHUNK), F32),
        ),
        in_specs=[VM] * 5 + [ANY, ANY],
        out_specs=(VM, VM, ANY, ANY),
        scratch_shapes=[
            pltpu.VMEM((8, 8, CHUNK), F32),
            pltpu.VMEM((7, 8, CHUNK), F32),
            pltpu.VMEM((8, CHUNK), F32),
            pltpu.VMEM((4, 8, CHUNK), F32),
            pltpu.SemaphoreType.DMA((2, 7)),
            pltpu.SemaphoreType.DMA((2, 3)),
        ]
        + sum_scratch(length, width)
        + scatter_scratch(gq.shape[0])
        + scatter_scratch(1),
        compiler_params=params(4),
        name="scatter_attention",
    )(dn1, tok, dmid, sums, packs, gq, go)


FIRST_SCALE = 1.0 / (1.0 - BETA_FIRST**STEP)
SECOND_SCALE = 1.0 / (1.0 - BETA_SECOND**STEP)


def folded(values):
    rows, cols = values.shape
    total = None
    for i in range(rows // 8):
        for j in range(cols // 128):
            tile = values[i * 8 : i * 8 + 8, j * 128 : j * 128 + 128]
            total = tile if total is None else total + tile
    return total


def updated(weight, gradient, first_old, second_old):
    first_new = BETA_FIRST * first_old + (1.0 - BETA_FIRST) * gradient
    second_new = BETA_SECOND * second_old + (1.0 - BETA_SECOND) * gradient * gradient
    update = first_new * FIRST_SCALE / (
        jnp.sqrt(second_new * SECOND_SCALE) + ADAM_EPS
    ) + WEIGHT_DECAY * weight
    return (update, first_new, second_new)


def adam_kernel(*refs):
    sources = [refs[kind * 5 : kind * 5 + 4] for kind in range(4)]
    norm_grad, norm_master, norm_first, norm_second = [refs[kind * 5 + 4] for kind in range(4)]
    outs = [refs[20 + kind * 5 : 24 + kind * 5] for kind in range(3)]
    norm_outs = [refs[24 + kind * 5] for kind in range(3)]
    tile = refs[35]
    held = [refs[36 + kind * 4 : 40 + kind * 4] for kind in range(4)]
    load_sem, store_sem = refs[52:54]
    blocks = [(i, j) for i in range(4) for j in range(sources[0][i].shape[0])]
    loads = []
    for index, (i, j) in enumerate(blocks):
        loads.append([])
        for kind in range(4):
            copy = pltpu.make_async_copy(
                sources[kind][i].at[j], held[kind][i].at[j], load_sem.at[kind, index]
            )
            copy.start()
            loads[index].append(copy)
    weight = norm_master[...]
    update, first_new, second_new = updated(
        weight, norm_grad[0:4, :], norm_first[...], norm_second[...]
    )
    for out, value in zip(norm_outs, (update, first_new, second_new)):
        out[...] = value
    for row, value in ((4, weight), (12, update)):
        square = value * value * 0.25
        tile[row : row + 4, :] = square[:, :128] + square[:, 128:]
    stores = []
    sums = None
    for index, (i, j) in enumerate(blocks):
        if j == 0:
            sums = (jnp.zeros((8, 128), F32), jnp.zeros((8, 128), F32))
        for copy in loads[index]:
            copy.wait()
        grads, masters, firsts, seconds = [held[kind][i] for kind in range(4)]

        def step(k, carry):
            at = pl.ds(pl.multiple_of(k * 16, 16), 16)
            weight = masters[j, at, :]
            update, first_new, second_new = updated(
                weight, grads[j, at, :], firsts[j, at, :], seconds[j, at, :]
            )
            grads[j, at, :] = update
            firsts[j, at, :] = first_new
            seconds[j, at, :] = second_new
            return (carry[0] + folded(weight * weight), carry[1] + folded(update * update))

        sums = lax.fori_loop(0, grads.shape[1] // 16, step, sums)
        for kind, source in enumerate((grads, firsts, seconds)):
            copy = pltpu.make_async_copy(
                source.at[j], outs[kind][i].at[j], store_sem.at[kind, index]
            )
            copy.start()
            stores.append(copy)
        if j == grads.shape[0] - 1:
            tile[i : i + 1, :] = jnp.sum(sums[0], 0, keepdims=True)
            tile[8 + i : 9 + i, :] = jnp.sum(sums[1], 0, keepdims=True)
    for copy in stores:
        copy.wait()


def adam_call(grads, masters, firsts, seconds):
    shapes = [master.shape for master in masters]
    like = [jax.ShapeDtypeStruct(shape, F32) for shape in shapes]
    specs = [ANY] * 4 + [VM]
    count = sum(shape[0] for shape in shapes[:4])
    results = pl.pallas_call(
        adam_kernel,
        out_shape=like * 3 + [jax.ShapeDtypeStruct((16, 128), F32)],
        in_specs=specs * 4,
        out_specs=specs * 3 + [VM],
        scratch_shapes=[pltpu.VMEM(shape, F32) for shape in shapes[:4]] * 4
        + [pltpu.SemaphoreType.DMA((4, count)), pltpu.SemaphoreType.DMA((3, count))],
        compiler_params=local_params(),
        name="adam",
    )(*grads, *masters, *firsts, *seconds)
    return results[0:5], results[5:10], results[10:15], results[15]


def total_kernel(tile, norms, tiles_z, plane_tile, tiles, zs, ps):
    here = Here()
    greet(here, PLANE, (1, 2, 3))
    sent = []
    for step in (2, 1, 3):
        sent.append(
            push(tile, tiles_z.at[here.z], zs.at[0, step - 1], zs.at[1, step - 1], here.along(step))
        )
    tiles_z[pl.ds(here.z, 1)] = tile[...][None]
    for copy in sent:
        copy.wait()
    plane_tile[...] = ((tiles_z[0] + tiles_z[1]) + tiles_z[2]) + tiles_z[3]
    me = here.chunk(0, 0, 0)
    sent = []
    for index, peer in enumerate(PLANE):
        sent.append(
            push(plane_tile, tiles.at[me], ps.at[0, index], ps.at[1, index], here.plane(*peer))
        )
    tiles[pl.ds(me, 1)] = plane_tile[...][None]
    for copy in sent:
        copy.wait()
    total = tiles[0]
    for k in range(1, 8):
        total = total + tiles[k]
    roots = jnp.sqrt(jnp.sum(total, 1, keepdims=True))
    norms[...] = jnp.broadcast_to(roots, norms.shape)


def total_call(tile):
    return pl.pallas_call(
        total_kernel,
        out_shape=jax.ShapeDtypeStruct((16, 128), F32),
        in_specs=[VM],
        out_specs=VM,
        scratch_shapes=[
            pltpu.VMEM((4, 16, 128), F32),
            pltpu.VMEM((16, 128), F32),
            pltpu.VMEM((8, 16, 128), F32),
            pltpu.SemaphoreType.DMA((2, 3)),
            pltpu.SemaphoreType.DMA((2, 7)),
        ],
        compiler_params=params(5),
        name="norm_totals",
    )(tile)


def weight_kernel(*refs):
    norms, updates, masters = refs[0], refs[1:6], refs[6:11]
    outs = refs[11:16]
    held = (refs[16:20], refs[20:24])
    load_sem, store_sem = refs[24:26]
    blocks = [(i, j) for i in range(4) for j in range(updates[i].shape[0])]
    loads = []
    for index, (i, j) in enumerate(blocks):
        loads.append([])
        for kind, source in enumerate((updates, masters)):
            copy = pltpu.make_async_copy(
                source[i].at[j], held[kind][i].at[j], load_sem.at[kind, index]
            )
            copy.start()
            loads[index].append(copy)
    scales = LEARN_RATE * (norms[0:8, 0:1] / norms[8:16, 0:1])
    outs[4][...] = masters[4][...] - scales[4:8, :] * updates[4][...]
    stores = []
    for index, (i, j) in enumerate(blocks):
        for copy in loads[index]:
            copy.wait()
        held[1][i][j] = held[1][i][j] - scales[i : i + 1, :] * held[0][i][j]
        copy = pltpu.make_async_copy(held[1][i].at[j], outs[i].at[j], store_sem.at[index])
        copy.start()
        stores.append(copy)
    for copy in stores:
        copy.wait()


def weight_call(norms, updates, masters):
    shapes = [master.shape for master in masters]
    specs = [ANY] * 4 + [VM]
    count = sum(shape[0] for shape in shapes[:4])
    return pl.pallas_call(
        weight_kernel,
        out_shape=[jax.ShapeDtypeStruct(shape, F32) for shape in shapes],
        in_specs=[VM] + specs * 2,
        out_specs=specs,
        scratch_shapes=[pltpu.VMEM(shape, F32) for shape in shapes[:4]] * 2
        + [pltpu.SemaphoreType.DMA((2, count)), pltpu.SemaphoreType.DMA((count,))],
        compiler_params=local_params(),
        name="new_weights",
    )(norms, *updates, *masters)


def turn(values, cosine, sine):
    return values * cosine + pltpu.roll(values, HEAD_DIM // 2, 1) * sine


def dot(left, right, dims=((1,), (0,))):
    return lax.dot_general(left, right, (dims, ((), ())), preferred_element_type=F32)


def attention_weights(queries, key_rows, lowest):
    scores = dot(queries, key_rows, ((1,), (1,)))
    row = lax.broadcasted_iota(jnp.int32, scores.shape, 0)
    col = lax.broadcasted_iota(jnp.int32, scores.shape, 1)
    allowed = (col <= row) & (col.astype(F32) >= lowest)
    scores = jnp.where(allowed, scores, MASKED)
    exp_scores = jnp.exp(scores - jnp.max(scores, -1, keepdims=True))
    return exp_scores / jnp.sum(exp_scores, -1, keepdims=True)


def attend_body(head0, n1, wq, wo, tables, q_out, k_out, v_out, a_out, part):
    length = tables.shape[2]
    rows_in = n1[...].reshape(2 * length, n1.shape[2])
    projected = [dot(rows_in, wq[j]) for j in range(3)]
    for s in range(2):
        rows = slice(s * length, (s + 1) * length)
        cosine, sine = tables[s, 0], tables[s, 1]
        lowest = tables[s, 2, :, 0:1]
        for h in range(2):
            cols = slice(h * HEAD_DIM, (h + 1) * HEAD_DIM)
            queries = (turn(projected[0][rows, cols], cosine, sine) * HEAD_DIM ** (-0.5)).astype(BF16)
            key_rows = turn(projected[1][rows, cols], cosine, sine).astype(BF16)
            value_rows = projected[2][rows, cols].astype(BF16)
            weights = attention_weights(queries, key_rows, lowest).astype(BF16)
            heads = dot(weights, value_rows)
            active = tables[s, 4] > (head0 + h).astype(F32)
            q_out[rows, cols] = queries
            k_out[rows, cols] = key_rows
            v_out[rows, cols] = value_rows
            a_out[rows, cols] = jnp.where(active, heads, 0.0).astype(BF16)


def attend_out(a_out, wo, part, s):
    length = part.shape[1]
    part[s] = dot(a_out[pl.ds(pl.multiple_of(s * length, length), length), :], wo[0]).astype(BF16)


def fill_table(table, position, bucket, head_count):
    length = table.shape[1]
    row = lax.broadcasted_iota(jnp.int32, (length, length), 0)
    col = lax.broadcasted_iota(jnp.int32, (length, length), 1)

    def column(values):
        return jnp.sum(jnp.where(row == col, values.astype(F32), 0.0), 1, keepdims=True)

    place = column(position)
    lane = lax.broadcasted_iota(jnp.int32, (length, HALF), 1)
    half = HEAD_DIM // 2
    second = lane >= half
    freq_index = jnp.where(second, lane - half, lane).astype(F32)
    angles = place * jnp.exp(freq_index * (-2.0 * math.log(ROPE_BASE) / HEAD_DIM))
    table[0] = jnp.cos(angles)
    sine = jnp.sin(angles)
    table[1] = jnp.where(second, sine, -sine)
    index = lax.broadcasted_iota(jnp.int32, (length, HALF), 0).astype(F32)
    table[2] = index - place
    table[3] = jnp.broadcast_to(column(bucket), (length, HALF))
    table[4] = jnp.broadcast_to(head_count.astype(F32), (length, HALF))


def local_params():
    return pltpu.CompilerParams(vmem_limit_bytes=60 << 20)


def ffn_kernel(n2, cot, bucket, wu, wd, dn2, ffn, gu, gd, back_sum, ffn_sum):
    quarter = pl.program_id(0)

    @pl.when(quarter == 0)
    def _():
        back_sum[...] = jnp.zeros_like(back_sum)
        ffn_sum[...] = jnp.zeros_like(ffn_sum)

    rows_in = n2[...]
    grads_in = cot[...]
    hidden = dot(rows_in, wu[0])
    live = bucket[:, 0:1] >= quarter.astype(F32)
    rectified = jnp.maximum(jnp.where(live, hidden, 0.0), 0.0)
    squared = (rectified * rectified).astype(BF16)
    grad_square = dot(grads_in, wd[0], ((1,), (1,)))
    grad_hidden = (grad_square * 2.0 * rectified).astype(BF16)
    ffn_sum[...] += dot(squared, wd[0])
    back_sum[...] += dot(grad_hidden, wu[0], ((1,), (1,)))
    gu[0] = dot(rows_in, grad_hidden, ((0,), (0,))).astype(BF16)
    gd[0] = dot(squared, grads_in, ((0,), (0,))).astype(BF16)

    @pl.when(quarter == 3)
    def _():
        dn2[...] = back_sum[...].astype(dn2.dtype)
        ffn[...] = ffn_sum[...].astype(ffn.dtype)


def ffn_call(n2, cot, bucket, wu, wd):
    _, length, width = n2.shape
    total = 2 * length
    whole = lambda shape: pl.BlockSpec(shape, lambda r: (0,) * len(shape))
    per = lambda shape: pl.BlockSpec((1,) + shape, lambda r: (r, 0, 0))
    dn2, ffn, gu, gd = pl.pallas_call(
        ffn_kernel,
        grid=(4,),
        out_shape=(
            jax.ShapeDtypeStruct((total, width), BF16),
            jax.ShapeDtypeStruct((total, width), BF16),
            jax.ShapeDtypeStruct((4, width, CHUNK), BF16),
            jax.ShapeDtypeStruct((4, CHUNK, width), BF16),
        ),
        in_specs=[
            whole((total, width)),
            whole((total, width)),
            whole((total, HALF)),
            per((width, CHUNK)),
            per((CHUNK, width)),
        ],
        out_specs=(
            whole((total, width)),
            whole((total, width)),
            per((width, CHUNK)),
            per((CHUNK, width)),
        ),
        scratch_shapes=[pltpu.VMEM((total, width), F32), pltpu.VMEM((total, width), F32)],
        compiler_params=local_params(),
        name="ffn",
    )(n2.reshape(total, width), cot.reshape(total, width), bucket, wu, wd)
    return dn2.reshape(2, length, width), ffn.reshape(2, length, width), gu, gd


def attend_back_kernel(
    head0, gm, n1, a_rows, q_rows, k_rows, v_rows, wq, wo, tables,
    dn1, gq, go, dp,
):
    length = tables.shape[2]
    grads = gm[...]
    go[0] = dot(a_rows[...], grads, ((0,), (0,))).astype(BF16)
    grad_att = dot(grads, wo[0], ((1,), (1,))).astype(BF16)
    for s in range(2):
        rows = slice(s * length, (s + 1) * length)
        cosine, sine = tables[s, 0], tables[s, 1]
        lowest = tables[s, 2, :, 0:1]
        for h in range(2):
            cols = slice(h * HEAD_DIM, (h + 1) * HEAD_DIM)
            active = tables[s, 4] > (head0[0] + h).astype(F32)
            grad_heads = jnp.where(active, grad_att[rows, cols].astype(F32), 0.0).astype(BF16)
            queries, key_rows, value_rows = q_rows[rows, cols], k_rows[rows, cols], v_rows[rows, cols]
            weights = attention_weights(queries, key_rows, lowest)
            grad_weights = dot(grad_heads, value_rows, ((1,), (1,)))
            inner = jnp.sum(weights * grad_weights, -1, keepdims=True)
            grad_scores = (weights * (grad_weights - inner)).astype(BF16)
            grad_query = dot(grad_scores, key_rows) * HEAD_DIM ** (-0.5)
            grad_keys = dot(grad_scores, queries, ((0,), (0,)))
            grad_values = dot(weights.astype(BF16), grad_heads, ((0,), (0,)))
            dp[0, rows, cols] = turn(grad_query, cosine, -sine).astype(BF16)
            dp[1, rows, cols] = turn(grad_keys, cosine, -sine).astype(BF16)
            dp[2, rows, cols] = grad_values.astype(BF16)
    for s in range(2):
        rows = slice(s * length, (s + 1) * length)
        total = dot(dp[0, rows, :], wq[0], ((1,), (1,)))
        total = total + dot(dp[1, rows, :], wq[1], ((1,), (1,)))
        total = total + dot(dp[2, rows, :], wq[2], ((1,), (1,)))
        dn1[s] = total.astype(dn1.dtype)
    rows_in = n1[...]
    for j in range(3):
        gq[j] = dot(rows_in, dp[j], ((0,), (0,))).astype(BF16)


def attend_back_call(head0, gm, n1, a_rows, q_rows, k_rows, v_rows, wq, wo, tables):
    _, length, width = n1.shape
    return pl.pallas_call(
        attend_back_kernel,
        out_shape=(
            jax.ShapeDtypeStruct((2, length, width), BF16),
            jax.ShapeDtypeStruct((3, width, CHUNK), BF16),
            jax.ShapeDtypeStruct((1, CHUNK, width), BF16),
        ),
        in_specs=[SM] + [VM] * 9,
        out_specs=(VM,) * 3,
        scratch_shapes=[pltpu.VMEM((3, 2 * length, CHUNK), BF16)],
        compiler_params=local_params(),
        name="attend_back",
    )(
        head0, gm.reshape(2 * length, width), n1.reshape(2 * length, width),
        a_rows, q_rows, k_rows, v_rows, wq, wo, tables,
    )


def fast_body(
    tokens, cotangent, head_counts, positions, buckets,
    in_master, out_master, up_master, down_master, norm_master,
    in_first, out_first, up_first, down_first, norm_first,
    in_second, out_second, up_second, down_second, norm_second,
):
    length = tokens.shape[1]
    groups_data = lax.axis_size("dp") * lax.axis_size("expert")
    tok, cot = tokens[0], cotangent[0]
    (n1, both_cot, tables, packs, n2, mid, q_rows, k_rows, v_rows, a_rows), (wq, wo, wu, wd) = front_call(
        head_counts, positions, buckets, tok, cot, norm_master,
        (in_master, out_master[None], up_master, down_master),
    )
    bucket_share = jnp.sum(packs[:, 4, :4], 0) / (length * groups_data)
    heads_here = 2 * CHUNK // HEAD_DIM
    core = lax.rem(lax.axis_index("dp"), 2)
    head0 = (lax.axis_index("tensor") * heads_here + core * (heads_here // 2))[None].astype(jnp.int32)
    place = lax.axis_index("tensor") * ROWS
    tok_own = lax.dynamic_slice_in_dim(tok, place, ROWS, 0)
    cot_own = lax.dynamic_slice_in_dim(cot, place, ROWS, 0)
    bucket = tables[:, 3].reshape(2 * length, HALF)
    dn2, ffn, gu, gd = ffn_call(n2, both_cot, bucket, wu, wd)
    gm, dmid, out_own, sums, up_sum, down_sum = third_call(dn2, ffn, mid, cot_own, packs, gu, gd)
    dn1, gq, go = attend_back_call(head0, gm, n1, a_rows, q_rows, k_rows, v_rows, wq, wo, tables)
    gather_tensor = lambda rows: lax.all_gather(rows, "tensor", axis=0, tiled=True).astype(F32)
    output = gather_tensor(out_own)
    ig_own, norm_sum, in_sum, out_sum = fourth_call(dn1, tok_own, dmid, sums, packs, gq, go)
    input_grad = gather_tensor(ig_own)
    masters = (in_master, out_master[None], up_master, down_master, norm_master)
    firsts = (in_first, out_first[None], up_first, down_first, norm_first)
    seconds = (in_second, out_second[None], up_second, down_second, norm_second)
    updates, moments, squares, tile = adam_call(
        (in_sum, out_sum, up_sum, down_sum, norm_sum), masters, firsts, seconds
    )
    norms = total_call(tile)
    weights = weight_call(norms, updates, masters)
    flat = lambda group: (group[0], group[1][0], group[2], group[3], group[4])
    return (
        output[None],
        input_grad[None],
        bucket_share,
        norms[:, 0].reshape(2, 8),
        *flat(weights),
        *flat(moments),
        *flat(squares),
    )


def solution(mesh):
    placed = (
        P(("dp", "expert"), None, None),
        P(("dp", "expert"), None, None),
        P(("dp", "expert")),
        P(("dp", "expert"), None),
        P(("dp", "expert"), None),
        P(None, ("dp", "expert"), "tensor"),
        P("tensor", ("dp", "expert")),
        P(None, ("dp", "expert"), "tensor"),
        P(None, "tensor", ("dp", "expert")),
        P(None, ("dp", "expert")),
        P(None, ("dp", "expert"), "tensor"),
        P("tensor", ("dp", "expert")),
        P(None, ("dp", "expert"), "tensor"),
        P(None, "tensor", ("dp", "expert")),
        P(None, ("dp", "expert")),
        P(None, ("dp", "expert"), "tensor"),
        P("tensor", ("dp", "expert")),
        P(None, ("dp", "expert"), "tensor"),
        P(None, "tensor", ("dp", "expert")),
        P(None, ("dp", "expert")),
    )
    shape = dict(mesh.shape)
    fits = shape == {"dp": 4, "expert": 2, "tensor": 4}
    return jax.shard_map(
        fast_body if fits else body,
        mesh=mesh,
        in_specs=placed,
        out_specs=(
            P(("dp", "expert"), None, None),
            P(("dp", "expert"), None, None),
            P(),
            P(),
            P(None, ("dp", "expert"), "tensor"),
            P("tensor", ("dp", "expert")),
            P(None, ("dp", "expert"), "tensor"),
            P(None, "tensor", ("dp", "expert")),
            P(None, ("dp", "expert")),
            P(None, ("dp", "expert"), "tensor"),
            P("tensor", ("dp", "expert")),
            P(None, ("dp", "expert"), "tensor"),
            P(None, "tensor", ("dp", "expert")),
            P(None, ("dp", "expert")),
            P(None, ("dp", "expert"), "tensor"),
            P("tensor", ("dp", "expert")),
            P(None, ("dp", "expert"), "tensor"),
            P(None, "tensor", ("dp", "expert")),
            P(None, ("dp", "expert")),
        ),
        check_vma=False,
    )
```

```python
import math

import jax
import jax.numpy as jnp
from jax import lax
from jax.experimental import pallas as pl
from jax.experimental.pallas import tpu as pltpu
from jax.sharding import PartitionSpec as P

HEAD_DIM = 128
STEP = 10


NORM_EPS = 1e-05
BETA_FIRST = 0.9
BETA_SECOND = 0.999
ADAM_EPS = 1e-06
WEIGHT_DECAY = 0.01
LEARN_RATE = 0.25
MASKED = -1e30
ROPE_BASE = 10000.0


def layer_norm(values, gain_row, shift_row):
    center = values - jnp.mean(values, -1, keepdims=True)
    variance = jnp.mean(center * center, -1, keepdims=True)
    inv_std = lax.rsqrt(variance + NORM_EPS)
    normed = center * inv_std
    return (normed * gain_row + shift_row, normed, inv_std)


def norm_back_rows(grad_out, normed, inv_std, gain_row):
    scaled = grad_out * gain_row
    inner_part = (
        scaled
        - jnp.mean(scaled, -1, keepdims=True)
        - normed * jnp.mean(scaled * normed, -1, keepdims=True)
    )
    return (inner_part * inv_std, jnp.sum(grad_out * normed, 0), jnp.sum(grad_out, 0))


def rope_angles(position_row):
    freq_index = jnp.arange(HEAD_DIM // 2, dtype=jnp.float32)
    inverse = jnp.exp(freq_index * (-2.0 * jnp.log(ROPE_BASE) / HEAD_DIM))
    return position_row.astype(jnp.float32)[:, None] * inverse[None, :]


def rotary(values, angles, sign_value):
    half_dim = values.shape[-1] // 2
    cosine = jnp.cos(angles)[:, None, :]
    sine_part = sign_value * jnp.sin(angles)[:, None, :]
    first_half = values[..., :half_dim]
    second_half = values[..., half_dim:]
    return jnp.concatenate(
        [
            first_half * cosine - second_half * sine_part,
            second_half * cosine + first_half * sine_part,
        ],
        -1,
    )


def block_mask(key_index, position_row, block_start, block_rows):
    query_index = block_start + jnp.arange(block_rows, dtype=jnp.int32)
    return (key_index[None, :] <= query_index[:, None]) & (
        key_index[None, :] >= (query_index - position_row)[:, None]
    )


def attend_forward(queries, key_rows, value_rows, position_row, block_rows):
    length = queries.shape[0]
    key_index = jnp.arange(length, dtype=jnp.int32)

    def one_block(block_start):
        allowed = block_mask(key_index, position_row, block_start, block_rows)
        scores = jnp.einsum("qhd,khd->hqk", queries, key_rows, preferred_element_type=jnp.float32)
        scores = jnp.where(allowed[None], scores, MASKED)
        row_peak = jnp.max(scores, -1, keepdims=True)
        exp_scores = jnp.exp(scores - row_peak)
        row_total = jnp.sum(exp_scores, -1, keepdims=True)
        attn_weights = (exp_scores / row_total).astype(jnp.bfloat16)
        block_out = jnp.einsum(
            "hqk,khd->qhd", attn_weights, value_rows, preferred_element_type=jnp.float32
        )
        return (block_out, row_peak[..., 0] + jnp.log(row_total[..., 0]))

    starts = jnp.arange(length // block_rows, dtype=jnp.int32) * block_rows
    block_outs, log_totals = lax.map(one_block, starts)
    return (block_outs.reshape(queries.shape), log_totals, starts)


def attend_backward(
    queries, key_rows, value_rows, position_row, grad_heads, log_totals, starts, block_rows
):
    length = queries.shape[0]
    key_index = jnp.arange(length, dtype=jnp.int32)

    def one_block(carried, inputs):
        block_start, block_log = inputs
        allowed = block_mask(key_index, position_row, block_start, block_rows)
        scores = jnp.einsum("qhd,khd->hqk", queries, key_rows, preferred_element_type=jnp.float32)
        scores = jnp.where(allowed[None], scores, MASKED)
        attn_probs = jnp.exp(scores - block_log[..., None])
        grad_probs = jnp.einsum(
            "qhd,khd->hqk", grad_heads, value_rows, preferred_element_type=jnp.float32
        )
        row_inner = jnp.sum(attn_probs * grad_probs, -1, keepdims=True)
        grad_scores = (attn_probs * (grad_probs - row_inner)).astype(jnp.bfloat16)
        grad_query = jnp.einsum(
            "hqk,khd->qhd", grad_scores, key_rows, preferred_element_type=jnp.float32
        )
        grad_keys = carried[0] + jnp.einsum(
            "hqk,qhd->khd", grad_scores, queries, preferred_element_type=jnp.float32
        )
        grad_values = carried[1] + jnp.einsum(
            "hqk,qhd->khd",
            attn_probs.astype(jnp.bfloat16),
            grad_heads,
            preferred_element_type=jnp.float32,
        )
        return ((grad_keys, grad_values), grad_query)

    start_state = (jnp.zeros(key_rows.shape, jnp.float32), jnp.zeros(value_rows.shape, jnp.float32))
    (grad_keys, grad_values), grad_query = lax.scan(one_block, start_state, (starts, log_totals))
    return (grad_query.reshape(queries.shape), grad_keys, grad_values)


def gather_rows(values, source_rows):
    padded = jnp.concatenate([values, jnp.zeros((1, values.shape[1]), values.dtype)], 0)
    return padded[source_rows]


def ffn_forward(rows_in, bucket, up_work, down_work):
    row_count = rows_in.shape[0]
    mixed_sum = jnp.zeros((row_count, down_work.shape[2]), jnp.float32)
    hiddens = []
    for quarter in range(4):

        def live_part():
            hidden = jnp.dot(rows_in, up_work[quarter], preferred_element_type=jnp.float32)
            squared = jnp.square(jnp.maximum(hidden, 0.0)).astype(jnp.bfloat16)
            return (
                hidden,
                jnp.dot(squared, down_work[quarter], preferred_element_type=jnp.float32),
            )

        def dead_part():
            return (
                jnp.zeros((row_count, up_work.shape[2]), jnp.float32),
                jnp.zeros_like(mixed_sum),
            )

        hidden, contribution = lax.cond(bucket >= quarter, live_part, dead_part)
        hiddens.append(hidden)
        mixed_sum = mixed_sum + contribution
    return (mixed_sum, hiddens)


def ffn_backward(rows_in, grads_in, bucket, hiddens, up_work, down_work):
    grad_rows = jnp.zeros((rows_in.shape[0], up_work.shape[1]), jnp.float32)
    grad_up = []
    grad_down = []
    for quarter in range(4):
        hidden = hiddens[quarter]

        def live_part():
            rectified = jnp.maximum(hidden, 0.0)
            squared = jnp.square(rectified).astype(jnp.bfloat16)
            grad_square = jnp.einsum(
                "rd,ud->ru", grads_in, down_work[quarter], preferred_element_type=jnp.float32
            )
            grad_hidden = (grad_square * 2.0 * rectified).astype(jnp.bfloat16)
            return (
                jnp.einsum("rd,ru->du", rows_in, grad_hidden, preferred_element_type=jnp.float32),
                jnp.einsum("ru,rd->ud", squared, grads_in, preferred_element_type=jnp.float32),
                jnp.einsum(
                    "ru,du->rd", grad_hidden, up_work[quarter], preferred_element_type=jnp.float32
                ),
            )

        def dead_part():
            return (
                jnp.zeros(up_work.shape[1:], jnp.float32),
                jnp.zeros(down_work.shape[1:], jnp.float32),
                jnp.zeros_like(grad_rows),
            )

        part_up, part_down, part_rows = lax.cond(bucket >= quarter, live_part, dead_part)
        grad_up.append(part_up)
        grad_down.append(part_down)
        grad_rows = grad_rows + part_rows
    return (grad_rows, jnp.stack(grad_up), jnp.stack(grad_down))


def ffn_total(partial_value):
    return lax.psum(partial_value, "tensor")


def ffn_grad_total(partial_value):
    return lax.psum(partial_value, "tensor")


def adam_terms(weight, gradient, first_old, second_old):
    first_new = BETA_FIRST * first_old + (1.0 - BETA_FIRST) * gradient
    second_new = BETA_SECOND * second_old + (1.0 - BETA_SECOND) * gradient * gradient
    update = (
        first_new
        / (1.0 - BETA_FIRST**STEP)
        / (jnp.sqrt(second_new / (1.0 - BETA_SECOND**STEP)) + ADAM_EPS)
        + WEIGHT_DECAY * weight
    )
    return (update, first_new, second_new)


def finish(output, input_grad, bucket_share, masters, firsts, seconds, grad_shards, tensor_count):
    norm_master = masters[4]
    adam_out = [
        adam_terms(masters[member], grad_shards[member], firsts[member], seconds[member])
        for member in range(5)
    ]
    weight_sq = jnp.concatenate(
        [
            jnp.stack([jnp.sum(masters[member] * masters[member]) for member in range(4)]),
            jnp.sum(norm_master * norm_master, 1) / tensor_count,
        ]
    )
    update_sq = jnp.concatenate(
        [
            jnp.stack([jnp.sum(adam_out[member][0] * adam_out[member][0]) for member in range(4)]),
            jnp.sum(adam_out[4][0] * adam_out[4][0], 1) / tensor_count,
        ]
    )
    weight_tot, update_tot = lax.psum((weight_sq, update_sq), ("dp", "expert", "tensor"))
    weight_norms = jnp.sqrt(weight_tot)
    update_norms = jnp.sqrt(update_tot)
    ratios = weight_norms / update_norms
    new_weights = [
        masters[member] - LEARN_RATE * ratios[member] * adam_out[member][0] for member in range(4)
    ]
    norm_new = norm_master - LEARN_RATE * ratios[4:, None] * adam_out[4][0]
    lamb_norms = jnp.stack([weight_norms, update_norms])
    return (
        output[None],
        input_grad[None],
        bucket_share,
        lamb_norms,
        new_weights[0],
        new_weights[1],
        new_weights[2],
        new_weights[3],
        norm_new,
        adam_out[0][1],
        adam_out[1][1],
        adam_out[2][1],
        adam_out[3][1],
        adam_out[4][1],
        adam_out[0][2],
        adam_out[1][2],
        adam_out[2][2],
        adam_out[3][2],
        adam_out[4][2],
    )


def body(
    tokens,
    cotangent,
    head_counts,
    positions,
    buckets,
    in_master,
    out_master,
    up_master,
    down_master,
    norm_master,
    in_first,
    out_first,
    up_first,
    down_first,
    norm_first,
    in_second,
    out_second,
    up_second,
    down_second,
    norm_second,
):
    in_work, out_work, up_work, down_work, norm_work = (
        lax.all_gather(in_master.astype(jnp.bfloat16), ("dp", "expert"), axis=1, tiled=True),
        lax.all_gather(out_master.astype(jnp.bfloat16), ("dp", "expert"), axis=1, tiled=True),
        lax.all_gather(up_master.astype(jnp.bfloat16), ("dp", "expert"), axis=1, tiled=True),
        lax.all_gather(down_master.astype(jnp.bfloat16), ("dp", "expert"), axis=2, tiled=True),
        lax.all_gather(norm_master.astype(jnp.bfloat16), ("dp", "expert"), axis=1, tiled=True),
    )
    length = tokens.shape[1]
    model_width = tokens.shape[2]
    heads_here = in_work.shape[2] // HEAD_DIM
    block_rows = min(512, length)
    head_scale = HEAD_DIM ** (-0.5)
    groups_data = lax.axis_size("dp") * lax.axis_size("expert")
    tensor_count = lax.axis_size("tensor")
    experts = lax.axis_size("expert")
    norm_gains = norm_work.astype(jnp.float32)
    inputs = tokens[0].astype(jnp.float32)
    first_norm, first_hat, first_inv = layer_norm(inputs, norm_gains[0], norm_gains[1])
    first_in = first_norm.astype(jnp.bfloat16)
    projected = jnp.einsum("td,jde->jte", first_in, in_work, preferred_element_type=jnp.float32)
    projected = projected.reshape(3, length, heads_here, HEAD_DIM)
    angles = rope_angles(positions[0])
    queries = (rotary(projected[0], angles, 1.0) * head_scale).astype(jnp.bfloat16)
    key_rows = rotary(projected[1], angles, 1.0).astype(jnp.bfloat16)
    value_rows = projected[2].astype(jnp.bfloat16)
    head_ids = lax.axis_index("tensor") * heads_here + jnp.arange(heads_here, dtype=jnp.int32)
    active = (head_ids < head_counts[0]).astype(jnp.float32)
    head_outs, log_totals, starts = attend_forward(
        queries, key_rows, value_rows, positions[0], block_rows
    )
    attended = (
        (head_outs * active[None, :, None])
        .astype(jnp.bfloat16)
        .reshape(length, heads_here * HEAD_DIM)
    )
    attn_part = jnp.dot(attended, out_work, preferred_element_type=jnp.float32)
    middle = inputs + lax.psum(attn_part, "tensor")
    second_norm, second_hat, second_inv = layer_norm(middle, norm_gains[2], norm_gains[3])
    second_in = second_norm.astype(jnp.bfloat16)
    bucket_ids = buckets[0]
    onehot = (bucket_ids[:, None] == jnp.arange(4, dtype=jnp.int32)[None, :]).astype(jnp.int32)
    bucket_rank = jnp.sum((jnp.cumsum(onehot, 0) - onehot) * onehot, 1)
    local_counts = jnp.sum(onehot, 0).astype(jnp.float32)
    bucket_share = lax.psum(local_counts, ("dp", "expert")) / (length * groups_data)
    most_rows = 5 * length // 16
    owner_group = max(experts // 4, 1)
    per_owner = max(4 // experts, 1)
    slot_rows = (most_rows + owner_group - 1) // owner_group
    capacity = per_owner * slot_rows
    slot_of = (
        (bucket_ids // per_owner * owner_group + bucket_rank % owner_group) * capacity
        + bucket_ids % per_owner * slot_rows
        + bucket_rank // owner_group
    )
    slot_total = experts * capacity
    source_rows = (
        jnp.full((slot_total,), length, jnp.int32)
        .at[slot_of]
        .set(jnp.arange(length, dtype=jnp.int32))
    )
    outgoing = gather_rows(second_in, source_rows).reshape(experts, capacity, model_width)
    incoming = lax.all_to_all(outgoing, "expert", split_axis=0, concat_axis=0, tiled=True).reshape(
        experts, per_owner, slot_rows, model_width
    )
    owner_index = lax.axis_index("expert")
    owned_ids = [owner_index // owner_group * per_owner + member for member in range(per_owner)]
    ffn_inputs = [
        incoming[:, member].reshape(experts * slot_rows, model_width) for member in range(per_owner)
    ]
    results = [
        ffn_forward(ffn_inputs[member], owned_ids[member], up_work, down_work)
        for member in range(per_owner)
    ]
    partial_value = jnp.stack(
        [
            results[member][0].reshape(experts, slot_rows, model_width)
            for member in range(per_owner)
        ],
        1,
    )
    summed = ffn_total(partial_value.reshape(experts, capacity, model_width)).astype(jnp.bfloat16)
    returned = lax.all_to_all(summed, "expert", split_axis=0, concat_axis=0, tiled=True)
    branch_out = returned.reshape(slot_total, model_width)[slot_of]
    output = middle + branch_out.astype(jnp.float32)
    grad_branch = cotangent[0]
    outgoing_grad = gather_rows(grad_branch, source_rows).reshape(experts, capacity, model_width)
    incoming_grad = lax.all_to_all(
        outgoing_grad, "expert", split_axis=0, concat_axis=0, tiled=True
    ).reshape(experts, per_owner, slot_rows, model_width)
    ffn_grads = [
        incoming_grad[:, member].reshape(experts * slot_rows, model_width)
        for member in range(per_owner)
    ]
    back_parts = [
        ffn_backward(
            ffn_inputs[member],
            ffn_grads[member],
            owned_ids[member],
            results[member][1],
            up_work,
            down_work,
        )
        for member in range(len(owned_ids))
    ]
    grad_up = back_parts[0][1]
    grad_down = back_parts[0][2]
    for member in range(1, len(owned_ids)):
        grad_up = grad_up + back_parts[member][1]
        grad_down = grad_down + back_parts[member][2]
    rows_back = jnp.stack(
        [
            back_parts[member][0].reshape(experts, slot_rows, model_width)
            for member in range(per_owner)
        ],
        1,
    )
    summed_back = ffn_grad_total(rows_back.reshape(experts, capacity, model_width)).astype(
        jnp.bfloat16
    )
    returned_back = lax.all_to_all(summed_back, "expert", split_axis=0, concat_axis=0, tiled=True)
    grad_second = returned_back.reshape(slot_total, model_width)[slot_of].astype(jnp.float32)
    grad_mid_norm, gain_second, shift_second = norm_back_rows(
        grad_second, second_hat, second_inv, norm_gains[2]
    )
    grad_middle = grad_branch.astype(jnp.float32) + grad_mid_norm
    grad_attn = grad_middle.astype(jnp.bfloat16)
    grad_attended = jnp.einsum("td,ed->te", grad_attn, out_work, preferred_element_type=jnp.float32)
    grad_out_w = jnp.einsum("te,td->ed", attended, grad_attn, preferred_element_type=jnp.float32)
    grad_heads = (
        grad_attended.astype(jnp.bfloat16).reshape(length, heads_here, HEAD_DIM)
        * active.astype(jnp.bfloat16)[None, :, None]
    )
    grad_query, grad_keys, grad_values = attend_backward(
        queries, key_rows, value_rows, positions[0], grad_heads, log_totals, starts, block_rows
    )
    grad_projected = jnp.stack(
        [
            rotary(grad_query * head_scale, angles, -1.0),
            rotary(grad_keys, angles, -1.0),
            grad_values,
        ]
    )
    grad_projected = grad_projected.reshape(3, length, heads_here * HEAD_DIM).astype(jnp.bfloat16)
    grad_in_w = jnp.einsum(
        "td,jte->jde", first_in, grad_projected, preferred_element_type=jnp.float32
    )
    grad_first_part = jnp.einsum(
        "jte,jde->td", grad_projected, in_work, preferred_element_type=jnp.float32
    )
    grad_first = lax.psum(grad_first_part, "tensor")
    grad_input_norm, gain_first, shift_first = norm_back_rows(
        grad_first, first_hat, first_inv, norm_gains[0]
    )
    input_grad = grad_middle + grad_input_norm
    grad_norm = jnp.stack([gain_first, shift_first, gain_second, shift_second])
    in_sum, out_sum, up_sum, down_sum, norm_sum = (
        lax.psum_scatter(grad_in_w, ("dp", "expert"), scatter_dimension=1, tiled=True),
        lax.psum_scatter(grad_out_w, ("dp", "expert"), scatter_dimension=1, tiled=True),
        lax.psum_scatter(grad_up, ("dp", "expert"), scatter_dimension=1, tiled=True),
        lax.psum_scatter(grad_down, ("dp", "expert"), scatter_dimension=2, tiled=True),
        lax.psum_scatter(grad_norm, ("dp", "expert"), scatter_dimension=1, tiled=True),
    )
    masters = (in_master, out_master, up_master, down_master, norm_master)
    firsts = (in_first, out_first, up_first, down_first, norm_first)
    seconds = (in_second, out_second, up_second, down_second, norm_second)
    grad_shards = (in_sum, out_sum, up_sum, down_sum, norm_sum)
    return finish(output, input_grad, bucket_share, masters, firsts, seconds, grad_shards, tensor_count)


MESH = pl.DeviceIdType.MESH
ANY = pl.BlockSpec(memory_space=pl.ANY)
VM = pl.BlockSpec(memory_space=pltpu.VMEM)
SM = pl.BlockSpec(memory_space=pltpu.SMEM)

F32 = jnp.float32
BF16 = jnp.bfloat16
CHUNK = 256
HALF = 128
ROWS = 64


class Here:
    def __init__(self):
        d = lax.axis_index("dp")
        self.x, self.c = d // 2, lax.rem(d, 2)
        self.y = lax.axis_index("expert")
        self.z = lax.axis_index("tensor")

    def plane(self, dx, dc, dy):
        x = 1 - self.x if dx else self.x
        c = 1 - self.c if dc else self.c
        y = 1 - self.y if dy else self.y
        return (x * 2 + c, y, self.z)

    def chunk(self, dx, dc, dy):
        x = 1 - self.x if dx else self.x
        c = 1 - self.c if dc else self.c
        y = 1 - self.y if dy else self.y
        return (x * 2 + c) * 2 + y

    def chunk_of(self, dx, dy, core):
        x = 1 - self.x if dx else self.x
        y = 1 - self.y if dy else self.y
        return (x * 2 + core) * 2 + y

    def along(self, step):
        return (self.x * 2 + self.c, self.y, lax.rem(self.z + step, 4))

    def behind(self, step):
        return lax.rem(self.z + 4 - step, 4)


PARTNER = (0, 1, 0)
PLANE = [(a, b, g) for a in (0, 1) for b in (0, 1) for g in (0, 1) if a + b + g > 0]
SIDES = [(1, 0, 0), (1, 1, 0), (0, 0, 1), (0, 1, 1)]


def greet(here, plane_peers, tensor_peers):
    barrier = pltpu.get_barrier_semaphore()
    for peer in plane_peers:
        pl.semaphore_signal(barrier, inc=1, device_id=here.plane(*peer), device_id_type=MESH)
    for step in tensor_peers:
        pl.semaphore_signal(barrier, inc=1, device_id=here.along(step), device_id_type=MESH)
    pl.semaphore_wait(barrier, len(plane_peers) + len(tensor_peers))


def push(src, dst, send, recv, device):
    copy = pltpu.make_async_remote_copy(
        src_ref=src, dst_ref=dst, send_sem=send, recv_sem=recv, device_id=device, device_id_type=MESH
    )
    copy.start()
    return copy


def block(index, size):
    return pl.ds(pl.multiple_of(index * size, size), size)


def rows_chunk(ref, k):
    return ref.at[:, block(k, CHUNK), :]


def rows_part(ref, k, part):
    return ref.at[:, pl.ds(pl.multiple_of(k * CHUNK + part * HALF, HALF), HALF), :]


def cols_chunk(ref, k):
    return ref.at[:, :, block(k, CHUNK)]


def cols_part(ref, k, part):
    return ref.at[:, part * HALF : part * HALF + HALF, block(k, CHUNK)]


class Gather:
    def __init__(self, here, by_rows, shard, whole, first, relay, local):
        self.here, self.by_rows, self.shard, self.whole = here, by_rows, shard, whole
        self.first, self.relay, self.local = first, relay, local
        self.copies = []

    def half(self, core):
        if self.by_rows:
            return self.shard.at[:, :, block(core, CHUNK)]
        return self.shard.at[:, block(core, CHUNK), :]

    def chunk(self, k):
        return rows_chunk(self.whole, k) if self.by_rows else cols_chunk(self.whole, k)

    def part(self, k, part):
        return rows_part(self.whole, k, part) if self.by_rows else cols_part(self.whole, k, part)

    def start(self):
        here = self.here
        mine = self.chunk(here.chunk(0, 0, 0))
        for index, side in enumerate(SIDES + [PARTNER]):
            core = 1 - here.c if side[1] else here.c
            self.copies.append(
                push(
                    self.half(core),
                    mine,
                    self.first.at[0, index],
                    self.first.at[1, index],
                    here.plane(*side),
                )
            )
        self.own = pltpu.make_async_copy(self.half(here.c), mine, self.local)
        self.own.start()

    def forward(self):
        here = self.here
        self.onward = []
        for index in range(4):
            side = SIDES[index]
            self.copies[index].wait_recv()
            part = 0 if side[0] else 1
            where = self.part(here.chunk(*side), part)
            target = (0, 0, 1) if side[0] else (1, 0, 0)
            self.onward.append(
                push(
                    where,
                    where,
                    self.relay.at[0, index],
                    self.relay.at[1, index],
                    here.plane(*target),
                )
            )

    def finish(self):
        for index in range(4):
            self.copies[index].wait_send()
        self.copies[4].wait()
        self.own.wait()
        for copy in self.onward:
            copy.wait()


def gather_sems():
    return [
        pltpu.SemaphoreType.DMA((2, 5)),
        pltpu.SemaphoreType.DMA((2, 4)),
        pltpu.SemaphoreType.DMA,
    ]


class Scatter:
    def __init__(self, here, by_rows, grad, total, bufs):
        self.here, self.by_rows, self.grad, self.total = here, by_rows, grad, total
        self.got, self.got_two = bufs[:2]
        self.one_sem, self.two_sem, self.last_sem, self.local = bufs[2:6]
        self.final = bufs[6]

    def part(self, dx, dy, core, side):
        k = self.here.chunk_of(dx, dy, core)
        return rows_part(self.grad, k, side) if self.by_rows else cols_part(self.grad, k, side)

    def start(self):
        here = self.here
        self.first = []
        for side in (0, 1):
            near, far = ((1, 0), (1, 1)) if side == 0 else ((0, 1), (1, 1))
            target = here.plane(1, 0, 0) if side == 0 else here.plane(0, 0, 1)
            for slot in range(4):
                chip = far if slot >= 2 else near
                index = side * 4 + slot
                self.first.append(
                    push(
                        self.part(chip[0], chip[1], slot % 2, side),
                        self.got.at[index],
                        self.one_sem.at[0, index],
                        self.one_sem.at[1, index],
                        target,
                    )
                )

    def middle(self):
        here = self.here
        self.second = []
        for side in (0, 1):
            target = here.plane(0, 0, 1) if side == 0 else here.plane(1, 0, 0)
            chip = (0, 1) if side == 0 else (1, 0)
            for slot in (2, 3):
                index = side * 4 + slot
                two = side * 2 + slot - 2
                mine = self.part(chip[0], chip[1], slot - 2, side)
                self.first[index].wait_recv()
                mine[...] = (mine[...].astype(F32) + self.got[index].astype(F32)).astype(BF16)
                self.second.append(
                    push(
                        mine,
                        self.got_two.at[two],
                        self.two_sem.at[0, two],
                        self.two_sem.at[1, two],
                        target,
                    )
                )

    def last(self):
        here = self.here
        for side in (0, 1):
            for slot in (0, 1):
                index = side * 4 + slot
                two = side * 2 + slot
                self.first[index].wait_recv()
                self.second[two].wait_recv()
                self.final[slot, :, side * HALF : side * HALF + HALF, :] = (
                    self.part(0, 0, slot, side)[...].astype(F32) + self.got[index].astype(F32)
                ) + self.got_two[two].astype(F32)
        if self.by_rows:
            where = self.total.at[:, :, block(here.c, CHUNK)]
        else:
            where = self.total.at[:, block(here.c, CHUNK), :]
        self.keep = pltpu.make_async_copy(self.final.at[here.c], where, self.local)
        self.keep.start()
        self.give = push(
            self.final.at[1 - here.c],
            where,
            self.last_sem.at[0],
            self.last_sem.at[1],
            here.plane(*PARTNER),
        )

    def sent(self):
        self.keep.wait()
        self.give.wait_send()

    def finish(self):
        for copy in self.first:
            copy.wait_send()
        for copy in self.second:
            copy.wait_send()
        self.give.wait_recv()


def scatter_scratch(width):
    return [
        pltpu.VMEM((8, width, HALF, CHUNK), BF16),
        pltpu.VMEM((4, width, HALF, CHUNK), BF16),
        pltpu.SemaphoreType.DMA((2, 8)),
        pltpu.SemaphoreType.DMA((2, 4)),
        pltpu.SemaphoreType.DMA((2,)),
        pltpu.SemaphoreType.DMA,
    ]


SCATTER = 6


class TensorSum:
    def __init__(self, here, part, bufs):
        self.here, self.part = here, part
        self.pair, self.out, self.inn, self.pair_sem, self.sem = bufs

    def start(self):
        here = self.here
        self.swap = push(
            self.part.at[1 - here.c],
            self.pair,
            self.pair_sem.at[0],
            self.pair_sem.at[1],
            here.plane(*PARTNER),
        )

    def spread(self):
        here = self.here
        self.swap.wait_recv()
        self.sent = []
        for step in (2, 1, 3):
            rows = block(lax.rem(here.z + step, 4), ROWS)
            self.out[step - 1] = (
                self.part[here.c, rows, :].astype(F32) + self.pair[rows, :].astype(F32)
            ).astype(self.out.dtype)
            self.sent.append(
                push(
                    self.out.at[step - 1],
                    self.inn.at[step - 1],
                    self.sem.at[0, step - 1],
                    self.sem.at[1, step - 1],
                    here.along(step),
                )
            )

    def result(self):
        here = self.here
        rows = block(here.z, ROWS)
        total = self.part[here.c, rows, :].astype(F32) + self.pair[rows, :].astype(F32)
        for copy in self.sent:
            copy.wait_recv()
        for step in (1, 2, 3):
            total = total + self.inn[step - 1].astype(F32)
        return total

    def finish(self):
        self.swap.wait_send()
        for copy in self.sent:
            copy.wait_send()


def sum_scratch(length, width):
    return [
        pltpu.VMEM((length, width), BF16),
        pltpu.VMEM((3, ROWS, width), BF16),
        pltpu.VMEM((3, ROWS, width), BF16),
        pltpu.SemaphoreType.DMA((2,)),
        pltpu.SemaphoreType.DMA((2, 3)),
    ]


class TensorGather:
    def __init__(self, here, mine, whole, sem, pair_sem, local):
        self.here, self.mine, self.whole = here, mine, whole
        self.sem, self.pair_sem, self.local = sem, pair_sem, local

    def start(self):
        here = self.here
        place = self.whole.at[here.c, block(here.z, ROWS), :]
        self.sent = []
        for step in (2, 1, 3):
            self.sent.append(
                push(
                    self.mine,
                    place,
                    self.sem.at[0, step - 1],
                    self.sem.at[1, step - 1],
                    here.along(step),
                )
            )
        self.shared = [
            push(
                self.mine,
                place,
                self.pair_sem.at[0, 0],
                self.pair_sem.at[1, 0],
                here.plane(*PARTNER),
            )
        ]
        self.own = pltpu.make_async_copy(self.mine, place, self.local)
        self.own.start()

    def forward(self):
        here = self.here
        for index, step in enumerate((2, 1, 3)):
            self.sent[index].wait_recv()
            place = self.whole.at[here.c, block(here.behind(step), ROWS), :]
            self.shared.append(
                push(
                    place,
                    place,
                    self.pair_sem.at[0, step],
                    self.pair_sem.at[1, step],
                    here.plane(*PARTNER),
                )
            )

    def finish(self):
        for copy in self.sent:
            copy.wait_send()
        for copy in self.shared:
            copy.wait()
        self.own.wait()


def normed(values):
    center = values - jnp.mean(values, -1, keepdims=True)
    variance = jnp.mean(center * center, -1, keepdims=True)
    inv_std = lax.rsqrt(variance + NORM_EPS)
    return (center * inv_std, inv_std)


def norm_row(packs, row):
    return jnp.concatenate([packs[k, row : row + 1, :] for k in range(8)], 1)


def params(ident, limit=60):
    return pltpu.CompilerParams(
        collective_id=ident, has_side_effects=True, vmem_limit_bytes=limit << 20
    )


def cast_rows(raw, shard):
    count, rows, _ = raw.shape
    for j in range(count):

        def step(i, carry):
            at = pl.ds(pl.multiple_of(i * 32, 32), 32)
            shard[j, at, :] = raw[j, at, :].astype(BF16)
            return carry

        lax.fori_loop(0, rows // 32, step, 0)


def front_kernel(*refs):
    head_count, position, bucket, tok, cot, norm_master = refs[:6]
    masters = refs[6:10]
    n1, both_cot, tables, packs, n2, mid, q_out, k_out, v_out, a_out = refs[10:20]
    wholes = refs[20:24]
    raws, shards = refs[24:28], refs[28:32]
    raw_sem, n2_own, part, small, pair, local = refs[32:38]
    sums, tensor_sems, gather_refs = refs[38:43], refs[43:46], refs[46:58]
    here = Here()
    loads = []
    for i in range(4):
        loads.append(pltpu.make_async_copy(masters[i], raws[i], raw_sem.at[i]))
        loads[i].start()
    me = here.chunk(0, 0, 0)
    lane = lax.broadcasted_iota(jnp.int32, (1, CHUNK), 1)
    counts = jnp.zeros((1, CHUNK), F32)
    for c in range(4):
        count = jnp.sum((bucket[...] == c).astype(F32), 1, keepdims=True)
        counts = counts + jnp.where(lane == c, count, 0.0)
    packs[pl.ds(me, 1)] = jnp.concatenate(
        [norm_master[...].astype(BF16).astype(F32), counts, jnp.zeros((3, CHUNK), F32)], 0
    )[None]
    gathers = [
        Gather(here, i in (0, 2), shards[i], wholes[i], *gather_refs[i * 3 : i * 3 + 3])
        for i in range(4)
    ]
    loads[0].wait()
    cast_rows(raws[0], shards[0])
    greet(here, PLANE, (1, 2, 3))
    gathers[0].start()
    packed = []
    for index, peer in enumerate(PLANE):
        packed.append(
            push(
                packs.at[me], packs.at[me],
                small.at[0, index], small.at[1, index], here.plane(*peer),
            )
        )
    partner = here.plane(*PARTNER)
    table = tables.at[here.c]
    fill_table(table, position[...], bucket[...], head_count[0])
    shared = [
        push(table, table, pair.at[0, 0], pair.at[1, 0], partner),
        push(cot, both_cot.at[here.c], pair.at[0, 1], pair.at[1, 1], partner),
    ]
    keep = pltpu.make_async_copy(cot, both_cot.at[here.c], local)
    keep.start()
    for i in range(1, 4):
        loads[i].wait()
        cast_rows(raws[i], shards[i])
    for copy in packed:
        copy.wait()
    gain, shift = norm_row(packs, 0), norm_row(packs, 1)
    mine = n1.at[here.c]

    def rows_step(i, carry):
        rows = block(i, 32)
        hat, _ = normed(tok[rows, :].astype(F32))
        mine[rows, :] = (hat * gain + shift).astype(BF16)
        return carry

    lax.fori_loop(0, tok.shape[0] // 32, rows_step, 0)
    shared.append(push(mine, mine, pair.at[0, 2], pair.at[1, 2], partner))
    gathers[1].start()
    gathers[0].forward()
    gathers[1].forward()
    gathers[0].finish()
    gathers[2].start()
    gathers[3].start()
    shared[0].wait_recv()
    shared[2].wait_recv()
    head0 = here.z * 4 + here.c * 2
    attend_body(head0, n1, wholes[0], wholes[1], tables, q_out, k_out, v_out, a_out, part)
    gathers[1].finish()
    total = TensorSum(here, part, sums)
    attend_out(a_out, wholes[1], part, 1 - here.c)
    total.start()
    attend_out(a_out, wholes[1], part, here.c)
    total.spread()
    rows = block(here.z, ROWS)
    middle = tok[rows, :].astype(F32) + total.result()
    mid[...] = middle
    hat, _ = normed(middle)
    n2_own[...] = (hat * norm_row(packs, 2) + norm_row(packs, 3)).astype(BF16)
    gather = TensorGather(here, n2_own, n2, *tensor_sems)
    gather.start()
    gathers[2].forward()
    gathers[3].forward()
    gather.forward()
    total.finish()
    gather.finish()
    gathers[2].finish()
    gathers[3].finish()
    keep.wait()
    shared[0].wait_send()
    shared[1].wait()
    shared[2].wait_send()


def front_call(head_count, position, bucket, tok, cot, norm_master, masters):
    length, width = tok.shape
    both = jax.ShapeDtypeStruct((2, length, width), BF16)
    thin = jax.ShapeDtypeStruct((2 * length, CHUNK), BF16)
    wholes = [
        jax.ShapeDtypeStruct((3, width, CHUNK), BF16),
        jax.ShapeDtypeStruct((1, CHUNK, width), BF16),
        jax.ShapeDtypeStruct((4, width, CHUNK), BF16),
        jax.ShapeDtypeStruct((4, CHUNK, width), BF16),
    ]
    results = pl.pallas_call(
        front_kernel,
        out_shape=[
            both,
            both,
            jax.ShapeDtypeStruct((2, 5, length, HALF), F32),
            jax.ShapeDtypeStruct((8, 8, CHUNK), F32),
            both,
            jax.ShapeDtypeStruct((ROWS, width), F32),
            thin, thin, thin, thin,
        ]
        + wholes,
        in_specs=[SM, VM, VM, VM, VM, VM] + [ANY] * 4,
        out_specs=[VM, ANY, VM, VM, ANY, VM, VM, VM, VM, VM, VM, VM, ANY, ANY],
        scratch_shapes=[pltpu.VMEM(master.shape, F32) for master in masters]
        + [pltpu.VMEM(master.shape, BF16) for master in masters]
        + [
            pltpu.SemaphoreType.DMA((4,)),
            pltpu.VMEM((ROWS, width), BF16),
            pltpu.VMEM((2, length, width), BF16),
            pltpu.SemaphoreType.DMA((2, 7)),
            pltpu.SemaphoreType.DMA((2, 3)),
            pltpu.SemaphoreType.DMA,
        ]
        + sum_scratch(length, width)
        + tensor_gather_sems()
        + gather_sems() * 4,
        compiler_params=params(1),
        name="front",
    )(head_count, position, bucket, tok, cot, norm_master, *masters)
    return results[:10], results[10:]


def tensor_gather_sems():
    return [
        pltpu.SemaphoreType.DMA((2, 3)),
        pltpu.SemaphoreType.DMA((2, 4)),
        pltpu.SemaphoreType.DMA,
    ]


def norm_back(grad_out, hat, inv_std, gain):
    scaled = grad_out * gain
    inner = (
        scaled
        - jnp.mean(scaled, -1, keepdims=True)
        - hat * jnp.mean(scaled * hat, -1, keepdims=True)
    )
    return (
        inner * inv_std,
        jnp.sum(grad_out * hat, 0, keepdims=True),
        jnp.sum(grad_out, 0, keepdims=True),
    )


def ffn_hidden(r, n2, cot, bucket, wu, wd, squares, grad_hidden):
    width = n2.shape[2]
    hidden = dot(n2[...].reshape(-1, width), wu[r])
    live = bucket >= jnp.float32(r)
    rectified = jnp.maximum(jnp.where(live, hidden, 0.0), 0.0)
    squares[r] = (rectified * rectified).astype(BF16)
    grad_square = dot(cot[...].reshape(-1, width), wd[r], ((1,), (1,)))
    grad_hidden[r] = (grad_square * 2.0 * rectified).astype(BF16)


def ffn_rows(s, left, right, part, transposed):
    length, width = part.shape[1:]
    rows = pl.ds(pl.multiple_of(s * length, length), length)
    for n in range(width // (2 * CHUNK)):
        cols = slice(n * 2 * CHUNK, (n + 1) * 2 * CHUNK)
        total = None
        for r in range(4):
            if transposed:
                term = dot(left[r, rows, :], right[r, cols, :], ((1,), (1,)))
            else:
                term = dot(left[r, rows, :], right[r, :, cols])
            total = term if total is None else total + term
        part[s, :, cols] = total.astype(BF16)


def attend_back_body(head0, gm, qkva, wq, wo, tables, dp, part):
    length = tables.shape[2]
    width = gm.shape[2]
    q_rows, k_rows, v_rows = qkva.at[0], qkva.at[1], qkva.at[2]
    grad_att = dot(gm[...].reshape(2 * length, width), wo[...], ((1,), (1,))).astype(BF16)
    for s in range(2):
        rows = slice(s * length, (s + 1) * length)
        cosine, sine = tables[s, 0], tables[s, 1]
        lowest = tables[s, 2, :, 0:1]
        for h in range(2):
            cols = slice(h * HEAD_DIM, (h + 1) * HEAD_DIM)
            active = tables[s, 4] > (head0 + h).astype(F32)
            grad_heads = jnp.where(active, grad_att[rows, cols].astype(F32), 0.0).astype(BF16)
            queries, key_rows, value_rows = q_rows[rows, cols], k_rows[rows, cols], v_rows[rows, cols]
            weights = attention_weights(queries, key_rows, lowest)
            grad_weights = dot(grad_heads, value_rows, ((1,), (1,)))
            inner = jnp.sum(weights * grad_weights, -1, keepdims=True)
            grad_scores = (weights * (grad_weights - inner)).astype(BF16)
            grad_query = dot(grad_scores, key_rows) * HEAD_DIM ** (-0.5)
            grad_keys = dot(grad_scores, queries, ((0,), (0,)))
            grad_values = dot(weights.astype(BF16), grad_heads, ((0,), (0,)))
            dp[0, rows, cols] = turn(grad_query, cosine, -sine).astype(BF16)
            dp[1, rows, cols] = turn(grad_keys, cosine, -sine).astype(BF16)
            dp[2, rows, cols] = grad_values.astype(BF16)


def attend_back_rows(s, dp, wq, part):
    length = part.shape[1]
    rows = pl.ds(pl.multiple_of(s * length, length), length)
    total = dot(dp[0, rows, :], wq[0], ((1,), (1,)))
    total = total + dot(dp[1, rows, :], wq[1], ((1,), (1,)))
    total = total + dot(dp[2, rows, :], wq[2], ((1,), (1,)))
    part[s] = total.astype(BF16)


def norm_share(here, values, bufs):
    slices, heard, plane_sum, heard_z, ns, nz = bufs
    for k in range(8):
        slices[k, 0:4, :] = values[:, k * CHUNK : (k + 1) * CHUNK]
        slices[k, 4:8, :] = jnp.zeros((4, CHUNK), F32)
    copies = []
    for index, peer in enumerate(PLANE):
        copies.append(
            push(
                slices.at[here.chunk(*peer)],
                heard.at[index],
                ns.at[0, index],
                ns.at[1, index],
                here.plane(*peer),
            )
        )
    return copies


def norm_share_along(here, copies, bufs):
    slices, heard, plane_sum, heard_z, ns, nz = bufs
    mine = slices[here.chunk(0, 0, 0)]
    for index in range(7):
        copies[index].wait()
        mine = mine + heard[index]
    plane_sum[...] = mine
    onward = []
    for step in (1, 2, 3):
        onward.append(
            push(
                plane_sum,
                heard_z.at[here.z],
                nz.at[0, step - 1],
                nz.at[1, step - 1],
                here.along(step),
            )
        )
    heard_z[pl.ds(here.z, 1)] = mine[None]
    return onward


def back_kernel(*refs):
    n2, cot, tables, packs, mid = refs[0:5]
    tok, wq, wo, wu, wd, n1, q_rows, k_rows, v_rows, a_rows = refs[5:15]
    out_all, ig_own, norm_total, q_sum, o_sum, u_sum, d_sum = refs[15:22]
    wu_v, wd_v, qkva, tok_own, load_sem, squares, grad_hidden, part, part_f, dp = refs[22:32]
    gu, gd, gq, go, gm, gm_own, dmid, sums, out_own = refs[32:41]
    back_bufs, branch_bufs, final_one, final_two = refs[41:46], refs[46:51], refs[51], refs[52]
    gm_sems, out_sems, norm_bufs = refs[53:56], refs[56:58], refs[58:64]
    rest = refs[64:]
    here = Here()
    loads = []

    def load(src, dst):
        copy = pltpu.make_async_copy(src, dst, load_sem.at[len(loads)])
        copy.start()
        loads.append(copy)
        return copy

    first = [(load(wu.at[r], wu_v.at[r]), load(wd.at[r], wd_v.at[r])) for r in range(4)]
    small = [load(src, qkva.at[i]) for i, src in enumerate((q_rows, k_rows, v_rows, a_rows))]
    place = block(here.z, ROWS)
    small.append(load(tok.at[place, :], tok_own))
    scatters = [
        Scatter(here, by_rows, grad, total, rest[i * SCATTER : (i + 1) * SCATTER] + (final,))
        for i, (by_rows, grad, total, final) in enumerate(
            (
                (True, gu, u_sum, final_one),
                (False, gd, d_sum, final_two),
                (True, gq, q_sum, final_one.at[:, 0:3]),
                (False, go, o_sum, final_one.at[:, 3:4]),
            )
        )
    ]
    scatter_u, scatter_d, scatter_q, scatter_o = scatters
    bucket = jnp.concatenate([tables[0, 3, :, 0:1], tables[1, 3, :, 0:1]], 0)
    for r in range(4):
        first[r][0].wait()
        first[r][1].wait()
        ffn_hidden(r, n2, cot, bucket, wu_v, wd_v, squares, grad_hidden)
    other = 1 - here.c
    back = TensorSum(here, part, back_bufs)
    ffn_rows(other, grad_hidden, wu_v, part, True)
    greet(here, PLANE, (1, 2, 3))
    back.start()
    ffn_rows(here.c, grad_hidden, wu_v, part, True)
    back.spread()
    load_q = load(wq, wu_v.at[0:3])
    length, width = n2.shape[1:]
    rows_in = n2[...].reshape(2 * length, width)
    for r in range(4):
        gu[r] = dot(rows_in, grad_hidden[r], ((0,), (0,))).astype(BF16)
    scatter_u.start()
    grads_in = cot[...].reshape(2 * length, width)
    for r in range(4):
        gd[r] = dot(squares[r], grads_in, ((0,), (0,))).astype(BF16)
    scatter_d.start()
    branch = TensorSum(here, part_f, branch_bufs)
    ffn_rows(other, squares, wd_v, part_f, False)
    branch.start()
    ffn_rows(here.c, squares, wd_v, part_f, False)
    load_n1 = load(n1, wd_v.at[0:2])
    load_o = load(wo, wd_v.at[2:3])
    grad_n2 = back.result().astype(BF16).astype(F32)
    hat, inv_std = normed(mid[...])
    grad_mid, gain_sum, shift_sum = norm_back(grad_n2, hat, inv_std, norm_row(packs, 2))
    grad_mid = cot[here.c, place, :].astype(F32) + grad_mid
    dmid[...] = grad_mid
    gm_own[...] = grad_mid.astype(BF16)
    gather = TensorGather(here, gm_own, gm, *gm_sems)
    gather.start()
    sums[0:1, :] = gain_sum
    sums[1:2, :] = shift_sum
    scatter_u.middle()
    gather.forward()
    branch.spread()
    for copy in small:
        copy.wait()
    load_o.wait()
    load_q.wait()
    load_n1.wait()
    gather.finish()
    back.finish()
    head0 = here.z * 4 + here.c * 2
    attend_back_body(head0, gm, qkva, wu_v, wd_v.at[2], tables, dp, part)
    last = TensorSum(here, part, back_bufs)
    attend_back_rows(other, dp, wu_v, part)
    last.start()
    attend_back_rows(here.c, dp, wu_v, part)
    last.spread()
    rows_in = wd_v[0:2].reshape(2 * length, width)
    for j in range(3):
        gq[j] = dot(rows_in, dp[j], ((0,), (0,))).astype(BF16)
    scatter_q.start()
    go[0] = dot(qkva[3], gm[...].reshape(2 * length, width), ((0,), (0,))).astype(BF16)
    scatter_o.start()
    scatter_d.middle()
    out_own[...] = (mid[...] + branch.result().astype(BF16).astype(F32)).astype(BF16)
    out_place = out_all.at[place, :]
    out_copies = [
        push(
            out_own, out_place, out_sems[0].at[0, step - 1], out_sems[0].at[1, step - 1],
            here.along(step),
        )
        for step in (2, 1, 3)
    ]
    keep = pltpu.make_async_copy(out_own, out_place, out_sems[1])
    keep.start()
    grad_n1 = last.result()
    hat, inv_std = normed(tok_own[...].astype(F32))
    grad_in, gain_sum, shift_sum = norm_back(grad_n1, hat, inv_std, norm_row(packs, 0))
    ig_own[...] = (dmid[...] + grad_in).astype(BF16)
    norm_copies = norm_share(
        here, jnp.concatenate([gain_sum, shift_sum, sums[...]], 0), norm_bufs
    )
    scatter_u.last()
    scatter_q.middle()
    scatter_o.middle()
    onward = norm_share_along(here, norm_copies, norm_bufs)
    scatter_d.last()
    for copy in onward:
        copy.wait()
    heard_z = norm_bufs[3]
    norm_total[...] = ((heard_z[0] + heard_z[1]) + heard_z[2]) + heard_z[3]
    scatter_u.sent()
    scatter_q.last()
    scatter_o.last()
    branch.finish()
    last.finish()
    keep.wait()
    for copy in out_copies:
        copy.wait()
    for scatter in scatters[1:]:
        scatter.sent()
    for scatter in scatters:
        scatter.finish()


def back_call(n2, cot, tables, packs, mid, tok, wq, wo, wu, wd, n1, rows):
    _, length, width = n2.shape
    both = pltpu.VMEM((2, length, width), BF16)
    results = pl.pallas_call(
        back_kernel,
        out_shape=[
            jax.ShapeDtypeStruct((length, width), BF16),
            jax.ShapeDtypeStruct((ROWS, width), BF16),
            jax.ShapeDtypeStruct((8, CHUNK), F32),
            jax.ShapeDtypeStruct((3, CHUNK, 2 * CHUNK), F32),
            jax.ShapeDtypeStruct((1, 2 * CHUNK, CHUNK), F32),
            jax.ShapeDtypeStruct((4, CHUNK, 2 * CHUNK), F32),
            jax.ShapeDtypeStruct((4, 2 * CHUNK, CHUNK), F32),
        ],
        in_specs=[VM] * 5 + [ANY] * 10,
        out_specs=[ANY, VM, VM, ANY, ANY, ANY, ANY],
        scratch_shapes=[
            pltpu.VMEM(wu.shape, BF16),
            pltpu.VMEM(wd.shape, BF16),
            pltpu.VMEM((4, 2 * length, CHUNK), BF16),
            pltpu.VMEM((ROWS, width), BF16),
            pltpu.SemaphoreType.DMA((16,)),
            pltpu.VMEM((4, 2 * length, CHUNK), BF16),
            pltpu.VMEM((4, 2 * length, CHUNK), BF16),
            both,
            both,
            pltpu.VMEM((3, 2 * length, CHUNK), BF16),
            pltpu.VMEM(wu.shape, BF16),
            pltpu.VMEM(wd.shape, BF16),
            pltpu.VMEM(wq.shape, BF16),
            pltpu.VMEM(wo.shape, BF16),
            both,
            pltpu.VMEM((ROWS, width), BF16),
            pltpu.VMEM((ROWS, width), F32),
            pltpu.VMEM((2, width), F32),
            pltpu.VMEM((ROWS, width), BF16),
        ]
        + sum_scratch(length, width) * 2
        + [pltpu.VMEM((2, 4, CHUNK, CHUNK), F32)] * 2
        + tensor_gather_sems()
        + [pltpu.SemaphoreType.DMA((2, 3)), pltpu.SemaphoreType.DMA]
        + [
            pltpu.VMEM((8, 8, CHUNK), F32),
            pltpu.VMEM((7, 8, CHUNK), F32),
            pltpu.VMEM((8, CHUNK), F32),
            pltpu.VMEM((4, 8, CHUNK), F32),
            pltpu.SemaphoreType.DMA((2, 7)),
            pltpu.SemaphoreType.DMA((2, 3)),
        ]
        + scatter_scratch(4)
        + scatter_scratch(4)
        + scatter_scratch(3)
        + scatter_scratch(1),
        compiler_params=params(3),
        name="back",
    )(n2, cot, tables, packs, mid, tok, wq, wo, wu, wd, n1, *rows)
    return results


FIRST_SCALE = 1.0 / (1.0 - BETA_FIRST**STEP)
SECOND_SCALE = 1.0 / (1.0 - BETA_SECOND**STEP)


def folded(values):
    rows, cols = values.shape
    total = None
    for i in range(rows // 8):
        for j in range(cols // 128):
            tile = values[i * 8 : i * 8 + 8, j * 128 : j * 128 + 128]
            total = tile if total is None else total + tile
    return total


def updated(weight, gradient, first_old, second_old):
    first_new = BETA_FIRST * first_old + (1.0 - BETA_FIRST) * gradient
    second_new = BETA_SECOND * second_old + (1.0 - BETA_SECOND) * gradient * gradient
    update = first_new * FIRST_SCALE / (
        jnp.sqrt(second_new * SECOND_SCALE) + ADAM_EPS
    ) + WEIGHT_DECAY * weight
    return (update, first_new, second_new)


AHEAD = 4


def adam_kernel(*refs):
    sources = [refs[kind * 5 : kind * 5 + 4] for kind in range(4)]
    norm_grad, norm_master, norm_first, norm_second = [refs[kind * 5 + 4] for kind in range(4)]
    out_all = refs[20]
    outs = [refs[21 + kind * 5 : 25 + kind * 5] for kind in range(3)]
    norm_outs = [refs[25 + kind * 5] for kind in range(3)]
    tile, output = refs[36:38]
    held = [refs[38 + kind * 4 : 42 + kind * 4] for kind in range(4)]
    load_sem, store_sem = refs[54:56]
    blocks = [(i, j) for i in range(4) for j in range(sources[0][i].shape[0])]
    loads = []

    def load():
        index = len(loads)
        if index == len(blocks):
            return
        i, j = blocks[index]
        loads.append([])
        for kind in range(4):
            copy = pltpu.make_async_copy(
                sources[kind][i].at[j], held[kind][i].at[j], load_sem.at[kind, index]
            )
            copy.start()
            loads[index].append(copy)

    for _ in range(AHEAD):
        load()
    output[...] = out_all[...].astype(F32)
    weight = norm_master[...]
    update, first_new, second_new = updated(
        weight, norm_grad[0:4, :], norm_first[...], norm_second[...]
    )
    for out, value in zip(norm_outs, (update, first_new, second_new)):
        out[...] = value
    for row, value in ((4, weight), (12, update)):
        square = value * value * 0.25
        tile[row : row + 4, :] = square[:, :128] + square[:, 128:]
    stores = []
    sums = None
    for index, (i, j) in enumerate(blocks):
        if j == 0:
            sums = (jnp.zeros((8, 128), F32), jnp.zeros((8, 128), F32))
        for copy in loads[index]:
            copy.wait()
        load()
        grads, masters, firsts, seconds = [held[kind][i] for kind in range(4)]

        def step(k, carry):
            at = pl.ds(pl.multiple_of(k * 16, 16), 16)
            weight = masters[j, at, :]
            update, first_new, second_new = updated(
                weight, grads[j, at, :], firsts[j, at, :], seconds[j, at, :]
            )
            grads[j, at, :] = update
            firsts[j, at, :] = first_new
            seconds[j, at, :] = second_new
            return (carry[0] + folded(weight * weight), carry[1] + folded(update * update))

        sums = lax.fori_loop(0, grads.shape[1] // 16, step, sums)
        for kind, source in enumerate((grads, firsts, seconds)):
            copy = pltpu.make_async_copy(
                source.at[j], outs[kind][i].at[j], store_sem.at[kind, index]
            )
            copy.start()
            stores.append(copy)
        if j == grads.shape[0] - 1:
            tile[i : i + 1, :] = jnp.sum(sums[0], 0, keepdims=True)
            tile[8 + i : 9 + i, :] = jnp.sum(sums[1], 0, keepdims=True)
    for copy in stores:
        copy.wait()


def adam_call(grads, masters, firsts, seconds, out_all):
    shapes = [master.shape for master in masters]
    like = [jax.ShapeDtypeStruct(shape, F32) for shape in shapes]
    specs = [ANY] * 4 + [VM]
    count = sum(shape[0] for shape in shapes[:4])
    results = pl.pallas_call(
        adam_kernel,
        out_shape=like * 3
        + [jax.ShapeDtypeStruct((16, 128), F32), jax.ShapeDtypeStruct(out_all.shape, F32)],
        in_specs=specs * 4 + [VM],
        out_specs=specs * 3 + [VM, VM],
        scratch_shapes=[pltpu.VMEM(shape, F32) for shape in shapes[:4]] * 4
        + [pltpu.SemaphoreType.DMA((4, count)), pltpu.SemaphoreType.DMA((3, count))],
        compiler_params=local_params(60),
        name="adam",
    )(*grads, *masters, *firsts, *seconds, out_all)
    return results[0:5], results[5:10], results[10:15], results[15], results[16]


def total_kernel(tile, norms, tiles_z, plane_tile, tiles, zs, ps):
    here = Here()
    greet(here, PLANE, (1, 2, 3))
    sent = []
    for step in (2, 1, 3):
        sent.append(
            push(tile, tiles_z.at[here.z], zs.at[0, step - 1], zs.at[1, step - 1], here.along(step))
        )
    tiles_z[pl.ds(here.z, 1)] = tile[...][None]
    for copy in sent:
        copy.wait()
    plane_tile[...] = ((tiles_z[0] + tiles_z[1]) + tiles_z[2]) + tiles_z[3]
    me = here.chunk(0, 0, 0)
    sent = []
    for index, peer in enumerate(PLANE):
        sent.append(
            push(plane_tile, tiles.at[me], ps.at[0, index], ps.at[1, index], here.plane(*peer))
        )
    tiles[pl.ds(me, 1)] = plane_tile[...][None]
    for copy in sent:
        copy.wait()
    total = tiles[0]
    for k in range(1, 8):
        total = total + tiles[k]
    roots = jnp.sqrt(jnp.sum(total, 1, keepdims=True))
    norms[...] = jnp.broadcast_to(roots, norms.shape)


def total_call(tile):
    return pl.pallas_call(
        total_kernel,
        out_shape=jax.ShapeDtypeStruct((16, 128), F32),
        in_specs=[VM],
        out_specs=VM,
        scratch_shapes=[
            pltpu.VMEM((4, 16, 128), F32),
            pltpu.VMEM((16, 128), F32),
            pltpu.VMEM((8, 16, 128), F32),
            pltpu.SemaphoreType.DMA((2, 3)),
            pltpu.SemaphoreType.DMA((2, 7)),
        ],
        compiler_params=params(5),
        name="norm_totals",
    )(tile)


def weight_kernel(*refs):
    norms, updates, masters, packs = refs[0], refs[1:6], refs[6:11], refs[11]
    ig_rows = refs[12:16]
    outs = refs[16:21]
    igrad, lamb_norms, share = refs[21:24]
    held = (refs[24:28], refs[28:32])
    load_sem, store_sem = refs[32:34]
    blocks = [(i, j) for i in range(4) for j in range(updates[i].shape[0])]
    loads = []

    def load():
        index = len(loads)
        if index == len(blocks):
            return
        i, j = blocks[index]
        loads.append([])
        for kind, source in enumerate((updates, masters)):
            copy = pltpu.make_async_copy(
                source[i].at[j], held[kind][i].at[j], load_sem.at[kind, index]
            )
            copy.start()
            loads[index].append(copy)

    for _ in range(AHEAD):
        load()
    scales = LEARN_RATE * (norms[0:8, 0:1] / norms[8:16, 0:1])
    outs[4][...] = masters[4][...] - scales[4:8, :] * updates[4][...]
    row = lax.broadcasted_iota(jnp.int32, norms.shape, 0)
    lane = lax.broadcasted_iota(jnp.int32, norms.shape, 1)
    flat = jnp.sum(jnp.where(row == lane, norms[...], 0.0), 0, keepdims=True)
    lamb_norms[0:1, :] = flat[:, 0:8]
    lamb_norms[1:2, :] = flat[:, 8:16]
    counts = packs[0, 4:5, :]
    for k in range(1, 8):
        counts = counts + packs[k, 4:5, :]
    share[...] = counts[:, 0:4] / (igrad.shape[0] * 8)
    here = Here()
    for step in range(4):
        igrad[block(here.behind(step), ROWS), :] = ig_rows[step][...].astype(F32)
    stores = []
    for index, (i, j) in enumerate(blocks):
        for copy in loads[index]:
            copy.wait()
        load()
        held[1][i][j] = held[1][i][j] - scales[i : i + 1, :] * held[0][i][j]
        copy = pltpu.make_async_copy(held[1][i].at[j], outs[i].at[j], store_sem.at[index])
        copy.start()
        stores.append(copy)
    for copy in stores:
        copy.wait()


def weight_call(norms, updates, masters, packs, ig_rows):
    shapes = [master.shape for master in masters]
    specs = [ANY] * 4 + [VM]
    count = sum(shape[0] for shape in shapes[:4])
    rows, width = ig_rows[0].shape
    return pl.pallas_call(
        weight_kernel,
        out_shape=[jax.ShapeDtypeStruct(shape, F32) for shape in shapes]
        + [
            jax.ShapeDtypeStruct((4 * rows, width), F32),
            jax.ShapeDtypeStruct((2, 8), F32),
            jax.ShapeDtypeStruct((1, 4), F32),
        ],
        in_specs=[VM] + specs * 2 + [VM] * 5,
        out_specs=specs + [VM, VM, VM],
        scratch_shapes=[pltpu.VMEM(shape, F32) for shape in shapes[:4]] * 2
        + [pltpu.SemaphoreType.DMA((2, count)), pltpu.SemaphoreType.DMA((count,))],
        compiler_params=local_params(60),
        name="new_weights",
    )(norms, *updates, *masters, packs, *ig_rows)


def turn(values, cosine, sine):
    return values * cosine + pltpu.roll(values, HEAD_DIM // 2, 1) * sine


def dot(left, right, dims=((1,), (0,))):
    return lax.dot_general(left, right, (dims, ((), ())), preferred_element_type=F32)


def attention_weights(queries, key_rows, lowest):
    scores = dot(queries, key_rows, ((1,), (1,)))
    row = lax.broadcasted_iota(jnp.int32, scores.shape, 0)
    col = lax.broadcasted_iota(jnp.int32, scores.shape, 1)
    allowed = (col <= row) & (col.astype(F32) >= lowest)
    scores = jnp.where(allowed, scores, MASKED)
    exp_scores = jnp.exp(scores - jnp.max(scores, -1, keepdims=True))
    return exp_scores / jnp.sum(exp_scores, -1, keepdims=True)


def attend_body(head0, n1, wq, wo, tables, q_out, k_out, v_out, a_out, part):
    length = tables.shape[2]
    rows_in = n1[...].reshape(2 * length, n1.shape[2])
    projected = [dot(rows_in, wq[j]) for j in range(3)]
    for s in range(2):
        rows = slice(s * length, (s + 1) * length)
        cosine, sine = tables[s, 0], tables[s, 1]
        lowest = tables[s, 2, :, 0:1]
        for h in range(2):
            cols = slice(h * HEAD_DIM, (h + 1) * HEAD_DIM)
            queries = (turn(projected[0][rows, cols], cosine, sine) * HEAD_DIM ** (-0.5)).astype(BF16)
            key_rows = turn(projected[1][rows, cols], cosine, sine).astype(BF16)
            value_rows = projected[2][rows, cols].astype(BF16)
            weights = attention_weights(queries, key_rows, lowest).astype(BF16)
            heads = dot(weights, value_rows)
            active = tables[s, 4] > (head0 + h).astype(F32)
            q_out[rows, cols] = queries
            k_out[rows, cols] = key_rows
            v_out[rows, cols] = value_rows
            a_out[rows, cols] = jnp.where(active, heads, 0.0).astype(BF16)


def attend_out(a_out, wo, part, s):
    length = part.shape[1]
    part[s] = dot(a_out[pl.ds(pl.multiple_of(s * length, length), length), :], wo[0]).astype(BF16)


def fill_table(table, position, bucket, head_count):
    length = table.shape[1]
    row = lax.broadcasted_iota(jnp.int32, (length, length), 0)
    col = lax.broadcasted_iota(jnp.int32, (length, length), 1)

    def column(values):
        return jnp.sum(jnp.where(row == col, values.astype(F32), 0.0), 1, keepdims=True)

    place = column(position)
    lane = lax.broadcasted_iota(jnp.int32, (length, HALF), 1)
    half = HEAD_DIM // 2
    second = lane >= half
    freq_index = jnp.where(second, lane - half, lane).astype(F32)
    angles = place * jnp.exp(freq_index * (-2.0 * math.log(ROPE_BASE) / HEAD_DIM))
    table[0] = jnp.cos(angles)
    sine = jnp.sin(angles)
    table[1] = jnp.where(second, sine, -sine)
    index = lax.broadcasted_iota(jnp.int32, (length, HALF), 0).astype(F32)
    table[2] = index - place
    table[3] = jnp.broadcast_to(column(bucket), (length, HALF))
    table[4] = jnp.broadcast_to(head_count.astype(F32), (length, HALF))


def local_params(limit):
    return pltpu.CompilerParams(vmem_limit_bytes=limit << 20)


def fast_body(
    tokens, cotangent, head_counts, positions, buckets,
    in_master, out_master, up_master, down_master, norm_master,
    in_first, out_first, up_first, down_first, norm_first,
    in_second, out_second, up_second, down_second, norm_second,
):
    tok, cot = tokens[0], cotangent[0]
    (n1, both_cot, tables, packs, n2, mid, q_rows, k_rows, v_rows, a_rows), (wq, wo, wu, wd) = front_call(
        head_counts, positions, buckets, tok, cot, norm_master,
        (in_master, out_master[None], up_master, down_master),
    )
    out_all, ig_own, norm_sum, in_sum, out_sum, up_sum, down_sum = back_call(
        n2, both_cot, tables, packs, mid, tok, wq, wo, wu, wd, n1,
        (q_rows, k_rows, v_rows, a_rows),
    )
    ig_rows = [ig_own] + [
        lax.ppermute(ig_own, "tensor", [(i, (i + step) % 4) for i in range(4)])
        for step in (1, 2, 3)
    ]
    masters = (in_master, out_master[None], up_master, down_master, norm_master)
    firsts = (in_first, out_first[None], up_first, down_first, norm_first)
    seconds = (in_second, out_second[None], up_second, down_second, norm_second)
    updates, moments, squares, tile, output = adam_call(
        (in_sum, out_sum, up_sum, down_sum, norm_sum), masters, firsts, seconds, out_all
    )
    norms = total_call(tile)
    *weights, input_grad, lamb_norms, share = weight_call(
        norms, updates, masters, packs, ig_rows
    )
    flat = lambda group: (group[0], group[1][0], group[2], group[3], group[4])
    return (
        output[None],
        input_grad[None],
        share[0],
        lamb_norms,
        *flat(weights),
        *flat(moments),
        *flat(squares),
    )


def solution(mesh):
    placed = (
        P(("dp", "expert"), None, None),
        P(("dp", "expert"), None, None),
        P(("dp", "expert")),
        P(("dp", "expert"), None),
        P(("dp", "expert"), None),
        P(None, ("dp", "expert"), "tensor"),
        P("tensor", ("dp", "expert")),
        P(None, ("dp", "expert"), "tensor"),
        P(None, "tensor", ("dp", "expert")),
        P(None, ("dp", "expert")),
        P(None, ("dp", "expert"), "tensor"),
        P("tensor", ("dp", "expert")),
        P(None, ("dp", "expert"), "tensor"),
        P(None, "tensor", ("dp", "expert")),
        P(None, ("dp", "expert")),
        P(None, ("dp", "expert"), "tensor"),
        P("tensor", ("dp", "expert")),
        P(None, ("dp", "expert"), "tensor"),
        P(None, "tensor", ("dp", "expert")),
        P(None, ("dp", "expert")),
    )
    shape = dict(mesh.shape)
    fits = shape == {"dp": 4, "expert": 2, "tensor": 4}
    return jax.shard_map(
        fast_body if fits else body,
        mesh=mesh,
        in_specs=placed,
        out_specs=(
            P(("dp", "expert"), None, None),
            P(("dp", "expert"), None, None),
            P(),
            P(),
            P(None, ("dp", "expert"), "tensor"),
            P("tensor", ("dp", "expert")),
            P(None, ("dp", "expert"), "tensor"),
            P(None, "tensor", ("dp", "expert")),
            P(None, ("dp", "expert")),
            P(None, ("dp", "expert"), "tensor"),
            P("tensor", ("dp", "expert")),
            P(None, ("dp", "expert"), "tensor"),
            P(None, "tensor", ("dp", "expert")),
            P(None, ("dp", "expert")),
            P(None, ("dp", "expert"), "tensor"),
            P("tensor", ("dp", "expert")),
            P(None, ("dp", "expert"), "tensor"),
            P(None, "tensor", ("dp", "expert")),
            P(None, ("dp", "expert")),
        ),
        check_vma=False,
    )
```

```python
import math

import jax
import jax.numpy as jnp
from jax import lax
from jax.experimental import pallas as pl
from jax.experimental.pallas import tpu as pltpu
from jax.sharding import PartitionSpec as P

HEAD_DIM = 128
STEP = 10


NORM_EPS = 1e-05
BETA_FIRST = 0.9
BETA_SECOND = 0.999
ADAM_EPS = 1e-06
WEIGHT_DECAY = 0.01
LEARN_RATE = 0.25
MASKED = -1e30
ROPE_BASE = 10000.0


def layer_norm(values, gain_row, shift_row):
    center = values - jnp.mean(values, -1, keepdims=True)
    variance = jnp.mean(center * center, -1, keepdims=True)
    inv_std = lax.rsqrt(variance + NORM_EPS)
    normed = center * inv_std
    return (normed * gain_row + shift_row, normed, inv_std)


def norm_back_rows(grad_out, normed, inv_std, gain_row):
    scaled = grad_out * gain_row
    inner_part = (
        scaled
        - jnp.mean(scaled, -1, keepdims=True)
        - normed * jnp.mean(scaled * normed, -1, keepdims=True)
    )
    return (inner_part * inv_std, jnp.sum(grad_out * normed, 0), jnp.sum(grad_out, 0))


def rope_angles(position_row):
    freq_index = jnp.arange(HEAD_DIM // 2, dtype=jnp.float32)
    inverse = jnp.exp(freq_index * (-2.0 * jnp.log(ROPE_BASE) / HEAD_DIM))
    return position_row.astype(jnp.float32)[:, None] * inverse[None, :]


def rotary(values, angles, sign_value):
    half_dim = values.shape[-1] // 2
    cosine = jnp.cos(angles)[:, None, :]
    sine_part = sign_value * jnp.sin(angles)[:, None, :]
    first_half = values[..., :half_dim]
    second_half = values[..., half_dim:]
    return jnp.concatenate(
        [
            first_half * cosine - second_half * sine_part,
            second_half * cosine + first_half * sine_part,
        ],
        -1,
    )


def block_mask(key_index, position_row, block_start, block_rows):
    query_index = block_start + jnp.arange(block_rows, dtype=jnp.int32)
    return (key_index[None, :] <= query_index[:, None]) & (
        key_index[None, :] >= (query_index - position_row)[:, None]
    )


def attend_forward(queries, key_rows, value_rows, position_row, block_rows):
    length = queries.shape[0]
    key_index = jnp.arange(length, dtype=jnp.int32)

    def one_block(block_start):
        allowed = block_mask(key_index, position_row, block_start, block_rows)
        scores = jnp.einsum("qhd,khd->hqk", queries, key_rows, preferred_element_type=jnp.float32)
        scores = jnp.where(allowed[None], scores, MASKED)
        row_peak = jnp.max(scores, -1, keepdims=True)
        exp_scores = jnp.exp(scores - row_peak)
        row_total = jnp.sum(exp_scores, -1, keepdims=True)
        attn_weights = (exp_scores / row_total).astype(jnp.bfloat16)
        block_out = jnp.einsum(
            "hqk,khd->qhd", attn_weights, value_rows, preferred_element_type=jnp.float32
        )
        return (block_out, row_peak[..., 0] + jnp.log(row_total[..., 0]))

    starts = jnp.arange(length // block_rows, dtype=jnp.int32) * block_rows
    block_outs, log_totals = lax.map(one_block, starts)
    return (block_outs.reshape(queries.shape), log_totals, starts)


def attend_backward(
    queries, key_rows, value_rows, position_row, grad_heads, log_totals, starts, block_rows
):
    length = queries.shape[0]
    key_index = jnp.arange(length, dtype=jnp.int32)

    def one_block(carried, inputs):
        block_start, block_log = inputs
        allowed = block_mask(key_index, position_row, block_start, block_rows)
        scores = jnp.einsum("qhd,khd->hqk", queries, key_rows, preferred_element_type=jnp.float32)
        scores = jnp.where(allowed[None], scores, MASKED)
        attn_probs = jnp.exp(scores - block_log[..., None])
        grad_probs = jnp.einsum(
            "qhd,khd->hqk", grad_heads, value_rows, preferred_element_type=jnp.float32
        )
        row_inner = jnp.sum(attn_probs * grad_probs, -1, keepdims=True)
        grad_scores = (attn_probs * (grad_probs - row_inner)).astype(jnp.bfloat16)
        grad_query = jnp.einsum(
            "hqk,khd->qhd", grad_scores, key_rows, preferred_element_type=jnp.float32
        )
        grad_keys = carried[0] + jnp.einsum(
            "hqk,qhd->khd", grad_scores, queries, preferred_element_type=jnp.float32
        )
        grad_values = carried[1] + jnp.einsum(
            "hqk,qhd->khd",
            attn_probs.astype(jnp.bfloat16),
            grad_heads,
            preferred_element_type=jnp.float32,
        )
        return ((grad_keys, grad_values), grad_query)

    start_state = (jnp.zeros(key_rows.shape, jnp.float32), jnp.zeros(value_rows.shape, jnp.float32))
    (grad_keys, grad_values), grad_query = lax.scan(one_block, start_state, (starts, log_totals))
    return (grad_query.reshape(queries.shape), grad_keys, grad_values)


def gather_rows(values, source_rows):
    padded = jnp.concatenate([values, jnp.zeros((1, values.shape[1]), values.dtype)], 0)
    return padded[source_rows]


def ffn_forward(rows_in, bucket, up_work, down_work):
    row_count = rows_in.shape[0]
    mixed_sum = jnp.zeros((row_count, down_work.shape[2]), jnp.float32)
    hiddens = []
    for quarter in range(4):

        def live_part():
            hidden = jnp.dot(rows_in, up_work[quarter], preferred_element_type=jnp.float32)
            squared = jnp.square(jnp.maximum(hidden, 0.0)).astype(jnp.bfloat16)
            return (
                hidden,
                jnp.dot(squared, down_work[quarter], preferred_element_type=jnp.float32),
            )

        def dead_part():
            return (
                jnp.zeros((row_count, up_work.shape[2]), jnp.float32),
                jnp.zeros_like(mixed_sum),
            )

        hidden, contribution = lax.cond(bucket >= quarter, live_part, dead_part)
        hiddens.append(hidden)
        mixed_sum = mixed_sum + contribution
    return (mixed_sum, hiddens)


def ffn_backward(rows_in, grads_in, bucket, hiddens, up_work, down_work):
    grad_rows = jnp.zeros((rows_in.shape[0], up_work.shape[1]), jnp.float32)
    grad_up = []
    grad_down = []
    for quarter in range(4):
        hidden = hiddens[quarter]

        def live_part():
            rectified = jnp.maximum(hidden, 0.0)
            squared = jnp.square(rectified).astype(jnp.bfloat16)
            grad_square = jnp.einsum(
                "rd,ud->ru", grads_in, down_work[quarter], preferred_element_type=jnp.float32
            )
            grad_hidden = (grad_square * 2.0 * rectified).astype(jnp.bfloat16)
            return (
                jnp.einsum("rd,ru->du", rows_in, grad_hidden, preferred_element_type=jnp.float32),
                jnp.einsum("ru,rd->ud", squared, grads_in, preferred_element_type=jnp.float32),
                jnp.einsum(
                    "ru,du->rd", grad_hidden, up_work[quarter], preferred_element_type=jnp.float32
                ),
            )

        def dead_part():
            return (
                jnp.zeros(up_work.shape[1:], jnp.float32),
                jnp.zeros(down_work.shape[1:], jnp.float32),
                jnp.zeros_like(grad_rows),
            )

        part_up, part_down, part_rows = lax.cond(bucket >= quarter, live_part, dead_part)
        grad_up.append(part_up)
        grad_down.append(part_down)
        grad_rows = grad_rows + part_rows
    return (grad_rows, jnp.stack(grad_up), jnp.stack(grad_down))


def ffn_total(partial_value):
    return lax.psum(partial_value, "tensor")


def ffn_grad_total(partial_value):
    return lax.psum(partial_value, "tensor")


def adam_terms(weight, gradient, first_old, second_old):
    first_new = BETA_FIRST * first_old + (1.0 - BETA_FIRST) * gradient
    second_new = BETA_SECOND * second_old + (1.0 - BETA_SECOND) * gradient * gradient
    update = (
        first_new
        / (1.0 - BETA_FIRST**STEP)
        / (jnp.sqrt(second_new / (1.0 - BETA_SECOND**STEP)) + ADAM_EPS)
        + WEIGHT_DECAY * weight
    )
    return (update, first_new, second_new)


def finish(output, input_grad, bucket_share, masters, firsts, seconds, grad_shards, tensor_count):
    norm_master = masters[4]
    adam_out = [
        adam_terms(masters[member], grad_shards[member], firsts[member], seconds[member])
        for member in range(5)
    ]
    weight_sq = jnp.concatenate(
        [
            jnp.stack([jnp.sum(masters[member] * masters[member]) for member in range(4)]),
            jnp.sum(norm_master * norm_master, 1) / tensor_count,
        ]
    )
    update_sq = jnp.concatenate(
        [
            jnp.stack([jnp.sum(adam_out[member][0] * adam_out[member][0]) for member in range(4)]),
            jnp.sum(adam_out[4][0] * adam_out[4][0], 1) / tensor_count,
        ]
    )
    weight_tot, update_tot = lax.psum((weight_sq, update_sq), ("dp", "expert", "tensor"))
    weight_norms = jnp.sqrt(weight_tot)
    update_norms = jnp.sqrt(update_tot)
    ratios = weight_norms / update_norms
    new_weights = [
        masters[member] - LEARN_RATE * ratios[member] * adam_out[member][0] for member in range(4)
    ]
    norm_new = norm_master - LEARN_RATE * ratios[4:, None] * adam_out[4][0]
    lamb_norms = jnp.stack([weight_norms, update_norms])
    return (
        output[None],
        input_grad[None],
        bucket_share,
        lamb_norms,
        new_weights[0],
        new_weights[1],
        new_weights[2],
        new_weights[3],
        norm_new,
        adam_out[0][1],
        adam_out[1][1],
        adam_out[2][1],
        adam_out[3][1],
        adam_out[4][1],
        adam_out[0][2],
        adam_out[1][2],
        adam_out[2][2],
        adam_out[3][2],
        adam_out[4][2],
    )


def body(
    tokens,
    cotangent,
    head_counts,
    positions,
    buckets,
    in_master,
    out_master,
    up_master,
    down_master,
    norm_master,
    in_first,
    out_first,
    up_first,
    down_first,
    norm_first,
    in_second,
    out_second,
    up_second,
    down_second,
    norm_second,
):
    in_work, out_work, up_work, down_work, norm_work = (
        lax.all_gather(in_master.astype(jnp.bfloat16), ("dp", "expert"), axis=1, tiled=True),
        lax.all_gather(out_master.astype(jnp.bfloat16), ("dp", "expert"), axis=1, tiled=True),
        lax.all_gather(up_master.astype(jnp.bfloat16), ("dp", "expert"), axis=1, tiled=True),
        lax.all_gather(down_master.astype(jnp.bfloat16), ("dp", "expert"), axis=2, tiled=True),
        lax.all_gather(norm_master.astype(jnp.bfloat16), ("dp", "expert"), axis=1, tiled=True),
    )
    length = tokens.shape[1]
    model_width = tokens.shape[2]
    heads_here = in_work.shape[2] // HEAD_DIM
    block_rows = min(512, length)
    head_scale = HEAD_DIM ** (-0.5)
    groups_data = lax.axis_size("dp") * lax.axis_size("expert")
    tensor_count = lax.axis_size("tensor")
    experts = lax.axis_size("expert")
    norm_gains = norm_work.astype(jnp.float32)
    inputs = tokens[0].astype(jnp.float32)
    first_norm, first_hat, first_inv = layer_norm(inputs, norm_gains[0], norm_gains[1])
    first_in = first_norm.astype(jnp.bfloat16)
    projected = jnp.einsum("td,jde->jte", first_in, in_work, preferred_element_type=jnp.float32)
    projected = projected.reshape(3, length, heads_here, HEAD_DIM)
    angles = rope_angles(positions[0])
    queries = (rotary(projected[0], angles, 1.0) * head_scale).astype(jnp.bfloat16)
    key_rows = rotary(projected[1], angles, 1.0).astype(jnp.bfloat16)
    value_rows = projected[2].astype(jnp.bfloat16)
    head_ids = lax.axis_index("tensor") * heads_here + jnp.arange(heads_here, dtype=jnp.int32)
    active = (head_ids < head_counts[0]).astype(jnp.float32)
    head_outs, log_totals, starts = attend_forward(
        queries, key_rows, value_rows, positions[0], block_rows
    )
    attended = (
        (head_outs * active[None, :, None])
        .astype(jnp.bfloat16)
        .reshape(length, heads_here * HEAD_DIM)
    )
    attn_part = jnp.dot(attended, out_work, preferred_element_type=jnp.float32)
    middle = inputs + lax.psum(attn_part, "tensor")
    second_norm, second_hat, second_inv = layer_norm(middle, norm_gains[2], norm_gains[3])
    second_in = second_norm.astype(jnp.bfloat16)
    bucket_ids = buckets[0]
    onehot = (bucket_ids[:, None] == jnp.arange(4, dtype=jnp.int32)[None, :]).astype(jnp.int32)
    bucket_rank = jnp.sum((jnp.cumsum(onehot, 0) - onehot) * onehot, 1)
    local_counts = jnp.sum(onehot, 0).astype(jnp.float32)
    bucket_share = lax.psum(local_counts, ("dp", "expert")) / (length * groups_data)
    most_rows = 5 * length // 16
    owner_group = max(experts // 4, 1)
    per_owner = max(4 // experts, 1)
    slot_rows = (most_rows + owner_group - 1) // owner_group
    capacity = per_owner * slot_rows
    slot_of = (
        (bucket_ids // per_owner * owner_group + bucket_rank % owner_group) * capacity
        + bucket_ids % per_owner * slot_rows
        + bucket_rank // owner_group
    )
    slot_total = experts * capacity
    source_rows = (
        jnp.full((slot_total,), length, jnp.int32)
        .at[slot_of]
        .set(jnp.arange(length, dtype=jnp.int32))
    )
    outgoing = gather_rows(second_in, source_rows).reshape(experts, capacity, model_width)
    incoming = lax.all_to_all(outgoing, "expert", split_axis=0, concat_axis=0, tiled=True).reshape(
        experts, per_owner, slot_rows, model_width
    )
    owner_index = lax.axis_index("expert")
    owned_ids = [owner_index // owner_group * per_owner + member for member in range(per_owner)]
    ffn_inputs = [
        incoming[:, member].reshape(experts * slot_rows, model_width) for member in range(per_owner)
    ]
    results = [
        ffn_forward(ffn_inputs[member], owned_ids[member], up_work, down_work)
        for member in range(per_owner)
    ]
    partial_value = jnp.stack(
        [
            results[member][0].reshape(experts, slot_rows, model_width)
            for member in range(per_owner)
        ],
        1,
    )
    summed = ffn_total(partial_value.reshape(experts, capacity, model_width)).astype(jnp.bfloat16)
    returned = lax.all_to_all(summed, "expert", split_axis=0, concat_axis=0, tiled=True)
    branch_out = returned.reshape(slot_total, model_width)[slot_of]
    output = middle + branch_out.astype(jnp.float32)
    grad_branch = cotangent[0]
    outgoing_grad = gather_rows(grad_branch, source_rows).reshape(experts, capacity, model_width)
    incoming_grad = lax.all_to_all(
        outgoing_grad, "expert", split_axis=0, concat_axis=0, tiled=True
    ).reshape(experts, per_owner, slot_rows, model_width)
    ffn_grads = [
        incoming_grad[:, member].reshape(experts * slot_rows, model_width)
        for member in range(per_owner)
    ]
    back_parts = [
        ffn_backward(
            ffn_inputs[member],
            ffn_grads[member],
            owned_ids[member],
            results[member][1],
            up_work,
            down_work,
        )
        for member in range(len(owned_ids))
    ]
    grad_up = back_parts[0][1]
    grad_down = back_parts[0][2]
    for member in range(1, len(owned_ids)):
        grad_up = grad_up + back_parts[member][1]
        grad_down = grad_down + back_parts[member][2]
    rows_back = jnp.stack(
        [
            back_parts[member][0].reshape(experts, slot_rows, model_width)
            for member in range(per_owner)
        ],
        1,
    )
    summed_back = ffn_grad_total(rows_back.reshape(experts, capacity, model_width)).astype(
        jnp.bfloat16
    )
    returned_back = lax.all_to_all(summed_back, "expert", split_axis=0, concat_axis=0, tiled=True)
    grad_second = returned_back.reshape(slot_total, model_width)[slot_of].astype(jnp.float32)
    grad_mid_norm, gain_second, shift_second = norm_back_rows(
        grad_second, second_hat, second_inv, norm_gains[2]
    )
    grad_middle = grad_branch.astype(jnp.float32) + grad_mid_norm
    grad_attn = grad_middle.astype(jnp.bfloat16)
    grad_attended = jnp.einsum("td,ed->te", grad_attn, out_work, preferred_element_type=jnp.float32)
    grad_out_w = jnp.einsum("te,td->ed", attended, grad_attn, preferred_element_type=jnp.float32)
    grad_heads = (
        grad_attended.astype(jnp.bfloat16).reshape(length, heads_here, HEAD_DIM)
        * active.astype(jnp.bfloat16)[None, :, None]
    )
    grad_query, grad_keys, grad_values = attend_backward(
        queries, key_rows, value_rows, positions[0], grad_heads, log_totals, starts, block_rows
    )
    grad_projected = jnp.stack(
        [
            rotary(grad_query * head_scale, angles, -1.0),
            rotary(grad_keys, angles, -1.0),
            grad_values,
        ]
    )
    grad_projected = grad_projected.reshape(3, length, heads_here * HEAD_DIM).astype(jnp.bfloat16)
    grad_in_w = jnp.einsum(
        "td,jte->jde", first_in, grad_projected, preferred_element_type=jnp.float32
    )
    grad_first_part = jnp.einsum(
        "jte,jde->td", grad_projected, in_work, preferred_element_type=jnp.float32
    )
    grad_first = lax.psum(grad_first_part, "tensor")
    grad_input_norm, gain_first, shift_first = norm_back_rows(
        grad_first, first_hat, first_inv, norm_gains[0]
    )
    input_grad = grad_middle + grad_input_norm
    grad_norm = jnp.stack([gain_first, shift_first, gain_second, shift_second])
    in_sum, out_sum, up_sum, down_sum, norm_sum = (
        lax.psum_scatter(grad_in_w, ("dp", "expert"), scatter_dimension=1, tiled=True),
        lax.psum_scatter(grad_out_w, ("dp", "expert"), scatter_dimension=1, tiled=True),
        lax.psum_scatter(grad_up, ("dp", "expert"), scatter_dimension=1, tiled=True),
        lax.psum_scatter(grad_down, ("dp", "expert"), scatter_dimension=2, tiled=True),
        lax.psum_scatter(grad_norm, ("dp", "expert"), scatter_dimension=1, tiled=True),
    )
    masters = (in_master, out_master, up_master, down_master, norm_master)
    firsts = (in_first, out_first, up_first, down_first, norm_first)
    seconds = (in_second, out_second, up_second, down_second, norm_second)
    grad_shards = (in_sum, out_sum, up_sum, down_sum, norm_sum)
    return finish(output, input_grad, bucket_share, masters, firsts, seconds, grad_shards, tensor_count)


MESH = pl.DeviceIdType.MESH
ANY = pl.BlockSpec(memory_space=pl.ANY)
VM = pl.BlockSpec(memory_space=pltpu.VMEM)
SM = pl.BlockSpec(memory_space=pltpu.SMEM)

F32 = jnp.float32
BF16 = jnp.bfloat16
CHUNK = 256
HALF = 128
ROWS = 64


class Here:
    def __init__(self):
        d = lax.axis_index("dp")
        self.x, self.c = d // 2, lax.rem(d, 2)
        self.y = lax.axis_index("expert")
        self.z = lax.axis_index("tensor")

    def plane(self, dx, dc, dy):
        x = 1 - self.x if dx else self.x
        c = 1 - self.c if dc else self.c
        y = 1 - self.y if dy else self.y
        return (x * 2 + c, y, self.z)

    def chunk(self, dx, dc, dy):
        x = 1 - self.x if dx else self.x
        c = 1 - self.c if dc else self.c
        y = 1 - self.y if dy else self.y
        return (x * 2 + c) * 2 + y

    def chunk_of(self, dx, dy, core):
        x = 1 - self.x if dx else self.x
        y = 1 - self.y if dy else self.y
        return (x * 2 + core) * 2 + y

    def along(self, step):
        return (self.x * 2 + self.c, self.y, lax.rem(self.z + step, 4))

    def behind(self, step):
        return lax.rem(self.z + 4 - step, 4)


PARTNER = (0, 1, 0)
PLANE = [(a, b, g) for a in (0, 1) for b in (0, 1) for g in (0, 1) if a + b + g > 0]
SIDES = [(1, 0, 0), (1, 1, 0), (0, 0, 1), (0, 1, 1)]


def greet(here, plane_peers, tensor_peers):
    barrier = pltpu.get_barrier_semaphore()
    for peer in plane_peers:
        pl.semaphore_signal(barrier, inc=1, device_id=here.plane(*peer), device_id_type=MESH)
    for step in tensor_peers:
        pl.semaphore_signal(barrier, inc=1, device_id=here.along(step), device_id_type=MESH)
    pl.semaphore_wait(barrier, len(plane_peers) + len(tensor_peers))


def push(src, dst, send, recv, device):
    copy = pltpu.make_async_remote_copy(
        src_ref=src, dst_ref=dst, send_sem=send, recv_sem=recv, device_id=device, device_id_type=MESH
    )
    copy.start()
    return copy


def block(index, size):
    return pl.ds(pl.multiple_of(index * size, size), size)


def rows_chunk(ref, k):
    return ref.at[:, block(k, CHUNK), :]


def rows_part(ref, k, part):
    return ref.at[:, pl.ds(pl.multiple_of(k * CHUNK + part * HALF, HALF), HALF), :]


def cols_chunk(ref, k):
    return ref.at[:, :, block(k, CHUNK)]


def cols_part(ref, k, part):
    return ref.at[:, part * HALF : part * HALF + HALF, block(k, CHUNK)]


class Gather:
    def __init__(self, here, by_rows, shard, whole, first, relay, local):
        self.here, self.by_rows, self.shard, self.whole = here, by_rows, shard, whole
        self.first, self.relay, self.local = first, relay, local
        self.copies = []

    def half(self, core):
        if self.by_rows:
            return self.shard.at[:, :, block(core, CHUNK)]
        return self.shard.at[:, block(core, CHUNK), :]

    def chunk(self, k):
        return rows_chunk(self.whole, k) if self.by_rows else cols_chunk(self.whole, k)

    def part(self, k, part):
        return rows_part(self.whole, k, part) if self.by_rows else cols_part(self.whole, k, part)

    def start(self):
        here = self.here
        mine = self.chunk(here.chunk(0, 0, 0))
        for index, side in enumerate(SIDES + [PARTNER]):
            core = 1 - here.c if side[1] else here.c
            self.copies.append(
                push(
                    self.half(core),
                    mine,
                    self.first.at[0, index],
                    self.first.at[1, index],
                    here.plane(*side),
                )
            )
        self.own = pltpu.make_async_copy(self.half(here.c), mine, self.local)
        self.own.start()

    def forward(self):
        here = self.here
        self.onward = []
        for index in range(4):
            side = SIDES[index]
            self.copies[index].wait_recv()
            part = 0 if side[0] else 1
            where = self.part(here.chunk(*side), part)
            target = (0, 0, 1) if side[0] else (1, 0, 0)
            self.onward.append(
                push(
                    where,
                    where,
                    self.relay.at[0, index],
                    self.relay.at[1, index],
                    here.plane(*target),
                )
            )

    def finish(self):
        for index in range(4):
            self.copies[index].wait_send()
        self.copies[4].wait()
        self.own.wait()
        for copy in self.onward:
            copy.wait()


def gather_sems():
    return [
        pltpu.SemaphoreType.DMA((2, 5)),
        pltpu.SemaphoreType.DMA((2, 4)),
        pltpu.SemaphoreType.DMA,
    ]


class Scatter:
    def __init__(self, here, by_rows, grad, total, bufs):
        self.here, self.by_rows, self.grad, self.total = here, by_rows, grad, total
        self.got, self.got_two = bufs[:2]
        self.one_sem, self.two_sem, self.last_sem, self.local = bufs[2:6]
        self.final = bufs[6]

    def part(self, dx, dy, core, side):
        k = self.here.chunk_of(dx, dy, core)
        return rows_part(self.grad, k, side) if self.by_rows else cols_part(self.grad, k, side)

    def start(self):
        here = self.here
        self.first = []
        for side in (0, 1):
            near, far = ((1, 0), (1, 1)) if side == 0 else ((0, 1), (1, 1))
            target = here.plane(1, 0, 0) if side == 0 else here.plane(0, 0, 1)
            for slot in range(4):
                chip = far if slot >= 2 else near
                index = side * 4 + slot
                self.first.append(
                    push(
                        self.part(chip[0], chip[1], slot % 2, side),
                        self.got.at[index],
                        self.one_sem.at[0, index],
                        self.one_sem.at[1, index],
                        target,
                    )
                )

    def middle(self):
        here = self.here
        self.second = []
        for side in (0, 1):
            target = here.plane(0, 0, 1) if side == 0 else here.plane(1, 0, 0)
            chip = (0, 1) if side == 0 else (1, 0)
            for slot in (2, 3):
                index = side * 4 + slot
                two = side * 2 + slot - 2
                mine = self.part(chip[0], chip[1], slot - 2, side)
                self.first[index].wait_recv()
                mine[...] = (mine[...].astype(F32) + self.got[index].astype(F32)).astype(BF16)
                self.second.append(
                    push(
                        mine,
                        self.got_two.at[two],
                        self.two_sem.at[0, two],
                        self.two_sem.at[1, two],
                        target,
                    )
                )

    def last(self):
        here = self.here
        for side in (0, 1):
            for slot in (0, 1):
                index = side * 4 + slot
                two = side * 2 + slot
                self.first[index].wait_recv()
                self.second[two].wait_recv()
                self.final[slot, :, side * HALF : side * HALF + HALF, :] = (
                    self.part(0, 0, slot, side)[...].astype(F32) + self.got[index].astype(F32)
                ) + self.got_two[two].astype(F32)
        if self.by_rows:
            where = self.total.at[:, :, block(here.c, CHUNK)]
        else:
            where = self.total.at[:, block(here.c, CHUNK), :]
        self.keep = pltpu.make_async_copy(self.final.at[here.c], where, self.local)
        self.keep.start()
        self.give = push(
            self.final.at[1 - here.c],
            where,
            self.last_sem.at[0],
            self.last_sem.at[1],
            here.plane(*PARTNER),
        )

    def sent(self):
        self.keep.wait()
        self.give.wait_send()

    def finish(self):
        for copy in self.first:
            copy.wait_send()
        for copy in self.second:
            copy.wait_send()
        self.give.wait_recv()


def scatter_scratch(width):
    return [
        pltpu.VMEM((8, width, HALF, CHUNK), BF16),
        pltpu.VMEM((4, width, HALF, CHUNK), BF16),
        pltpu.SemaphoreType.DMA((2, 8)),
        pltpu.SemaphoreType.DMA((2, 4)),
        pltpu.SemaphoreType.DMA((2,)),
        pltpu.SemaphoreType.DMA,
    ]


SCATTER = 6


class TensorSum:
    def __init__(self, here, part, bufs):
        self.here, self.part = here, part
        self.pair, self.out, self.inn, self.pair_sem, self.sem = bufs

    def start(self):
        here = self.here
        self.swap = push(
            self.part.at[1 - here.c],
            self.pair,
            self.pair_sem.at[0],
            self.pair_sem.at[1],
            here.plane(*PARTNER),
        )

    def spread(self):
        here = self.here
        self.swap.wait_recv()
        self.sent = []
        for step in (2, 1, 3):
            rows = block(lax.rem(here.z + step, 4), ROWS)
            self.out[step - 1] = (
                self.part[here.c, rows, :].astype(F32) + self.pair[rows, :].astype(F32)
            ).astype(self.out.dtype)
            self.sent.append(
                push(
                    self.out.at[step - 1],
                    self.inn.at[step - 1],
                    self.sem.at[0, step - 1],
                    self.sem.at[1, step - 1],
                    here.along(step),
                )
            )

    def result(self):
        here = self.here
        rows = block(here.z, ROWS)
        total = self.part[here.c, rows, :].astype(F32) + self.pair[rows, :].astype(F32)
        for copy in self.sent:
            copy.wait_recv()
        for step in (1, 2, 3):
            total = total + self.inn[step - 1].astype(F32)
        return total

    def finish(self):
        self.swap.wait_send()
        for copy in self.sent:
            copy.wait_send()


def sum_scratch(length, width):
    return [
        pltpu.VMEM((length, width), BF16),
        pltpu.VMEM((3, ROWS, width), BF16),
        pltpu.VMEM((3, ROWS, width), BF16),
        pltpu.SemaphoreType.DMA((2,)),
        pltpu.SemaphoreType.DMA((2, 3)),
    ]


class TensorGather:
    def __init__(self, here, mine, whole, sem, pair_sem, local):
        self.here, self.mine, self.whole = here, mine, whole
        self.sem, self.pair_sem, self.local = sem, pair_sem, local

    def start(self):
        here = self.here
        place = self.whole.at[here.c, block(here.z, ROWS), :]
        self.sent = []
        for step in (2, 1, 3):
            self.sent.append(
                push(
                    self.mine,
                    place,
                    self.sem.at[0, step - 1],
                    self.sem.at[1, step - 1],
                    here.along(step),
                )
            )
        self.shared = [
            push(
                self.mine,
                place,
                self.pair_sem.at[0, 0],
                self.pair_sem.at[1, 0],
                here.plane(*PARTNER),
            )
        ]
        self.own = pltpu.make_async_copy(self.mine, place, self.local)
        self.own.start()

    def forward(self):
        here = self.here
        for index, step in enumerate((2, 1, 3)):
            self.sent[index].wait_recv()
            place = self.whole.at[here.c, block(here.behind(step), ROWS), :]
            self.shared.append(
                push(
                    place,
                    place,
                    self.pair_sem.at[0, step],
                    self.pair_sem.at[1, step],
                    here.plane(*PARTNER),
                )
            )

    def finish(self):
        for copy in self.sent:
            copy.wait_send()
        for copy in self.shared:
            copy.wait()
        self.own.wait()


class LineSum:
    def __init__(self, here, part, bufs):
        self.here, self.part = here, part
        self.pair, self.slot, self.pair_sem, self.sem = bufs

    def start(self):
        here = self.here
        self.swap = push(
            self.part.at[1 - here.c],
            self.pair,
            self.pair_sem.at[0],
            self.pair_sem.at[1],
            here.plane(*PARTNER),
        )

    def own(self, z):
        rows = block(z, ROWS)
        return self.part[self.here.c, rows, :].astype(F32) + self.pair[rows, :].astype(F32)

    def depth(self, way):
        return self.here.z if way == 0 else 3 - self.here.z

    def hop(self, way, k, src):
        here = self.here
        return pltpu.make_async_remote_copy(
            src_ref=src,
            dst_ref=self.slot.at[way, k],
            send_sem=self.sem.at[0, way, k],
            recv_sem=self.sem.at[1, way, k],
            device_id=(here.x * 2 + here.c, here.y, here.z + (1 if way == 0 else -1)),
            device_id_type=MESH,
        )

    def take(self, way, k):
        here = self.here
        pltpu.make_async_remote_copy(
            src_ref=self.slot.at[way, k],
            dst_ref=self.slot.at[way, k],
            send_sem=self.sem.at[0, way, k],
            recv_sem=self.sem.at[1, way, k],
            device_id=(here.x * 2 + here.c, here.y, here.z - (1 if way == 0 else -1)),
            device_id_type=MESH,
        ).wait_recv()

    def stage(self, k):
        here = self.here
        if k == 0:
            self.swap.wait_recv()
        for way in (0, 1):
            depth = self.depth(way)
            shard = here.z + 3 - k if way == 0 else here.z - 3 + k

            @pl.when(depth == 0)
            def _():
                self.slot[way, k] = self.own(shard).astype(BF16)
                self.hop(way, k, self.slot.at[way, k]).start()

            if k > 0:

                @pl.when((depth >= 1) & (depth <= k))
                def _():
                    self.take(way, k - 1)
                    self.slot[way, k - 1] = (
                        self.own(shard) + self.slot[way, k - 1].astype(F32)
                    ).astype(BF16)
                    self.hop(way, k, self.slot.at[way, k - 1]).start()

    def result(self):
        total = self.own(self.here.z)
        for way in (0, 1):
            depth = self.depth(way)

            @pl.when(depth >= 1)
            def _():
                self.take(way, 2)

            total = total + jnp.where(depth >= 1, self.slot[way, 2].astype(F32), 0.0)
        return total

    def finish(self):
        self.swap.wait_send()
        for way in (0, 1):
            for k in range(3):

                @pl.when(self.depth(way) <= k)
                def _():
                    self.hop(way, k, self.slot.at[way, k]).wait_send()


def line_scratch(length, width):
    return [
        pltpu.VMEM((length, width), BF16),
        pltpu.VMEM((2, 3, ROWS, width), BF16),
        pltpu.SemaphoreType.DMA((2,)),
        pltpu.SemaphoreType.DMA((2, 2, 3)),
    ]


class LineGather:
    def __init__(self, here, place, sem):
        self.here, self.place, self.sem = here, place, sem

    def hop(self, way, k):
        here = self.here
        step = 1 if way == 0 else -1
        spot = self.place(here.z - k * step)
        return pltpu.make_async_remote_copy(
            src_ref=spot,
            dst_ref=spot,
            send_sem=self.sem.at[0, way, k],
            recv_sem=self.sem.at[1, way, k],
            device_id=(here.x * 2 + here.c, here.y, here.z + step),
            device_id_type=MESH,
        )

    def arrival(self, way, k):
        here = self.here
        step = 1 if way == 0 else -1
        spot = self.place(here.z - (k + 1) * step)
        return pltpu.make_async_remote_copy(
            src_ref=spot,
            dst_ref=spot,
            send_sem=self.sem.at[0, way, k],
            recv_sem=self.sem.at[1, way, k],
            device_id=(here.x * 2 + here.c, here.y, here.z - step),
            device_id_type=MESH,
        )

    def sends(self, way, k):
        z = self.here.z
        return (z >= k) & (z < 3) if way == 0 else (z <= 3 - k) & (z > 0)

    def gets(self, way, k):
        z = self.here.z
        return z >= k + 1 if way == 0 else z <= 2 - k

    def start(self):
        for way in (0, 1):

            @pl.when(self.sends(way, 0))
            def _():
                self.hop(way, 0).start()

    def onward(self, k, then=None):
        for way in (0, 1):

            @pl.when(self.gets(way, k))
            def _():
                self.arrival(way, k).wait_recv()
                if then is not None:
                    then(self.here.z - (k + 1) * (1 if way == 0 else -1))

            if k < 2:

                @pl.when(self.sends(way, k + 1))
                def _():
                    self.hop(way, k + 1).start()

    def finish(self):
        for way in (0, 1):
            for k in range(3):

                @pl.when(self.sends(way, k))
                def _():
                    self.hop(way, k).wait_send()


def normed(values):
    center = values - jnp.mean(values, -1, keepdims=True)
    variance = jnp.mean(center * center, -1, keepdims=True)
    inv_std = lax.rsqrt(variance + NORM_EPS)
    return (center * inv_std, inv_std)


def norm_row(packs, row):
    return jnp.concatenate([packs[k, row : row + 1, :] for k in range(8)], 1)


def params(ident, limit=60):
    return pltpu.CompilerParams(
        collective_id=ident, has_side_effects=True, vmem_limit_bytes=limit << 20
    )


def cast_rows(raw, shard):
    count, rows, _ = raw.shape
    for j in range(count):

        def step(i, carry):
            at = pl.ds(pl.multiple_of(i * 32, 32), 32)
            shard[j, at, :] = raw[j, at, :].astype(BF16)
            return carry

        lax.fori_loop(0, rows // 32, step, 0)


def front_kernel(*refs):
    head_count, position, bucket, tok, cot, norm_master = refs[:6]
    masters = refs[6:10]
    n1, both_cot, tables, packs, n2, mid, q_out, k_out, v_out, a_out = refs[10:20]
    wholes = refs[20:24]
    raws, shards = refs[24:28], refs[28:32]
    raw_sem, n2_own, part, small, pair, local = refs[32:38]
    sums, tensor_sems, gather_refs = refs[38:43], refs[43:46], refs[46:58]
    here = Here()
    loads = []
    for i in range(4):
        loads.append(pltpu.make_async_copy(masters[i], raws[i], raw_sem.at[i]))
        loads[i].start()
    me = here.chunk(0, 0, 0)
    lane = lax.broadcasted_iota(jnp.int32, (1, CHUNK), 1)
    counts = jnp.zeros((1, CHUNK), F32)
    for c in range(4):
        count = jnp.sum((bucket[...] == c).astype(F32), 1, keepdims=True)
        counts = counts + jnp.where(lane == c, count, 0.0)
    packs[pl.ds(me, 1)] = jnp.concatenate(
        [norm_master[...].astype(BF16).astype(F32), counts, jnp.zeros((3, CHUNK), F32)], 0
    )[None]
    gathers = [
        Gather(here, i in (0, 2), shards[i], wholes[i], *gather_refs[i * 3 : i * 3 + 3])
        for i in range(4)
    ]
    loads[0].wait()
    cast_rows(raws[0], shards[0])
    greet(here, PLANE, (1, 2, 3))
    gathers[0].start()
    packed = []
    for index, peer in enumerate(PLANE):
        packed.append(
            push(
                packs.at[me], packs.at[me],
                small.at[0, index], small.at[1, index], here.plane(*peer),
            )
        )
    partner = here.plane(*PARTNER)
    table = tables.at[here.c]
    fill_table(table, position[...], bucket[...], head_count[0])
    shared = [
        push(table, table, pair.at[0, 0], pair.at[1, 0], partner),
        push(cot, both_cot.at[here.c], pair.at[0, 1], pair.at[1, 1], partner),
    ]
    keep = pltpu.make_async_copy(cot, both_cot.at[here.c], local)
    keep.start()
    for i in range(1, 4):
        loads[i].wait()
        cast_rows(raws[i], shards[i])
    for copy in packed:
        copy.wait()
    gain, shift = norm_row(packs, 0), norm_row(packs, 1)
    mine = n1.at[here.c]

    def rows_step(i, carry):
        rows = block(i, 32)
        hat, _ = normed(tok[rows, :].astype(F32))
        mine[rows, :] = (hat * gain + shift).astype(BF16)
        return carry

    lax.fori_loop(0, tok.shape[0] // 32, rows_step, 0)
    shared.append(push(mine, mine, pair.at[0, 2], pair.at[1, 2], partner))
    gathers[1].start()
    gathers[0].forward()
    gathers[1].forward()
    gathers[0].finish()
    gathers[2].start()
    gathers[3].start()
    shared[0].wait_recv()
    shared[2].wait_recv()
    head0 = here.z * 4 + here.c * 2
    attend_body(head0, n1, wholes[0], wholes[1], tables, q_out, k_out, v_out, a_out, part)
    gathers[1].finish()
    total = TensorSum(here, part, sums)
    attend_out(a_out, wholes[1], part, 1 - here.c)
    total.start()
    attend_out(a_out, wholes[1], part, here.c)
    total.spread()
    rows = block(here.z, ROWS)
    middle = tok[rows, :].astype(F32) + total.result()
    mid[...] = middle
    hat, _ = normed(middle)
    n2_own[...] = (hat * norm_row(packs, 2) + norm_row(packs, 3)).astype(BF16)
    gather = TensorGather(here, n2_own, n2, *tensor_sems)
    gather.start()
    gathers[2].forward()
    gathers[3].forward()
    gather.forward()
    total.finish()
    gather.finish()
    gathers[2].finish()
    gathers[3].finish()
    keep.wait()
    shared[0].wait_send()
    shared[1].wait()
    shared[2].wait_send()


def front_call(head_count, position, bucket, tok, cot, norm_master, masters):
    length, width = tok.shape
    both = jax.ShapeDtypeStruct((2, length, width), BF16)
    thin = jax.ShapeDtypeStruct((2 * length, CHUNK), BF16)
    wholes = [
        jax.ShapeDtypeStruct((3, width, CHUNK), BF16),
        jax.ShapeDtypeStruct((1, CHUNK, width), BF16),
        jax.ShapeDtypeStruct((4, width, CHUNK), BF16),
        jax.ShapeDtypeStruct((4, CHUNK, width), BF16),
    ]
    results = pl.pallas_call(
        front_kernel,
        out_shape=[
            both,
            both,
            jax.ShapeDtypeStruct((2, 5, length, HALF), F32),
            jax.ShapeDtypeStruct((8, 8, CHUNK), F32),
            both,
            jax.ShapeDtypeStruct((ROWS, width), F32),
            thin, thin, thin, thin,
        ]
        + wholes,
        in_specs=[SM, VM, VM, VM, VM, VM] + [ANY] * 4,
        out_specs=[VM, ANY, VM, VM, ANY, VM, VM, VM, VM, VM, VM, VM, ANY, ANY],
        scratch_shapes=[pltpu.VMEM(master.shape, F32) for master in masters]
        + [pltpu.VMEM(master.shape, BF16) for master in masters]
        + [
            pltpu.SemaphoreType.DMA((4,)),
            pltpu.VMEM((ROWS, width), BF16),
            pltpu.VMEM((2, length, width), BF16),
            pltpu.SemaphoreType.DMA((2, 7)),
            pltpu.SemaphoreType.DMA((2, 3)),
            pltpu.SemaphoreType.DMA,
        ]
        + sum_scratch(length, width)
        + tensor_gather_sems()
        + gather_sems() * 4,
        compiler_params=params(1),
        name="front",
    )(head_count, position, bucket, tok, cot, norm_master, *masters)
    return results[:10], results[10:]


def tensor_gather_sems():
    return [
        pltpu.SemaphoreType.DMA((2, 3)),
        pltpu.SemaphoreType.DMA((2, 4)),
        pltpu.SemaphoreType.DMA,
    ]


def norm_back(grad_out, hat, inv_std, gain):
    scaled = grad_out * gain
    inner = (
        scaled
        - jnp.mean(scaled, -1, keepdims=True)
        - hat * jnp.mean(scaled * hat, -1, keepdims=True)
    )
    return (
        inner * inv_std,
        jnp.sum(grad_out * hat, 0, keepdims=True),
        jnp.sum(grad_out, 0, keepdims=True),
    )


def ffn_hidden(r, n2, cot, bucket, wu, wd, squares, grad_hidden):
    width = n2.shape[2]
    hidden = dot(n2[...].reshape(-1, width), wu[r])
    live = bucket >= jnp.float32(r)
    rectified = jnp.maximum(jnp.where(live, hidden, 0.0), 0.0)
    squares[r] = (rectified * rectified).astype(BF16)
    grad_square = dot(cot[...].reshape(-1, width), wd[r], ((1,), (1,)))
    grad_hidden[r] = (grad_square * 2.0 * rectified).astype(BF16)


def ffn_rows(s, left, right, part, transposed):
    length, width = part.shape[1:]
    rows = pl.ds(pl.multiple_of(s * length, length), length)
    for n in range(width // (2 * CHUNK)):
        cols = slice(n * 2 * CHUNK, (n + 1) * 2 * CHUNK)
        total = None
        for r in range(4):
            if transposed:
                term = dot(left[r, rows, :], right[r, cols, :], ((1,), (1,)))
            else:
                term = dot(left[r, rows, :], right[r, :, cols])
            total = term if total is None else total + term
        part[s, :, cols] = total.astype(BF16)


def attend_back_body(head0, gm, qkva, wq, wo, tables, dp, part):
    length = tables.shape[2]
    width = gm.shape[2]
    q_rows, k_rows, v_rows = qkva.at[0], qkva.at[1], qkva.at[2]
    grad_att = dot(gm[...].reshape(2 * length, width), wo[...], ((1,), (1,))).astype(BF16)
    for s in range(2):
        rows = slice(s * length, (s + 1) * length)
        cosine, sine = tables[s, 0], tables[s, 1]
        lowest = tables[s, 2, :, 0:1]
        for h in range(2):
            cols = slice(h * HEAD_DIM, (h + 1) * HEAD_DIM)
            active = tables[s, 4] > (head0 + h).astype(F32)
            grad_heads = jnp.where(active, grad_att[rows, cols].astype(F32), 0.0).astype(BF16)
            queries, key_rows, value_rows = q_rows[rows, cols], k_rows[rows, cols], v_rows[rows, cols]
            weights = attention_weights(queries, key_rows, lowest)
            grad_weights = dot(grad_heads, value_rows, ((1,), (1,)))
            inner = jnp.sum(weights * grad_weights, -1, keepdims=True)
            grad_scores = (weights * (grad_weights - inner)).astype(BF16)
            grad_query = dot(grad_scores, key_rows) * HEAD_DIM ** (-0.5)
            grad_keys = dot(grad_scores, queries, ((0,), (0,)))
            grad_values = dot(weights.astype(BF16), grad_heads, ((0,), (0,)))
            dp[0, rows, cols] = turn(grad_query, cosine, -sine).astype(BF16)
            dp[1, rows, cols] = turn(grad_keys, cosine, -sine).astype(BF16)
            dp[2, rows, cols] = grad_values.astype(BF16)


def attend_back_rows(s, dp, wq, part):
    length = part.shape[1]
    rows = pl.ds(pl.multiple_of(s * length, length), length)
    total = dot(dp[0, rows, :], wq[0], ((1,), (1,)))
    total = total + dot(dp[1, rows, :], wq[1], ((1,), (1,)))
    total = total + dot(dp[2, rows, :], wq[2], ((1,), (1,)))
    part[s] = total.astype(BF16)


def norm_share(here, values, bufs):
    slices, heard, plane_sum, heard_z, ns, nz = bufs
    for k in range(8):
        slices[k, 0:4, :] = values[:, k * CHUNK : (k + 1) * CHUNK]
        slices[k, 4:8, :] = jnp.zeros((4, CHUNK), F32)
    copies = []
    for index, peer in enumerate(PLANE):
        copies.append(
            push(
                slices.at[here.chunk(*peer)],
                heard.at[index],
                ns.at[0, index],
                ns.at[1, index],
                here.plane(*peer),
            )
        )
    return copies


def norm_share_along(here, copies, bufs):
    slices, heard, plane_sum, heard_z, ns, nz = bufs
    mine = slices[here.chunk(0, 0, 0)]
    for index in range(7):
        copies[index].wait()
        mine = mine + heard[index]
    plane_sum[...] = mine
    onward = []
    for step in (1, 2, 3):
        onward.append(
            push(
                plane_sum,
                heard_z.at[here.z],
                nz.at[0, step - 1],
                nz.at[1, step - 1],
                here.along(step),
            )
        )
    heard_z[pl.ds(here.z, 1)] = mine[None]
    return onward


def back_kernel(*refs):
    n2, cot, tables, packs, mid = refs[0:5]
    tok, wq, wo, wu, wd, n1, q_rows, k_rows, v_rows, a_rows = refs[5:15]
    out_all, ig_own, norm_total, q_sum, o_sum, u_sum, d_sum = refs[15:22]
    wu_v, wd_v, qkva, tok_own, load_sem, squares, grad_hidden, part, part_f, dp = refs[22:32]
    gu, gd, gq, go, gm, dmid, sums, out_v = refs[32:40]
    back_bufs, branch_bufs, final_one, final_two = refs[40:44], refs[44:48], refs[48], refs[49]
    gm_sem, gm_pair, out_sem, keep_sem, norm_bufs = *refs[50:54], refs[54:60]
    rest = refs[60:]
    here = Here()
    loads = []

    def load(src, dst):
        copy = pltpu.make_async_copy(src, dst, load_sem.at[len(loads)])
        copy.start()
        loads.append(copy)
        return copy

    first = [(load(wu.at[r], wu_v.at[r]), load(wd.at[r], wd_v.at[r])) for r in range(4)]
    small = [load(src, qkva.at[i]) for i, src in enumerate((q_rows, k_rows, v_rows, a_rows))]
    place = block(here.z, ROWS)
    small.append(load(tok.at[place, :], tok_own))
    scatters = [
        Scatter(here, by_rows, grad, total, rest[i * SCATTER : (i + 1) * SCATTER] + (final,))
        for i, (by_rows, grad, total, final) in enumerate(
            (
                (True, gu.at[0:1], u_sum.at[0:1], final_one.at[:, 0:1]),
                (False, gd.at[0:1], d_sum.at[0:1], final_two.at[:, 0:1]),
                (True, gu.at[1:4], u_sum.at[1:4], final_one.at[:, 1:4]),
                (False, gd.at[1:4], d_sum.at[1:4], final_two.at[:, 1:4]),
                (True, gq, q_sum, final_one.at[:, 0:3]),
                (False, go, o_sum, final_one.at[:, 3:4]),
            )
        )
    ]
    early_u, early_d, scatter_u, scatter_d, scatter_q, scatter_o = scatters
    length, width = n2.shape[1:]

    def up_gradient(r):
        rows_in = n2[...].reshape(2 * length, width)
        gu[r] = dot(rows_in, grad_hidden[r], ((0,), (0,))).astype(BF16)

    def down_gradient(r):
        grads_in = cot[...].reshape(2 * length, width)
        gd[r] = dot(squares[r], grads_in, ((0,), (0,))).astype(BF16)

    bucket = jnp.concatenate([tables[0, 3, :, 0:1], tables[1, 3, :, 0:1]], 0)
    for r in range(4):
        first[r][0].wait()
        first[r][1].wait()
        ffn_hidden(r, n2, cot, bucket, wu_v, wd_v, squares, grad_hidden)
        if r == 0:
            up_gradient(0)
            greet(here, PLANE, (1, 2, 3))
            early_u.start()
            down_gradient(0)
            early_d.start()
    other = 1 - here.c
    back = LineSum(here, part, back_bufs)
    ffn_rows(other, grad_hidden, wu_v, part, True)
    back.start()
    ffn_rows(here.c, grad_hidden, wu_v, part, True)
    back.stage(0)
    load_q = load(wq, wu_v.at[0:3])
    for r in range(1, 4):
        up_gradient(r)
    scatter_u.start()
    down_gradient(1)
    back.stage(1)
    down_gradient(2)
    down_gradient(3)
    scatter_d.start()
    branch = LineSum(here, part_f, branch_bufs)
    ffn_rows(other, squares, wd_v, part_f, False)
    branch.start()
    back.stage(2)
    ffn_rows(here.c, squares, wd_v, part_f, False)
    load_n1 = load(n1, wd_v.at[0:2])
    load_o = load(wo, wd_v.at[2:3])
    grad_n2 = back.result().astype(BF16).astype(F32)
    back.finish()
    hat, inv_std = normed(mid[...])
    grad_mid, gain_sum, shift_sum = norm_back(grad_n2, hat, inv_std, norm_row(packs, 2))
    grad_mid = cot[here.c, place, :].astype(F32) + grad_mid
    dmid[...] = grad_mid
    gm[pl.ds(here.c, 1), place, :] = grad_mid.astype(BF16)[None]
    gather = LineGather(here, lambda z: gm.at[here.c, block(z, ROWS), :], gm_sem)
    gather.start()
    early_u.middle()
    early_d.middle()

    def shared(z):
        spot = gm.at[here.c, block(z, ROWS), :]
        return pltpu.make_async_remote_copy(
            src_ref=spot,
            dst_ref=spot,
            send_sem=gm_pair.at[0, z],
            recv_sem=gm_pair.at[1, z],
            device_id=here.plane(*PARTNER),
            device_id_type=MESH,
        )

    shared(here.z).start()
    sums[0:1, :] = gain_sum
    sums[1:2, :] = shift_sum
    gather.onward(0, lambda z: shared(z).start())
    branch.stage(0)
    gather.onward(1, lambda z: shared(z).start())
    gather.onward(2, lambda z: shared(z).start())
    branch.stage(1)
    scatter_u.middle()
    for copy in small:
        copy.wait()
    load_o.wait()
    load_q.wait()
    load_n1.wait()
    gather.finish()
    for z in range(4):
        shared(z).wait()
    head0 = here.z * 4 + here.c * 2
    attend_back_body(head0, gm, qkva, wu_v, wd_v.at[2], tables, dp, part)
    branch.stage(2)
    last = LineSum(here, part, back_bufs)
    attend_back_rows(other, dp, wu_v, part)
    last.start()
    attend_back_rows(here.c, dp, wu_v, part)
    last.stage(0)
    scatter_d.middle()
    rows_in = wd_v[0:2].reshape(2 * length, width)
    for j in range(3):
        gq[j] = dot(rows_in, dp[j], ((0,), (0,))).astype(BF16)
    scatter_q.start()
    last.stage(1)
    go[0] = dot(qkva[3], gm[...].reshape(2 * length, width), ((0,), (0,))).astype(BF16)
    scatter_o.start()
    early_u.last()
    early_d.last()
    last.stage(2)
    out_v[place, :] = (mid[...] + branch.result().astype(BF16).astype(F32)).astype(BF16)
    spread = LineGather(here, lambda z: out_v.at[block(z, ROWS), :], out_sem)
    spread.start()
    scatter_u.last()
    spread.onward(0)
    grad_n1 = last.result()
    hat, inv_std = normed(tok_own[...].astype(F32))
    grad_in, gain_sum, shift_sum = norm_back(grad_n1, hat, inv_std, norm_row(packs, 0))
    ig_own[...] = (dmid[...] + grad_in).astype(BF16)
    norm_copies = norm_share(
        here, jnp.concatenate([gain_sum, shift_sum, sums[...]], 0), norm_bufs
    )
    scatter_q.middle()
    scatter_o.middle()
    spread.onward(1)
    spread.onward(2)
    keep = pltpu.make_async_copy(out_v, out_all, keep_sem)
    keep.start()
    onward = norm_share_along(here, norm_copies, norm_bufs)
    scatter_d.last()
    for copy in onward:
        copy.wait()
    heard_z = norm_bufs[3]
    norm_total[...] = ((heard_z[0] + heard_z[1]) + heard_z[2]) + heard_z[3]
    early_u.sent()
    scatter_u.sent()
    scatter_q.last()
    scatter_o.last()
    branch.finish()
    last.finish()
    spread.finish()
    keep.wait()
    for scatter in (early_d, scatter_d, scatter_q, scatter_o):
        scatter.sent()
    for scatter in scatters:
        scatter.finish()


def back_call(n2, cot, tables, packs, mid, tok, wq, wo, wu, wd, n1, rows):
    _, length, width = n2.shape
    both = pltpu.VMEM((2, length, width), BF16)
    results = pl.pallas_call(
        back_kernel,
        out_shape=[
            jax.ShapeDtypeStruct((length, width), BF16),
            jax.ShapeDtypeStruct((ROWS, width), BF16),
            jax.ShapeDtypeStruct((8, CHUNK), F32),
            jax.ShapeDtypeStruct((3, CHUNK, 2 * CHUNK), F32),
            jax.ShapeDtypeStruct((1, 2 * CHUNK, CHUNK), F32),
            jax.ShapeDtypeStruct((4, CHUNK, 2 * CHUNK), F32),
            jax.ShapeDtypeStruct((4, 2 * CHUNK, CHUNK), F32),
        ],
        in_specs=[VM] * 5 + [ANY] * 10,
        out_specs=[ANY, VM, VM, ANY, ANY, ANY, ANY],
        scratch_shapes=[
            pltpu.VMEM(wu.shape, BF16),
            pltpu.VMEM(wd.shape, BF16),
            pltpu.VMEM((4, 2 * length, CHUNK), BF16),
            pltpu.VMEM((ROWS, width), BF16),
            pltpu.SemaphoreType.DMA((16,)),
            pltpu.VMEM((4, 2 * length, CHUNK), BF16),
            pltpu.VMEM((4, 2 * length, CHUNK), BF16),
            both,
            both,
            pltpu.VMEM((3, 2 * length, CHUNK), BF16),
            pltpu.VMEM(wu.shape, BF16),
            pltpu.VMEM(wd.shape, BF16),
            pltpu.VMEM(wq.shape, BF16),
            pltpu.VMEM(wo.shape, BF16),
            both,
            pltpu.VMEM((ROWS, width), F32),
            pltpu.VMEM((2, width), F32),
            pltpu.VMEM((length, width), BF16),
        ]
        + line_scratch(length, width) * 2
        + [pltpu.VMEM((2, 4, CHUNK, CHUNK), F32)] * 2
        + [
            pltpu.SemaphoreType.DMA((2, 2, 3)),
            pltpu.SemaphoreType.DMA((2, 4)),
            pltpu.SemaphoreType.DMA((2, 2, 3)),
            pltpu.SemaphoreType.DMA,
            pltpu.VMEM((8, 8, CHUNK), F32),
            pltpu.VMEM((7, 8, CHUNK), F32),
            pltpu.VMEM((8, CHUNK), F32),
            pltpu.VMEM((4, 8, CHUNK), F32),
            pltpu.SemaphoreType.DMA((2, 7)),
            pltpu.SemaphoreType.DMA((2, 3)),
        ]
        + (scatter_scratch(1) * 2 + scatter_scratch(3) * 2)
        + scatter_scratch(3)
        + scatter_scratch(1),
        compiler_params=params(3),
        name="back",
    )(n2, cot, tables, packs, mid, tok, wq, wo, wu, wd, n1, *rows)
    return results


FIRST_SCALE = 1.0 / (1.0 - BETA_FIRST**STEP)
SECOND_SCALE = 1.0 / (1.0 - BETA_SECOND**STEP)


def folded(values):
    rows, cols = values.shape
    total = None
    for i in range(rows // 8):
        for j in range(cols // 128):
            tile = values[i * 8 : i * 8 + 8, j * 128 : j * 128 + 128]
            total = tile if total is None else total + tile
    return total


def updated(weight, gradient, first_old, second_old):
    first_new = BETA_FIRST * first_old + (1.0 - BETA_FIRST) * gradient
    second_new = BETA_SECOND * second_old + (1.0 - BETA_SECOND) * gradient * gradient
    update = first_new * FIRST_SCALE / (
        jnp.sqrt(second_new * SECOND_SCALE) + ADAM_EPS
    ) + WEIGHT_DECAY * weight
    return (update, first_new, second_new)


AHEAD = 4


def adam_kernel(*refs):
    sources = [refs[kind * 5 : kind * 5 + 4] for kind in range(4)]
    norm_grad, norm_master, norm_first, norm_second = [refs[kind * 5 + 4] for kind in range(4)]
    out_all = refs[20]
    outs = [refs[21 + kind * 5 : 25 + kind * 5] for kind in range(3)]
    norm_outs = [refs[25 + kind * 5] for kind in range(3)]
    tile, output = refs[36:38]
    held = [refs[38 + kind * 4 : 42 + kind * 4] for kind in range(4)]
    load_sem, store_sem = refs[54:56]
    blocks = [(i, j) for i in range(4) for j in range(sources[0][i].shape[0])]
    loads = []

    def load():
        index = len(loads)
        if index == len(blocks):
            return
        i, j = blocks[index]
        loads.append([])
        for kind in range(4):
            copy = pltpu.make_async_copy(
                sources[kind][i].at[j], held[kind][i].at[j], load_sem.at[kind, index]
            )
            copy.start()
            loads[index].append(copy)

    for _ in range(AHEAD):
        load()
    output[...] = out_all[...].astype(F32)
    weight = norm_master[...]
    update, first_new, second_new = updated(
        weight, norm_grad[0:4, :], norm_first[...], norm_second[...]
    )
    for out, value in zip(norm_outs, (update, first_new, second_new)):
        out[...] = value
    for row, value in ((4, weight), (12, update)):
        square = value * value * 0.25
        tile[row : row + 4, :] = square[:, :128] + square[:, 128:]
    stores = []
    sums = None
    for index, (i, j) in enumerate(blocks):
        if j == 0:
            sums = (jnp.zeros((8, 128), F32), jnp.zeros((8, 128), F32))
        for copy in loads[index]:
            copy.wait()
        load()
        grads, masters, firsts, seconds = [held[kind][i] for kind in range(4)]

        def step(k, carry):
            at = pl.ds(pl.multiple_of(k * 16, 16), 16)
            weight = masters[j, at, :]
            update, first_new, second_new = updated(
                weight, grads[j, at, :], firsts[j, at, :], seconds[j, at, :]
            )
            grads[j, at, :] = update
            firsts[j, at, :] = first_new
            seconds[j, at, :] = second_new
            return (carry[0] + folded(weight * weight), carry[1] + folded(update * update))

        sums = lax.fori_loop(0, grads.shape[1] // 16, step, sums)
        for kind, source in enumerate((grads, firsts, seconds)):
            copy = pltpu.make_async_copy(
                source.at[j], outs[kind][i].at[j], store_sem.at[kind, index]
            )
            copy.start()
            stores.append(copy)
        if j == grads.shape[0] - 1:
            tile[i : i + 1, :] = jnp.sum(sums[0], 0, keepdims=True)
            tile[8 + i : 9 + i, :] = jnp.sum(sums[1], 0, keepdims=True)
    for copy in stores:
        copy.wait()


def adam_call(grads, masters, firsts, seconds, out_all):
    shapes = [master.shape for master in masters]
    like = [jax.ShapeDtypeStruct(shape, F32) for shape in shapes]
    specs = [ANY] * 4 + [VM]
    count = sum(shape[0] for shape in shapes[:4])
    results = pl.pallas_call(
        adam_kernel,
        out_shape=like * 3
        + [jax.ShapeDtypeStruct((16, 128), F32), jax.ShapeDtypeStruct(out_all.shape, F32)],
        in_specs=specs * 4 + [VM],
        out_specs=specs * 3 + [VM, VM],
        scratch_shapes=[pltpu.VMEM(shape, F32) for shape in shapes[:4]] * 4
        + [pltpu.SemaphoreType.DMA((4, count)), pltpu.SemaphoreType.DMA((3, count))],
        compiler_params=local_params(60),
        name="adam",
    )(*grads, *masters, *firsts, *seconds, out_all)
    return results[0:5], results[5:10], results[10:15], results[15], results[16]


def total_kernel(tile, norms, tiles_z, plane_tile, tiles, zs, ps):
    here = Here()
    greet(here, PLANE, (1, 2, 3))
    sent = []
    for step in (2, 1, 3):
        sent.append(
            push(tile, tiles_z.at[here.z], zs.at[0, step - 1], zs.at[1, step - 1], here.along(step))
        )
    tiles_z[pl.ds(here.z, 1)] = tile[...][None]
    for copy in sent:
        copy.wait()
    plane_tile[...] = ((tiles_z[0] + tiles_z[1]) + tiles_z[2]) + tiles_z[3]
    me = here.chunk(0, 0, 0)
    sent = []
    for index, peer in enumerate(PLANE):
        sent.append(
            push(plane_tile, tiles.at[me], ps.at[0, index], ps.at[1, index], here.plane(*peer))
        )
    tiles[pl.ds(me, 1)] = plane_tile[...][None]
    for copy in sent:
        copy.wait()
    total = tiles[0]
    for k in range(1, 8):
        total = total + tiles[k]
    roots = jnp.sqrt(jnp.sum(total, 1, keepdims=True))
    norms[...] = jnp.broadcast_to(roots, norms.shape)


def total_call(tile):
    return pl.pallas_call(
        total_kernel,
        out_shape=jax.ShapeDtypeStruct((16, 128), F32),
        in_specs=[VM],
        out_specs=VM,
        scratch_shapes=[
            pltpu.VMEM((4, 16, 128), F32),
            pltpu.VMEM((16, 128), F32),
            pltpu.VMEM((8, 16, 128), F32),
            pltpu.SemaphoreType.DMA((2, 3)),
            pltpu.SemaphoreType.DMA((2, 7)),
        ],
        compiler_params=params(5),
        name="norm_totals",
    )(tile)


def weight_kernel(*refs):
    norms, updates, masters, packs = refs[0], refs[1:6], refs[6:11], refs[11]
    ig_rows = refs[12:16]
    outs = refs[16:21]
    igrad, lamb_norms, share = refs[21:24]
    held = (refs[24:28], refs[28:32])
    load_sem, store_sem = refs[32:34]
    blocks = [(i, j) for i in range(4) for j in range(updates[i].shape[0])]
    loads = []

    def load():
        index = len(loads)
        if index == len(blocks):
            return
        i, j = blocks[index]
        loads.append([])
        for kind, source in enumerate((updates, masters)):
            copy = pltpu.make_async_copy(
                source[i].at[j], held[kind][i].at[j], load_sem.at[kind, index]
            )
            copy.start()
            loads[index].append(copy)

    for _ in range(AHEAD):
        load()
    scales = LEARN_RATE * (norms[0:8, 0:1] / norms[8:16, 0:1])
    outs[4][...] = masters[4][...] - scales[4:8, :] * updates[4][...]
    row = lax.broadcasted_iota(jnp.int32, norms.shape, 0)
    lane = lax.broadcasted_iota(jnp.int32, norms.shape, 1)
    flat = jnp.sum(jnp.where(row == lane, norms[...], 0.0), 0, keepdims=True)
    lamb_norms[0:1, :] = flat[:, 0:8]
    lamb_norms[1:2, :] = flat[:, 8:16]
    counts = packs[0, 4:5, :]
    for k in range(1, 8):
        counts = counts + packs[k, 4:5, :]
    share[...] = counts[:, 0:4] / (igrad.shape[0] * 8)
    here = Here()
    for step in range(4):
        igrad[block(here.behind(step), ROWS), :] = ig_rows[step][...].astype(F32)
    stores = []
    for index, (i, j) in enumerate(blocks):
        for copy in loads[index]:
            copy.wait()
        load()
        held[1][i][j] = held[1][i][j] - scales[i : i + 1, :] * held[0][i][j]
        copy = pltpu.make_async_copy(held[1][i].at[j], outs[i].at[j], store_sem.at[index])
        copy.start()
        stores.append(copy)
    for copy in stores:
        copy.wait()


def weight_call(norms, updates, masters, packs, ig_rows):
    shapes = [master.shape for master in masters]
    specs = [ANY] * 4 + [VM]
    count = sum(shape[0] for shape in shapes[:4])
    rows, width = ig_rows[0].shape
    return pl.pallas_call(
        weight_kernel,
        out_shape=[jax.ShapeDtypeStruct(shape, F32) for shape in shapes]
        + [
            jax.ShapeDtypeStruct((4 * rows, width), F32),
            jax.ShapeDtypeStruct((2, 8), F32),
            jax.ShapeDtypeStruct((1, 4), F32),
        ],
        in_specs=[VM] + specs * 2 + [VM] * 5,
        out_specs=specs + [VM, VM, VM],
        scratch_shapes=[pltpu.VMEM(shape, F32) for shape in shapes[:4]] * 2
        + [pltpu.SemaphoreType.DMA((2, count)), pltpu.SemaphoreType.DMA((count,))],
        compiler_params=local_params(60),
        name="new_weights",
    )(norms, *updates, *masters, packs, *ig_rows)


def turn(values, cosine, sine):
    return values * cosine + pltpu.roll(values, HEAD_DIM // 2, 1) * sine


def dot(left, right, dims=((1,), (0,))):
    return lax.dot_general(left, right, (dims, ((), ())), preferred_element_type=F32)


def attention_weights(queries, key_rows, lowest):
    scores = dot(queries, key_rows, ((1,), (1,)))
    row = lax.broadcasted_iota(jnp.int32, scores.shape, 0)
    col = lax.broadcasted_iota(jnp.int32, scores.shape, 1)
    allowed = (col <= row) & (col.astype(F32) >= lowest)
    scores = jnp.where(allowed, scores, MASKED)
    exp_scores = jnp.exp(scores - jnp.max(scores, -1, keepdims=True))
    return exp_scores / jnp.sum(exp_scores, -1, keepdims=True)


def attend_body(head0, n1, wq, wo, tables, q_out, k_out, v_out, a_out, part):
    length = tables.shape[2]
    rows_in = n1[...].reshape(2 * length, n1.shape[2])
    projected = [dot(rows_in, wq[j]) for j in range(3)]
    for s in range(2):
        rows = slice(s * length, (s + 1) * length)
        cosine, sine = tables[s, 0], tables[s, 1]
        lowest = tables[s, 2, :, 0:1]
        for h in range(2):
            cols = slice(h * HEAD_DIM, (h + 1) * HEAD_DIM)
            queries = (turn(projected[0][rows, cols], cosine, sine) * HEAD_DIM ** (-0.5)).astype(BF16)
            key_rows = turn(projected[1][rows, cols], cosine, sine).astype(BF16)
            value_rows = projected[2][rows, cols].astype(BF16)
            weights = attention_weights(queries, key_rows, lowest).astype(BF16)
            heads = dot(weights, value_rows)
            active = tables[s, 4] > (head0 + h).astype(F32)
            q_out[rows, cols] = queries
            k_out[rows, cols] = key_rows
            v_out[rows, cols] = value_rows
            a_out[rows, cols] = jnp.where(active, heads, 0.0).astype(BF16)


def attend_out(a_out, wo, part, s):
    length = part.shape[1]
    part[s] = dot(a_out[pl.ds(pl.multiple_of(s * length, length), length), :], wo[0]).astype(BF16)


def fill_table(table, position, bucket, head_count):
    length = table.shape[1]
    row = lax.broadcasted_iota(jnp.int32, (length, length), 0)
    col = lax.broadcasted_iota(jnp.int32, (length, length), 1)

    def column(values):
        return jnp.sum(jnp.where(row == col, values.astype(F32), 0.0), 1, keepdims=True)

    place = column(position)
    lane = lax.broadcasted_iota(jnp.int32, (length, HALF), 1)
    half = HEAD_DIM // 2
    second = lane >= half
    freq_index = jnp.where(second, lane - half, lane).astype(F32)
    angles = place * jnp.exp(freq_index * (-2.0 * math.log(ROPE_BASE) / HEAD_DIM))
    table[0] = jnp.cos(angles)
    sine = jnp.sin(angles)
    table[1] = jnp.where(second, sine, -sine)
    index = lax.broadcasted_iota(jnp.int32, (length, HALF), 0).astype(F32)
    table[2] = index - place
    table[3] = jnp.broadcast_to(column(bucket), (length, HALF))
    table[4] = jnp.broadcast_to(head_count.astype(F32), (length, HALF))


def local_params(limit):
    return pltpu.CompilerParams(vmem_limit_bytes=limit << 20)


def fast_body(
    tokens, cotangent, head_counts, positions, buckets,
    in_master, out_master, up_master, down_master, norm_master,
    in_first, out_first, up_first, down_first, norm_first,
    in_second, out_second, up_second, down_second, norm_second,
):
    tok, cot = tokens[0], cotangent[0]
    (n1, both_cot, tables, packs, n2, mid, q_rows, k_rows, v_rows, a_rows), (wq, wo, wu, wd) = front_call(
        head_counts, positions, buckets, tok, cot, norm_master,
        (in_master, out_master[None], up_master, down_master),
    )
    out_all, ig_own, norm_sum, in_sum, out_sum, up_sum, down_sum = back_call(
        n2, both_cot, tables, packs, mid, tok, wq, wo, wu, wd, n1,
        (q_rows, k_rows, v_rows, a_rows),
    )
    ig_rows = [ig_own] + [
        lax.ppermute(ig_own, "tensor", [(i, (i + step) % 4) for i in range(4)])
        for step in (1, 2, 3)
    ]
    masters = (in_master, out_master[None], up_master, down_master, norm_master)
    firsts = (in_first, out_first[None], up_first, down_first, norm_first)
    seconds = (in_second, out_second[None], up_second, down_second, norm_second)
    updates, moments, squares, tile, output = adam_call(
        (in_sum, out_sum, up_sum, down_sum, norm_sum), masters, firsts, seconds, out_all
    )
    norms = total_call(tile)
    *weights, input_grad, lamb_norms, share = weight_call(
        norms, updates, masters, packs, ig_rows
    )
    flat = lambda group: (group[0], group[1][0], group[2], group[3], group[4])
    return (
        output[None],
        input_grad[None],
        share[0],
        lamb_norms,
        *flat(weights),
        *flat(moments),
        *flat(squares),
    )


def solution(mesh):
    placed = (
        P(("dp", "expert"), None, None),
        P(("dp", "expert"), None, None),
        P(("dp", "expert")),
        P(("dp", "expert"), None),
        P(("dp", "expert"), None),
        P(None, ("dp", "expert"), "tensor"),
        P("tensor", ("dp", "expert")),
        P(None, ("dp", "expert"), "tensor"),
        P(None, "tensor", ("dp", "expert")),
        P(None, ("dp", "expert")),
        P(None, ("dp", "expert"), "tensor"),
        P("tensor", ("dp", "expert")),
        P(None, ("dp", "expert"), "tensor"),
        P(None, "tensor", ("dp", "expert")),
        P(None, ("dp", "expert")),
        P(None, ("dp", "expert"), "tensor"),
        P("tensor", ("dp", "expert")),
        P(None, ("dp", "expert"), "tensor"),
        P(None, "tensor", ("dp", "expert")),
        P(None, ("dp", "expert")),
    )
    shape = dict(mesh.shape)
    fits = shape == {"dp": 4, "expert": 2, "tensor": 4}
    return jax.shard_map(
        fast_body if fits else body,
        mesh=mesh,
        in_specs=placed,
        out_specs=(
            P(("dp", "expert"), None, None),
            P(("dp", "expert"), None, None),
            P(),
            P(),
            P(None, ("dp", "expert"), "tensor"),
            P("tensor", ("dp", "expert")),
            P(None, ("dp", "expert"), "tensor"),
            P(None, "tensor", ("dp", "expert")),
            P(None, ("dp", "expert")),
            P(None, ("dp", "expert"), "tensor"),
            P("tensor", ("dp", "expert")),
            P(None, ("dp", "expert"), "tensor"),
            P(None, "tensor", ("dp", "expert")),
            P(None, ("dp", "expert")),
            P(None, ("dp", "expert"), "tensor"),
            P("tensor", ("dp", "expert")),
            P(None, ("dp", "expert"), "tensor"),
            P(None, "tensor", ("dp", "expert")),
            P(None, ("dp", "expert")),
        ),
        check_vma=False,
    )
```

```python
import math

import jax
import jax.numpy as jnp
from jax import lax
from jax.experimental import pallas as pl
from jax.experimental.pallas import tpu as pltpu
from jax.sharding import PartitionSpec as P

HEAD_DIM = 128
STEP = 10


NORM_EPS = 1e-05
BETA_FIRST = 0.9
BETA_SECOND = 0.999
ADAM_EPS = 1e-06
WEIGHT_DECAY = 0.01
LEARN_RATE = 0.25
MASKED = -1e30
ROPE_BASE = 10000.0


def layer_norm(values, gain_row, shift_row):
    center = values - jnp.mean(values, -1, keepdims=True)
    variance = jnp.mean(center * center, -1, keepdims=True)
    inv_std = lax.rsqrt(variance + NORM_EPS)
    normed = center * inv_std
    return (normed * gain_row + shift_row, normed, inv_std)


def norm_back_rows(grad_out, normed, inv_std, gain_row):
    scaled = grad_out * gain_row
    inner_part = (
        scaled
        - jnp.mean(scaled, -1, keepdims=True)
        - normed * jnp.mean(scaled * normed, -1, keepdims=True)
    )
    return (inner_part * inv_std, jnp.sum(grad_out * normed, 0), jnp.sum(grad_out, 0))


def rope_angles(position_row):
    freq_index = jnp.arange(HEAD_DIM // 2, dtype=jnp.float32)
    inverse = jnp.exp(freq_index * (-2.0 * jnp.log(ROPE_BASE) / HEAD_DIM))
    return position_row.astype(jnp.float32)[:, None] * inverse[None, :]


def rotary(values, angles, sign_value):
    half_dim = values.shape[-1] // 2
    cosine = jnp.cos(angles)[:, None, :]
    sine_part = sign_value * jnp.sin(angles)[:, None, :]
    first_half = values[..., :half_dim]
    second_half = values[..., half_dim:]
    return jnp.concatenate(
        [
            first_half * cosine - second_half * sine_part,
            second_half * cosine + first_half * sine_part,
        ],
        -1,
    )


def block_mask(key_index, position_row, block_start, block_rows):
    query_index = block_start + jnp.arange(block_rows, dtype=jnp.int32)
    return (key_index[None, :] <= query_index[:, None]) & (
        key_index[None, :] >= (query_index - position_row)[:, None]
    )


def attend_forward(queries, key_rows, value_rows, position_row, block_rows):
    length = queries.shape[0]
    key_index = jnp.arange(length, dtype=jnp.int32)

    def one_block(block_start):
        allowed = block_mask(key_index, position_row, block_start, block_rows)
        scores = jnp.einsum("qhd,khd->hqk", queries, key_rows, preferred_element_type=jnp.float32)
        scores = jnp.where(allowed[None], scores, MASKED)
        row_peak = jnp.max(scores, -1, keepdims=True)
        exp_scores = jnp.exp(scores - row_peak)
        row_total = jnp.sum(exp_scores, -1, keepdims=True)
        attn_weights = (exp_scores / row_total).astype(jnp.bfloat16)
        block_out = jnp.einsum(
            "hqk,khd->qhd", attn_weights, value_rows, preferred_element_type=jnp.float32
        )
        return (block_out, row_peak[..., 0] + jnp.log(row_total[..., 0]))

    starts = jnp.arange(length // block_rows, dtype=jnp.int32) * block_rows
    block_outs, log_totals = lax.map(one_block, starts)
    return (block_outs.reshape(queries.shape), log_totals, starts)


def attend_backward(
    queries, key_rows, value_rows, position_row, grad_heads, log_totals, starts, block_rows
):
    length = queries.shape[0]
    key_index = jnp.arange(length, dtype=jnp.int32)

    def one_block(carried, inputs):
        block_start, block_log = inputs
        allowed = block_mask(key_index, position_row, block_start, block_rows)
        scores = jnp.einsum("qhd,khd->hqk", queries, key_rows, preferred_element_type=jnp.float32)
        scores = jnp.where(allowed[None], scores, MASKED)
        attn_probs = jnp.exp(scores - block_log[..., None])
        grad_probs = jnp.einsum(
            "qhd,khd->hqk", grad_heads, value_rows, preferred_element_type=jnp.float32
        )
        row_inner = jnp.sum(attn_probs * grad_probs, -1, keepdims=True)
        grad_scores = (attn_probs * (grad_probs - row_inner)).astype(jnp.bfloat16)
        grad_query = jnp.einsum(
            "hqk,khd->qhd", grad_scores, key_rows, preferred_element_type=jnp.float32
        )
        grad_keys = carried[0] + jnp.einsum(
            "hqk,qhd->khd", grad_scores, queries, preferred_element_type=jnp.float32
        )
        grad_values = carried[1] + jnp.einsum(
            "hqk,qhd->khd",
            attn_probs.astype(jnp.bfloat16),
            grad_heads,
            preferred_element_type=jnp.float32,
        )
        return ((grad_keys, grad_values), grad_query)

    start_state = (jnp.zeros(key_rows.shape, jnp.float32), jnp.zeros(value_rows.shape, jnp.float32))
    (grad_keys, grad_values), grad_query = lax.scan(one_block, start_state, (starts, log_totals))
    return (grad_query.reshape(queries.shape), grad_keys, grad_values)


def gather_rows(values, source_rows):
    padded = jnp.concatenate([values, jnp.zeros((1, values.shape[1]), values.dtype)], 0)
    return padded[source_rows]


def ffn_forward(rows_in, bucket, up_work, down_work):
    row_count = rows_in.shape[0]
    mixed_sum = jnp.zeros((row_count, down_work.shape[2]), jnp.float32)
    hiddens = []
    for quarter in range(4):

        def live_part():
            hidden = jnp.dot(rows_in, up_work[quarter], preferred_element_type=jnp.float32)
            squared = jnp.square(jnp.maximum(hidden, 0.0)).astype(jnp.bfloat16)
            return (
                hidden,
                jnp.dot(squared, down_work[quarter], preferred_element_type=jnp.float32),
            )

        def dead_part():
            return (
                jnp.zeros((row_count, up_work.shape[2]), jnp.float32),
                jnp.zeros_like(mixed_sum),
            )

        hidden, contribution = lax.cond(bucket >= quarter, live_part, dead_part)
        hiddens.append(hidden)
        mixed_sum = mixed_sum + contribution
    return (mixed_sum, hiddens)


def ffn_backward(rows_in, grads_in, bucket, hiddens, up_work, down_work):
    grad_rows = jnp.zeros((rows_in.shape[0], up_work.shape[1]), jnp.float32)
    grad_up = []
    grad_down = []
    for quarter in range(4):
        hidden = hiddens[quarter]

        def live_part():
            rectified = jnp.maximum(hidden, 0.0)
            squared = jnp.square(rectified).astype(jnp.bfloat16)
            grad_square = jnp.einsum(
                "rd,ud->ru", grads_in, down_work[quarter], preferred_element_type=jnp.float32
            )
            grad_hidden = (grad_square * 2.0 * rectified).astype(jnp.bfloat16)
            return (
                jnp.einsum("rd,ru->du", rows_in, grad_hidden, preferred_element_type=jnp.float32),
                jnp.einsum("ru,rd->ud", squared, grads_in, preferred_element_type=jnp.float32),
                jnp.einsum(
                    "ru,du->rd", grad_hidden, up_work[quarter], preferred_element_type=jnp.float32
                ),
            )

        def dead_part():
            return (
                jnp.zeros(up_work.shape[1:], jnp.float32),
                jnp.zeros(down_work.shape[1:], jnp.float32),
                jnp.zeros_like(grad_rows),
            )

        part_up, part_down, part_rows = lax.cond(bucket >= quarter, live_part, dead_part)
        grad_up.append(part_up)
        grad_down.append(part_down)
        grad_rows = grad_rows + part_rows
    return (grad_rows, jnp.stack(grad_up), jnp.stack(grad_down))


def ffn_total(partial_value):
    return lax.psum(partial_value, "tensor")


def ffn_grad_total(partial_value):
    return lax.psum(partial_value, "tensor")


def adam_terms(weight, gradient, first_old, second_old):
    first_new = BETA_FIRST * first_old + (1.0 - BETA_FIRST) * gradient
    second_new = BETA_SECOND * second_old + (1.0 - BETA_SECOND) * gradient * gradient
    update = (
        first_new
        / (1.0 - BETA_FIRST**STEP)
        / (jnp.sqrt(second_new / (1.0 - BETA_SECOND**STEP)) + ADAM_EPS)
        + WEIGHT_DECAY * weight
    )
    return (update, first_new, second_new)


def finish(output, input_grad, bucket_share, masters, firsts, seconds, grad_shards, tensor_count):
    norm_master = masters[4]
    adam_out = [
        adam_terms(masters[member], grad_shards[member], firsts[member], seconds[member])
        for member in range(5)
    ]
    weight_sq = jnp.concatenate(
        [
            jnp.stack([jnp.sum(masters[member] * masters[member]) for member in range(4)]),
            jnp.sum(norm_master * norm_master, 1) / tensor_count,
        ]
    )
    update_sq = jnp.concatenate(
        [
            jnp.stack([jnp.sum(adam_out[member][0] * adam_out[member][0]) for member in range(4)]),
            jnp.sum(adam_out[4][0] * adam_out[4][0], 1) / tensor_count,
        ]
    )
    weight_tot, update_tot = lax.psum((weight_sq, update_sq), ("dp", "expert", "tensor"))
    weight_norms = jnp.sqrt(weight_tot)
    update_norms = jnp.sqrt(update_tot)
    ratios = weight_norms / update_norms
    new_weights = [
        masters[member] - LEARN_RATE * ratios[member] * adam_out[member][0] for member in range(4)
    ]
    norm_new = norm_master - LEARN_RATE * ratios[4:, None] * adam_out[4][0]
    lamb_norms = jnp.stack([weight_norms, update_norms])
    return (
        output[None],
        input_grad[None],
        bucket_share,
        lamb_norms,
        new_weights[0],
        new_weights[1],
        new_weights[2],
        new_weights[3],
        norm_new,
        adam_out[0][1],
        adam_out[1][1],
        adam_out[2][1],
        adam_out[3][1],
        adam_out[4][1],
        adam_out[0][2],
        adam_out[1][2],
        adam_out[2][2],
        adam_out[3][2],
        adam_out[4][2],
    )


def body(
    tokens,
    cotangent,
    head_counts,
    positions,
    buckets,
    in_master,
    out_master,
    up_master,
    down_master,
    norm_master,
    in_first,
    out_first,
    up_first,
    down_first,
    norm_first,
    in_second,
    out_second,
    up_second,
    down_second,
    norm_second,
):
    in_work, out_work, up_work, down_work, norm_work = (
        lax.all_gather(in_master.astype(jnp.bfloat16), ("dp", "expert"), axis=1, tiled=True),
        lax.all_gather(out_master.astype(jnp.bfloat16), ("dp", "expert"), axis=1, tiled=True),
        lax.all_gather(up_master.astype(jnp.bfloat16), ("dp", "expert"), axis=1, tiled=True),
        lax.all_gather(down_master.astype(jnp.bfloat16), ("dp", "expert"), axis=2, tiled=True),
        lax.all_gather(norm_master.astype(jnp.bfloat16), ("dp", "expert"), axis=1, tiled=True),
    )
    length = tokens.shape[1]
    model_width = tokens.shape[2]
    heads_here = in_work.shape[2] // HEAD_DIM
    block_rows = min(512, length)
    head_scale = HEAD_DIM ** (-0.5)
    groups_data = lax.axis_size("dp") * lax.axis_size("expert")
    tensor_count = lax.axis_size("tensor")
    experts = lax.axis_size("expert")
    norm_gains = norm_work.astype(jnp.float32)
    inputs = tokens[0].astype(jnp.float32)
    first_norm, first_hat, first_inv = layer_norm(inputs, norm_gains[0], norm_gains[1])
    first_in = first_norm.astype(jnp.bfloat16)
    projected = jnp.einsum("td,jde->jte", first_in, in_work, preferred_element_type=jnp.float32)
    projected = projected.reshape(3, length, heads_here, HEAD_DIM)
    angles = rope_angles(positions[0])
    queries = (rotary(projected[0], angles, 1.0) * head_scale).astype(jnp.bfloat16)
    key_rows = rotary(projected[1], angles, 1.0).astype(jnp.bfloat16)
    value_rows = projected[2].astype(jnp.bfloat16)
    head_ids = lax.axis_index("tensor") * heads_here + jnp.arange(heads_here, dtype=jnp.int32)
    active = (head_ids < head_counts[0]).astype(jnp.float32)
    head_outs, log_totals, starts = attend_forward(
        queries, key_rows, value_rows, positions[0], block_rows
    )
    attended = (
        (head_outs * active[None, :, None])
        .astype(jnp.bfloat16)
        .reshape(length, heads_here * HEAD_DIM)
    )
    attn_part = jnp.dot(attended, out_work, preferred_element_type=jnp.float32)
    middle = inputs + lax.psum(attn_part, "tensor")
    second_norm, second_hat, second_inv = layer_norm(middle, norm_gains[2], norm_gains[3])
    second_in = second_norm.astype(jnp.bfloat16)
    bucket_ids = buckets[0]
    onehot = (bucket_ids[:, None] == jnp.arange(4, dtype=jnp.int32)[None, :]).astype(jnp.int32)
    bucket_rank = jnp.sum((jnp.cumsum(onehot, 0) - onehot) * onehot, 1)
    local_counts = jnp.sum(onehot, 0).astype(jnp.float32)
    bucket_share = lax.psum(local_counts, ("dp", "expert")) / (length * groups_data)
    most_rows = 5 * length // 16
    owner_group = max(experts // 4, 1)
    per_owner = max(4 // experts, 1)
    slot_rows = (most_rows + owner_group - 1) // owner_group
    capacity = per_owner * slot_rows
    slot_of = (
        (bucket_ids // per_owner * owner_group + bucket_rank % owner_group) * capacity
        + bucket_ids % per_owner * slot_rows
        + bucket_rank // owner_group
    )
    slot_total = experts * capacity
    source_rows = (
        jnp.full((slot_total,), length, jnp.int32)
        .at[slot_of]
        .set(jnp.arange(length, dtype=jnp.int32))
    )
    outgoing = gather_rows(second_in, source_rows).reshape(experts, capacity, model_width)
    incoming = lax.all_to_all(outgoing, "expert", split_axis=0, concat_axis=0, tiled=True).reshape(
        experts, per_owner, slot_rows, model_width
    )
    owner_index = lax.axis_index("expert")
    owned_ids = [owner_index // owner_group * per_owner + member for member in range(per_owner)]
    ffn_inputs = [
        incoming[:, member].reshape(experts * slot_rows, model_width) for member in range(per_owner)
    ]
    results = [
        ffn_forward(ffn_inputs[member], owned_ids[member], up_work, down_work)
        for member in range(per_owner)
    ]
    partial_value = jnp.stack(
        [
            results[member][0].reshape(experts, slot_rows, model_width)
            for member in range(per_owner)
        ],
        1,
    )
    summed = ffn_total(partial_value.reshape(experts, capacity, model_width)).astype(jnp.bfloat16)
    returned = lax.all_to_all(summed, "expert", split_axis=0, concat_axis=0, tiled=True)
    branch_out = returned.reshape(slot_total, model_width)[slot_of]
    output = middle + branch_out.astype(jnp.float32)
    grad_branch = cotangent[0]
    outgoing_grad = gather_rows(grad_branch, source_rows).reshape(experts, capacity, model_width)
    incoming_grad = lax.all_to_all(
        outgoing_grad, "expert", split_axis=0, concat_axis=0, tiled=True
    ).reshape(experts, per_owner, slot_rows, model_width)
    ffn_grads = [
        incoming_grad[:, member].reshape(experts * slot_rows, model_width)
        for member in range(per_owner)
    ]
    back_parts = [
        ffn_backward(
            ffn_inputs[member],
            ffn_grads[member],
            owned_ids[member],
            results[member][1],
            up_work,
            down_work,
        )
        for member in range(len(owned_ids))
    ]
    grad_up = back_parts[0][1]
    grad_down = back_parts[0][2]
    for member in range(1, len(owned_ids)):
        grad_up = grad_up + back_parts[member][1]
        grad_down = grad_down + back_parts[member][2]
    rows_back = jnp.stack(
        [
            back_parts[member][0].reshape(experts, slot_rows, model_width)
            for member in range(per_owner)
        ],
        1,
    )
    summed_back = ffn_grad_total(rows_back.reshape(experts, capacity, model_width)).astype(
        jnp.bfloat16
    )
    returned_back = lax.all_to_all(summed_back, "expert", split_axis=0, concat_axis=0, tiled=True)
    grad_second = returned_back.reshape(slot_total, model_width)[slot_of].astype(jnp.float32)
    grad_mid_norm, gain_second, shift_second = norm_back_rows(
        grad_second, second_hat, second_inv, norm_gains[2]
    )
    grad_middle = grad_branch.astype(jnp.float32) + grad_mid_norm
    grad_attn = grad_middle.astype(jnp.bfloat16)
    grad_attended = jnp.einsum("td,ed->te", grad_attn, out_work, preferred_element_type=jnp.float32)
    grad_out_w = jnp.einsum("te,td->ed", attended, grad_attn, preferred_element_type=jnp.float32)
    grad_heads = (
        grad_attended.astype(jnp.bfloat16).reshape(length, heads_here, HEAD_DIM)
        * active.astype(jnp.bfloat16)[None, :, None]
    )
    grad_query, grad_keys, grad_values = attend_backward(
        queries, key_rows, value_rows, positions[0], grad_heads, log_totals, starts, block_rows
    )
    grad_projected = jnp.stack(
        [
            rotary(grad_query * head_scale, angles, -1.0),
            rotary(grad_keys, angles, -1.0),
            grad_values,
        ]
    )
    grad_projected = grad_projected.reshape(3, length, heads_here * HEAD_DIM).astype(jnp.bfloat16)
    grad_in_w = jnp.einsum(
        "td,jte->jde", first_in, grad_projected, preferred_element_type=jnp.float32
    )
    grad_first_part = jnp.einsum(
        "jte,jde->td", grad_projected, in_work, preferred_element_type=jnp.float32
    )
    grad_first = lax.psum(grad_first_part, "tensor")
    grad_input_norm, gain_first, shift_first = norm_back_rows(
        grad_first, first_hat, first_inv, norm_gains[0]
    )
    input_grad = grad_middle + grad_input_norm
    grad_norm = jnp.stack([gain_first, shift_first, gain_second, shift_second])
    in_sum, out_sum, up_sum, down_sum, norm_sum = (
        lax.psum_scatter(grad_in_w, ("dp", "expert"), scatter_dimension=1, tiled=True),
        lax.psum_scatter(grad_out_w, ("dp", "expert"), scatter_dimension=1, tiled=True),
        lax.psum_scatter(grad_up, ("dp", "expert"), scatter_dimension=1, tiled=True),
        lax.psum_scatter(grad_down, ("dp", "expert"), scatter_dimension=2, tiled=True),
        lax.psum_scatter(grad_norm, ("dp", "expert"), scatter_dimension=1, tiled=True),
    )
    masters = (in_master, out_master, up_master, down_master, norm_master)
    firsts = (in_first, out_first, up_first, down_first, norm_first)
    seconds = (in_second, out_second, up_second, down_second, norm_second)
    grad_shards = (in_sum, out_sum, up_sum, down_sum, norm_sum)
    return finish(output, input_grad, bucket_share, masters, firsts, seconds, grad_shards, tensor_count)


MESH = pl.DeviceIdType.MESH
ANY = pl.BlockSpec(memory_space=pl.ANY)
VM = pl.BlockSpec(memory_space=pltpu.VMEM)
SM = pl.BlockSpec(memory_space=pltpu.SMEM)

F32 = jnp.float32
BF16 = jnp.bfloat16
CHUNK = 256
HALF = 128
ROWS = 64


class Here:
    def __init__(self):
        d = lax.axis_index("dp")
        self.x, self.c = d // 2, lax.rem(d, 2)
        self.y = lax.axis_index("expert")
        self.z = lax.axis_index("tensor")

    def plane(self, dx, dc, dy):
        x = 1 - self.x if dx else self.x
        c = 1 - self.c if dc else self.c
        y = 1 - self.y if dy else self.y
        return (x * 2 + c, y, self.z)

    def chunk(self, dx, dc, dy):
        x = 1 - self.x if dx else self.x
        c = 1 - self.c if dc else self.c
        y = 1 - self.y if dy else self.y
        return (x * 2 + c) * 2 + y

    def chunk_of(self, dx, dy, core):
        x = 1 - self.x if dx else self.x
        y = 1 - self.y if dy else self.y
        return (x * 2 + core) * 2 + y

    def along(self, step):
        return (self.x * 2 + self.c, self.y, lax.rem(self.z + step, 4))

    def behind(self, step):
        return lax.rem(self.z + 4 - step, 4)


PARTNER = (0, 1, 0)
PLANE = [(a, b, g) for a in (0, 1) for b in (0, 1) for g in (0, 1) if a + b + g > 0]
SIDES = [(1, 0, 0), (1, 1, 0), (0, 0, 1), (0, 1, 1)]


def greet(here, plane_peers, tensor_peers):
    barrier = pltpu.get_barrier_semaphore()
    for peer in plane_peers:
        pl.semaphore_signal(barrier, inc=1, device_id=here.plane(*peer), device_id_type=MESH)
    for step in tensor_peers:
        pl.semaphore_signal(barrier, inc=1, device_id=here.along(step), device_id_type=MESH)
    pl.semaphore_wait(barrier, len(plane_peers) + len(tensor_peers))


def push(src, dst, send, recv, device):
    copy = pltpu.make_async_remote_copy(
        src_ref=src, dst_ref=dst, send_sem=send, recv_sem=recv, device_id=device, device_id_type=MESH
    )
    copy.start()
    return copy


def block(index, size):
    return pl.ds(pl.multiple_of(index * size, size), size)


def rows_chunk(ref, k):
    return ref.at[:, block(k, CHUNK), :]


def rows_part(ref, k, part):
    return ref.at[:, pl.ds(pl.multiple_of(k * CHUNK + part * HALF, HALF), HALF), :]


def cols_chunk(ref, k):
    return ref.at[:, :, block(k, CHUNK)]


def cols_part(ref, k, part):
    return ref.at[:, part * HALF : part * HALF + HALF, block(k, CHUNK)]


class Gather:
    def __init__(self, here, by_rows, shard, whole, first, relay, local):
        self.here, self.by_rows, self.shard, self.whole = here, by_rows, shard, whole
        self.first, self.relay, self.local = first, relay, local
        self.copies = []

    def half(self, core):
        if self.by_rows:
            return self.shard.at[:, :, block(core, CHUNK)]
        return self.shard.at[:, block(core, CHUNK), :]

    def chunk(self, k):
        return rows_chunk(self.whole, k) if self.by_rows else cols_chunk(self.whole, k)

    def part(self, k, part):
        return rows_part(self.whole, k, part) if self.by_rows else cols_part(self.whole, k, part)

    def start(self):
        here = self.here
        mine = self.chunk(here.chunk(0, 0, 0))
        for index, side in enumerate(SIDES + [PARTNER]):
            core = 1 - here.c if side[1] else here.c
            self.copies.append(
                push(
                    self.half(core),
                    mine,
                    self.first.at[0, index],
                    self.first.at[1, index],
                    here.plane(*side),
                )
            )
        self.own = pltpu.make_async_copy(self.half(here.c), mine, self.local)
        self.own.start()

    def forward(self):
        here = self.here
        self.onward = []
        for index in range(4):
            side = SIDES[index]
            self.copies[index].wait_recv()
            part = 0 if side[0] else 1
            where = self.part(here.chunk(*side), part)
            target = (0, 0, 1) if side[0] else (1, 0, 0)
            self.onward.append(
                push(
                    where,
                    where,
                    self.relay.at[0, index],
                    self.relay.at[1, index],
                    here.plane(*target),
                )
            )

    def finish(self):
        for index in range(4):
            self.copies[index].wait_send()
        self.copies[4].wait()
        self.own.wait()
        for copy in self.onward:
            copy.wait()


def gather_sems():
    return [
        pltpu.SemaphoreType.DMA((2, 5)),
        pltpu.SemaphoreType.DMA((2, 4)),
        pltpu.SemaphoreType.DMA,
    ]


class Scatter:
    def __init__(self, here, by_rows, grad, total, bufs):
        self.here, self.by_rows, self.grad, self.total = here, by_rows, grad, total
        self.got, self.got_two = bufs[:2]
        self.one_sem, self.two_sem, self.last_sem, self.local = bufs[2:6]
        self.final = bufs[6]

    def part(self, dx, dy, core, side):
        k = self.here.chunk_of(dx, dy, core)
        return rows_part(self.grad, k, side) if self.by_rows else cols_part(self.grad, k, side)

    def start(self):
        here = self.here
        self.first = []
        for side in (0, 1):
            near, far = ((1, 0), (1, 1)) if side == 0 else ((0, 1), (1, 1))
            target = here.plane(1, 0, 0) if side == 0 else here.plane(0, 0, 1)
            for slot in range(4):
                chip = far if slot >= 2 else near
                index = side * 4 + slot
                self.first.append(
                    push(
                        self.part(chip[0], chip[1], slot % 2, side),
                        self.got.at[index],
                        self.one_sem.at[0, index],
                        self.one_sem.at[1, index],
                        target,
                    )
                )

    def middle(self):
        here = self.here
        self.second = []
        for side in (0, 1):
            target = here.plane(0, 0, 1) if side == 0 else here.plane(1, 0, 0)
            chip = (0, 1) if side == 0 else (1, 0)
            for slot in (2, 3):
                index = side * 4 + slot
                two = side * 2 + slot - 2
                mine = self.part(chip[0], chip[1], slot - 2, side)
                self.first[index].wait_recv()
                got = self.got.at[index]

                def step(i, carry):
                    spot = (i // 4, block(lax.rem(i, 4), 32), slice(None))
                    mine[spot] = (mine[spot].astype(F32) + got[spot].astype(F32)).astype(BF16)
                    return carry

                lax.fori_loop(0, got.shape[0] * 4, step, 0)
                self.second.append(
                    push(
                        mine,
                        self.got_two.at[two],
                        self.two_sem.at[0, two],
                        self.two_sem.at[1, two],
                        target,
                    )
                )

    def last(self):
        here = self.here
        for side in (0, 1):
            for slot in (0, 1):
                index = side * 4 + slot
                two = side * 2 + slot
                self.first[index].wait_recv()
                self.second[two].wait_recv()
                mine, got, got_two = self.part(0, 0, slot, side), self.got.at[index], self.got_two.at[two]
                final = self.final.at[slot, :, side * HALF : side * HALF + HALF, :]

                def step(i, carry):
                    spot = (i // 4, block(lax.rem(i, 4), 32), slice(None))
                    final[spot] = (mine[spot].astype(F32) + got[spot].astype(F32)) + got_two[
                        spot
                    ].astype(F32)
                    return carry

                lax.fori_loop(0, got.shape[0] * 4, step, 0)
        if self.by_rows:
            where = self.total.at[:, :, block(here.c, CHUNK)]
        else:
            where = self.total.at[:, block(here.c, CHUNK), :]
        self.keep = pltpu.make_async_copy(self.final.at[here.c], where, self.local)
        self.keep.start()
        self.give = push(
            self.final.at[1 - here.c],
            where,
            self.last_sem.at[0],
            self.last_sem.at[1],
            here.plane(*PARTNER),
        )

    def sent(self):
        self.keep.wait()
        self.give.wait_send()

    def finish(self):
        for copy in self.first:
            copy.wait_send()
        for copy in self.second:
            copy.wait_send()
        self.give.wait_recv()


def scatter_scratch(width):
    return [
        pltpu.VMEM((8, width, HALF, CHUNK), BF16),
        pltpu.VMEM((4, width, HALF, CHUNK), BF16),
        pltpu.SemaphoreType.DMA((2, 8)),
        pltpu.SemaphoreType.DMA((2, 4)),
        pltpu.SemaphoreType.DMA((2,)),
        pltpu.SemaphoreType.DMA,
    ]


SCATTER = 6


class TensorSum:
    def __init__(self, here, part, bufs):
        self.here, self.part = here, part
        self.pair, self.out, self.inn, self.pair_sem, self.sem = bufs

    def start(self):
        here = self.here
        self.swap = push(
            self.part.at[1 - here.c],
            self.pair,
            self.pair_sem.at[0],
            self.pair_sem.at[1],
            here.plane(*PARTNER),
        )

    def spread(self):
        here = self.here
        self.swap.wait_recv()
        self.sent = []
        for step in (2, 1, 3):
            rows = block(lax.rem(here.z + step, 4), ROWS)
            self.out[step - 1] = (
                self.part[here.c, rows, :].astype(F32) + self.pair[rows, :].astype(F32)
            ).astype(self.out.dtype)
            self.sent.append(
                push(
                    self.out.at[step - 1],
                    self.inn.at[step - 1],
                    self.sem.at[0, step - 1],
                    self.sem.at[1, step - 1],
                    here.along(step),
                )
            )

    def result(self):
        here = self.here
        rows = block(here.z, ROWS)
        total = self.part[here.c, rows, :].astype(F32) + self.pair[rows, :].astype(F32)
        for copy in self.sent:
            copy.wait_recv()
        for step in (1, 2, 3):
            total = total + self.inn[step - 1].astype(F32)
        return total

    def finish(self):
        self.swap.wait_send()
        for copy in self.sent:
            copy.wait_send()


def sum_scratch(length, width):
    return [
        pltpu.VMEM((length, width), BF16),
        pltpu.VMEM((3, ROWS, width), BF16),
        pltpu.VMEM((3, ROWS, width), BF16),
        pltpu.SemaphoreType.DMA((2,)),
        pltpu.SemaphoreType.DMA((2, 3)),
    ]


class TensorGather:
    def __init__(self, here, mine, whole, sem, pair_sem, local):
        self.here, self.mine, self.whole = here, mine, whole
        self.sem, self.pair_sem, self.local = sem, pair_sem, local

    def start(self):
        here = self.here
        place = self.whole.at[here.c, block(here.z, ROWS), :]
        self.sent = []
        for step in (2, 1, 3):
            self.sent.append(
                push(
                    self.mine,
                    place,
                    self.sem.at[0, step - 1],
                    self.sem.at[1, step - 1],
                    here.along(step),
                )
            )
        self.shared = [
            push(
                self.mine,
                place,
                self.pair_sem.at[0, 0],
                self.pair_sem.at[1, 0],
                here.plane(*PARTNER),
            )
        ]
        self.own = pltpu.make_async_copy(self.mine, place, self.local)
        self.own.start()

    def forward(self):
        here = self.here
        for index, step in enumerate((2, 1, 3)):
            self.sent[index].wait_recv()
            place = self.whole.at[here.c, block(here.behind(step), ROWS), :]
            self.shared.append(
                push(
                    place,
                    place,
                    self.pair_sem.at[0, step],
                    self.pair_sem.at[1, step],
                    here.plane(*PARTNER),
                )
            )

    def finish(self):
        for copy in self.sent:
            copy.wait_send()
        for copy in self.shared:
            copy.wait()
        self.own.wait()


class LineSum:
    def __init__(self, here, part, bufs):
        self.here, self.part = here, part
        self.pair, self.slot, self.pair_sem, self.sem = bufs

    def start(self):
        here = self.here
        self.swap = push(
            self.part.at[1 - here.c],
            self.pair,
            self.pair_sem.at[0],
            self.pair_sem.at[1],
            here.plane(*PARTNER),
        )

    def own(self, z):
        rows = block(z, ROWS)
        return self.part[self.here.c, rows, :].astype(F32) + self.pair[rows, :].astype(F32)

    def depth(self, way):
        return self.here.z if way == 0 else 3 - self.here.z

    def hop(self, way, k, src):
        here = self.here
        return pltpu.make_async_remote_copy(
            src_ref=src,
            dst_ref=self.slot.at[way, k],
            send_sem=self.sem.at[0, way, k],
            recv_sem=self.sem.at[1, way, k],
            device_id=(here.x * 2 + here.c, here.y, here.z + (1 if way == 0 else -1)),
            device_id_type=MESH,
        )

    def take(self, way, k):
        here = self.here
        pltpu.make_async_remote_copy(
            src_ref=self.slot.at[way, k],
            dst_ref=self.slot.at[way, k],
            send_sem=self.sem.at[0, way, k],
            recv_sem=self.sem.at[1, way, k],
            device_id=(here.x * 2 + here.c, here.y, here.z - (1 if way == 0 else -1)),
            device_id_type=MESH,
        ).wait_recv()

    def stage(self, k):
        here = self.here
        if k == 0:
            self.swap.wait_recv()
        for way in (0, 1):
            depth = self.depth(way)
            shard = here.z + 3 - k if way == 0 else here.z - 3 + k

            @pl.when(depth == 0)
            def _():
                self.slot[way, k] = self.own(shard).astype(BF16)
                self.hop(way, k, self.slot.at[way, k]).start()

            if k > 0:

                @pl.when((depth >= 1) & (depth <= k))
                def _():
                    self.take(way, k - 1)
                    self.slot[way, k - 1] = (
                        self.own(shard) + self.slot[way, k - 1].astype(F32)
                    ).astype(BF16)
                    self.hop(way, k, self.slot.at[way, k - 1]).start()

    def result(self):
        total = self.own(self.here.z)
        for way in (0, 1):
            depth = self.depth(way)

            @pl.when(depth >= 1)
            def _():
                self.take(way, 2)

            total = total + jnp.where(depth >= 1, self.slot[way, 2].astype(F32), 0.0)
        return total

    def finish(self):
        self.swap.wait_send()
        for way in (0, 1):
            for k in range(3):

                @pl.when(self.depth(way) <= k)
                def _():
                    self.hop(way, k, self.slot.at[way, k]).wait_send()


def line_scratch(length, width):
    return [
        pltpu.VMEM((length, width), BF16),
        pltpu.VMEM((2, 3, ROWS, width), BF16),
        pltpu.SemaphoreType.DMA((2,)),
        pltpu.SemaphoreType.DMA((2, 2, 3)),
    ]


class LineGather:
    def __init__(self, here, place, sem):
        self.here, self.place, self.sem = here, place, sem

    def hop(self, way, k):
        here = self.here
        step = 1 if way == 0 else -1
        spot = self.place(here.z - k * step)
        return pltpu.make_async_remote_copy(
            src_ref=spot,
            dst_ref=spot,
            send_sem=self.sem.at[0, way, k],
            recv_sem=self.sem.at[1, way, k],
            device_id=(here.x * 2 + here.c, here.y, here.z + step),
            device_id_type=MESH,
        )

    def arrival(self, way, k):
        here = self.here
        step = 1 if way == 0 else -1
        spot = self.place(here.z - (k + 1) * step)
        return pltpu.make_async_remote_copy(
            src_ref=spot,
            dst_ref=spot,
            send_sem=self.sem.at[0, way, k],
            recv_sem=self.sem.at[1, way, k],
            device_id=(here.x * 2 + here.c, here.y, here.z - step),
            device_id_type=MESH,
        )

    def sends(self, way, k):
        z = self.here.z
        return (z >= k) & (z < 3) if way == 0 else (z <= 3 - k) & (z > 0)

    def gets(self, way, k):
        z = self.here.z
        return z >= k + 1 if way == 0 else z <= 2 - k

    def start(self):
        for way in (0, 1):

            @pl.when(self.sends(way, 0))
            def _():
                self.hop(way, 0).start()

    def onward(self, k, then=None):
        for way in (0, 1):

            @pl.when(self.gets(way, k))
            def _():
                self.arrival(way, k).wait_recv()
                if then is not None:
                    then(self.here.z - (k + 1) * (1 if way == 0 else -1))

            if k < 2:

                @pl.when(self.sends(way, k + 1))
                def _():
                    self.hop(way, k + 1).start()

    def finish(self):
        for way in (0, 1):
            for k in range(3):

                @pl.when(self.sends(way, k))
                def _():
                    self.hop(way, k).wait_send()


def normed(values):
    center = values - jnp.mean(values, -1, keepdims=True)
    variance = jnp.mean(center * center, -1, keepdims=True)
    inv_std = lax.rsqrt(variance + NORM_EPS)
    return (center * inv_std, inv_std)


def norm_row(packs, row):
    return jnp.concatenate([packs[k, row : row + 1, :] for k in range(8)], 1)


def params(ident, limit=60):
    return pltpu.CompilerParams(
        collective_id=ident, has_side_effects=True, vmem_limit_bytes=limit << 20
    )


def cast_rows(raw, shard):
    count, rows, _ = raw.shape
    for j in range(count):

        def step(i, carry):
            at = pl.ds(pl.multiple_of(i * 32, 32), 32)
            shard[j, at, :] = raw[j, at, :].astype(BF16)
            return carry

        lax.fori_loop(0, rows // 32, step, 0)


def front_kernel(*refs):
    head_count, position, bucket, tok, cot, norm_master = refs[:6]
    masters = refs[6:10]
    n1, both_cot, tables, packs, n2, mid, q_out, k_out, v_out, a_out = refs[10:20]
    wholes = refs[20:24]
    raws, shards = refs[24:28], refs[28:32]
    raw_sem, n2_own, part, small, pair, local = refs[32:38]
    sums, tensor_sems, gather_refs = refs[38:43], refs[43:46], refs[46:58]
    here = Here()
    loads = []
    for i in range(4):
        loads.append(pltpu.make_async_copy(masters[i], raws[i], raw_sem.at[i]))
        loads[i].start()
    me = here.chunk(0, 0, 0)
    lane = lax.broadcasted_iota(jnp.int32, (1, CHUNK), 1)
    counts = jnp.zeros((1, CHUNK), F32)
    for c in range(4):
        count = jnp.sum((bucket[...] == c).astype(F32), 1, keepdims=True)
        counts = counts + jnp.where(lane == c, count, 0.0)
    packs[pl.ds(me, 1)] = jnp.concatenate(
        [norm_master[...].astype(BF16).astype(F32), counts, jnp.zeros((3, CHUNK), F32)], 0
    )[None]
    gathers = [
        Gather(here, i in (0, 2), shards[i], wholes[i], *gather_refs[i * 3 : i * 3 + 3])
        for i in range(4)
    ]
    loads[0].wait()
    cast_rows(raws[0], shards[0])
    greet(here, PLANE, (1, 2, 3))
    gathers[0].start()
    packed = []
    for index, peer in enumerate(PLANE):
        packed.append(
            push(
                packs.at[me], packs.at[me],
                small.at[0, index], small.at[1, index], here.plane(*peer),
            )
        )
    partner = here.plane(*PARTNER)
    table = tables.at[here.c]
    fill_table(table, position[...], bucket[...], head_count[0])
    shared = [
        push(table, table, pair.at[0, 0], pair.at[1, 0], partner),
        push(cot, both_cot.at[here.c], pair.at[0, 1], pair.at[1, 1], partner),
    ]
    keep = pltpu.make_async_copy(cot, both_cot.at[here.c], local)
    keep.start()
    for i in range(1, 4):
        loads[i].wait()
        cast_rows(raws[i], shards[i])
    for copy in packed:
        copy.wait()
    gain, shift = norm_row(packs, 0), norm_row(packs, 1)
    mine = n1.at[here.c]

    def rows_step(i, carry):
        rows = block(i, 32)
        hat, _ = normed(tok[rows, :].astype(F32))
        mine[rows, :] = (hat * gain + shift).astype(BF16)
        return carry

    lax.fori_loop(0, tok.shape[0] // 32, rows_step, 0)
    shared.append(push(mine, mine, pair.at[0, 2], pair.at[1, 2], partner))
    gathers[1].start()
    gathers[0].forward()
    gathers[1].forward()
    gathers[0].finish()
    gathers[2].start()
    gathers[3].start()
    shared[0].wait_recv()
    shared[2].wait_recv()
    head0 = here.z * 4 + here.c * 2
    attend_body(head0, n1, wholes[0], wholes[1], tables, q_out, k_out, v_out, a_out, part)
    gathers[1].finish()
    total = TensorSum(here, part, sums)
    attend_out(a_out, wholes[1], part, 1 - here.c)
    total.start()
    attend_out(a_out, wholes[1], part, here.c)
    total.spread()
    rows = block(here.z, ROWS)
    middle = tok[rows, :].astype(F32) + total.result()
    mid[...] = middle
    hat, _ = normed(middle)
    n2_own[...] = (hat * norm_row(packs, 2) + norm_row(packs, 3)).astype(BF16)
    gather = TensorGather(here, n2_own, n2, *tensor_sems)
    gather.start()
    gathers[2].forward()
    gathers[3].forward()
    gather.forward()
    total.finish()
    gather.finish()
    gathers[2].finish()
    gathers[3].finish()
    keep.wait()
    shared[0].wait_send()
    shared[1].wait()
    shared[2].wait_send()


def front_call(head_count, position, bucket, tok, cot, norm_master, masters):
    length, width = tok.shape
    both = jax.ShapeDtypeStruct((2, length, width), BF16)
    thin = jax.ShapeDtypeStruct((2 * length, CHUNK), BF16)
    wholes = [
        jax.ShapeDtypeStruct((3, width, CHUNK), BF16),
        jax.ShapeDtypeStruct((1, CHUNK, width), BF16),
        jax.ShapeDtypeStruct((4, width, CHUNK), BF16),
        jax.ShapeDtypeStruct((4, CHUNK, width), BF16),
    ]
    results = pl.pallas_call(
        front_kernel,
        out_shape=[
            both,
            both,
            jax.ShapeDtypeStruct((2, 5, length, HALF), F32),
            jax.ShapeDtypeStruct((8, 8, CHUNK), F32),
            both,
            jax.ShapeDtypeStruct((ROWS, width), F32),
            thin, thin, thin, thin,
        ]
        + wholes,
        in_specs=[SM, VM, VM, VM, VM, VM] + [ANY] * 4,
        out_specs=[VM, ANY, VM, VM, ANY, VM, VM, VM, VM, VM, VM, VM, ANY, ANY],
        scratch_shapes=[pltpu.VMEM(master.shape, F32) for master in masters]
        + [pltpu.VMEM(master.shape, BF16) for master in masters]
        + [
            pltpu.SemaphoreType.DMA((4,)),
            pltpu.VMEM((ROWS, width), BF16),
            pltpu.VMEM((2, length, width), BF16),
            pltpu.SemaphoreType.DMA((2, 7)),
            pltpu.SemaphoreType.DMA((2, 3)),
            pltpu.SemaphoreType.DMA,
        ]
        + sum_scratch(length, width)
        + tensor_gather_sems()
        + gather_sems() * 4,
        compiler_params=params(1),
        name="front",
    )(head_count, position, bucket, tok, cot, norm_master, *masters)
    return results[:10], results[10:]


def tensor_gather_sems():
    return [
        pltpu.SemaphoreType.DMA((2, 3)),
        pltpu.SemaphoreType.DMA((2, 4)),
        pltpu.SemaphoreType.DMA,
    ]


def norm_back(grad_out, hat, inv_std, gain):
    scaled = grad_out * gain
    inner = (
        scaled
        - jnp.mean(scaled, -1, keepdims=True)
        - hat * jnp.mean(scaled * hat, -1, keepdims=True)
    )
    return (
        inner * inv_std,
        jnp.sum(grad_out * hat, 0, keepdims=True),
        jnp.sum(grad_out, 0, keepdims=True),
    )


def ffn_hidden(r, n2, cot, bucket, wu, wd, squares, grad_hidden):
    width = n2.shape[2]
    hidden = dot(n2[...].reshape(-1, width), wu[r])
    live = bucket >= jnp.float32(r)
    rectified = jnp.maximum(jnp.where(live, hidden, 0.0), 0.0)
    squares[r] = (rectified * rectified).astype(BF16)
    grad_square = dot(cot[...].reshape(-1, width), wd[r], ((1,), (1,)))
    grad_hidden[r] = (grad_square * 2.0 * rectified).astype(BF16)


def ffn_rows(s, left, right, part, transposed):
    length, width = part.shape[1:]
    rows = pl.ds(pl.multiple_of(s * length, length), length)
    for n in range(width // (2 * CHUNK)):
        cols = slice(n * 2 * CHUNK, (n + 1) * 2 * CHUNK)
        total = None
        for r in range(4):
            if transposed:
                term = dot(left[r, rows, :], right[r, cols, :], ((1,), (1,)))
            else:
                term = dot(left[r, rows, :], right[r, :, cols])
            total = term if total is None else total + term
        part[s, :, cols] = total.astype(BF16)


def attend_back_body(head0, gm, qkva, wq, wo, tables, dp, part):
    length = tables.shape[2]
    width = gm.shape[2]
    q_rows, k_rows, v_rows = qkva.at[0], qkva.at[1], qkva.at[2]
    grad_att = dot(gm[...].reshape(2 * length, width), wo[...], ((1,), (1,))).astype(BF16)
    for s in range(2):
        rows = slice(s * length, (s + 1) * length)
        cosine, sine = tables[s, 0], tables[s, 1]
        lowest = tables[s, 2, :, 0:1]
        for h in range(2):
            cols = slice(h * HEAD_DIM, (h + 1) * HEAD_DIM)
            active = tables[s, 4] > (head0 + h).astype(F32)
            grad_heads = jnp.where(active, grad_att[rows, cols].astype(F32), 0.0).astype(BF16)
            queries, key_rows, value_rows = q_rows[rows, cols], k_rows[rows, cols], v_rows[rows, cols]
            weights = attention_weights(queries, key_rows, lowest)
            grad_weights = dot(grad_heads, value_rows, ((1,), (1,)))
            inner = jnp.sum(weights * grad_weights, -1, keepdims=True)
            grad_scores = (weights * (grad_weights - inner)).astype(BF16)
            grad_query = dot(grad_scores, key_rows) * HEAD_DIM ** (-0.5)
            grad_keys = dot(grad_scores, queries, ((0,), (0,)))
            grad_values = dot(weights.astype(BF16), grad_heads, ((0,), (0,)))
            dp[0, rows, cols] = turn(grad_query, cosine, -sine).astype(BF16)
            dp[1, rows, cols] = turn(grad_keys, cosine, -sine).astype(BF16)
            dp[2, rows, cols] = grad_values.astype(BF16)


def attend_back_rows(s, dp, wq, part):
    length = part.shape[1]
    rows = pl.ds(pl.multiple_of(s * length, length), length)
    total = dot(dp[0, rows, :], wq[0], ((1,), (1,)))
    total = total + dot(dp[1, rows, :], wq[1], ((1,), (1,)))
    total = total + dot(dp[2, rows, :], wq[2], ((1,), (1,)))
    part[s] = total.astype(BF16)


def norm_share(here, values, bufs):
    slices, heard, plane_sum, heard_z, ns, nz = bufs
    for k in range(8):
        slices[k, 0:4, :] = values[:, k * CHUNK : (k + 1) * CHUNK]
        slices[k, 4:8, :] = jnp.zeros((4, CHUNK), F32)
    copies = []
    for index, peer in enumerate(PLANE):
        copies.append(
            push(
                slices.at[here.chunk(*peer)],
                heard.at[index],
                ns.at[0, index],
                ns.at[1, index],
                here.plane(*peer),
            )
        )
    return copies


def norm_share_along(here, copies, bufs):
    slices, heard, plane_sum, heard_z, ns, nz = bufs
    mine = slices[here.chunk(0, 0, 0)]
    for index in range(7):
        copies[index].wait()
        mine = mine + heard[index]
    plane_sum[...] = mine
    onward = []
    for step in (1, 2, 3):
        onward.append(
            push(
                plane_sum,
                heard_z.at[here.z],
                nz.at[0, step - 1],
                nz.at[1, step - 1],
                here.along(step),
            )
        )
    heard_z[pl.ds(here.z, 1)] = mine[None]
    return onward


def back_kernel(*refs):
    n2, cot, tables, packs, mid = refs[0:5]
    tok, wq, wo, wu, wd, n1, q_rows, k_rows, v_rows, a_rows = refs[5:15]
    out_all, ig_own, norm_total, q_sum, o_sum, u_sum, d_sum = refs[15:22]
    wu_v, wd_v, qkva, tok_own, load_sem, squares, grad_hidden, part, part_f, dp = refs[22:32]
    gu, gd, gq, go, gm, dmid, sums, out_v = refs[32:40]
    back_bufs, branch_bufs, final_one, final_two = refs[40:44], refs[44:48], refs[48], refs[49]
    gm_sem, gm_pair, out_sem, keep_sem, norm_bufs = *refs[50:54], refs[54:60]
    rest = refs[60:]
    here = Here()
    loads = []

    def load(src, dst):
        copy = pltpu.make_async_copy(src, dst, load_sem.at[len(loads)])
        copy.start()
        loads.append(copy)
        return copy

    first = [(load(wu.at[r], wu_v.at[r]), load(wd.at[r], wd_v.at[r])) for r in range(4)]
    small = [load(src, qkva.at[i]) for i, src in enumerate((q_rows, k_rows, v_rows, a_rows))]
    place = block(here.z, ROWS)
    small.append(load(tok.at[place, :], tok_own))
    scatters = [
        Scatter(here, by_rows, grad, total, rest[i * SCATTER : (i + 1) * SCATTER] + (final,))
        for i, (by_rows, grad, total, final) in enumerate(
            (
                (True, gu.at[0:1], u_sum.at[0:1], final_one.at[:, 0:1]),
                (False, gd.at[0:1], d_sum.at[0:1], final_two.at[:, 0:1]),
                (True, gu.at[1:4], u_sum.at[1:4], final_one.at[:, 1:4]),
                (False, gd.at[1:4], d_sum.at[1:4], final_two.at[:, 1:4]),
                (True, gq, q_sum, final_one.at[:, 0:3]),
                (False, go, o_sum, final_one.at[:, 3:4]),
            )
        )
    ]
    early_u, early_d, scatter_u, scatter_d, scatter_q, scatter_o = scatters
    length, width = n2.shape[1:]

    def up_gradient(r):
        rows_in = n2[...].reshape(2 * length, width)
        gu[r] = dot(rows_in, grad_hidden[r], ((0,), (0,))).astype(BF16)

    def down_gradient(r):
        grads_in = cot[...].reshape(2 * length, width)
        gd[r] = dot(squares[r], grads_in, ((0,), (0,))).astype(BF16)

    bucket = jnp.concatenate([tables[0, 3, :, 0:1], tables[1, 3, :, 0:1]], 0)
    for r in range(4):
        first[r][0].wait()
        first[r][1].wait()
        ffn_hidden(r, n2, cot, bucket, wu_v, wd_v, squares, grad_hidden)
        if r == 0:
            up_gradient(0)
            greet(here, PLANE, (1, 2, 3))
            early_u.start()
            down_gradient(0)
            early_d.start()
    other = 1 - here.c
    back = LineSum(here, part, back_bufs)
    ffn_rows(other, grad_hidden, wu_v, part, True)
    back.start()
    ffn_rows(here.c, grad_hidden, wu_v, part, True)
    back.stage(0)
    load_q = load(wq, wu_v.at[0:3])
    for r in range(1, 4):
        up_gradient(r)
    scatter_u.start()
    down_gradient(1)
    back.stage(1)
    down_gradient(2)
    down_gradient(3)
    scatter_d.start()
    branch = LineSum(here, part_f, branch_bufs)
    ffn_rows(other, squares, wd_v, part_f, False)
    branch.start()
    back.stage(2)
    ffn_rows(here.c, squares, wd_v, part_f, False)
    load_n1 = load(n1, wd_v.at[0:2])
    load_o = load(wo, wd_v.at[2:3])
    grad_n2 = back.result().astype(BF16).astype(F32)
    back.finish()
    hat, inv_std = normed(mid[...])
    grad_mid, gain_sum, shift_sum = norm_back(grad_n2, hat, inv_std, norm_row(packs, 2))
    grad_mid = cot[here.c, place, :].astype(F32) + grad_mid
    dmid[...] = grad_mid
    gm[pl.ds(here.c, 1), place, :] = grad_mid.astype(BF16)[None]
    gather = LineGather(here, lambda z: gm.at[here.c, block(z, ROWS), :], gm_sem)
    gather.start()
    early_u.middle()
    early_d.middle()

    def shared(z):
        spot = gm.at[here.c, block(z, ROWS), :]
        return pltpu.make_async_remote_copy(
            src_ref=spot,
            dst_ref=spot,
            send_sem=gm_pair.at[0, z],
            recv_sem=gm_pair.at[1, z],
            device_id=here.plane(*PARTNER),
            device_id_type=MESH,
        )

    shared(here.z).start()
    sums[0:1, :] = gain_sum
    sums[1:2, :] = shift_sum
    gather.onward(0, lambda z: shared(z).start())
    branch.stage(0)
    gather.onward(1, lambda z: shared(z).start())
    gather.onward(2, lambda z: shared(z).start())
    branch.stage(1)
    scatter_u.middle()
    for copy in small:
        copy.wait()
    load_o.wait()
    load_q.wait()
    load_n1.wait()
    gather.finish()
    for z in range(4):
        shared(z).wait()
    head0 = here.z * 4 + here.c * 2
    attend_back_body(head0, gm, qkva, wu_v, wd_v.at[2], tables, dp, part)
    branch.stage(2)
    last = LineSum(here, part, back_bufs)
    attend_back_rows(other, dp, wu_v, part)
    last.start()
    attend_back_rows(here.c, dp, wu_v, part)
    last.stage(0)
    scatter_d.middle()
    rows_in = wd_v[0:2].reshape(2 * length, width)
    for j in range(3):
        gq[j] = dot(rows_in, dp[j], ((0,), (0,))).astype(BF16)
    scatter_q.start()
    last.stage(1)
    go[0] = dot(qkva[3], gm[...].reshape(2 * length, width), ((0,), (0,))).astype(BF16)
    scatter_o.start()
    early_u.last()
    early_d.last()
    last.stage(2)
    out_v[place, :] = (mid[...] + branch.result().astype(BF16).astype(F32)).astype(BF16)
    spread = LineGather(here, lambda z: out_v.at[block(z, ROWS), :], out_sem)
    spread.start()
    scatter_u.last()
    spread.onward(0)
    grad_n1 = last.result()
    hat, inv_std = normed(tok_own[...].astype(F32))
    grad_in, gain_sum, shift_sum = norm_back(grad_n1, hat, inv_std, norm_row(packs, 0))
    ig_own[...] = (dmid[...] + grad_in).astype(BF16)
    norm_copies = norm_share(
        here, jnp.concatenate([gain_sum, shift_sum, sums[...]], 0), norm_bufs
    )
    scatter_q.middle()
    scatter_o.middle()
    spread.onward(1)
    spread.onward(2)
    keep = pltpu.make_async_copy(out_v, out_all, keep_sem)
    keep.start()
    onward = norm_share_along(here, norm_copies, norm_bufs)
    scatter_d.last()
    for copy in onward:
        copy.wait()
    heard_z = norm_bufs[3]
    norm_total[...] = ((heard_z[0] + heard_z[1]) + heard_z[2]) + heard_z[3]
    early_u.sent()
    scatter_u.sent()
    scatter_q.last()
    scatter_o.last()
    branch.finish()
    last.finish()
    spread.finish()
    keep.wait()
    for scatter in (early_d, scatter_d, scatter_q, scatter_o):
        scatter.sent()
    for scatter in scatters:
        scatter.finish()


def back_call(n2, cot, tables, packs, mid, tok, wq, wo, wu, wd, n1, rows):
    _, length, width = n2.shape
    both = pltpu.VMEM((2, length, width), BF16)
    results = pl.pallas_call(
        back_kernel,
        out_shape=[
            jax.ShapeDtypeStruct((length, width), BF16),
            jax.ShapeDtypeStruct((ROWS, width), BF16),
            jax.ShapeDtypeStruct((8, CHUNK), F32),
            jax.ShapeDtypeStruct((3, CHUNK, 2 * CHUNK), F32),
            jax.ShapeDtypeStruct((1, 2 * CHUNK, CHUNK), F32),
            jax.ShapeDtypeStruct((4, CHUNK, 2 * CHUNK), F32),
            jax.ShapeDtypeStruct((4, 2 * CHUNK, CHUNK), F32),
        ],
        in_specs=[VM] * 5 + [ANY] * 10,
        out_specs=[ANY, VM, VM, ANY, ANY, ANY, ANY],
        scratch_shapes=[
            pltpu.VMEM(wu.shape, BF16),
            pltpu.VMEM(wd.shape, BF16),
            pltpu.VMEM((4, 2 * length, CHUNK), BF16),
            pltpu.VMEM((ROWS, width), BF16),
            pltpu.SemaphoreType.DMA((16,)),
            pltpu.VMEM((4, 2 * length, CHUNK), BF16),
            pltpu.VMEM((4, 2 * length, CHUNK), BF16),
            both,
            both,
            pltpu.VMEM((3, 2 * length, CHUNK), BF16),
            pltpu.VMEM(wu.shape, BF16),
            pltpu.VMEM(wd.shape, BF16),
            pltpu.VMEM(wq.shape, BF16),
            pltpu.VMEM(wo.shape, BF16),
            both,
            pltpu.VMEM((ROWS, width), F32),
            pltpu.VMEM((2, width), F32),
            pltpu.VMEM((length, width), BF16),
        ]
        + line_scratch(length, width) * 2
        + [pltpu.VMEM((2, 4, CHUNK, CHUNK), F32)] * 2
        + [
            pltpu.SemaphoreType.DMA((2, 2, 3)),
            pltpu.SemaphoreType.DMA((2, 4)),
            pltpu.SemaphoreType.DMA((2, 2, 3)),
            pltpu.SemaphoreType.DMA,
            pltpu.VMEM((8, 8, CHUNK), F32),
            pltpu.VMEM((7, 8, CHUNK), F32),
            pltpu.VMEM((8, CHUNK), F32),
            pltpu.VMEM((4, 8, CHUNK), F32),
            pltpu.SemaphoreType.DMA((2, 7)),
            pltpu.SemaphoreType.DMA((2, 3)),
        ]
        + (scatter_scratch(1) * 2 + scatter_scratch(3) * 2)
        + scatter_scratch(3)
        + scatter_scratch(1),
        compiler_params=params(3),
        name="back",
    )(n2, cot, tables, packs, mid, tok, wq, wo, wu, wd, n1, *rows)
    return results


FIRST_SCALE = 1.0 / (1.0 - BETA_FIRST**STEP)
SECOND_SCALE = 1.0 / (1.0 - BETA_SECOND**STEP)


def folded(values):
    rows, cols = values.shape
    total = None
    for i in range(rows // 8):
        for j in range(cols // 128):
            tile = values[i * 8 : i * 8 + 8, j * 128 : j * 128 + 128]
            total = tile if total is None else total + tile
    return total


def updated(weight, gradient, first_old, second_old):
    first_new = BETA_FIRST * first_old + (1.0 - BETA_FIRST) * gradient
    second_new = BETA_SECOND * second_old + (1.0 - BETA_SECOND) * gradient * gradient
    update = first_new * FIRST_SCALE / (
        jnp.sqrt(second_new * SECOND_SCALE) + ADAM_EPS
    ) + WEIGHT_DECAY * weight
    return (update, first_new, second_new)


AHEAD = 4


def adam_kernel(*refs):
    sources = [refs[kind * 5 : kind * 5 + 4] for kind in range(4)]
    norm_grad, norm_master, norm_first, norm_second = [refs[kind * 5 + 4] for kind in range(4)]
    out_all = refs[20]
    outs = [refs[21 + kind * 5 : 25 + kind * 5] for kind in range(3)]
    norm_outs = [refs[25 + kind * 5] for kind in range(3)]
    tile, output = refs[36:38]
    held = [refs[38 + kind * 4 : 42 + kind * 4] for kind in range(4)]
    load_sem, store_sem = refs[54:56]
    blocks = [(i, j) for i in range(4) for j in range(sources[0][i].shape[0])]
    bases = [sum(source.shape[0] for source in sources[0][:i]) for i in range(4)]

    def loading(kind, i, j):
        return pltpu.make_async_copy(
            sources[kind][i].at[j], held[kind][i].at[j], load_sem.at[kind, bases[i] + j]
        )

    def storing(kind, i, j):
        return pltpu.make_async_copy(
            held[(0, 2, 3)[kind]][i].at[j], outs[kind][i].at[j], store_sem.at[kind, bases[i] + j]
        )

    for i, j in blocks:
        for kind in range(4):
            loading(kind, i, j).start()
    output[...] = out_all[...].astype(F32)
    weight = norm_master[...]
    update, first_new, second_new = updated(
        weight, norm_grad[0:4, :], norm_first[...], norm_second[...]
    )
    for out, value in zip(norm_outs, (update, first_new, second_new)):
        out[...] = value
    for row, value in ((4, weight), (12, update)):
        square = value * value * 0.25
        tile[row : row + 4, :] = square[:, :128] + square[:, 128:]
    for i in range(4):
        grads, masters, firsts, seconds = [held[kind][i] for kind in range(4)]

        def one_block(j, sums):
            for kind in range(4):
                loading(kind, i, j).wait()

            def step(k, carry):
                at = pl.ds(pl.multiple_of(k * 32, 32), 32)
                weight = masters[j, at, :]
                update, first_new, second_new = updated(
                    weight, grads[j, at, :], firsts[j, at, :], seconds[j, at, :]
                )
                grads[j, at, :] = update
                firsts[j, at, :] = first_new
                seconds[j, at, :] = second_new
                return (carry[0] + folded(weight * weight), carry[1] + folded(update * update))

            sums = lax.fori_loop(0, grads.shape[1] // 32, step, sums)
            for kind in range(3):
                storing(kind, i, j).start()
            return sums

        zero = jnp.zeros((8, 128), F32)
        sums = lax.fori_loop(0, grads.shape[0], one_block, (zero, zero))
        tile[i : i + 1, :] = jnp.sum(sums[0], 0, keepdims=True)
        tile[8 + i : 9 + i, :] = jnp.sum(sums[1], 0, keepdims=True)
    for i, j in blocks:
        for kind in range(3):
            storing(kind, i, j).wait()


def adam_call(grads, masters, firsts, seconds, out_all):
    shapes = [master.shape for master in masters]
    like = [jax.ShapeDtypeStruct(shape, F32) for shape in shapes]
    specs = [ANY] * 4 + [VM]
    count = sum(shape[0] for shape in shapes[:4])
    results = pl.pallas_call(
        adam_kernel,
        out_shape=like * 3
        + [jax.ShapeDtypeStruct((16, 128), F32), jax.ShapeDtypeStruct(out_all.shape, F32)],
        in_specs=specs * 4 + [VM],
        out_specs=specs * 3 + [VM, VM],
        scratch_shapes=[pltpu.VMEM(shape, F32) for shape in shapes[:4]] * 4
        + [pltpu.SemaphoreType.DMA((4, count)), pltpu.SemaphoreType.DMA((3, count))],
        compiler_params=local_params(60),
        name="adam",
    )(*grads, *masters, *firsts, *seconds, out_all)
    return results[0:5], results[5:10], results[10:15], results[15], results[16]


def total_kernel(tile, norms, tiles_z, plane_tile, tiles, zs, ps):
    here = Here()
    greet(here, PLANE, (1, 2, 3))
    sent = []
    for step in (2, 1, 3):
        sent.append(
            push(tile, tiles_z.at[here.z], zs.at[0, step - 1], zs.at[1, step - 1], here.along(step))
        )
    tiles_z[pl.ds(here.z, 1)] = tile[...][None]
    for copy in sent:
        copy.wait()
    plane_tile[...] = ((tiles_z[0] + tiles_z[1]) + tiles_z[2]) + tiles_z[3]
    me = here.chunk(0, 0, 0)
    sent = []
    for index, peer in enumerate(PLANE):
        sent.append(
            push(plane_tile, tiles.at[me], ps.at[0, index], ps.at[1, index], here.plane(*peer))
        )
    tiles[pl.ds(me, 1)] = plane_tile[...][None]
    for copy in sent:
        copy.wait()
    total = tiles[0]
    for k in range(1, 8):
        total = total + tiles[k]
    roots = jnp.sqrt(jnp.sum(total, 1, keepdims=True))
    norms[...] = jnp.broadcast_to(roots, norms.shape)


def total_call(tile):
    return pl.pallas_call(
        total_kernel,
        out_shape=jax.ShapeDtypeStruct((16, 128), F32),
        in_specs=[VM],
        out_specs=VM,
        scratch_shapes=[
            pltpu.VMEM((4, 16, 128), F32),
            pltpu.VMEM((16, 128), F32),
            pltpu.VMEM((8, 16, 128), F32),
            pltpu.SemaphoreType.DMA((2, 3)),
            pltpu.SemaphoreType.DMA((2, 7)),
        ],
        compiler_params=params(5),
        name="norm_totals",
    )(tile)


def weight_kernel(*refs):
    norms, updates, masters, packs = refs[0], refs[1:6], refs[6:11], refs[11]
    ig_rows = refs[12:16]
    outs = refs[16:21]
    igrad, lamb_norms, share = refs[21:24]
    held = (refs[24:28], refs[28:32])
    load_sem, store_sem = refs[32:34]
    blocks = [(i, j) for i in range(4) for j in range(updates[i].shape[0])]
    loads = []

    def load():
        index = len(loads)
        if index == len(blocks):
            return
        i, j = blocks[index]
        loads.append([])
        for kind, source in enumerate((updates, masters)):
            copy = pltpu.make_async_copy(
                source[i].at[j], held[kind][i].at[j], load_sem.at[kind, index]
            )
            copy.start()
            loads[index].append(copy)

    for _ in range(AHEAD):
        load()
    scales = LEARN_RATE * (norms[0:8, 0:1] / norms[8:16, 0:1])
    outs[4][...] = masters[4][...] - scales[4:8, :] * updates[4][...]
    row = lax.broadcasted_iota(jnp.int32, norms.shape, 0)
    lane = lax.broadcasted_iota(jnp.int32, norms.shape, 1)
    flat = jnp.sum(jnp.where(row == lane, norms[...], 0.0), 0, keepdims=True)
    lamb_norms[0:1, :] = flat[:, 0:8]
    lamb_norms[1:2, :] = flat[:, 8:16]
    counts = packs[0, 4:5, :]
    for k in range(1, 8):
        counts = counts + packs[k, 4:5, :]
    share[...] = counts[:, 0:4] / (igrad.shape[0] * 8)
    here = Here()
    for step in range(4):
        igrad[block(here.behind(step), ROWS), :] = ig_rows[step][...].astype(F32)
    stores = []
    for index, (i, j) in enumerate(blocks):
        for copy in loads[index]:
            copy.wait()
        load()
        scale = scales[i : i + 1, :]

        def step(k, carry):
            at = pl.ds(pl.multiple_of(k * 32, 32), 32)
            held[1][i][j, at, :] = held[1][i][j, at, :] - scale * held[0][i][j, at, :]
            return carry

        lax.fori_loop(0, held[1][i].shape[1] // 32, step, 0)
        copy = pltpu.make_async_copy(held[1][i].at[j], outs[i].at[j], store_sem.at[index])
        copy.start()
        stores.append(copy)
    for copy in stores:
        copy.wait()


def weight_call(norms, updates, masters, packs, ig_rows):
    shapes = [master.shape for master in masters]
    specs = [ANY] * 4 + [VM]
    count = sum(shape[0] for shape in shapes[:4])
    rows, width = ig_rows[0].shape
    return pl.pallas_call(
        weight_kernel,
        out_shape=[jax.ShapeDtypeStruct(shape, F32) for shape in shapes]
        + [
            jax.ShapeDtypeStruct((4 * rows, width), F32),
            jax.ShapeDtypeStruct((2, 8), F32),
            jax.ShapeDtypeStruct((1, 4), F32),
        ],
        in_specs=[VM] + specs * 2 + [VM] * 5,
        out_specs=specs + [VM, VM, VM],
        scratch_shapes=[pltpu.VMEM(shape, F32) for shape in shapes[:4]] * 2
        + [pltpu.SemaphoreType.DMA((2, count)), pltpu.SemaphoreType.DMA((count,))],
        compiler_params=local_params(60),
        name="new_weights",
    )(norms, *updates, *masters, packs, *ig_rows)


def turn(values, cosine, sine):
    return values * cosine + pltpu.roll(values, HEAD_DIM // 2, 1) * sine


def dot(left, right, dims=((1,), (0,))):
    return lax.dot_general(left, right, (dims, ((), ())), preferred_element_type=F32)


def attention_weights(queries, key_rows, lowest):
    scores = dot(queries, key_rows, ((1,), (1,)))
    row = lax.broadcasted_iota(jnp.int32, scores.shape, 0)
    col = lax.broadcasted_iota(jnp.int32, scores.shape, 1)
    allowed = (col <= row) & (col.astype(F32) >= lowest)
    scores = jnp.where(allowed, scores, MASKED)
    exp_scores = jnp.exp(scores - jnp.max(scores, -1, keepdims=True))
    return exp_scores / jnp.sum(exp_scores, -1, keepdims=True)


def attend_body(head0, n1, wq, wo, tables, q_out, k_out, v_out, a_out, part):
    length = tables.shape[2]
    rows_in = n1[...].reshape(2 * length, n1.shape[2])
    projected = [dot(rows_in, wq[j]) for j in range(3)]
    for s in range(2):
        rows = slice(s * length, (s + 1) * length)
        cosine, sine = tables[s, 0], tables[s, 1]
        lowest = tables[s, 2, :, 0:1]
        for h in range(2):
            cols = slice(h * HEAD_DIM, (h + 1) * HEAD_DIM)
            queries = (turn(projected[0][rows, cols], cosine, sine) * HEAD_DIM ** (-0.5)).astype(BF16)
            key_rows = turn(projected[1][rows, cols], cosine, sine).astype(BF16)
            value_rows = projected[2][rows, cols].astype(BF16)
            weights = attention_weights(queries, key_rows, lowest).astype(BF16)
            heads = dot(weights, value_rows)
            active = tables[s, 4] > (head0 + h).astype(F32)
            q_out[rows, cols] = queries
            k_out[rows, cols] = key_rows
            v_out[rows, cols] = value_rows
            a_out[rows, cols] = jnp.where(active, heads, 0.0).astype(BF16)


def attend_out(a_out, wo, part, s):
    length = part.shape[1]
    part[s] = dot(a_out[pl.ds(pl.multiple_of(s * length, length), length), :], wo[0]).astype(BF16)


def fill_table(table, position, bucket, head_count):
    length = table.shape[1]
    row = lax.broadcasted_iota(jnp.int32, (length, length), 0)
    col = lax.broadcasted_iota(jnp.int32, (length, length), 1)

    def column(values):
        return jnp.sum(jnp.where(row == col, values.astype(F32), 0.0), 1, keepdims=True)

    place = column(position)
    lane = lax.broadcasted_iota(jnp.int32, (length, HALF), 1)
    half = HEAD_DIM // 2
    second = lane >= half
    freq_index = jnp.where(second, lane - half, lane).astype(F32)
    angles = place * jnp.exp(freq_index * (-2.0 * math.log(ROPE_BASE) / HEAD_DIM))
    table[0] = jnp.cos(angles)
    sine = jnp.sin(angles)
    table[1] = jnp.where(second, sine, -sine)
    index = lax.broadcasted_iota(jnp.int32, (length, HALF), 0).astype(F32)
    table[2] = index - place
    table[3] = jnp.broadcast_to(column(bucket), (length, HALF))
    table[4] = jnp.broadcast_to(head_count.astype(F32), (length, HALF))


def local_params(limit):
    return pltpu.CompilerParams(vmem_limit_bytes=limit << 20)


def fast_body(
    tokens, cotangent, head_counts, positions, buckets,
    in_master, out_master, up_master, down_master, norm_master,
    in_first, out_first, up_first, down_first, norm_first,
    in_second, out_second, up_second, down_second, norm_second,
):
    tok, cot = tokens[0], cotangent[0]
    (n1, both_cot, tables, packs, n2, mid, q_rows, k_rows, v_rows, a_rows), (wq, wo, wu, wd) = front_call(
        head_counts, positions, buckets, tok, cot, norm_master,
        (in_master, out_master[None], up_master, down_master),
    )
    out_all, ig_own, norm_sum, in_sum, out_sum, up_sum, down_sum = back_call(
        n2, both_cot, tables, packs, mid, tok, wq, wo, wu, wd, n1,
        (q_rows, k_rows, v_rows, a_rows),
    )
    ig_rows = [ig_own] + [
        lax.ppermute(ig_own, "tensor", [(i, (i + step) % 4) for i in range(4)])
        for step in (1, 2, 3)
    ]
    masters = (in_master, out_master[None], up_master, down_master, norm_master)
    firsts = (in_first, out_first[None], up_first, down_first, norm_first)
    seconds = (in_second, out_second[None], up_second, down_second, norm_second)
    updates, moments, squares, tile, output = adam_call(
        (in_sum, out_sum, up_sum, down_sum, norm_sum), masters, firsts, seconds, out_all
    )
    norms = total_call(tile)
    *weights, input_grad, lamb_norms, share = weight_call(
        norms, updates, masters, packs, ig_rows
    )
    flat = lambda group: (group[0], group[1][0], group[2], group[3], group[4])
    return (
        output[None],
        input_grad[None],
        share[0],
        lamb_norms,
        *flat(weights),
        *flat(moments),
        *flat(squares),
    )


def solution(mesh):
    placed = (
        P(("dp", "expert"), None, None),
        P(("dp", "expert"), None, None),
        P(("dp", "expert")),
        P(("dp", "expert"), None),
        P(("dp", "expert"), None),
        P(None, ("dp", "expert"), "tensor"),
        P("tensor", ("dp", "expert")),
        P(None, ("dp", "expert"), "tensor"),
        P(None, "tensor", ("dp", "expert")),
        P(None, ("dp", "expert")),
        P(None, ("dp", "expert"), "tensor"),
        P("tensor", ("dp", "expert")),
        P(None, ("dp", "expert"), "tensor"),
        P(None, "tensor", ("dp", "expert")),
        P(None, ("dp", "expert")),
        P(None, ("dp", "expert"), "tensor"),
        P("tensor", ("dp", "expert")),
        P(None, ("dp", "expert"), "tensor"),
        P(None, "tensor", ("dp", "expert")),
        P(None, ("dp", "expert")),
    )
    shape = dict(mesh.shape)
    fits = shape == {"dp": 4, "expert": 2, "tensor": 4}
    return jax.shard_map(
        fast_body if fits else body,
        mesh=mesh,
        in_specs=placed,
        out_specs=(
            P(("dp", "expert"), None, None),
            P(("dp", "expert"), None, None),
            P(),
            P(),
            P(None, ("dp", "expert"), "tensor"),
            P("tensor", ("dp", "expert")),
            P(None, ("dp", "expert"), "tensor"),
            P(None, "tensor", ("dp", "expert")),
            P(None, ("dp", "expert")),
            P(None, ("dp", "expert"), "tensor"),
            P("tensor", ("dp", "expert")),
            P(None, ("dp", "expert"), "tensor"),
            P(None, "tensor", ("dp", "expert")),
            P(None, ("dp", "expert")),
            P(None, ("dp", "expert"), "tensor"),
            P("tensor", ("dp", "expert")),
            P(None, ("dp", "expert"), "tensor"),
            P(None, "tensor", ("dp", "expert")),
            P(None, ("dp", "expert")),
        ),
        check_vma=False,
    )
```

```python
import math

import jax
import jax.numpy as jnp
from jax import lax
from jax.experimental import pallas as pl
from jax.experimental.pallas import tpu as pltpu
from jax.sharding import PartitionSpec as P

HEAD_DIM = 128
STEP = 10


NORM_EPS = 1e-05
BETA_FIRST = 0.9
BETA_SECOND = 0.999
ADAM_EPS = 1e-06
WEIGHT_DECAY = 0.01
LEARN_RATE = 0.25
MASKED = -1e30
ROPE_BASE = 10000.0


def layer_norm(values, gain_row, shift_row):
    center = values - jnp.mean(values, -1, keepdims=True)
    variance = jnp.mean(center * center, -1, keepdims=True)
    inv_std = lax.rsqrt(variance + NORM_EPS)
    normed = center * inv_std
    return (normed * gain_row + shift_row, normed, inv_std)


def norm_back_rows(grad_out, normed, inv_std, gain_row):
    scaled = grad_out * gain_row
    inner_part = (
        scaled
        - jnp.mean(scaled, -1, keepdims=True)
        - normed * jnp.mean(scaled * normed, -1, keepdims=True)
    )
    return (inner_part * inv_std, jnp.sum(grad_out * normed, 0), jnp.sum(grad_out, 0))


def rope_angles(position_row):
    freq_index = jnp.arange(HEAD_DIM // 2, dtype=jnp.float32)
    inverse = jnp.exp(freq_index * (-2.0 * jnp.log(ROPE_BASE) / HEAD_DIM))
    return position_row.astype(jnp.float32)[:, None] * inverse[None, :]


def rotary(values, angles, sign_value):
    half_dim = values.shape[-1] // 2
    cosine = jnp.cos(angles)[:, None, :]
    sine_part = sign_value * jnp.sin(angles)[:, None, :]
    first_half = values[..., :half_dim]
    second_half = values[..., half_dim:]
    return jnp.concatenate(
        [
            first_half * cosine - second_half * sine_part,
            second_half * cosine + first_half * sine_part,
        ],
        -1,
    )


def block_mask(key_index, position_row, block_start, block_rows):
    query_index = block_start + jnp.arange(block_rows, dtype=jnp.int32)
    return (key_index[None, :] <= query_index[:, None]) & (
        key_index[None, :] >= (query_index - position_row)[:, None]
    )


def attend_forward(queries, key_rows, value_rows, position_row, block_rows):
    length = queries.shape[0]
    key_index = jnp.arange(length, dtype=jnp.int32)

    def one_block(block_start):
        allowed = block_mask(key_index, position_row, block_start, block_rows)
        scores = jnp.einsum("qhd,khd->hqk", queries, key_rows, preferred_element_type=jnp.float32)
        scores = jnp.where(allowed[None], scores, MASKED)
        row_peak = jnp.max(scores, -1, keepdims=True)
        exp_scores = jnp.exp(scores - row_peak)
        row_total = jnp.sum(exp_scores, -1, keepdims=True)
        attn_weights = (exp_scores / row_total).astype(jnp.bfloat16)
        block_out = jnp.einsum(
            "hqk,khd->qhd", attn_weights, value_rows, preferred_element_type=jnp.float32
        )
        return (block_out, row_peak[..., 0] + jnp.log(row_total[..., 0]))

    starts = jnp.arange(length // block_rows, dtype=jnp.int32) * block_rows
    block_outs, log_totals = lax.map(one_block, starts)
    return (block_outs.reshape(queries.shape), log_totals, starts)


def attend_backward(
    queries, key_rows, value_rows, position_row, grad_heads, log_totals, starts, block_rows
):
    length = queries.shape[0]
    key_index = jnp.arange(length, dtype=jnp.int32)

    def one_block(carried, inputs):
        block_start, block_log = inputs
        allowed = block_mask(key_index, position_row, block_start, block_rows)
        scores = jnp.einsum("qhd,khd->hqk", queries, key_rows, preferred_element_type=jnp.float32)
        scores = jnp.where(allowed[None], scores, MASKED)
        attn_probs = jnp.exp(scores - block_log[..., None])
        grad_probs = jnp.einsum(
            "qhd,khd->hqk", grad_heads, value_rows, preferred_element_type=jnp.float32
        )
        row_inner = jnp.sum(attn_probs * grad_probs, -1, keepdims=True)
        grad_scores = (attn_probs * (grad_probs - row_inner)).astype(jnp.bfloat16)
        grad_query = jnp.einsum(
            "hqk,khd->qhd", grad_scores, key_rows, preferred_element_type=jnp.float32
        )
        grad_keys = carried[0] + jnp.einsum(
            "hqk,qhd->khd", grad_scores, queries, preferred_element_type=jnp.float32
        )
        grad_values = carried[1] + jnp.einsum(
            "hqk,qhd->khd",
            attn_probs.astype(jnp.bfloat16),
            grad_heads,
            preferred_element_type=jnp.float32,
        )
        return ((grad_keys, grad_values), grad_query)

    start_state = (jnp.zeros(key_rows.shape, jnp.float32), jnp.zeros(value_rows.shape, jnp.float32))
    (grad_keys, grad_values), grad_query = lax.scan(one_block, start_state, (starts, log_totals))
    return (grad_query.reshape(queries.shape), grad_keys, grad_values)


def gather_rows(values, source_rows):
    padded = jnp.concatenate([values, jnp.zeros((1, values.shape[1]), values.dtype)], 0)
    return padded[source_rows]


def ffn_forward(rows_in, bucket, up_work, down_work):
    row_count = rows_in.shape[0]
    mixed_sum = jnp.zeros((row_count, down_work.shape[2]), jnp.float32)
    hiddens = []
    for quarter in range(4):

        def live_part():
            hidden = jnp.dot(rows_in, up_work[quarter], preferred_element_type=jnp.float32)
            squared = jnp.square(jnp.maximum(hidden, 0.0)).astype(jnp.bfloat16)
            return (
                hidden,
                jnp.dot(squared, down_work[quarter], preferred_element_type=jnp.float32),
            )

        def dead_part():
            return (
                jnp.zeros((row_count, up_work.shape[2]), jnp.float32),
                jnp.zeros_like(mixed_sum),
            )

        hidden, contribution = lax.cond(bucket >= quarter, live_part, dead_part)
        hiddens.append(hidden)
        mixed_sum = mixed_sum + contribution
    return (mixed_sum, hiddens)


def ffn_backward(rows_in, grads_in, bucket, hiddens, up_work, down_work):
    grad_rows = jnp.zeros((rows_in.shape[0], up_work.shape[1]), jnp.float32)
    grad_up = []
    grad_down = []
    for quarter in range(4):
        hidden = hiddens[quarter]

        def live_part():
            rectified = jnp.maximum(hidden, 0.0)
            squared = jnp.square(rectified).astype(jnp.bfloat16)
            grad_square = jnp.einsum(
                "rd,ud->ru", grads_in, down_work[quarter], preferred_element_type=jnp.float32
            )
            grad_hidden = (grad_square * 2.0 * rectified).astype(jnp.bfloat16)
            return (
                jnp.einsum("rd,ru->du", rows_in, grad_hidden, preferred_element_type=jnp.float32),
                jnp.einsum("ru,rd->ud", squared, grads_in, preferred_element_type=jnp.float32),
                jnp.einsum(
                    "ru,du->rd", grad_hidden, up_work[quarter], preferred_element_type=jnp.float32
                ),
            )

        def dead_part():
            return (
                jnp.zeros(up_work.shape[1:], jnp.float32),
                jnp.zeros(down_work.shape[1:], jnp.float32),
                jnp.zeros_like(grad_rows),
            )

        part_up, part_down, part_rows = lax.cond(bucket >= quarter, live_part, dead_part)
        grad_up.append(part_up)
        grad_down.append(part_down)
        grad_rows = grad_rows + part_rows
    return (grad_rows, jnp.stack(grad_up), jnp.stack(grad_down))


def ffn_total(partial_value):
    return lax.psum(partial_value, "tensor")


def ffn_grad_total(partial_value):
    return lax.psum(partial_value, "tensor")


def adam_terms(weight, gradient, first_old, second_old):
    first_new = BETA_FIRST * first_old + (1.0 - BETA_FIRST) * gradient
    second_new = BETA_SECOND * second_old + (1.0 - BETA_SECOND) * gradient * gradient
    update = (
        first_new
        / (1.0 - BETA_FIRST**STEP)
        / (jnp.sqrt(second_new / (1.0 - BETA_SECOND**STEP)) + ADAM_EPS)
        + WEIGHT_DECAY * weight
    )
    return (update, first_new, second_new)


def finish(output, input_grad, bucket_share, masters, firsts, seconds, grad_shards, tensor_count):
    norm_master = masters[4]
    adam_out = [
        adam_terms(masters[member], grad_shards[member], firsts[member], seconds[member])
        for member in range(5)
    ]
    weight_sq = jnp.concatenate(
        [
            jnp.stack([jnp.sum(masters[member] * masters[member]) for member in range(4)]),
            jnp.sum(norm_master * norm_master, 1) / tensor_count,
        ]
    )
    update_sq = jnp.concatenate(
        [
            jnp.stack([jnp.sum(adam_out[member][0] * adam_out[member][0]) for member in range(4)]),
            jnp.sum(adam_out[4][0] * adam_out[4][0], 1) / tensor_count,
        ]
    )
    weight_tot, update_tot = lax.psum((weight_sq, update_sq), ("dp", "expert", "tensor"))
    weight_norms = jnp.sqrt(weight_tot)
    update_norms = jnp.sqrt(update_tot)
    ratios = weight_norms / update_norms
    new_weights = [
        masters[member] - LEARN_RATE * ratios[member] * adam_out[member][0] for member in range(4)
    ]
    norm_new = norm_master - LEARN_RATE * ratios[4:, None] * adam_out[4][0]
    lamb_norms = jnp.stack([weight_norms, update_norms])
    return (
        output[None],
        input_grad[None],
        bucket_share,
        lamb_norms,
        new_weights[0],
        new_weights[1],
        new_weights[2],
        new_weights[3],
        norm_new,
        adam_out[0][1],
        adam_out[1][1],
        adam_out[2][1],
        adam_out[3][1],
        adam_out[4][1],
        adam_out[0][2],
        adam_out[1][2],
        adam_out[2][2],
        adam_out[3][2],
        adam_out[4][2],
    )


def body(
    tokens,
    cotangent,
    head_counts,
    positions,
    buckets,
    in_master,
    out_master,
    up_master,
    down_master,
    norm_master,
    in_first,
    out_first,
    up_first,
    down_first,
    norm_first,
    in_second,
    out_second,
    up_second,
    down_second,
    norm_second,
):
    in_work, out_work, up_work, down_work, norm_work = (
        lax.all_gather(in_master.astype(jnp.bfloat16), ("dp", "expert"), axis=1, tiled=True),
        lax.all_gather(out_master.astype(jnp.bfloat16), ("dp", "expert"), axis=1, tiled=True),
        lax.all_gather(up_master.astype(jnp.bfloat16), ("dp", "expert"), axis=1, tiled=True),
        lax.all_gather(down_master.astype(jnp.bfloat16), ("dp", "expert"), axis=2, tiled=True),
        lax.all_gather(norm_master.astype(jnp.bfloat16), ("dp", "expert"), axis=1, tiled=True),
    )
    length = tokens.shape[1]
    model_width = tokens.shape[2]
    heads_here = in_work.shape[2] // HEAD_DIM
    block_rows = min(512, length)
    head_scale = HEAD_DIM ** (-0.5)
    groups_data = lax.axis_size("dp") * lax.axis_size("expert")
    tensor_count = lax.axis_size("tensor")
    experts = lax.axis_size("expert")
    norm_gains = norm_work.astype(jnp.float32)
    inputs = tokens[0].astype(jnp.float32)
    first_norm, first_hat, first_inv = layer_norm(inputs, norm_gains[0], norm_gains[1])
    first_in = first_norm.astype(jnp.bfloat16)
    projected = jnp.einsum("td,jde->jte", first_in, in_work, preferred_element_type=jnp.float32)
    projected = projected.reshape(3, length, heads_here, HEAD_DIM)
    angles = rope_angles(positions[0])
    queries = (rotary(projected[0], angles, 1.0) * head_scale).astype(jnp.bfloat16)
    key_rows = rotary(projected[1], angles, 1.0).astype(jnp.bfloat16)
    value_rows = projected[2].astype(jnp.bfloat16)
    head_ids = lax.axis_index("tensor") * heads_here + jnp.arange(heads_here, dtype=jnp.int32)
    active = (head_ids < head_counts[0]).astype(jnp.float32)
    head_outs, log_totals, starts = attend_forward(
        queries, key_rows, value_rows, positions[0], block_rows
    )
    attended = (
        (head_outs * active[None, :, None])
        .astype(jnp.bfloat16)
        .reshape(length, heads_here * HEAD_DIM)
    )
    attn_part = jnp.dot(attended, out_work, preferred_element_type=jnp.float32)
    middle = inputs + lax.psum(attn_part, "tensor")
    second_norm, second_hat, second_inv = layer_norm(middle, norm_gains[2], norm_gains[3])
    second_in = second_norm.astype(jnp.bfloat16)
    bucket_ids = buckets[0]
    onehot = (bucket_ids[:, None] == jnp.arange(4, dtype=jnp.int32)[None, :]).astype(jnp.int32)
    bucket_rank = jnp.sum((jnp.cumsum(onehot, 0) - onehot) * onehot, 1)
    local_counts = jnp.sum(onehot, 0).astype(jnp.float32)
    bucket_share = lax.psum(local_counts, ("dp", "expert")) / (length * groups_data)
    most_rows = 5 * length // 16
    owner_group = max(experts // 4, 1)
    per_owner = max(4 // experts, 1)
    slot_rows = (most_rows + owner_group - 1) // owner_group
    capacity = per_owner * slot_rows
    slot_of = (
        (bucket_ids // per_owner * owner_group + bucket_rank % owner_group) * capacity
        + bucket_ids % per_owner * slot_rows
        + bucket_rank // owner_group
    )
    slot_total = experts * capacity
    source_rows = (
        jnp.full((slot_total,), length, jnp.int32)
        .at[slot_of]
        .set(jnp.arange(length, dtype=jnp.int32))
    )
    outgoing = gather_rows(second_in, source_rows).reshape(experts, capacity, model_width)
    incoming = lax.all_to_all(outgoing, "expert", split_axis=0, concat_axis=0, tiled=True).reshape(
        experts, per_owner, slot_rows, model_width
    )
    owner_index = lax.axis_index("expert")
    owned_ids = [owner_index // owner_group * per_owner + member for member in range(per_owner)]
    ffn_inputs = [
        incoming[:, member].reshape(experts * slot_rows, model_width) for member in range(per_owner)
    ]
    results = [
        ffn_forward(ffn_inputs[member], owned_ids[member], up_work, down_work)
        for member in range(per_owner)
    ]
    partial_value = jnp.stack(
        [
            results[member][0].reshape(experts, slot_rows, model_width)
            for member in range(per_owner)
        ],
        1,
    )
    summed = ffn_total(partial_value.reshape(experts, capacity, model_width)).astype(jnp.bfloat16)
    returned = lax.all_to_all(summed, "expert", split_axis=0, concat_axis=0, tiled=True)
    branch_out = returned.reshape(slot_total, model_width)[slot_of]
    output = middle + branch_out.astype(jnp.float32)
    grad_branch = cotangent[0]
    outgoing_grad = gather_rows(grad_branch, source_rows).reshape(experts, capacity, model_width)
    incoming_grad = lax.all_to_all(
        outgoing_grad, "expert", split_axis=0, concat_axis=0, tiled=True
    ).reshape(experts, per_owner, slot_rows, model_width)
    ffn_grads = [
        incoming_grad[:, member].reshape(experts * slot_rows, model_width)
        for member in range(per_owner)
    ]
    back_parts = [
        ffn_backward(
            ffn_inputs[member],
            ffn_grads[member],
            owned_ids[member],
            results[member][1],
            up_work,
            down_work,
        )
        for member in range(len(owned_ids))
    ]
    grad_up = back_parts[0][1]
    grad_down = back_parts[0][2]
    for member in range(1, len(owned_ids)):
        grad_up = grad_up + back_parts[member][1]
        grad_down = grad_down + back_parts[member][2]
    rows_back = jnp.stack(
        [
            back_parts[member][0].reshape(experts, slot_rows, model_width)
            for member in range(per_owner)
        ],
        1,
    )
    summed_back = ffn_grad_total(rows_back.reshape(experts, capacity, model_width)).astype(
        jnp.bfloat16
    )
    returned_back = lax.all_to_all(summed_back, "expert", split_axis=0, concat_axis=0, tiled=True)
    grad_second = returned_back.reshape(slot_total, model_width)[slot_of].astype(jnp.float32)
    grad_mid_norm, gain_second, shift_second = norm_back_rows(
        grad_second, second_hat, second_inv, norm_gains[2]
    )
    grad_middle = grad_branch.astype(jnp.float32) + grad_mid_norm
    grad_attn = grad_middle.astype(jnp.bfloat16)
    grad_attended = jnp.einsum("td,ed->te", grad_attn, out_work, preferred_element_type=jnp.float32)
    grad_out_w = jnp.einsum("te,td->ed", attended, grad_attn, preferred_element_type=jnp.float32)
    grad_heads = (
        grad_attended.astype(jnp.bfloat16).reshape(length, heads_here, HEAD_DIM)
        * active.astype(jnp.bfloat16)[None, :, None]
    )
    grad_query, grad_keys, grad_values = attend_backward(
        queries, key_rows, value_rows, positions[0], grad_heads, log_totals, starts, block_rows
    )
    grad_projected = jnp.stack(
        [
            rotary(grad_query * head_scale, angles, -1.0),
            rotary(grad_keys, angles, -1.0),
            grad_values,
        ]
    )
    grad_projected = grad_projected.reshape(3, length, heads_here * HEAD_DIM).astype(jnp.bfloat16)
    grad_in_w = jnp.einsum(
        "td,jte->jde", first_in, grad_projected, preferred_element_type=jnp.float32
    )
    grad_first_part = jnp.einsum(
        "jte,jde->td", grad_projected, in_work, preferred_element_type=jnp.float32
    )
    grad_first = lax.psum(grad_first_part, "tensor")
    grad_input_norm, gain_first, shift_first = norm_back_rows(
        grad_first, first_hat, first_inv, norm_gains[0]
    )
    input_grad = grad_middle + grad_input_norm
    grad_norm = jnp.stack([gain_first, shift_first, gain_second, shift_second])
    in_sum, out_sum, up_sum, down_sum, norm_sum = (
        lax.psum_scatter(grad_in_w, ("dp", "expert"), scatter_dimension=1, tiled=True),
        lax.psum_scatter(grad_out_w, ("dp", "expert"), scatter_dimension=1, tiled=True),
        lax.psum_scatter(grad_up, ("dp", "expert"), scatter_dimension=1, tiled=True),
        lax.psum_scatter(grad_down, ("dp", "expert"), scatter_dimension=2, tiled=True),
        lax.psum_scatter(grad_norm, ("dp", "expert"), scatter_dimension=1, tiled=True),
    )
    masters = (in_master, out_master, up_master, down_master, norm_master)
    firsts = (in_first, out_first, up_first, down_first, norm_first)
    seconds = (in_second, out_second, up_second, down_second, norm_second)
    grad_shards = (in_sum, out_sum, up_sum, down_sum, norm_sum)
    return finish(output, input_grad, bucket_share, masters, firsts, seconds, grad_shards, tensor_count)


MESH = pl.DeviceIdType.MESH
ANY = pl.BlockSpec(memory_space=pl.ANY)
VM = pl.BlockSpec(memory_space=pltpu.VMEM)
SM = pl.BlockSpec(memory_space=pltpu.SMEM)

F32 = jnp.float32
BF16 = jnp.bfloat16
CHUNK = 256
HALF = 128
ROWS = 64


class Here:
    def __init__(self):
        d = lax.axis_index("dp")
        self.x, self.c = d // 2, lax.rem(d, 2)
        self.y = lax.axis_index("expert")
        self.z = lax.axis_index("tensor")

    def plane(self, dx, dc, dy):
        x = 1 - self.x if dx else self.x
        c = 1 - self.c if dc else self.c
        y = 1 - self.y if dy else self.y
        return (x * 2 + c, y, self.z)

    def chunk(self, dx, dc, dy):
        x = 1 - self.x if dx else self.x
        c = 1 - self.c if dc else self.c
        y = 1 - self.y if dy else self.y
        return (x * 2 + c) * 2 + y

    def chunk_of(self, dx, dy, core):
        x = 1 - self.x if dx else self.x
        y = 1 - self.y if dy else self.y
        return (x * 2 + core) * 2 + y

    def along(self, step):
        return (self.x * 2 + self.c, self.y, lax.rem(self.z + step, 4))

    def behind(self, step):
        return lax.rem(self.z + 4 - step, 4)


PARTNER = (0, 1, 0)
PLANE = [(a, b, g) for a in (0, 1) for b in (0, 1) for g in (0, 1) if a + b + g > 0]
SIDES = [(1, 0, 0), (1, 1, 0), (0, 0, 1), (0, 1, 1)]


def greet(here, plane_peers, tensor_peers):
    barrier = pltpu.get_barrier_semaphore()
    for peer in plane_peers:
        pl.semaphore_signal(barrier, inc=1, device_id=here.plane(*peer), device_id_type=MESH)
    for step in tensor_peers:
        pl.semaphore_signal(barrier, inc=1, device_id=here.along(step), device_id_type=MESH)
    pl.semaphore_wait(barrier, len(plane_peers) + len(tensor_peers))


def push(src, dst, send, recv, device):
    copy = pltpu.make_async_remote_copy(
        src_ref=src, dst_ref=dst, send_sem=send, recv_sem=recv, device_id=device, device_id_type=MESH
    )
    copy.start()
    return copy


def block(index, size):
    return pl.ds(pl.multiple_of(index * size, size), size)


def rows_chunk(ref, k):
    return ref.at[:, block(k, CHUNK), :]


def rows_part(ref, k, part):
    return ref.at[:, pl.ds(pl.multiple_of(k * CHUNK + part * HALF, HALF), HALF), :]


def cols_chunk(ref, k):
    return ref.at[:, :, block(k, CHUNK)]


def cols_part(ref, k, part):
    return ref.at[:, part * HALF : part * HALF + HALF, block(k, CHUNK)]


class Gather:
    def __init__(self, here, by_rows, shard, whole, first, relay, local):
        self.here, self.by_rows, self.shard, self.whole = here, by_rows, shard, whole
        self.first, self.relay, self.local = first, relay, local
        self.copies = []

    def half(self, core):
        if self.by_rows:
            return self.shard.at[:, :, block(core, CHUNK)]
        return self.shard.at[:, block(core, CHUNK), :]

    def chunk(self, k):
        return rows_chunk(self.whole, k) if self.by_rows else cols_chunk(self.whole, k)

    def part(self, k, part):
        return rows_part(self.whole, k, part) if self.by_rows else cols_part(self.whole, k, part)

    def start(self):
        here = self.here
        mine = self.chunk(here.chunk(0, 0, 0))
        for index, side in enumerate(SIDES + [PARTNER]):
            core = 1 - here.c if side[1] else here.c
            self.copies.append(
                push(
                    self.half(core),
                    mine,
                    self.first.at[0, index],
                    self.first.at[1, index],
                    here.plane(*side),
                )
            )
        self.own = pltpu.make_async_copy(self.half(here.c), mine, self.local)
        self.own.start()

    def forward(self):
        here = self.here
        self.onward = []
        for index in range(4):
            side = SIDES[index]
            self.copies[index].wait_recv()
            part = 0 if side[0] else 1
            where = self.part(here.chunk(*side), part)
            target = (0, 0, 1) if side[0] else (1, 0, 0)
            self.onward.append(
                push(
                    where,
                    where,
                    self.relay.at[0, index],
                    self.relay.at[1, index],
                    here.plane(*target),
                )
            )

    def finish(self):
        for index in range(4):
            self.copies[index].wait_send()
        self.copies[4].wait()
        self.own.wait()
        for copy in self.onward:
            copy.wait()


def gather_sems():
    return [
        pltpu.SemaphoreType.DMA((2, 5)),
        pltpu.SemaphoreType.DMA((2, 4)),
        pltpu.SemaphoreType.DMA,
    ]


class Scatter:
    def __init__(self, here, by_rows, grad, total, bufs):
        self.here, self.by_rows, self.grad, self.total = here, by_rows, grad, total
        self.got, self.got_two = bufs[:2]
        self.one_sem, self.two_sem, self.last_sem, self.local = bufs[2:6]
        self.final = bufs[6]

    def part(self, dx, dy, core, side):
        k = self.here.chunk_of(dx, dy, core)
        return rows_part(self.grad, k, side) if self.by_rows else cols_part(self.grad, k, side)

    def start(self):
        here = self.here
        self.first = []
        for side in (0, 1):
            near, far = ((1, 0), (1, 1)) if side == 0 else ((0, 1), (1, 1))
            target = here.plane(1, 0, 0) if side == 0 else here.plane(0, 0, 1)
            for slot in range(4):
                chip = far if slot >= 2 else near
                index = side * 4 + slot
                self.first.append(
                    push(
                        self.part(chip[0], chip[1], slot % 2, side),
                        self.got.at[index],
                        self.one_sem.at[0, index],
                        self.one_sem.at[1, index],
                        target,
                    )
                )

    def middle(self):
        here = self.here
        self.second = []
        for side in (0, 1):
            target = here.plane(0, 0, 1) if side == 0 else here.plane(1, 0, 0)
            chip = (0, 1) if side == 0 else (1, 0)
            for slot in (2, 3):
                index = side * 4 + slot
                two = side * 2 + slot - 2
                mine = self.part(chip[0], chip[1], slot - 2, side)
                self.first[index].wait_recv()
                got = self.got.at[index]

                def step(i, carry):
                    spot = (i // 4, block(lax.rem(i, 4), 32), slice(None))
                    mine[spot] = (mine[spot].astype(F32) + got[spot].astype(F32)).astype(BF16)
                    return carry

                lax.fori_loop(0, got.shape[0] * 4, step, 0)
                self.second.append(
                    push(
                        mine,
                        self.got_two.at[two],
                        self.two_sem.at[0, two],
                        self.two_sem.at[1, two],
                        target,
                    )
                )

    def last(self):
        here = self.here
        for side in (0, 1):
            for slot in (0, 1):
                index = side * 4 + slot
                two = side * 2 + slot
                self.first[index].wait_recv()
                self.second[two].wait_recv()
                mine, got, got_two = self.part(0, 0, slot, side), self.got.at[index], self.got_two.at[two]
                final = self.final.at[slot, :, side * HALF : side * HALF + HALF, :]

                def step(i, carry):
                    spot = (i // 4, block(lax.rem(i, 4), 32), slice(None))
                    final[spot] = (mine[spot].astype(F32) + got[spot].astype(F32)) + got_two[
                        spot
                    ].astype(F32)
                    return carry

                lax.fori_loop(0, got.shape[0] * 4, step, 0)
        if self.by_rows:
            where = self.total.at[:, :, block(here.c, CHUNK)]
        else:
            where = self.total.at[:, block(here.c, CHUNK), :]
        self.keep = pltpu.make_async_copy(self.final.at[here.c], where, self.local)
        self.keep.start()
        self.give = push(
            self.final.at[1 - here.c],
            where,
            self.last_sem.at[0],
            self.last_sem.at[1],
            here.plane(*PARTNER),
        )

    def sent(self):
        self.keep.wait()
        self.give.wait_send()

    def finish(self):
        for copy in self.first:
            copy.wait_send()
        for copy in self.second:
            copy.wait_send()
        self.give.wait_recv()


def scatter_scratch(width):
    return [
        pltpu.VMEM((8, width, HALF, CHUNK), BF16),
        pltpu.VMEM((4, width, HALF, CHUNK), BF16),
        pltpu.SemaphoreType.DMA((2, 8)),
        pltpu.SemaphoreType.DMA((2, 4)),
        pltpu.SemaphoreType.DMA((2,)),
        pltpu.SemaphoreType.DMA,
    ]


SCATTER = 6


class TensorSum:
    def __init__(self, here, part, bufs):
        self.here, self.part = here, part
        self.pair, self.out, self.inn, self.pair_sem, self.sem = bufs

    def start(self):
        here = self.here
        self.swap = push(
            self.part.at[1 - here.c],
            self.pair,
            self.pair_sem.at[0],
            self.pair_sem.at[1],
            here.plane(*PARTNER),
        )

    def spread(self):
        here = self.here
        self.swap.wait_recv()
        self.sent = []
        for step in (2, 1, 3):
            rows = block(lax.rem(here.z + step, 4), ROWS)
            self.out[step - 1] = (
                self.part[here.c, rows, :].astype(F32) + self.pair[rows, :].astype(F32)
            ).astype(self.out.dtype)
            self.sent.append(
                push(
                    self.out.at[step - 1],
                    self.inn.at[step - 1],
                    self.sem.at[0, step - 1],
                    self.sem.at[1, step - 1],
                    here.along(step),
                )
            )

    def result(self):
        here = self.here
        rows = block(here.z, ROWS)
        total = self.part[here.c, rows, :].astype(F32) + self.pair[rows, :].astype(F32)
        for copy in self.sent:
            copy.wait_recv()
        for step in (1, 2, 3):
            total = total + self.inn[step - 1].astype(F32)
        return total

    def finish(self):
        self.swap.wait_send()
        for copy in self.sent:
            copy.wait_send()


def sum_scratch(length, width):
    return [
        pltpu.VMEM((length, width), BF16),
        pltpu.VMEM((3, ROWS, width), BF16),
        pltpu.VMEM((3, ROWS, width), BF16),
        pltpu.SemaphoreType.DMA((2,)),
        pltpu.SemaphoreType.DMA((2, 3)),
    ]


class TensorGather:
    def __init__(self, here, mine, whole, sem, pair_sem, local):
        self.here, self.mine, self.whole = here, mine, whole
        self.sem, self.pair_sem, self.local = sem, pair_sem, local

    def start(self):
        here = self.here
        place = self.whole.at[here.c, block(here.z, ROWS), :]
        self.sent = []
        for step in (2, 1, 3):
            self.sent.append(
                push(
                    self.mine,
                    place,
                    self.sem.at[0, step - 1],
                    self.sem.at[1, step - 1],
                    here.along(step),
                )
            )
        self.shared = [
            push(
                self.mine,
                place,
                self.pair_sem.at[0, 0],
                self.pair_sem.at[1, 0],
                here.plane(*PARTNER),
            )
        ]
        self.own = pltpu.make_async_copy(self.mine, place, self.local)
        self.own.start()

    def forward(self):
        here = self.here
        for index, step in enumerate((2, 1, 3)):
            self.sent[index].wait_recv()
            place = self.whole.at[here.c, block(here.behind(step), ROWS), :]
            self.shared.append(
                push(
                    place,
                    place,
                    self.pair_sem.at[0, step],
                    self.pair_sem.at[1, step],
                    here.plane(*PARTNER),
                )
            )

    def finish(self):
        for copy in self.sent:
            copy.wait_send()
        for copy in self.shared:
            copy.wait()
        self.own.wait()


class LineSum:
    def __init__(self, here, part, bufs):
        self.here, self.part = here, part
        self.pair, self.slot, self.pair_sem, self.sem = bufs

    def start(self):
        here = self.here
        self.swap = push(
            self.part.at[1 - here.c],
            self.pair,
            self.pair_sem.at[0],
            self.pair_sem.at[1],
            here.plane(*PARTNER),
        )

    def own(self, z):
        rows = block(z, ROWS)
        return self.part[self.here.c, rows, :].astype(F32) + self.pair[rows, :].astype(F32)

    def depth(self, way):
        return self.here.z if way == 0 else 3 - self.here.z

    def hop(self, way, k, src):
        here = self.here
        return pltpu.make_async_remote_copy(
            src_ref=src,
            dst_ref=self.slot.at[way, k],
            send_sem=self.sem.at[0, way, k],
            recv_sem=self.sem.at[1, way, k],
            device_id=(here.x * 2 + here.c, here.y, here.z + (1 if way == 0 else -1)),
            device_id_type=MESH,
        )

    def take(self, way, k):
        here = self.here
        pltpu.make_async_remote_copy(
            src_ref=self.slot.at[way, k],
            dst_ref=self.slot.at[way, k],
            send_sem=self.sem.at[0, way, k],
            recv_sem=self.sem.at[1, way, k],
            device_id=(here.x * 2 + here.c, here.y, here.z - (1 if way == 0 else -1)),
            device_id_type=MESH,
        ).wait_recv()

    def stage(self, k):
        here = self.here
        if k == 0:
            self.swap.wait_recv()
        for way in (0, 1):
            depth = self.depth(way)
            shard = here.z + 3 - k if way == 0 else here.z - 3 + k

            @pl.when(depth == 0)
            def _():
                self.slot[way, k] = self.own(shard).astype(BF16)
                self.hop(way, k, self.slot.at[way, k]).start()

            if k > 0:

                @pl.when((depth >= 1) & (depth <= k))
                def _():
                    self.take(way, k - 1)
                    self.slot[way, k - 1] = (
                        self.own(shard) + self.slot[way, k - 1].astype(F32)
                    ).astype(BF16)
                    self.hop(way, k, self.slot.at[way, k - 1]).start()

    def result(self):
        total = self.own(self.here.z)
        for way in (0, 1):
            depth = self.depth(way)

            @pl.when(depth >= 1)
            def _():
                self.take(way, 2)

            total = total + jnp.where(depth >= 1, self.slot[way, 2].astype(F32), 0.0)
        return total

    def finish(self):
        self.swap.wait_send()
        for way in (0, 1):
            for k in range(3):

                @pl.when(self.depth(way) <= k)
                def _():
                    self.hop(way, k, self.slot.at[way, k]).wait_send()


def line_scratch(length, width):
    return [
        pltpu.VMEM((length, width), BF16),
        pltpu.VMEM((2, 3, ROWS, width), BF16),
        pltpu.SemaphoreType.DMA((2,)),
        pltpu.SemaphoreType.DMA((2, 2, 3)),
    ]


class LineGather:
    def __init__(self, here, place, sem):
        self.here, self.place, self.sem = here, place, sem

    def hop(self, way, k):
        here = self.here
        step = 1 if way == 0 else -1
        spot = self.place(here.z - k * step)
        return pltpu.make_async_remote_copy(
            src_ref=spot,
            dst_ref=spot,
            send_sem=self.sem.at[0, way, k],
            recv_sem=self.sem.at[1, way, k],
            device_id=(here.x * 2 + here.c, here.y, here.z + step),
            device_id_type=MESH,
        )

    def arrival(self, way, k):
        here = self.here
        step = 1 if way == 0 else -1
        spot = self.place(here.z - (k + 1) * step)
        return pltpu.make_async_remote_copy(
            src_ref=spot,
            dst_ref=spot,
            send_sem=self.sem.at[0, way, k],
            recv_sem=self.sem.at[1, way, k],
            device_id=(here.x * 2 + here.c, here.y, here.z - step),
            device_id_type=MESH,
        )

    def sends(self, way, k):
        z = self.here.z
        return (z >= k) & (z < 3) if way == 0 else (z <= 3 - k) & (z > 0)

    def gets(self, way, k):
        z = self.here.z
        return z >= k + 1 if way == 0 else z <= 2 - k

    def start(self):
        for way in (0, 1):

            @pl.when(self.sends(way, 0))
            def _():
                self.hop(way, 0).start()

    def onward(self, k, then=None):
        for way in (0, 1):

            @pl.when(self.gets(way, k))
            def _():
                self.arrival(way, k).wait_recv()
                if then is not None:
                    then(self.here.z - (k + 1) * (1 if way == 0 else -1))

            if k < 2:

                @pl.when(self.sends(way, k + 1))
                def _():
                    self.hop(way, k + 1).start()

    def finish(self):
        for way in (0, 1):
            for k in range(3):

                @pl.when(self.sends(way, k))
                def _():
                    self.hop(way, k).wait_send()


def normed(values):
    center = values - jnp.mean(values, -1, keepdims=True)
    variance = jnp.mean(center * center, -1, keepdims=True)
    inv_std = lax.rsqrt(variance + NORM_EPS)
    return (center * inv_std, inv_std)


def norm_row(packs, row):
    return jnp.concatenate([packs[k, row : row + 1, :] for k in range(8)], 1)


def params(ident, limit=60):
    return pltpu.CompilerParams(
        collective_id=ident, has_side_effects=True, vmem_limit_bytes=limit << 20
    )


def cast_rows(raw, shard):
    count, rows, _ = raw.shape
    for j in range(count):

        def step(i, carry):
            at = pl.ds(pl.multiple_of(i * 32, 32), 32)
            shard[j, at, :] = raw[j, at, :].astype(BF16)
            return carry

        lax.fori_loop(0, rows // 32, step, 0)


def front_kernel(*refs):
    head_count, position, bucket, tok, cot, norm_master = refs[:6]
    masters = refs[6:10]
    n1_hbm, both_cot, tables, packs, n2, mid = refs[10:16]
    homes = [n1_hbm, *refs[16:22]]
    n1, q_out, k_out, v_out, a_out, wq_all, wo_all, home_sem = refs[58:66]
    wholes = [wq_all, wo_all, *refs[22:24]]
    raws, shards = refs[24:28], refs[28:32]
    raw_sem, n2_own, part, small, pair, local = refs[32:38]
    sums, tensor_sems, gather_refs = refs[38:43], refs[43:46], refs[46:58]
    here = Here()
    loads = []
    for i in range(4):
        loads.append(pltpu.make_async_copy(masters[i], raws[i], raw_sem.at[i]))
        loads[i].start()
    me = here.chunk(0, 0, 0)
    lane = lax.broadcasted_iota(jnp.int32, (1, CHUNK), 1)
    counts = jnp.zeros((1, CHUNK), F32)
    for c in range(4):
        count = jnp.sum((bucket[...] == c).astype(F32), 1, keepdims=True)
        counts = counts + jnp.where(lane == c, count, 0.0)
    packs[pl.ds(me, 1)] = jnp.concatenate(
        [norm_master[...].astype(BF16).astype(F32), counts, jnp.zeros((3, CHUNK), F32)], 0
    )[None]
    gathers = [
        Gather(here, i in (0, 2), shards[i], wholes[i], *gather_refs[i * 3 : i * 3 + 3])
        for i in range(4)
    ]
    loads[0].wait()
    cast_rows(raws[0], shards[0])
    greet(here, PLANE, (1, 2, 3))
    gathers[0].start()
    packed = []
    for index, peer in enumerate(PLANE):
        packed.append(
            push(
                packs.at[me], packs.at[me],
                small.at[0, index], small.at[1, index], here.plane(*peer),
            )
        )
    partner = here.plane(*PARTNER)
    table = tables.at[here.c]
    fill_table(table, position[...], bucket[...], head_count[0])
    shared = [
        push(table, table, pair.at[0, 0], pair.at[1, 0], partner),
        push(cot, both_cot.at[here.c], pair.at[0, 1], pair.at[1, 1], partner),
    ]
    keep = pltpu.make_async_copy(cot, both_cot.at[here.c], local)
    keep.start()
    for i in range(1, 4):
        loads[i].wait()
        cast_rows(raws[i], shards[i])
    for copy in packed:
        copy.wait()
    gain, shift = norm_row(packs, 0), norm_row(packs, 1)
    mine = n1.at[here.c]

    def rows_step(i, carry):
        rows = block(i, 32)
        hat, _ = normed(tok[rows, :].astype(F32))
        mine[rows, :] = (hat * gain + shift).astype(BF16)
        return carry

    lax.fori_loop(0, tok.shape[0] // 32, rows_step, 0)
    shared.append(push(mine, mine, pair.at[0, 2], pair.at[1, 2], partner))
    gathers[1].start()
    gathers[0].forward()
    gathers[1].forward()
    gathers[0].finish()
    gathers[2].start()
    gathers[3].start()
    shared[0].wait_recv()
    shared[2].wait_recv()
    head0 = here.z * 4 + here.c * 2
    attend_body(head0, n1, wholes[0], wholes[1], tables, q_out, k_out, v_out, a_out, part)
    gathers[1].finish()
    total = TensorSum(here, part, sums)
    attend_out(a_out, wholes[1], part, 1 - here.c)
    total.start()
    attend_out(a_out, wholes[1], part, here.c)
    total.spread()
    homeward = [
        pltpu.make_async_copy(src, dst, home_sem.at[i])
        for i, (src, dst) in enumerate(
            zip((n1, q_out, k_out, v_out, a_out, wq_all, wo_all), homes)
        )
    ]
    for copy in homeward:
        copy.start()
    rows = block(here.z, ROWS)
    middle = tok[rows, :].astype(F32) + total.result()
    mid[...] = middle
    hat, _ = normed(middle)
    n2_own[...] = (hat * norm_row(packs, 2) + norm_row(packs, 3)).astype(BF16)
    gather = TensorGather(here, n2_own, n2, *tensor_sems)
    gather.start()
    gathers[2].forward()
    gathers[3].forward()
    gather.forward()
    total.finish()
    gather.finish()
    gathers[2].finish()
    gathers[3].finish()
    keep.wait()
    for copy in homeward:
        copy.wait()
    shared[0].wait_send()
    shared[1].wait()
    shared[2].wait_send()


def front_call(head_count, position, bucket, tok, cot, norm_master, masters):
    length, width = tok.shape
    both = jax.ShapeDtypeStruct((2, length, width), BF16)
    thin = jax.ShapeDtypeStruct((2 * length, CHUNK), BF16)
    wholes = [
        jax.ShapeDtypeStruct((3, width, CHUNK), BF16),
        jax.ShapeDtypeStruct((1, CHUNK, width), BF16),
        jax.ShapeDtypeStruct((4, width, CHUNK), BF16),
        jax.ShapeDtypeStruct((4, CHUNK, width), BF16),
    ]
    results = pl.pallas_call(
        front_kernel,
        out_shape=[
            both,
            both,
            jax.ShapeDtypeStruct((2, 5, length, HALF), F32),
            jax.ShapeDtypeStruct((8, 8, CHUNK), F32),
            both,
            jax.ShapeDtypeStruct((ROWS, width), F32),
            thin, thin, thin, thin,
        ]
        + wholes,
        in_specs=[SM, VM, VM, VM, VM, VM] + [ANY] * 4,
        out_specs=[ANY, ANY, VM, VM, ANY, VM] + [ANY] * 8,
        scratch_shapes=[pltpu.VMEM(master.shape, F32) for master in masters]
        + [pltpu.VMEM(master.shape, BF16) for master in masters]
        + [
            pltpu.SemaphoreType.DMA((4,)),
            pltpu.VMEM((ROWS, width), BF16),
            pltpu.VMEM((2, length, width), BF16),
            pltpu.SemaphoreType.DMA((2, 7)),
            pltpu.SemaphoreType.DMA((2, 3)),
            pltpu.SemaphoreType.DMA,
        ]
        + sum_scratch(length, width)
        + tensor_gather_sems()
        + gather_sems() * 4
        + [pltpu.VMEM(both.shape, BF16)]
        + [pltpu.VMEM(thin.shape, BF16)] * 4
        + [pltpu.VMEM(wholes[0].shape, BF16), pltpu.VMEM(wholes[1].shape, BF16)]
        + [pltpu.SemaphoreType.DMA((7,))],
        compiler_params=params(1),
        name="front",
    )(head_count, position, bucket, tok, cot, norm_master, *masters)
    return results[:10], results[10:]


def tensor_gather_sems():
    return [
        pltpu.SemaphoreType.DMA((2, 3)),
        pltpu.SemaphoreType.DMA((2, 4)),
        pltpu.SemaphoreType.DMA,
    ]


def norm_back(grad_out, hat, inv_std, gain):
    scaled = grad_out * gain
    inner = (
        scaled
        - jnp.mean(scaled, -1, keepdims=True)
        - hat * jnp.mean(scaled * hat, -1, keepdims=True)
    )
    return (
        inner * inv_std,
        jnp.sum(grad_out * hat, 0, keepdims=True),
        jnp.sum(grad_out, 0, keepdims=True),
    )


def ffn_hidden(r, n2, cot, bucket, wu, wd, squares, grad_hidden):
    width = n2.shape[2]
    hidden = dot(n2[...].reshape(-1, width), wu[r])
    live = bucket >= jnp.float32(r)
    rectified = jnp.maximum(jnp.where(live, hidden, 0.0), 0.0)
    squares[r] = (rectified * rectified).astype(BF16)
    grad_square = dot(cot[...].reshape(-1, width), wd[r], ((1,), (1,)))
    grad_hidden[r] = (grad_square * 2.0 * rectified).astype(BF16)


def ffn_rows(s, left, right, part, transposed):
    length, width = part.shape[1:]
    rows = pl.ds(pl.multiple_of(s * length, length), length)
    for n in range(width // (2 * CHUNK)):
        cols = slice(n * 2 * CHUNK, (n + 1) * 2 * CHUNK)
        total = None
        for r in range(4):
            if transposed:
                term = dot(left[r, rows, :], right[r, cols, :], ((1,), (1,)))
            else:
                term = dot(left[r, rows, :], right[r, :, cols])
            total = term if total is None else total + term
        part[s, :, cols] = total.astype(BF16)


def attend_back_body(head0, gm, qkva, wq, wo, tables, dp, part):
    length = tables.shape[2]
    width = gm.shape[2]
    q_rows, k_rows, v_rows = qkva.at[0], qkva.at[1], qkva.at[2]
    grad_att = dot(gm[...].reshape(2 * length, width), wo[...], ((1,), (1,))).astype(BF16)
    for s in range(2):
        rows = slice(s * length, (s + 1) * length)
        cosine, sine = tables[s, 0], tables[s, 1]
        lowest = tables[s, 2, :, 0:1]
        for h in range(2):
            cols = slice(h * HEAD_DIM, (h + 1) * HEAD_DIM)
            active = tables[s, 4] > (head0 + h).astype(F32)
            grad_heads = jnp.where(active, grad_att[rows, cols].astype(F32), 0.0).astype(BF16)
            queries, key_rows, value_rows = q_rows[rows, cols], k_rows[rows, cols], v_rows[rows, cols]
            weights = attention_weights(queries, key_rows, lowest)
            grad_weights = dot(grad_heads, value_rows, ((1,), (1,)))
            inner = jnp.sum(weights * grad_weights, -1, keepdims=True)
            grad_scores = (weights * (grad_weights - inner)).astype(BF16)
            grad_query = dot(grad_scores, key_rows) * HEAD_DIM ** (-0.5)
            grad_keys = dot(grad_scores, queries, ((0,), (0,)))
            grad_values = dot(weights.astype(BF16), grad_heads, ((0,), (0,)))
            dp[0, rows, cols] = turn(grad_query, cosine, -sine).astype(BF16)
            dp[1, rows, cols] = turn(grad_keys, cosine, -sine).astype(BF16)
            dp[2, rows, cols] = grad_values.astype(BF16)


def attend_back_rows(s, dp, wq, part):
    length = part.shape[1]
    rows = pl.ds(pl.multiple_of(s * length, length), length)
    total = dot(dp[0, rows, :], wq[0], ((1,), (1,)))
    total = total + dot(dp[1, rows, :], wq[1], ((1,), (1,)))
    total = total + dot(dp[2, rows, :], wq[2], ((1,), (1,)))
    part[s] = total.astype(BF16)


def norm_share(here, values, bufs):
    slices, heard, plane_sum, heard_z, ns, nz = bufs
    for k in range(8):
        slices[k, 0:4, :] = values[:, k * CHUNK : (k + 1) * CHUNK]
        slices[k, 4:8, :] = jnp.zeros((4, CHUNK), F32)
    copies = []
    for index, peer in enumerate(PLANE):
        copies.append(
            push(
                slices.at[here.chunk(*peer)],
                heard.at[index],
                ns.at[0, index],
                ns.at[1, index],
                here.plane(*peer),
            )
        )
    return copies


def norm_share_along(here, copies, bufs):
    slices, heard, plane_sum, heard_z, ns, nz = bufs
    mine = slices[here.chunk(0, 0, 0)]
    for index in range(7):
        copies[index].wait()
        mine = mine + heard[index]
    plane_sum[...] = mine
    onward = []
    for step in (1, 2, 3):
        onward.append(
            push(
                plane_sum,
                heard_z.at[here.z],
                nz.at[0, step - 1],
                nz.at[1, step - 1],
                here.along(step),
            )
        )
    heard_z[pl.ds(here.z, 1)] = mine[None]
    return onward


def back_kernel(*refs):
    n2, cot, tables, packs, mid = refs[0:5]
    tok, wq, wo, wu, wd, n1, q_rows, k_rows, v_rows, a_rows = refs[5:15]
    out_all, ig_own, norm_total, q_sum, o_sum, u_sum, d_sum = refs[15:22]
    wu_v, wd_v, qkva, tok_own, load_sem, squares, grad_hidden, part, part_f, dp = refs[22:32]
    gu, gd, gq, go, gm, dmid, sums, out_v = refs[32:40]
    back_bufs, branch_bufs, final_one, final_two = refs[40:44], refs[44:48], refs[48], refs[49]
    gm_sem, gm_pair, out_sem, keep_sem, norm_bufs = *refs[50:54], refs[54:60]
    rest = refs[60:]
    here = Here()
    loads = []

    def load(src, dst):
        copy = pltpu.make_async_copy(src, dst, load_sem.at[len(loads)])
        copy.start()
        loads.append(copy)
        return copy

    first = [(load(wu.at[r], wu_v.at[r]), load(wd.at[r], wd_v.at[r])) for r in range(4)]
    small = [load(src, qkva.at[i]) for i, src in enumerate((q_rows, k_rows, v_rows, a_rows))]
    place = block(here.z, ROWS)
    small.append(load(tok.at[place, :], tok_own))
    scatters = [
        Scatter(here, by_rows, grad, total, rest[i * SCATTER : (i + 1) * SCATTER] + (final,))
        for i, (by_rows, grad, total, final) in enumerate(
            (
                (True, gu.at[0:1], u_sum.at[0:1], final_one.at[:, 0:1]),
                (False, gd.at[0:1], d_sum.at[0:1], final_two.at[:, 0:1]),
                (True, gu.at[1:4], u_sum.at[1:4], final_one.at[:, 1:4]),
                (False, gd.at[1:4], d_sum.at[1:4], final_two.at[:, 1:4]),
                (True, gq, q_sum, final_one.at[:, 0:3]),
                (False, go, o_sum, final_one.at[:, 3:4]),
            )
        )
    ]
    early_u, early_d, scatter_u, scatter_d, scatter_q, scatter_o = scatters
    length, width = n2.shape[1:]

    def up_gradient(r):
        rows_in = n2[...].reshape(2 * length, width)
        gu[r] = dot(rows_in, grad_hidden[r], ((0,), (0,))).astype(BF16)

    def down_gradient(r):
        grads_in = cot[...].reshape(2 * length, width)
        gd[r] = dot(squares[r], grads_in, ((0,), (0,))).astype(BF16)

    bucket = jnp.concatenate([tables[0, 3, :, 0:1], tables[1, 3, :, 0:1]], 0)
    for r in range(4):
        first[r][0].wait()
        first[r][1].wait()
        ffn_hidden(r, n2, cot, bucket, wu_v, wd_v, squares, grad_hidden)
        if r == 0:
            up_gradient(0)
            greet(here, PLANE, (1, 2, 3))
            early_u.start()
            down_gradient(0)
            early_d.start()
    other = 1 - here.c
    back = LineSum(here, part, back_bufs)
    ffn_rows(other, grad_hidden, wu_v, part, True)
    back.start()
    ffn_rows(here.c, grad_hidden, wu_v, part, True)
    back.stage(0)
    load_q = load(wq, wu_v.at[0:3])
    for r in range(1, 4):
        up_gradient(r)
    scatter_u.start()
    down_gradient(1)
    back.stage(1)
    down_gradient(2)
    down_gradient(3)
    scatter_d.start()
    branch = LineSum(here, part_f, branch_bufs)
    ffn_rows(other, squares, wd_v, part_f, False)
    branch.start()
    back.stage(2)
    ffn_rows(here.c, squares, wd_v, part_f, False)
    load_n1 = load(n1, wd_v.at[0:2])
    load_o = load(wo, wd_v.at[2:3])
    grad_n2 = back.result().astype(BF16).astype(F32)
    back.finish()
    hat, inv_std = normed(mid[...])
    grad_mid, gain_sum, shift_sum = norm_back(grad_n2, hat, inv_std, norm_row(packs, 2))
    grad_mid = cot[here.c, place, :].astype(F32) + grad_mid
    dmid[...] = grad_mid
    gm[pl.ds(here.c, 1), place, :] = grad_mid.astype(BF16)[None]
    gather = LineGather(here, lambda z: gm.at[here.c, block(z, ROWS), :], gm_sem)
    gather.start()
    early_u.middle()
    early_d.middle()

    def shared(z):
        spot = gm.at[here.c, block(z, ROWS), :]
        return pltpu.make_async_remote_copy(
            src_ref=spot,
            dst_ref=spot,
            send_sem=gm_pair.at[0, z],
            recv_sem=gm_pair.at[1, z],
            device_id=here.plane(*PARTNER),
            device_id_type=MESH,
        )

    shared(here.z).start()
    sums[0:1, :] = gain_sum
    sums[1:2, :] = shift_sum
    gather.onward(0, lambda z: shared(z).start())
    branch.stage(0)
    gather.onward(1, lambda z: shared(z).start())
    gather.onward(2, lambda z: shared(z).start())
    branch.stage(1)
    scatter_u.middle()
    for copy in small:
        copy.wait()
    load_o.wait()
    load_q.wait()
    load_n1.wait()
    gather.finish()
    for z in range(4):
        shared(z).wait()
    head0 = here.z * 4 + here.c * 2
    attend_back_body(head0, gm, qkva, wu_v, wd_v.at[2], tables, dp, part)
    branch.stage(2)
    last = LineSum(here, part, back_bufs)
    attend_back_rows(other, dp, wu_v, part)
    last.start()
    attend_back_rows(here.c, dp, wu_v, part)
    last.stage(0)
    scatter_d.middle()
    rows_in = wd_v[0:2].reshape(2 * length, width)
    for j in range(3):
        gq[j] = dot(rows_in, dp[j], ((0,), (0,))).astype(BF16)
    scatter_q.start()
    last.stage(1)
    go[0] = dot(qkva[3], gm[...].reshape(2 * length, width), ((0,), (0,))).astype(BF16)
    scatter_o.start()
    early_u.last()
    early_d.last()
    last.stage(2)
    out_v[place, :] = (mid[...] + branch.result().astype(BF16).astype(F32)).astype(BF16)
    spread = LineGather(here, lambda z: out_v.at[block(z, ROWS), :], out_sem)
    spread.start()
    scatter_u.last()
    spread.onward(0)
    grad_n1 = last.result()
    hat, inv_std = normed(tok_own[...].astype(F32))
    grad_in, gain_sum, shift_sum = norm_back(grad_n1, hat, inv_std, norm_row(packs, 0))
    ig_own[...] = (dmid[...] + grad_in).astype(BF16)
    norm_copies = norm_share(
        here, jnp.concatenate([gain_sum, shift_sum, sums[...]], 0), norm_bufs
    )
    scatter_q.middle()
    scatter_o.middle()
    spread.onward(1)
    spread.onward(2)
    keep = pltpu.make_async_copy(out_v, out_all, keep_sem)
    keep.start()
    onward = norm_share_along(here, norm_copies, norm_bufs)
    scatter_d.last()
    for copy in onward:
        copy.wait()
    heard_z = norm_bufs[3]
    norm_total[...] = ((heard_z[0] + heard_z[1]) + heard_z[2]) + heard_z[3]
    early_u.sent()
    scatter_u.sent()
    scatter_q.last()
    scatter_o.last()
    branch.finish()
    last.finish()
    spread.finish()
    keep.wait()
    for scatter in (early_d, scatter_d, scatter_q, scatter_o):
        scatter.sent()
    for scatter in scatters:
        scatter.finish()


def back_call(n2, cot, tables, packs, mid, tok, wq, wo, wu, wd, n1, rows):
    _, length, width = n2.shape
    both = pltpu.VMEM((2, length, width), BF16)
    results = pl.pallas_call(
        back_kernel,
        out_shape=[
            jax.ShapeDtypeStruct((length, width), BF16),
            jax.ShapeDtypeStruct((ROWS, width), BF16),
            jax.ShapeDtypeStruct((8, CHUNK), F32),
            jax.ShapeDtypeStruct((3, CHUNK, 2 * CHUNK), F32),
            jax.ShapeDtypeStruct((1, 2 * CHUNK, CHUNK), F32),
            jax.ShapeDtypeStruct((4, CHUNK, 2 * CHUNK), F32),
            jax.ShapeDtypeStruct((4, 2 * CHUNK, CHUNK), F32),
        ],
        in_specs=[VM] * 5 + [ANY] * 10,
        out_specs=[ANY, VM, VM, ANY, ANY, ANY, ANY],
        scratch_shapes=[
            pltpu.VMEM(wu.shape, BF16),
            pltpu.VMEM(wd.shape, BF16),
            pltpu.VMEM((4, 2 * length, CHUNK), BF16),
            pltpu.VMEM((ROWS, width), BF16),
            pltpu.SemaphoreType.DMA((16,)),
            pltpu.VMEM((4, 2 * length, CHUNK), BF16),
            pltpu.VMEM((4, 2 * length, CHUNK), BF16),
            both,
            both,
            pltpu.VMEM((3, 2 * length, CHUNK), BF16),
            pltpu.VMEM(wu.shape, BF16),
            pltpu.VMEM(wd.shape, BF16),
            pltpu.VMEM(wq.shape, BF16),
            pltpu.VMEM(wo.shape, BF16),
            both,
            pltpu.VMEM((ROWS, width), F32),
            pltpu.VMEM((2, width), F32),
            pltpu.VMEM((length, width), BF16),
        ]
        + line_scratch(length, width) * 2
        + [pltpu.VMEM((2, 4, CHUNK, CHUNK), F32)] * 2
        + [
            pltpu.SemaphoreType.DMA((2, 2, 3)),
            pltpu.SemaphoreType.DMA((2, 4)),
            pltpu.SemaphoreType.DMA((2, 2, 3)),
            pltpu.SemaphoreType.DMA,
            pltpu.VMEM((8, 8, CHUNK), F32),
            pltpu.VMEM((7, 8, CHUNK), F32),
            pltpu.VMEM((8, CHUNK), F32),
            pltpu.VMEM((4, 8, CHUNK), F32),
            pltpu.SemaphoreType.DMA((2, 7)),
            pltpu.SemaphoreType.DMA((2, 3)),
        ]
        + (scatter_scratch(1) * 2 + scatter_scratch(3) * 2)
        + scatter_scratch(3)
        + scatter_scratch(1),
        compiler_params=params(3),
        name="back",
    )(n2, cot, tables, packs, mid, tok, wq, wo, wu, wd, n1, *rows)
    return results


FIRST_SCALE = 1.0 / (1.0 - BETA_FIRST**STEP)
SECOND_SCALE = 1.0 / (1.0 - BETA_SECOND**STEP)


def folded(values):
    rows, cols = values.shape
    total = None
    for i in range(rows // 8):
        for j in range(cols // 128):
            tile = values[i * 8 : i * 8 + 8, j * 128 : j * 128 + 128]
            total = tile if total is None else total + tile
    return total


def updated(weight, gradient, first_old, second_old):
    first_new = BETA_FIRST * first_old + (1.0 - BETA_FIRST) * gradient
    second_new = BETA_SECOND * second_old + (1.0 - BETA_SECOND) * gradient * gradient
    update = first_new * FIRST_SCALE / (
        jnp.sqrt(second_new * SECOND_SCALE) + ADAM_EPS
    ) + WEIGHT_DECAY * weight
    return (update, first_new, second_new)


AHEAD = 4


def adam_kernel(*refs):
    sources = [refs[kind * 5 : kind * 5 + 4] for kind in range(4)]
    norm_grad, norm_master, norm_first, norm_second = [refs[kind * 5 + 4] for kind in range(4)]
    out_all = refs[20]
    outs = [refs[21 + kind * 5 : 25 + kind * 5] for kind in range(3)]
    norm_outs = [refs[25 + kind * 5] for kind in range(3)]
    tile, output = refs[36:38]
    held = [refs[38 + kind * 4 : 42 + kind * 4] for kind in range(4)]
    load_sem, store_sem = refs[54:56]
    blocks = [(i, j) for i in range(4) for j in range(sources[0][i].shape[0])]
    bases = [sum(source.shape[0] for source in sources[0][:i]) for i in range(4)]

    def loading(kind, i, j):
        return pltpu.make_async_copy(
            sources[kind][i].at[j], held[kind][i].at[j], load_sem.at[kind, bases[i] + j]
        )

    def storing(kind, i, j):
        return pltpu.make_async_copy(
            held[(0, 2, 3)[kind]][i].at[j], outs[kind][i].at[j], store_sem.at[kind, bases[i] + j]
        )

    for i, j in blocks:
        for kind in range(4):
            loading(kind, i, j).start()
    output[...] = out_all[...].astype(F32)
    weight = norm_master[...]
    update, first_new, second_new = updated(
        weight, norm_grad[0:4, :], norm_first[...], norm_second[...]
    )
    for out, value in zip(norm_outs, (update, first_new, second_new)):
        out[...] = value
    for row, value in ((4, weight), (12, update)):
        square = value * value * 0.25
        tile[row : row + 4, :] = square[:, :128] + square[:, 128:]
    for i in range(4):
        grads, masters, firsts, seconds = [held[kind][i] for kind in range(4)]

        def one_block(j, sums):
            for kind in range(4):
                loading(kind, i, j).wait()

            def step(k, carry):
                at = pl.ds(pl.multiple_of(k * 32, 32), 32)
                weight = masters[j, at, :]
                update, first_new, second_new = updated(
                    weight, grads[j, at, :], firsts[j, at, :], seconds[j, at, :]
                )
                grads[j, at, :] = update
                firsts[j, at, :] = first_new
                seconds[j, at, :] = second_new
                return (carry[0] + folded(weight * weight), carry[1] + folded(update * update))

            sums = lax.fori_loop(0, grads.shape[1] // 32, step, sums)
            for kind in range(3):
                storing(kind, i, j).start()
            return sums

        zero = jnp.zeros((8, 128), F32)
        sums = lax.fori_loop(0, grads.shape[0], one_block, (zero, zero))
        tile[i : i + 1, :] = jnp.sum(sums[0], 0, keepdims=True)
        tile[8 + i : 9 + i, :] = jnp.sum(sums[1], 0, keepdims=True)
    for i, j in blocks:
        for kind in range(3):
            storing(kind, i, j).wait()


def adam_call(grads, masters, firsts, seconds, out_all):
    shapes = [master.shape for master in masters]
    like = [jax.ShapeDtypeStruct(shape, F32) for shape in shapes]
    specs = [ANY] * 4 + [VM]
    count = sum(shape[0] for shape in shapes[:4])
    results = pl.pallas_call(
        adam_kernel,
        out_shape=like * 3
        + [jax.ShapeDtypeStruct((16, 128), F32), jax.ShapeDtypeStruct(out_all.shape, F32)],
        in_specs=specs * 4 + [VM],
        out_specs=specs * 3 + [VM, VM],
        scratch_shapes=[pltpu.VMEM(shape, F32) for shape in shapes[:4]] * 4
        + [pltpu.SemaphoreType.DMA((4, count)), pltpu.SemaphoreType.DMA((3, count))],
        compiler_params=local_params(60),
        name="adam",
    )(*grads, *masters, *firsts, *seconds, out_all)
    return results[0:5], results[5:10], results[10:15], results[15], results[16]


def total_kernel(tile, norms, tiles_z, plane_tile, tiles, zs, ps):
    here = Here()
    greet(here, PLANE, (1, 2, 3))
    sent = []
    for step in (2, 1, 3):
        sent.append(
            push(tile, tiles_z.at[here.z], zs.at[0, step - 1], zs.at[1, step - 1], here.along(step))
        )
    tiles_z[pl.ds(here.z, 1)] = tile[...][None]
    for copy in sent:
        copy.wait()
    plane_tile[...] = ((tiles_z[0] + tiles_z[1]) + tiles_z[2]) + tiles_z[3]
    me = here.chunk(0, 0, 0)
    sent = []
    for index, peer in enumerate(PLANE):
        sent.append(
            push(plane_tile, tiles.at[me], ps.at[0, index], ps.at[1, index], here.plane(*peer))
        )
    tiles[pl.ds(me, 1)] = plane_tile[...][None]
    for copy in sent:
        copy.wait()
    total = tiles[0]
    for k in range(1, 8):
        total = total + tiles[k]
    roots = jnp.sqrt(jnp.sum(total, 1, keepdims=True))
    norms[...] = jnp.broadcast_to(roots, norms.shape)


def total_call(tile):
    return pl.pallas_call(
        total_kernel,
        out_shape=jax.ShapeDtypeStruct((16, 128), F32),
        in_specs=[VM],
        out_specs=VM,
        scratch_shapes=[
            pltpu.VMEM((4, 16, 128), F32),
            pltpu.VMEM((16, 128), F32),
            pltpu.VMEM((8, 16, 128), F32),
            pltpu.SemaphoreType.DMA((2, 3)),
            pltpu.SemaphoreType.DMA((2, 7)),
        ],
        compiler_params=params(5),
        name="norm_totals",
    )(tile)


def weight_kernel(*refs):
    norms, updates, masters, packs = refs[0], refs[1:6], refs[6:11], refs[11]
    ig_rows = refs[12:16]
    outs = refs[16:21]
    igrad, lamb_norms, share = refs[21:24]
    held = (refs[24:28], refs[28:32])
    load_sem, store_sem = refs[32:34]
    blocks = [(i, j) for i in range(4) for j in range(updates[i].shape[0])]
    loads = []

    def load():
        index = len(loads)
        if index == len(blocks):
            return
        i, j = blocks[index]
        loads.append([])
        for kind, source in enumerate((updates, masters)):
            copy = pltpu.make_async_copy(
                source[i].at[j], held[kind][i].at[j], load_sem.at[kind, index]
            )
            copy.start()
            loads[index].append(copy)

    for _ in range(AHEAD):
        load()
    scales = LEARN_RATE * (norms[0:8, 0:1] / norms[8:16, 0:1])
    outs[4][...] = masters[4][...] - scales[4:8, :] * updates[4][...]
    row = lax.broadcasted_iota(jnp.int32, norms.shape, 0)
    lane = lax.broadcasted_iota(jnp.int32, norms.shape, 1)
    flat = jnp.sum(jnp.where(row == lane, norms[...], 0.0), 0, keepdims=True)
    lamb_norms[0:1, :] = flat[:, 0:8]
    lamb_norms[1:2, :] = flat[:, 8:16]
    counts = packs[0, 4:5, :]
    for k in range(1, 8):
        counts = counts + packs[k, 4:5, :]
    share[...] = counts[:, 0:4] / (igrad.shape[0] * 8)
    here = Here()
    for step in range(4):
        igrad[block(here.behind(step), ROWS), :] = ig_rows[step][...].astype(F32)
    stores = []
    for index, (i, j) in enumerate(blocks):
        for copy in loads[index]:
            copy.wait()
        load()
        scale = scales[i : i + 1, :]

        def step(k, carry):
            at = pl.ds(pl.multiple_of(k * 32, 32), 32)
            held[1][i][j, at, :] = held[1][i][j, at, :] - scale * held[0][i][j, at, :]
            return carry

        lax.fori_loop(0, held[1][i].shape[1] // 32, step, 0)
        copy = pltpu.make_async_copy(held[1][i].at[j], outs[i].at[j], store_sem.at[index])
        copy.start()
        stores.append(copy)
    for copy in stores:
        copy.wait()


def weight_call(norms, updates, masters, packs, ig_rows):
    shapes = [master.shape for master in masters]
    specs = [ANY] * 4 + [VM]
    count = sum(shape[0] for shape in shapes[:4])
    rows, width = ig_rows[0].shape
    return pl.pallas_call(
        weight_kernel,
        out_shape=[jax.ShapeDtypeStruct(shape, F32) for shape in shapes]
        + [
            jax.ShapeDtypeStruct((4 * rows, width), F32),
            jax.ShapeDtypeStruct((2, 8), F32),
            jax.ShapeDtypeStruct((1, 4), F32),
        ],
        in_specs=[VM] + specs * 2 + [VM] * 5,
        out_specs=specs + [VM, VM, VM],
        scratch_shapes=[pltpu.VMEM(shape, F32) for shape in shapes[:4]] * 2
        + [pltpu.SemaphoreType.DMA((2, count)), pltpu.SemaphoreType.DMA((count,))],
        compiler_params=local_params(60),
        name="new_weights",
    )(norms, *updates, *masters, packs, *ig_rows)


def turn(values, cosine, sine):
    return values * cosine + pltpu.roll(values, HEAD_DIM // 2, 1) * sine


def dot(left, right, dims=((1,), (0,))):
    return lax.dot_general(left, right, (dims, ((), ())), preferred_element_type=F32)


def attention_weights(queries, key_rows, lowest):
    scores = dot(queries, key_rows, ((1,), (1,)))
    row = lax.broadcasted_iota(jnp.int32, scores.shape, 0)
    col = lax.broadcasted_iota(jnp.int32, scores.shape, 1)
    allowed = (col <= row) & (col.astype(F32) >= lowest)
    scores = jnp.where(allowed, scores, MASKED)
    exp_scores = jnp.exp(scores - jnp.max(scores, -1, keepdims=True))
    return exp_scores / jnp.sum(exp_scores, -1, keepdims=True)


def attend_body(head0, n1, wq, wo, tables, q_out, k_out, v_out, a_out, part):
    length = tables.shape[2]
    rows_in = n1[...].reshape(2 * length, n1.shape[2])
    projected = [dot(rows_in, wq[j]) for j in range(3)]
    for s in range(2):
        rows = slice(s * length, (s + 1) * length)
        cosine, sine = tables[s, 0], tables[s, 1]
        lowest = tables[s, 2, :, 0:1]
        for h in range(2):
            cols = slice(h * HEAD_DIM, (h + 1) * HEAD_DIM)
            queries = (turn(projected[0][rows, cols], cosine, sine) * HEAD_DIM ** (-0.5)).astype(BF16)
            key_rows = turn(projected[1][rows, cols], cosine, sine).astype(BF16)
            value_rows = projected[2][rows, cols].astype(BF16)
            weights = attention_weights(queries, key_rows, lowest).astype(BF16)
            heads = dot(weights, value_rows)
            active = tables[s, 4] > (head0 + h).astype(F32)
            q_out[rows, cols] = queries
            k_out[rows, cols] = key_rows
            v_out[rows, cols] = value_rows
            a_out[rows, cols] = jnp.where(active, heads, 0.0).astype(BF16)


def attend_out(a_out, wo, part, s):
    length = part.shape[1]
    part[s] = dot(a_out[pl.ds(pl.multiple_of(s * length, length), length), :], wo[0]).astype(BF16)


def fill_table(table, position, bucket, head_count):
    length = table.shape[1]
    row = lax.broadcasted_iota(jnp.int32, (length, length), 0)
    col = lax.broadcasted_iota(jnp.int32, (length, length), 1)

    def column(values):
        return jnp.sum(jnp.where(row == col, values.astype(F32), 0.0), 1, keepdims=True)

    place = column(position)
    lane = lax.broadcasted_iota(jnp.int32, (length, HALF), 1)
    half = HEAD_DIM // 2
    second = lane >= half
    freq_index = jnp.where(second, lane - half, lane).astype(F32)
    angles = place * jnp.exp(freq_index * (-2.0 * math.log(ROPE_BASE) / HEAD_DIM))
    table[0] = jnp.cos(angles)
    sine = jnp.sin(angles)
    table[1] = jnp.where(second, sine, -sine)
    index = lax.broadcasted_iota(jnp.int32, (length, HALF), 0).astype(F32)
    table[2] = index - place
    table[3] = jnp.broadcast_to(column(bucket), (length, HALF))
    table[4] = jnp.broadcast_to(head_count.astype(F32), (length, HALF))


def local_params(limit):
    return pltpu.CompilerParams(vmem_limit_bytes=limit << 20)


def fast_body(
    tokens, cotangent, head_counts, positions, buckets,
    in_master, out_master, up_master, down_master, norm_master,
    in_first, out_first, up_first, down_first, norm_first,
    in_second, out_second, up_second, down_second, norm_second,
):
    tok, cot = tokens[0], cotangent[0]
    (n1, both_cot, tables, packs, n2, mid, q_rows, k_rows, v_rows, a_rows), (wq, wo, wu, wd) = front_call(
        head_counts, positions, buckets, tok, cot, norm_master,
        (in_master, out_master[None], up_master, down_master),
    )
    out_all, ig_own, norm_sum, in_sum, out_sum, up_sum, down_sum = back_call(
        n2, both_cot, tables, packs, mid, tok, wq, wo, wu, wd, n1,
        (q_rows, k_rows, v_rows, a_rows),
    )
    ig_rows = [ig_own] + [
        lax.ppermute(ig_own, "tensor", [(i, (i + step) % 4) for i in range(4)])
        for step in (1, 2, 3)
    ]
    masters = (in_master, out_master[None], up_master, down_master, norm_master)
    firsts = (in_first, out_first[None], up_first, down_first, norm_first)
    seconds = (in_second, out_second[None], up_second, down_second, norm_second)
    updates, moments, squares, tile, output = adam_call(
        (in_sum, out_sum, up_sum, down_sum, norm_sum), masters, firsts, seconds, out_all
    )
    norms = total_call(tile)
    *weights, input_grad, lamb_norms, share = weight_call(
        norms, updates, masters, packs, ig_rows
    )
    flat = lambda group: (group[0], group[1][0], group[2], group[3], group[4])
    return (
        output[None],
        input_grad[None],
        share[0],
        lamb_norms,
        *flat(weights),
        *flat(moments),
        *flat(squares),
    )


def solution(mesh):
    placed = (
        P(("dp", "expert"), None, None),
        P(("dp", "expert"), None, None),
        P(("dp", "expert")),
        P(("dp", "expert"), None),
        P(("dp", "expert"), None),
        P(None, ("dp", "expert"), "tensor"),
        P("tensor", ("dp", "expert")),
        P(None, ("dp", "expert"), "tensor"),
        P(None, "tensor", ("dp", "expert")),
        P(None, ("dp", "expert")),
        P(None, ("dp", "expert"), "tensor"),
        P("tensor", ("dp", "expert")),
        P(None, ("dp", "expert"), "tensor"),
        P(None, "tensor", ("dp", "expert")),
        P(None, ("dp", "expert")),
        P(None, ("dp", "expert"), "tensor"),
        P("tensor", ("dp", "expert")),
        P(None, ("dp", "expert"), "tensor"),
        P(None, "tensor", ("dp", "expert")),
        P(None, ("dp", "expert")),
    )
    shape = dict(mesh.shape)
    fits = shape == {"dp": 4, "expert": 2, "tensor": 4}
    return jax.shard_map(
        fast_body if fits else body,
        mesh=mesh,
        in_specs=placed,
        out_specs=(
            P(("dp", "expert"), None, None),
            P(("dp", "expert"), None, None),
            P(),
            P(),
            P(None, ("dp", "expert"), "tensor"),
            P("tensor", ("dp", "expert")),
            P(None, ("dp", "expert"), "tensor"),
            P(None, "tensor", ("dp", "expert")),
            P(None, ("dp", "expert")),
            P(None, ("dp", "expert"), "tensor"),
            P("tensor", ("dp", "expert")),
            P(None, ("dp", "expert"), "tensor"),
            P(None, "tensor", ("dp", "expert")),
            P(None, ("dp", "expert")),
            P(None, ("dp", "expert"), "tensor"),
            P("tensor", ("dp", "expert")),
            P(None, ("dp", "expert"), "tensor"),
            P(None, "tensor", ("dp", "expert")),
            P(None, ("dp", "expert")),
        ),
        check_vma=False,
    )
```
